32 devices in a mesh: seq: 4 (over x, core), fsdp: 8 (over z, y).
Axes of the slice: x: 2, y: 2, z: 4, core: 2. Of those that a mesh axis runs over, the one named last changes fastest.
Arguments:
- inputs: bfloat16 [8, 1024, 2048], P('fsdp', 'seq'), may hold values from -6 to 6
- query_weight: bfloat16 [2048, 2048], P('fsdp'), may hold values from -0.125 to 0.125
- key_weight: bfloat16 [2048, 512], P('fsdp'), may hold values from -0.125 to 0.125
- value_weight: bfloat16 [2048, 512], P('fsdp'), may hold values from -0.125 to 0.125
- output_weight: bfloat16 [2048, 2048], P('fsdp'), may hold values from -0.5 to 0.5
- gate_weight: bfloat16 [8192, 2048], P('fsdp'), may hold values from -0.125 to 0.125
- up_weight: bfloat16 [8192, 2048], P('fsdp'), may hold values from -0.125 to 0.125
- down_weight: bfloat16 [8192, 2048], P('fsdp'), may hold values from -0.0625 to 0.0625
- gain_attn: bfloat16 [2048], P('fsdp'), may hold values from 0.099609375 to 1.8984375
- gain_ffn: bfloat16 [2048], P('fsdp'), may hold values from 0.099609375 to 1.8984375
- cotangent: bfloat16 [8, 1024, 2048], P('fsdp', 'seq'), may hold values from -6 to 6
Outputs:
- outputs: bfloat16 [8, 1024, 2048], P('fsdp', 'seq')
- grad_inputs: bfloat16 [8, 1024, 2048], P('fsdp', 'seq')
- grad_w_query: float32 [2048, 2048], P('fsdp')
- grad_w_key: float32 [2048, 512], P('fsdp')
- grad_w_value: float32 [2048, 512], P('fsdp')
- grad_w_out: float32 [2048, 2048], P('fsdp')
- grad_w_gate: float32 [8192, 2048], P('fsdp')
- grad_w_up: float32 [8192, 2048], P('fsdp')
- grad_w_down: float32 [8192, 2048], P('fsdp')
- grad_gain_attn: float32 [2048], P('fsdp')
- grad_gain_ffn: float32 [2048], P('fsdp')
The draws below stay inside these ranges and needn't reach their ends.
All inputs are finite; a program needn't handle non-finite values.
Results may differ from the reference program's by a relative error of at most 0.02.
Values may be sent and summed in bfloat16 or wider, within the bound.
No kernel may reach another device: no remote copies, remote signals or barrier semaphores. Data moves between devices by JAX's collectives and lax.ppermute only.
A program may use at most 512 MiB of HBM per device.

```python
import math
import jax
import jax.numpy as jnp
from jax import lax

D = 2048
H = 32
KVH = 8
HD = 64
FF = 8192
SEQ_LEN = 1024
BLOCK = 256
QW = 2048
KVW = 512
BATCH = 8


def level_of(key, extent, shards, smallest, top_value):
    def one(position, blocks):
        steps = jax.random.uniform(jax.random.fold_in(jax.random.fold_in(key, 6), position), (blocks,), jnp.float32, smallest / len(shards), top_value / len(shards))
        return jnp.repeat(jnp.exp(steps), extent[position] // blocks).reshape((-1,) + (1,) * (len(extent) - position - 1))

    level = one(*shards[0])
    for cut in shards[1:]:
        level = level * one(*cut)
    return level


def normal_values(key, extent, scale, bound, cuts=(), kind=jnp.bfloat16):
    level = level_of(key, extent, cuts, -0.22, 0.18) if cuts else 1.0
    values = jax.random.normal(key, extent, jnp.float32) * scale * level
    return jnp.minimum(jnp.maximum(values, -bound), bound).astype(kind)


def setup_inputs(seed: int = 0) -> dict:
    arg_keys = jax.random.split(jax.random.key(seed), 12)
    return {
        "inputs": normal_values(arg_keys[0], (BATCH, SEQ_LEN, D), 1.0, 6.0, ((0, 8), (1, 4))),
        "query_weight": normal_values(arg_keys[1], (D, QW), D ** -0.5, 0.125, ((0, 8),)),
        "key_weight": normal_values(arg_keys[2], (D, KVW), D ** -0.5, 0.125, ((0, 8),)),
        "value_weight": normal_values(arg_keys[3], (D, KVW), D ** -0.5, 0.125, ((0, 8),)),
        "output_weight": normal_values(arg_keys[4], (QW, D), (QW // 16) ** -0.5, 0.5, ((0, 8),)),
        "gate_weight": normal_values(arg_keys[5], (FF, D), D ** -0.5, 0.125, ((0, 8),)),
        "up_weight": normal_values(arg_keys[6], (FF, D), D ** -0.5, 0.125, ((0, 8),)),
        "down_weight": normal_values(arg_keys[7], (FF, D), FF ** -0.5, 0.0625, ((0, 8),)),
        "gain_attn": jnp.clip(1.0 + 0.18 * jax.random.normal(arg_keys[8], (D,), jnp.float32), 0.099609375, 1.8984375).astype(jnp.bfloat16),
        "gain_ffn": jnp.clip(1.0 + 0.18 * jax.random.normal(arg_keys[9], (D,), jnp.float32), 0.099609375, 1.8984375).astype(jnp.bfloat16),
        "cotangent": normal_values(arg_keys[10], (BATCH, SEQ_LEN, D), 1.0, 6.0, ((0, 8), (1, 4))),
    }


EPSILON = 1e-05
THETA = 500000.0
TOP_PRECISION = lax.Precision.HIGHEST

@jax.custom_vjp
def reduced_input(v):
    return lax.optimization_barrier(v.astype(jnp.bfloat16)).astype(jnp.float32)

@jax.custom_vjp
def reduced_gradient(v):
    return v

def low_keep(v):
    return (reduced_input(v), None)

def low_pass(kept, grad):
    return (grad,)

def back_keep(v):
    return (v, None)

def back_low(kept, grad):
    return (reduced_input(grad),)
reduced_input.defvjp(low_keep, low_pass)
reduced_gradient.defvjp(back_keep, back_low)

def rms_scale(values, gain):
    return values * lax.rsqrt(lax.optimization_barrier(jnp.mean(values * values, axis=-1, keepdims=True)) + EPSILON) * gain

def rope_tables(positions):
    frequency = THETA ** (-(jnp.arange(HD // 2, dtype=jnp.float32) * 2.0) / HD)
    angles = positions.astype(jnp.float32)[:, None] * frequency[None, :]
    return (jnp.cos(angles), jnp.sin(angles))

def rotate(values, cos_table, sin_table):
    dims_in = values.shape
    pieces = values.reshape(dims_in[:-1] + (dims_in[-1] // HD, HD))
    half_one = pieces[..., :HD // 2]
    half_two = pieces[..., HD // 2:]
    cos_part = cos_table[:, None, :]
    sin_part = sin_table[:, None, :]
    turned = jnp.concatenate((half_one * cos_part - half_two * sin_part, half_two * cos_part + half_one * sin_part), axis=-1)
    return turned.reshape(dims_in)

def head_group(packed):
    query_block, key_one, value_one = packed
    group_size = query_block.shape[1] // HD
    query_heads = query_block.reshape(SEQ_LEN, group_size, HD)
    raw_scores = jnp.einsum('qgd,kd->gqk', query_heads, key_one, precision=TOP_PRECISION) * HD ** (-0.5)
    blocks = jnp.arange(SEQ_LEN) // BLOCK
    allowed = blocks[None, :] <= blocks[:, None]
    scores = reduced_gradient(jnp.where(allowed[None], raw_scores, -1000000000.0))
    soft_weights = reduced_input(jax.nn.softmax(scores, axis=-1))
    attn_out = jnp.einsum('gqk,kd->qgd', soft_weights, value_one, precision=TOP_PRECISION)
    return attn_out.reshape(SEQ_LEN, group_size * HD)

def attention(query_rows, keys_all, values_all):
    seq_count = query_rows.shape[0]
    group_size = H // KVH
    query_items = query_rows.reshape(seq_count, SEQ_LEN, KVH, group_size * HD).transpose(0, 2, 1, 3).reshape(seq_count * KVH, SEQ_LEN, group_size * HD)
    key_items = keys_all.reshape(seq_count, SEQ_LEN, KVH, HD).transpose(0, 2, 1, 3).reshape(seq_count * KVH, SEQ_LEN, HD)
    value_items = values_all.reshape(seq_count, SEQ_LEN, KVH, HD).transpose(0, 2, 1, 3).reshape(seq_count * KVH, SEQ_LEN, HD)
    attn_out = lax.map(jax.checkpoint(head_group), (query_items, key_items, value_items))
    return attn_out.reshape(seq_count, KVH, SEQ_LEN, group_size * HD).transpose(0, 2, 1, 3).reshape(seq_count, SEQ_LEN, H * HD)

def block_forward(partial_input, query_weight, key_weight, value_weight, output_weight, gate_weight, up_weight, down_weight, gain_attn, gain_ffn):
    cos_table, sin_table = rope_tables(jnp.arange(SEQ_LEN))
    attention_normed = reduced_input(rms_scale(partial_input, gain_attn))
    query_rows = reduced_gradient(jnp.einsum('pvq,qy->pvy', attention_normed, query_weight, precision=TOP_PRECISION))
    key_matrix = reduced_gradient(jnp.einsum('pvq,qy->pvy', attention_normed, key_weight, precision=TOP_PRECISION))
    value_matrix = reduced_input(reduced_gradient(jnp.einsum('pvq,qy->pvy', attention_normed, value_weight, precision=TOP_PRECISION)))
    query_rows = reduced_input(reduced_gradient(rotate(query_rows, cos_table, sin_table)))
    key_matrix = reduced_input(reduced_gradient(rotate(key_matrix, cos_table, sin_table)))
    attention_result = reduced_input(reduced_gradient(attention(query_rows, key_matrix, value_matrix)))
    residual_stream = partial_input + reduced_gradient(jnp.einsum('wzv,vh->wzh', attention_result, output_weight, precision=TOP_PRECISION))
    feedforward_normed = reduced_input(rms_scale(residual_stream, gain_ffn))
    gate_activation = reduced_gradient(jnp.einsum('irc,bc->irb', feedforward_normed, gate_weight, precision=TOP_PRECISION))
    up_activation = reduced_gradient(jnp.einsum('irc,bc->irb', feedforward_normed, up_weight, precision=TOP_PRECISION))
    hidden_state = reduced_input(jax.nn.silu(gate_activation) * up_activation)
    return residual_stream + reduced_gradient(jnp.einsum('okb,bg->okg', hidden_state, down_weight, precision=TOP_PRECISION))

def reference(inputs, query_weight, key_weight, value_weight, output_weight, gate_weight, up_weight, down_weight, gain_attn, gain_ffn, cotangent):
    params = tuple((matrix.astype(jnp.float32) for matrix in (query_weight, key_weight, value_weight, output_weight, gate_weight, up_weight, down_weight, gain_attn, gain_ffn)))
    group_seqs = math.gcd(BATCH, 4)
    rounds = BATCH // group_seqs
    stacked_in = inputs.astype(jnp.float32).reshape(rounds, group_seqs, SEQ_LEN, D)
    stacked_grad = cotangent.astype(jnp.float32).reshape(rounds, group_seqs, SEQ_LEN, D)

    def one_group(totals, pair):
        partial_input, part_grad = pair
        result, pull_back = jax.vjp(block_forward, partial_input, *params)
        grads = pull_back(part_grad)
        new_totals = tuple((left + right for left, right in zip(totals, grads[1:])))
        return (new_totals, (result.astype(jnp.bfloat16), grads[0].astype(jnp.bfloat16)))
    start_totals = tuple((jnp.zeros_like(param) for param in params))
    totals, (outs_main, outs_grad) = lax.scan(one_group, start_totals, (stacked_in, stacked_grad))
    return (outs_main.reshape(BATCH, SEQ_LEN, D), outs_grad.reshape(BATCH, SEQ_LEN, D), totals[0], totals[1], totals[2], totals[3], totals[4], totals[5], totals[6], totals[7], totals[8])
```

```python
from functools import partial

import jax
import jax.numpy as jnp
from jax import lax
from jax.sharding import PartitionSpec as P

KVH = 8
HD = 64
BLOCK = 256
LINE = 4

EPSILON = 1e-05
THETA = 500000.0
MASKED = -1000000000.0

BF = jnp.bfloat16
F32 = jnp.float32


def product(left, right):
    return jnp.dot(left, right, preferred_element_type=F32)


def left_product(left, right):
    return lax.dot_general(left, right, (((0,), (0,)), ((), ())), preferred_element_type=F32)


def right_product(left, right):
    return lax.dot_general(left, right, (((1,), (1,)), ((), ())), preferred_element_type=F32)


def after(value, *others):
    return lax.optimization_barrier((value,) + others)[0]


def columns():
    return lax.axis_size("fsdp") // LINE


def z_next(value):
    cols = columns()
    count = lax.axis_size("fsdp")
    return lax.ppermute(value, "fsdp", [(i, (i + cols) % count) for i in range(count)])


def y_next(value):
    cols = columns()
    count = lax.axis_size("fsdp")
    return lax.ppermute(
        value, "fsdp", [(i, i // cols * cols + (i + 1) % cols) for i in range(count)]
    )


def seq_swap(value, bit):
    return lax.ppermute(value, "seq", [(i, i ^ bit) for i in range(lax.axis_size("seq"))])


def core_swap(value):
    return seq_swap(value, 1)


def x_swap(value):
    return seq_swap(value, 2)


def ring_gather(value, step, count):
    pieces = [value]
    for _ in range(count - 1):
        pieces.append(step(pieces[-1]))
    return pieces


def ring_scatter(part_of, step, count):
    total = None
    for j in list(range(1, count)) + [0]:
        total = part_of(j) if total is None else part_of(j) + total.astype(F32)
        if j:
            total = step(total.astype(BF))
    return total


def all_sum(value):
    bit = 1
    while bit < lax.axis_size("seq"):
        value = value + seq_swap(value, bit)
        bit *= 2
    count = lax.axis_size("fsdp")
    bit = 1
    while bit < count:
        value = value + lax.ppermute(value, "fsdp", [(i, i ^ bit) for i in range(count)])
        bit *= 2
    return value


def half_of(array, which, axis=1):
    size = array.shape[axis] // 2
    return lax.dynamic_slice_in_dim(array, which * size, size, axis)


def join_halves(mine, other, core):
    return jnp.where(
        core == 0,
        jnp.concatenate([mine, other], axis=1),
        jnp.concatenate([other, mine], axis=1),
    )


def gather_rows(shard, core, z, y):
    cols = columns()
    rows, width = shard.shape
    half = width // 2
    full = jnp.zeros((rows * LINE * cols, width), shard.dtype)
    z_pieces = ring_gather(half_of(shard, core), z_next, LINE)
    for j, piece in enumerate(z_pieces):
        for k, sub in enumerate(ring_gather(piece, y_next, cols)):
            row = (((z - j) % LINE) * cols + (y - k) % cols) * rows
            full = lax.dynamic_update_slice(full, sub, (row, core * half))
            full = lax.dynamic_update_slice(full, core_swap(sub), (row, (1 - core) * half))
    return full


def gather_columns(shard, core, y):
    cols = columns()
    pieces = [shard]
    for piece in ring_gather(half_of(shard, core), y_next, cols)[1:]:
        pieces.append(join_halves(piece, core_swap(piece), core))
    return jnp.concatenate(pieces, axis=0)


def finish_sum(total, core):
    low = total.astype(BF)
    whole = (low.astype(F32) + x_swap(low).astype(F32)).astype(BF)
    return join_halves(whole, core_swap(whole), core).astype(F32)


def scatter_rows(left, right, core, z, y):
    cols = columns()
    rows = left.shape[1] // (LINE * cols)
    mine, other = half_of(right, core), half_of(right, 1 - core)

    def at(j, k):
        start = (((z - j) % LINE) * cols + (y - k) % cols) * rows
        block = lax.dynamic_slice_in_dim(left, start, rows, 1)
        sent = core_swap(left_product(block, other).astype(BF))
        return left_product(block, mine) + sent.astype(F32)

    def in_line(j):
        return ring_scatter(lambda k: at(j, k), y_next, cols)

    return finish_sum(ring_scatter(in_line, z_next, LINE), core)


def scatter_columns(left, right, core):
    cols = columns()
    rows = left.shape[1] // cols
    mine, other = half_of(right, core), half_of(right, 1 - core)

    def at(k):
        block = left[:, k * rows : (k + 1) * rows]
        sent = core_swap(left_product(block, other).astype(BF))
        return left_product(block, mine) + sent.astype(F32)

    return finish_sum(ring_scatter(at, y_next, cols), core)


def rms_norm(values, gain):
    scale = lax.rsqrt(jnp.mean(values * values, axis=-1, keepdims=True) + EPSILON)
    return (values * scale * gain, scale)


def rms_back(values, scale, gain, grad):
    weighted = grad * gain
    inner = jnp.mean(weighted * values, axis=-1, keepdims=True)
    return (scale * weighted - values * scale**3 * inner, jnp.sum(grad * values * scale, axis=0))


def swiglu_back(gate_activation, up_activation, grad_hidden):
    sigma = jax.nn.sigmoid(gate_activation)
    return (
        grad_hidden * up_activation * sigma * (1.0 + gate_activation * (1.0 - sigma)),
        grad_hidden * gate_activation * sigma,
    )


def rope_tables(positions):
    frequency = THETA ** (-(jnp.arange(HD // 2, dtype=F32) * 2.0) / HD)
    angles = positions.astype(F32)[:, None] * frequency[None, :]
    return (jnp.cos(angles), jnp.sin(angles))


def rotate(values, cos_table, sin_table):
    dims_in = values.shape
    pieces = values.reshape(dims_in[:-1] + (dims_in[-1] // HD, HD))
    half_one = pieces[..., : HD // 2]
    half_two = pieces[..., HD // 2 :]
    cos_part = cos_table[:, None, :]
    sin_part = sin_table[:, None, :]
    turned = jnp.concatenate(
        (half_one * cos_part - half_two * sin_part, half_two * cos_part + half_one * sin_part),
        axis=-1,
    )
    return turned.reshape(dims_in)


def to_heads(array, seq):
    parts = lax.axis_size("seq")
    tokens, width = array.shape
    each = width // parts
    full = jnp.zeros((parts * tokens, each), array.dtype)
    for k in range(parts):
        part = lax.dynamic_slice_in_dim(array, (seq ^ k) * each, each, 1)
        part = seq_swap(part, k) if k else part
        full = lax.dynamic_update_slice(full, part, ((seq ^ k) * tokens, 0))
    return full


def to_tokens(array, seq):
    parts = lax.axis_size("seq")
    tokens, each = array.shape[0] // parts, array.shape[1]
    full = jnp.zeros((tokens, parts * each), array.dtype)
    for k in range(parts):
        part = lax.dynamic_slice_in_dim(array, (seq ^ k) * tokens, tokens, 0)
        part = seq_swap(part, k) if k else part
        full = lax.dynamic_update_slice(full, part, (0, (seq ^ k) * each))
    return full


def to_items(array, groups):
    full_len = array.shape[0]
    return array.reshape(full_len, groups, -1).transpose(1, 0, 2)


def from_items(array):
    return array.transpose(1, 0, 2).reshape(array.shape[1], -1)


def masked_scores(query_heads, key_one, allowed):
    raw_scores = jnp.einsum(
        "qgd,kd->gqk", query_heads, key_one, preferred_element_type=F32
    ) * HD ** (-0.5)
    return jnp.where(allowed[None], raw_scores, MASKED)


def attend_forward(packed, allowed):
    query_block, key_one, value_one = packed
    full_len = query_block.shape[0]
    query_heads = query_block.reshape(full_len, -1, HD)
    scores = masked_scores(query_heads, key_one, allowed)
    top = jnp.max(scores, axis=-1, keepdims=True)
    shifted = jnp.exp(scores - top)
    total = jnp.sum(shifted, axis=-1, keepdims=True)
    soft_weights = shifted / total
    log_total = top[..., 0] + jnp.log(total[..., 0])
    attention_result = jnp.einsum(
        "gqk,kd->qgd", soft_weights.astype(BF), value_one, preferred_element_type=F32
    )
    return (attention_result.reshape(full_len, -1).astype(BF), log_total)


def attend_backward(packed, allowed):
    query_block, key_one, value_one, log_total, grad_block = packed
    full_len = query_block.shape[0]
    query_heads = query_block.reshape(full_len, -1, HD)
    grad_heads = grad_block.reshape(full_len, -1, HD)
    scores = masked_scores(query_heads, key_one, allowed)
    soft_weights = jnp.exp(scores - log_total[..., None])
    grad_weights = jnp.einsum("qgd,kd->gqk", grad_heads, value_one, preferred_element_type=F32)
    grad_value = jnp.einsum(
        "gqk,qgd->kd", soft_weights.astype(BF), grad_heads, preferred_element_type=F32
    )
    inner = jnp.sum(soft_weights * grad_weights, axis=-1, keepdims=True)
    grad_scores = (soft_weights * (grad_weights - inner)).astype(BF)
    grad_query = jnp.einsum(
        "gqk,kd->qgd", grad_scores, key_one, preferred_element_type=F32
    ) * HD ** (-0.5)
    grad_key = jnp.einsum(
        "gqk,qgd->kd", grad_scores, query_heads, preferred_element_type=F32
    ) * HD ** (-0.5)
    return (
        grad_query.reshape(full_len, -1).astype(BF),
        grad_key.astype(BF),
        grad_value.astype(BF),
    )


def shards(
    inputs,
    query_weight,
    key_weight,
    value_weight,
    output_weight,
    gate_weight,
    up_weight,
    down_weight,
    gain_attn,
    gain_ffn,
    cotangent,
):
    seq_count, local_len, width = inputs.shape
    assert seq_count == 1
    tokens = local_len
    full_len = local_len * lax.axis_size("seq")
    kv_local = KVH // lax.axis_size("seq")
    cols = columns()
    seq = lax.axis_index("seq")
    core = seq % 2
    fsdp = lax.axis_index("fsdp")
    z, y = fsdp // cols, fsdp % cols

    q_width, kv_width = query_weight.shape[1], key_weight.shape[1]
    gains = jnp.stack([gain_attn, gain_ffn])
    gain_full = jnp.zeros((2, width), BF)
    for j, piece in enumerate(ring_gather(gains, z_next, LINE)):
        for k, sub in enumerate(ring_gather(piece, y_next, cols)):
            start = (((z - j) % LINE) * cols + (y - k) % cols) * gains.shape[1]
            gain_full = lax.dynamic_update_slice(gain_full, sub, (0, start))
    gain_one, gain_two = gain_full[0].astype(F32), gain_full[1].astype(F32)

    qkv_shard = jnp.concatenate([query_weight, key_weight, value_weight], axis=1)
    qkv_weight = gather_rows(qkv_shard, core, z, y)
    out_weight = gather_rows(after(output_weight, qkv_weight), core, z, y)
    grad_out = cotangent.reshape(tokens, width)
    grad_all = jnp.concatenate(
        ring_gather(after(grad_out, out_weight), z_next, LINE), axis=0
    )
    gate_all = gather_columns(after(gate_weight, qkv_weight), core, y)
    up_all = gather_columns(after(up_weight, qkv_weight), core, y)
    down_all = gather_columns(after(down_weight, qkv_weight), core, y)

    flat_in = inputs.reshape(tokens, width).astype(F32)
    normed_one, scale_one = rms_norm(flat_in, gain_one)
    acts_one = normed_one.astype(BF)
    qkv_rows = product(acts_one, qkv_weight)
    positions = seq * local_len + jnp.arange(local_len)
    cos_table, sin_table = rope_tables(positions)
    query_sent = rotate(qkv_rows[:, :q_width], cos_table, sin_table).astype(BF)
    key_sent = rotate(qkv_rows[:, q_width : q_width + kv_width], cos_table, sin_table).astype(BF)
    value_sent = qkv_rows[:, q_width + kv_width :].astype(BF)
    query_heads, key_heads, value_heads = (
        to_heads(query_sent, seq),
        to_heads(key_sent, seq),
        to_heads(value_sent, seq),
    )
    blocks = jnp.arange(full_len) // BLOCK
    allowed = blocks[None, :] <= blocks[:, None]
    items = (
        to_items(query_heads, kv_local),
        to_items(key_heads, kv_local),
        to_items(value_heads, kv_local),
    )
    attention_result, log_totals = lax.map(partial(attend_forward, allowed=allowed), items)
    mixed_flat = to_tokens(from_items(attention_result), seq)
    residual_stream = flat_in + product(mixed_flat, out_weight)
    normed_two, scale_two = rms_norm(residual_stream, gain_two)
    acts_two = normed_two.astype(BF)

    acts_all = jnp.concatenate(ring_gather(acts_two, z_next, LINE), axis=0)
    gate_activation = right_product(acts_all, gate_all)
    up_activation = right_product(acts_all, up_all)
    hidden_state = (jax.nn.silu(gate_activation) * up_activation).astype(BF)
    grad_hidden = right_product(grad_all, down_all)
    grad_gate, grad_up = swiglu_back(gate_activation, up_activation, grad_hidden)
    grad_gate = grad_gate.astype(BF)
    grad_up = grad_up.astype(BF)

    grad_acts_part = product(grad_gate, gate_all) + product(grad_up, up_all)
    grad_acts_two = ring_scatter(
        lambda j: grad_acts_part[j * tokens : (j + 1) * tokens], z_next, LINE
    )
    ffn_part = product(hidden_state, down_all)
    ffn_out = ring_scatter(lambda j: ffn_part[j * tokens : (j + 1) * tokens], z_next, LINE)
    d_down = scatter_columns(hidden_state, grad_all, core)
    d_gate = scatter_columns(grad_gate, acts_all, core)
    d_up = scatter_columns(grad_up, acts_all, core)

    outputs = (residual_stream + ffn_out).astype(BF).reshape(seq_count, local_len, width)
    grad_mid, grad_gain_two = rms_back(residual_stream, scale_two, gain_two, grad_acts_two)
    grad_res = grad_out.astype(F32) + grad_mid
    grad_res_low = grad_res.astype(BF)
    d_out = scatter_rows(mixed_flat, grad_res_low, core, z, y)
    grad_mixed = right_product(grad_res_low, out_weight).astype(BF)
    grad_heads = to_heads(grad_mixed, seq)
    back_items = items + (log_totals, to_items(grad_heads, kv_local))
    grad_q_items, grad_k_items, grad_v_items = lax.map(
        partial(attend_backward, allowed=allowed), back_items
    )
    grad_q_tok, grad_k_tok, grad_v_tok = (
        to_tokens(from_items(grad_q_items), seq),
        to_tokens(from_items(grad_k_items), seq),
        to_tokens(from_items(grad_v_items), seq),
    )
    grad_query = rotate(grad_q_tok.astype(F32), cos_table, -sin_table).astype(BF)
    grad_key = rotate(grad_k_tok.astype(F32), cos_table, -sin_table).astype(BF)
    grad_qkv = jnp.concatenate([grad_query, grad_key, grad_v_tok], axis=1)
    grad_acts_one = right_product(grad_qkv, qkv_weight)
    d_qkv = scatter_rows(acts_one, grad_qkv, core, z, y)
    grad_in_mid, grad_gain_one = rms_back(flat_in, scale_one, gain_one, grad_acts_one)
    grad_inputs = (grad_res + grad_in_mid).astype(BF).reshape(seq_count, local_len, width)
    gain_sums = all_sum(jnp.stack([grad_gain_one, grad_gain_two]))
    gain_sums = lax.dynamic_slice_in_dim(gain_sums, fsdp * gain_attn.shape[0], gain_attn.shape[0], 1)
    return (
        outputs,
        grad_inputs,
        d_qkv[:, :q_width],
        d_qkv[:, q_width : q_width + kv_width],
        d_qkv[:, q_width + kv_width :],
        d_out,
        d_gate,
        d_up,
        d_down,
        gain_sums[0],
        gain_sums[1],
    )


def solution(mesh):
    token_spec, row_spec, gain_spec = P("fsdp", "seq", None), P("fsdp", None), P("fsdp")
    return jax.shard_map(
        shards,
        mesh=mesh,
        in_specs=(token_spec,) + (row_spec,) * 7 + (gain_spec,) * 2 + (token_spec,),
        out_specs=(token_spec,) * 2 + (row_spec,) * 7 + (gain_spec,) * 2,
        check_vma=False,
    )
```

```python
import functools

import jax
import jax.numpy as jnp
from jax import lax
from jax.experimental import pallas as pl
from jax.experimental.pallas import tpu as pltpu
from jax.sharding import PartitionSpec as P

KVH = 8
HD = 64
BLOCK = 256
LINE = 4

EPSILON = 1e-05
THETA = 500000.0
LOG2E = 1.4426950408889634

BF = jnp.bfloat16
F32 = jnp.float32


def after(value, *others):
    return lax.optimization_barrier((value,) + others)[0]


def columns():
    return lax.axis_size("fsdp") // LINE


def z_next(value):
    cols = columns()
    count = lax.axis_size("fsdp")
    return lax.ppermute(value, "fsdp", [(i, (i + cols) % count) for i in range(count)])


def y_next(value):
    cols = columns()
    count = lax.axis_size("fsdp")
    return lax.ppermute(
        value, "fsdp", [(i, i // cols * cols + (i + 1) % cols) for i in range(count)]
    )


def seq_swap(value, bit):
    return lax.ppermute(value, "seq", [(i, i ^ bit) for i in range(lax.axis_size("seq"))])


def core_swap(value):
    return seq_swap(value, 1)


def x_swap(value):
    return seq_swap(value, 2)


def ring_gather(value, step, count):
    pieces = [value]
    for _ in range(count - 1):
        pieces.append(step(pieces[-1]))
    return pieces


def ring_scatter(part_of, step, count):
    total = None
    for j in list(range(1, count)) + [0]:
        total = part_of(j) if total is None else part_of(j) + total.astype(F32)
        if j:
            total = step(total.astype(BF))
    return total


def all_sum(value):
    bit = 1
    while bit < lax.axis_size("seq"):
        value = value + seq_swap(value, bit)
        bit *= 2
    count = lax.axis_size("fsdp")
    bit = 1
    while bit < count:
        value = value + lax.ppermute(value, "fsdp", [(i, i ^ bit) for i in range(count)])
        bit *= 2
    return value


def dot_nt(a, b):
    return lax.dot_general(a, b, (((1,), (1,)), ((), ())), preferred_element_type=F32)

def dot_nn(a, b):
    return jnp.dot(a, b, preferred_element_type=F32)


def attend_forward_kernel(parts, heads, kv, seq_ref, *refs):
    packs, outs = refs[:parts], refs[parts : 2 * parts]
    lse_ref, q_s, k_s, vt_s, o_s = refs[2 * parts :]
    tokens = packs[0].shape[0]
    seq = seq_ref[0]
    group = heads // kv
    for k in range(parts):
        rows = pl.ds(pl.multiple_of((seq ^ k) * tokens, tokens), tokens)
        q_s[rows, :] = packs[k][:, : heads * HD]
        for g in range(kv):
            lane = (heads + g) * HD
            k_s[g, rows, :] = packs[k][:, lane : lane + HD]
            lane = (heads + kv + g) * HD
            vt_s[g, :, rows] = packs[k][:, lane : lane + HD].T
    full = parts * tokens
    for g in range(kv):
        for i in range(full // BLOCK):
            keys = (i + 1) * BLOCK
            rows = slice(i * BLOCK, keys)
            for pair in range(group // 2):
                halves = []
                for h in (g * group + 2 * pair, g * group + 2 * pair + 1):
                    scores = dot_nt(k_s[g, :keys, :], q_s[rows, h * HD : (h + 1) * HD])
                    scores = scores * (HD**-0.5 * LOG2E)
                    top = jnp.max(scores, axis=0, keepdims=True)
                    powers = jnp.exp2(scores - top)
                    total = jnp.sum(powers, axis=0, keepdims=True)
                    halves.append(dot_nn(vt_s[g, :, :keys], powers.astype(BF)) / total)
                    lse_ref[h : h + 1, rows] = top + jnp.log2(total)
                lane = (g * group + 2 * pair) * HD
                o_s[rows, lane : lane + 2 * HD] = jnp.concatenate(halves, axis=0).T.astype(BF)
    for k in range(parts):
        rows = pl.ds(pl.multiple_of((seq ^ k) * tokens, tokens), tokens)
        outs[k][...] = o_s[rows, :]


def attend_forward(seq, packs, heads, kv):
    parts = len(packs)
    tokens = packs[0].shape[0]
    full = parts * tokens
    vmem = pl.BlockSpec(memory_space=pltpu.VMEM)
    flops = 4 * heads * full * full * HD * 5 // 8
    return pl.pallas_call(
        functools.partial(attend_forward_kernel, parts, heads, kv),
        out_shape=[jax.ShapeDtypeStruct((tokens, heads * HD), BF)] * parts
        + [jax.ShapeDtypeStruct((heads, full), F32)],
        in_specs=[pl.BlockSpec(memory_space=pltpu.SMEM)] + [vmem] * parts,
        out_specs=[vmem] * (parts + 1),
        scratch_shapes=[
            pltpu.VMEM((full, heads * HD), BF),
            pltpu.VMEM((kv, full, HD), BF),
            pltpu.VMEM((kv, HD, full), BF),
            pltpu.VMEM((full, heads * HD), BF),
        ],
        compiler_params=pltpu.CompilerParams(vmem_limit_bytes=48 * 2**20),
        cost_estimate=pl.CostEstimate(flops=flops * 4, bytes_accessed=4 * 2**20, transcendentals=heads * full * full * 5 // 8),
        name="attend_forward",
    )(seq.reshape(1), *packs)


def attend_backward_kernel(parts, heads, kv, seq_ref, lse_ref, *refs):
    packs, grads, outs = refs[:parts], refs[parts : 2 * parts], refs[2 * parts : 3 * parts]
    q_s, k_s, kt_s, v_s, g_s, dq_s, dk_s, dv_s = refs[3 * parts :]
    tokens = packs[0].shape[0]
    seq = seq_ref[0]
    group = heads // kv
    for k in range(parts):
        rows = pl.ds(pl.multiple_of((seq ^ k) * tokens, tokens), tokens)
        q_s[rows, :] = packs[k][:, : heads * HD]
        g_s[rows, :] = grads[k][...]
        for g in range(kv):
            lane = (heads + g) * HD
            k_s[g, rows, :] = packs[k][:, lane : lane + HD]
            kt_s[g, :, rows] = packs[k][:, lane : lane + HD].T
            lane = (heads + kv + g) * HD
            v_s[g, rows, :] = packs[k][:, lane : lane + HD]
    full = parts * tokens
    dk_s[...] = jnp.zeros_like(dk_s)
    dv_s[...] = jnp.zeros_like(dv_s)
    for g in range(kv):
        for i in range(full // BLOCK):
            keys = (i + 1) * BLOCK
            rows = slice(i * BLOCK, keys)
            for pair in range(group // 2):
                halves = []
                for h in (g * group + 2 * pair, g * group + 2 * pair + 1):
                    query = q_s[rows, h * HD : (h + 1) * HD]
                    grad = g_s[rows, h * HD : (h + 1) * HD]
                    scores = dot_nt(k_s[g, :keys, :], query) * (HD**-0.5 * LOG2E)
                    probs = jnp.exp2(scores - lse_ref[h : h + 1, rows])
                    grad_probs = dot_nt(v_s[g, :keys, :], grad)
                    inner = jnp.sum(probs * grad_probs, axis=0, keepdims=True)
                    grad_scores = (probs * (grad_probs - inner)).astype(BF)
                    dv_s[g, :keys, :] += dot_nn(probs.astype(BF), grad)
                    dk_s[g, :keys, :] += dot_nn(grad_scores, query)
                    halves.append(dot_nn(kt_s[g, :, :keys], grad_scores) * HD**-0.5)
                lane = (g * group + 2 * pair) * HD
                dq_s[rows, lane : lane + 2 * HD] = jnp.concatenate(halves, axis=0).T.astype(BF)
    for k in range(parts):
        rows = pl.ds(pl.multiple_of((seq ^ k) * tokens, tokens), tokens)
        outs[k][:, : heads * HD] = dq_s[rows, :]
        for g in range(kv):
            lane = (heads + g) * HD
            outs[k][:, lane : lane + HD] = (dk_s[g, rows, :] * HD**-0.5).astype(BF)
            lane = (heads + kv + g) * HD
            outs[k][:, lane : lane + HD] = dv_s[g, rows, :].astype(BF)


def attend_backward(seq, lse, packs, grads, heads, kv):
    parts = len(packs)
    tokens = packs[0].shape[0]
    full = parts * tokens
    vmem = pl.BlockSpec(memory_space=pltpu.VMEM)
    flops = 10 * heads * full * full * HD * 5 // 8
    return pl.pallas_call(
        functools.partial(attend_backward_kernel, parts, heads, kv),
        out_shape=[jax.ShapeDtypeStruct(packs[0].shape, BF)] * parts,
        in_specs=[pl.BlockSpec(memory_space=pltpu.SMEM)] + [vmem] * (2 * parts + 1),
        out_specs=[vmem] * parts,
        scratch_shapes=[
            pltpu.VMEM((full, heads * HD), BF),
            pltpu.VMEM((kv, full, HD), BF),
            pltpu.VMEM((kv, HD, full), BF),
            pltpu.VMEM((kv, full, HD), BF),
            pltpu.VMEM((full, heads * HD), BF),
            pltpu.VMEM((full, heads * HD), BF),
            pltpu.VMEM((kv, full, HD), F32),
            pltpu.VMEM((kv, full, HD), F32),
        ],
        compiler_params=pltpu.CompilerParams(vmem_limit_bytes=48 * 2**20),
        cost_estimate=pl.CostEstimate(flops=flops * 4, bytes_accessed=8 * 2**20, transcendentals=heads * full * full * 5 // 8),
        name="attend_backward",
    )(seq.reshape(1), lse, *packs, *grads)


def smem():
    return pl.BlockSpec(memory_space=pltpu.SMEM)


def params(mib=56):
    return pltpu.CompilerParams(vmem_limit_bytes=mib * 2**20)


def cost(flops, moved):
    return pl.CostEstimate(flops=flops, bytes_accessed=moved, transcendentals=0)


def place(full, shape, pieces, offsets):
    count = len(pieces)
    given = [] if full is None else [full]

    def kernel(at_ref, *refs):
        sources, target, sems = refs[len(given) : -2], refs[-2], refs[-1]
        copies = []
        for i, source in enumerate(sources):
            rows, width = source.shape
            row = pl.multiple_of(at_ref[2 * i], rows)
            column = pl.multiple_of(at_ref[2 * i + 1], width)
            spot = target.at[pl.ds(row, rows), pl.ds(column, width)]
            copies.append(pltpu.make_async_copy(source, spot, sems.at[i]))
            copies[-1].start()
        for copy in copies:
            copy.wait()

    hbm = pl.BlockSpec(memory_space=pl.ANY)
    moved = 2 * sum(piece.size * 2 for piece in pieces)
    return pl.pallas_call(
        kernel,
        out_shape=jax.ShapeDtypeStruct(shape, pieces[0].dtype),
        in_specs=[smem()] + [hbm] * (len(given) + count),
        out_specs=hbm,
        scratch_shapes=[pltpu.SemaphoreType.DMA((count,))],
        input_output_aliases={1: 0} if given else {},
        compiler_params=params(16),
        cost_estimate=cost(0, moved),
        name="place",
    )(jnp.stack([jnp.int32(v) for pair in offsets for v in pair]), *given, *pieces)


def turn(values, cos_table, sin_table):
    width = values.shape[1]
    lane = lax.broadcasted_iota(jnp.int32, values.shape, 1)
    swapped = jnp.where(
        lane % HD < HD // 2,
        pltpu.roll(values, width - HD // 2, 1),
        pltpu.roll(values, HD // 2, 1),
    )
    return values * cos_table + swapped * sin_table


def project_in(seq, inputs, gain, weight, cos_table, sin_table, parts):
    tokens, width = inputs.shape
    tile = cos_table.shape[1]
    each = tile // parts
    pack = tile + 2 * each

    def kernel(seq_ref, in_ref, gain_ref, w_ref, cos_ref, sin_ref, acts_ref, *packs):
        step = pl.program_id(0)

        @pl.when(step == 0)
        def _():
            values = in_ref[...].astype(F32)
            scale = lax.rsqrt(jnp.mean(values * values, axis=-1, keepdims=True) + EPSILON)
            acts_ref[...] = (values * scale * gain_ref[...]).astype(BF)

        rows = dot_nn(acts_ref[...], w_ref[...])
        turned = jnp.where(
            step == parts + 1, rows, turn(rows, cos_ref[...], sin_ref[...])
        ).astype(BF)
        seq_now = seq_ref[0]
        for k in range(parts):

            @pl.when((seq_now ^ k) == step)
            def _():
                packs[k][:, :tile] = turned

            for d in range(parts):
                for which in range(2):

                    @pl.when(((seq_now ^ k) == d) & (step == parts + which))
                    def _():
                        lane = tile + which * each
                        packs[k][:, lane : lane + each] = turned[:, d * each : (d + 1) * each]

    def whole(shape):
        return pl.BlockSpec(shape, lambda n: (0,) * len(shape))

    return pl.pallas_call(
        kernel,
        grid=(parts + 2,),
        out_shape=[jax.ShapeDtypeStruct((tokens, width), BF)]
        + [jax.ShapeDtypeStruct((tokens, pack), BF)] * parts,
        in_specs=[
            smem(),
            whole((tokens, width)),
            whole((1, width)),
            pl.BlockSpec((width, tile), lambda n: (0, n)),
            whole((tokens, tile)),
            whole((tokens, tile)),
        ],
        out_specs=[whole((tokens, width))] + [whole((tokens, pack))] * parts,
        compiler_params=params(),
        cost_estimate=cost(2 * tokens * width * tile * (parts + 2), 2 * width * tile * (parts + 2)),
        name="project_in",
    )(seq.reshape(1), inputs, gain, weight, cos_table, sin_table)


def project_out(seq, mixed, inputs, gain, weight):
    parts = len(mixed)
    tokens, width = inputs.shape
    each = mixed[0].shape[1]
    tile = width // parts

    def kernel(seq_ref, *refs):
        parts_in, (in_ref, gain_ref, w_ref, flat_ref, res_ref, acts_ref) = refs[:parts], refs[parts:]
        step = pl.program_id(0)

        @pl.when(step == 0)
        def _():
            for k in range(parts):
                lane = pl.multiple_of((seq_ref[0] ^ k) * each, each)
                flat_ref[:, pl.ds(lane, each)] = parts_in[k][...]

        lanes = pl.ds(pl.multiple_of(step * tile, tile), tile)
        res_ref[:, lanes] = in_ref[:, lanes].astype(F32) + dot_nn(flat_ref[...], w_ref[...])

        @pl.when(step == parts - 1)
        def _():
            values = res_ref[...]
            scale = lax.rsqrt(jnp.mean(values * values, axis=-1, keepdims=True) + EPSILON)
            acts_ref[...] = (values * scale * gain_ref[...]).astype(BF)

    def whole(shape):
        return pl.BlockSpec(shape, lambda n: (0,) * len(shape))

    return pl.pallas_call(
        kernel,
        grid=(parts,),
        out_shape=[
            jax.ShapeDtypeStruct((tokens, parts * each), BF),
            jax.ShapeDtypeStruct((tokens, width), F32),
            jax.ShapeDtypeStruct((tokens, width), BF),
        ],
        in_specs=[smem()]
        + [whole((tokens, each))] * parts
        + [
            whole((tokens, width)),
            whole((1, width)),
            pl.BlockSpec((parts * each, tile), lambda n: (0, n)),
        ],
        out_specs=[whole((tokens, parts * each)), whole((tokens, width)), whole((tokens, width))],
        compiler_params=params(),
        cost_estimate=cost(2 * tokens * width * parts * each, 2 * width * parts * each),
        name="project_out",
    )(seq.reshape(1), *mixed, inputs, gain, weight)


def feed_forward(acts, grads, gate, up, down):
    tokens, width = acts.shape
    hidden = gate.shape[0]
    tile = 256
    steps = hidden // tile

    def kernel(a_ref, c_ref, g_ref, u_ref, d_ref, h_ref, gg_ref, gu_ref, o_ref, ga_ref, o_s, ga_s):
        step = pl.program_id(0)
        gate_act = dot_nt(a_ref[...], g_ref[...])
        up_act = dot_nt(a_ref[...], u_ref[...])
        grad_hidden = dot_nt(c_ref[...], d_ref[...])
        sigma = jax.nn.sigmoid(gate_act)
        silu = gate_act * sigma
        low = (silu * up_act).astype(BF)
        grad_gate = (grad_hidden * up_act * (sigma * (1.0 + gate_act * (1.0 - sigma)))).astype(BF)
        grad_up = (grad_hidden * silu).astype(BF)
        h_ref[...] = low
        gg_ref[...] = grad_gate
        gu_ref[...] = grad_up
        out = dot_nn(low, d_ref[...])
        grad = dot_nn(grad_gate, g_ref[...]) + dot_nn(grad_up, u_ref[...])

        @pl.when(step == 0)
        def _():
            o_s[...] = out
            ga_s[...] = grad

        @pl.when(step > 0)
        def _():
            o_s[...] += out
            ga_s[...] += grad

        @pl.when(step == steps - 1)
        def _():
            o_ref[...] = o_s[...].astype(BF)
            ga_ref[...] = ga_s[...].astype(BF)

    whole = pl.BlockSpec((tokens, width), lambda n: (0, 0))
    rows = pl.BlockSpec((tile, width), lambda n: (n, 0))
    lanes = pl.BlockSpec((tokens, tile), lambda n: (0, n))
    return pl.pallas_call(
        kernel,
        grid=(steps,),
        out_shape=[jax.ShapeDtypeStruct((tokens, hidden), BF)] * 3
        + [jax.ShapeDtypeStruct((tokens, width), BF)] * 2,
        in_specs=[whole, whole, rows, rows, rows],
        out_specs=[lanes] * 3 + [whole] * 2,
        scratch_shapes=[pltpu.VMEM((tokens, width), F32)] * 2,
        compiler_params=params(),
        cost_estimate=cost(12 * tokens * width * hidden, 6 * width * hidden),
        name="feed_forward",
    )(acts, grads, gate, up, down)


def middle_back(seq, terms, residual, grad_out, gain, weight, parts):
    tokens, width = residual.shape
    tile = weight.shape[0] // parts

    def kernel(seq_ref, t0_ref, t1_ref, res_ref, go_ref, gain_ref, w_ref, gr_ref, low_ref, gg_ref, *outs):
        step = pl.program_id(0)

        @pl.when(step == 0)
        def _():
            grad = t0_ref[...].astype(F32) + t1_ref[...].astype(F32)
            values = res_ref[...]
            scale = lax.rsqrt(jnp.mean(values * values, axis=-1, keepdims=True) + EPSILON)
            weighted = grad * gain_ref[...]
            inner = jnp.mean(weighted * values, axis=-1, keepdims=True)
            result = go_ref[...].astype(F32) + scale * weighted - values * (scale**3 * inner)
            gr_ref[...] = result
            low_ref[...] = result.astype(BF)
            gg_ref[...] = jnp.sum(grad * values * scale, axis=0, keepdims=True)

        part = dot_nt(low_ref[...], w_ref[...]).astype(BF)
        for k in range(parts):

            @pl.when((seq_ref[0] ^ k) == step)
            def _():
                outs[k][...] = part

    def whole(shape):
        return pl.BlockSpec(shape, lambda n: (0,) * len(shape))

    full, row = whole((tokens, width)), whole((1, width))
    return pl.pallas_call(
        kernel,
        grid=(parts,),
        out_shape=[
            jax.ShapeDtypeStruct((tokens, width), F32),
            jax.ShapeDtypeStruct((tokens, width), BF),
            jax.ShapeDtypeStruct((1, width), F32),
        ]
        + [jax.ShapeDtypeStruct((tokens, tile), BF)] * parts,
        in_specs=[smem(), full, full, full, full, row, pl.BlockSpec((tile, width), lambda n: (n, 0))],
        out_specs=[full, full, row] + [whole((tokens, tile))] * parts,
        compiler_params=params(),
        cost_estimate=cost(2 * tokens * width * tile * parts, 2 * width * tile * parts + 8 * tokens * width),
        name="middle_back",
    )(seq.reshape(1), terms[0], terms[1], residual, grad_out, gain, weight)


def unpack(seq, packs, cos_table, sin_table):
    parts = len(packs)
    tokens, tile = cos_table.shape
    each = tile // parts

    def kernel(seq_ref, *refs):
        ins, (cos_ref, sin_ref, out_ref) = refs[:parts], refs[parts:]
        for k in range(parts):
            at = seq_ref[0] ^ k
            queries = turn(ins[k][:, :tile].astype(F32), cos_ref[...], -sin_ref[...])
            out_ref[:, pl.ds(pl.multiple_of(at * tile, tile), tile)] = queries.astype(BF)
            keys = turn(
                ins[k][:, tile : tile + each].astype(F32), cos_ref[:, :each], -sin_ref[:, :each]
            )
            lane = pl.multiple_of(parts * tile + at * each, each)
            out_ref[:, pl.ds(lane, each)] = keys.astype(BF)
            lane = pl.multiple_of((parts + 1) * tile + at * each, each)
            out_ref[:, pl.ds(lane, each)] = ins[k][:, tile + each :]

    vmem = pl.BlockSpec(memory_space=pltpu.VMEM)
    return pl.pallas_call(
        kernel,
        out_shape=jax.ShapeDtypeStruct((tokens, (parts + 2) * tile), BF),
        in_specs=[smem()] + [vmem] * (parts + 2),
        out_specs=vmem,
        compiler_params=params(),
        cost_estimate=cost(0, 6 * 2**20),
        name="unpack",
    )(seq.reshape(1), *packs, cos_table, sin_table)


def inner_back(grad_qkv, weight, inputs, gain, grad_res):
    tokens, width = inputs.shape
    tile = 512
    steps = width // tile

    def kernel(gq_ref, w_ref, in_ref, gain_ref, gr_ref, out_ref, gg_ref, grad_s):
        step = pl.program_id(0)
        grad_s[:, pl.ds(pl.multiple_of(step * tile, tile), tile)] = dot_nt(gq_ref[...], w_ref[...])

        @pl.when(step == steps - 1)
        def _():
            grad = grad_s[...]
            values = in_ref[...].astype(F32)
            scale = lax.rsqrt(jnp.mean(values * values, axis=-1, keepdims=True) + EPSILON)
            weighted = grad * gain_ref[...]
            inner = jnp.mean(weighted * values, axis=-1, keepdims=True)
            result = gr_ref[...] + scale * weighted - values * (scale**3 * inner)
            out_ref[...] = result.astype(BF)
            gg_ref[...] = jnp.sum(grad * values * scale, axis=0, keepdims=True)

    def whole(shape):
        return pl.BlockSpec(shape, lambda n: (0,) * len(shape))

    full, row = whole((tokens, width)), whole((1, width))
    return pl.pallas_call(
        kernel,
        grid=(steps,),
        out_shape=[jax.ShapeDtypeStruct((tokens, width), BF), jax.ShapeDtypeStruct((1, width), F32)],
        in_specs=[
            whole(grad_qkv.shape),
            pl.BlockSpec((tile, weight.shape[1]), lambda n: (n, 0)),
            full,
            row,
            full,
        ],
        out_specs=[full, row],
        scratch_shapes=[pltpu.VMEM((tokens, width), F32)],
        compiler_params=params(),
        cost_estimate=cost(2 * tokens * weight.size, 2 * weight.size),
        name="inner_back",
    )(grad_qkv, weight, inputs, gain, grad_res)


def weight_grad(left, right, rows, row_block, half, adds=()):
    count = len(left)
    tokens = left[0].shape[0]
    width = right[0].shape[1] // 2
    tile = min(rows, 512)
    steps = rows // tile

    def kernel(at_ref, *refs):
        lefts, rights, extra, out = refs[:count], refs[count : 2 * count], refs[2 * count : -1], refs[-1]
        total = None
        for l_ref, r_ref in zip(lefts, rights):
            term = lax.dot_general(
                l_ref[...], r_ref[...], (((0,), (0,)), ((), ())), preferred_element_type=F32
            )
            total = term if total is None else total + term
        for ref in extra:
            total = total + ref[...].astype(F32)
        out[...] = total.astype(BF)

    def added(slot):
        return pl.BlockSpec((tile, width), lambda n, at: (at[2 + slot] + n, 0))

    spec = pltpu.PrefetchScalarGridSpec(
        num_scalar_prefetch=1,
        grid=(steps,),
        in_specs=[pl.BlockSpec((tokens, tile), lambda n, at: (0, at[0] + n))] * count
        + [pl.BlockSpec((tokens, width), lambda n, at: (0, at[1]))] * count
        + [added(i) for i in range(len(adds))],
        out_specs=pl.BlockSpec((tile, width), lambda n, at: (n, 0)),
    )
    at = jnp.stack(
        [jnp.int32(row_block) * steps, jnp.int32(half)] + [jnp.int32(b) * steps for _, b in adds]
    )
    return pl.pallas_call(
        kernel,
        grid_spec=spec,
        out_shape=jax.ShapeDtypeStruct((rows, width), BF),
        compiler_params=params(),
        cost_estimate=cost(2 * tokens * count * rows * width, 2 * (tokens * count + rows) * width),
        name="weight_grad",
    )(at, *left, *right, *[a for a, _ in adds])


def join(core, mine, other, widths):
    rows, half = mine.shape
    tile = min(rows, 256)

    def kernel(core_ref, mine_ref, other_ref, *refs):
        outs, full = refs[:-1], refs[-1]
        target = outs[0] if len(outs) == 1 else full
        at = pl.multiple_of(core_ref[0] * half, half)
        target[:, pl.ds(at, half)] = mine_ref[...].astype(F32)
        at = pl.multiple_of((1 - core_ref[0]) * half, half)
        target[:, pl.ds(at, half)] = other_ref[...].astype(F32)
        if len(outs) > 1:
            lane = 0
            for out in outs:
                out[...] = full[:, lane : lane + out.shape[1]]
                lane += out.shape[1]

    def block(width):
        return pl.BlockSpec((tile, width), lambda n: (n, 0))

    return pl.pallas_call(
        kernel,
        grid=(rows // tile,),
        out_shape=[jax.ShapeDtypeStruct((rows, width), F32) for width in widths],
        in_specs=[smem(), block(half), block(half)],
        out_specs=[block(width) for width in widths],
        scratch_shapes=[pltpu.VMEM((tile, 2 * half) if len(widths) > 1 else (8, 128), F32)],
        compiler_params=params(),
        cost_estimate=cost(0, rows * half * 12),
        name="join",
    )(core.reshape(1), mine, other)
def half_of(array, which, axis=1):
    size = array.shape[axis] // 2
    return lax.dynamic_slice_in_dim(array, which * size, size, axis)


def gather_rows(shard, start, core, z, y):
    cols = columns()
    rows, width = shard.shape
    half = width // 2
    shape = (rows * LINE * cols, width)
    full = None
    pieces = ring_gather(start, z_next, LINE)
    ends = []
    for j, piece in enumerate(pieces):
        placed, offsets = [], []
        subs = ring_gather(piece, y_next, cols)
        for k, sub in enumerate(subs):
            row = (((z - j) % LINE) * cols + (y - k) % cols) * rows
            if j == 0 and k == 0:
                placed.append(shard)
                offsets.append((row, 0))
                continue
            placed += [sub, core_swap(sub)]
            offsets += [(row, core * half), (row, (1 - core) * half)]
        ends.append(subs[-1])
        full = place(full, shape, placed, offsets)
    return full, pieces[-1], ends[-1]


def gather_columns(shard, start, core, side, y):
    cols = columns()
    rows, width = shard.shape
    half, part = width // 2, rows // 2
    placed, offsets = [shard], [(y * rows, 0)]
    subs = ring_gather(start, y_next, cols)
    for k, sub in enumerate(subs):
        if k == 0:
            continue
        row = (y - k) % cols * rows
        crossed = x_swap(sub)
        for piece, at in ((sub, side), (crossed, 1 - side)):
            placed += [piece, core_swap(piece)]
            offsets += [
                (row + at * part, core * half),
                (row + at * part, (1 - core) * half),
            ]
    return place(None, (rows * cols, width), placed, offsets), subs[-1]


def finish_sum(total, core, widths):
    low = total.astype(BF)
    whole = (low.astype(F32) + x_swap(low).astype(F32)).astype(BF)
    return join(core, whole, core_swap(whole), widths)


def scatter_rows(left, right, core, z, y, widths):
    cols = columns()
    rows = left.shape[1] // LINE
    each = rows // cols
    blocks = {}
    for j in list(range(1, LINE)) + [0]:
        line = (z - j) % LINE
        sent = core_swap(weight_grad([left], [right], rows, line, 1 - core))
        blocks[j] = weight_grad([left], [right], rows, line, core, [(sent, 0)])

    def in_line(j):
        def at(k):
            return lax.dynamic_slice_in_dim(blocks[j], (y - k) % cols * each, each, 0).astype(F32)

        return ring_scatter(at, y_next, cols)

    return finish_sum(ring_scatter(in_line, z_next, LINE), core, widths)


def scatter_columns(left, right, core, y):
    cols = columns()
    rows = left[0].shape[1]
    each = rows // cols
    sent = core_swap(weight_grad(left, right, rows, 0, 1 - core))
    total = None
    for k in list(range(1, cols)) + [0]:
        at = (y - k) % cols
        adds = [(sent, at)] + ([] if total is None else [(total, 0)])
        total = weight_grad(left, right, each, at, core, adds)
        if k:
            total = y_next(total)
    return finish_sum(total, core, [2 * total.shape[1]])


def rope_tables(positions, repeat):
    frequency = THETA ** (-(jnp.arange(HD // 2, dtype=F32) * 2.0) / HD)
    angles = positions.astype(F32)[:, None] * frequency[None, :]
    cos, sin = jnp.cos(angles), jnp.sin(angles)
    return (
        jnp.tile(jnp.concatenate([cos, cos], axis=1), (1, repeat)),
        jnp.tile(jnp.concatenate([-sin, sin], axis=1), (1, repeat)),
    )


def exchange(packs):
    return [packs[0]] + [seq_swap(packs[k], k) for k in range(1, len(packs))]


def shards(
    inputs,
    query_weight,
    key_weight,
    value_weight,
    output_weight,
    gate_weight,
    up_weight,
    down_weight,
    gain_attn,
    gain_ffn,
    cotangent,
):
    seq_count, local_len, width = inputs.shape
    assert seq_count == 1
    tokens = local_len
    parts = lax.axis_size("seq")
    kv_local = KVH // parts
    cols = columns()
    seq = lax.axis_index("seq")
    core, side = seq % 2, seq // 2
    fsdp = lax.axis_index("fsdp")
    z, y = fsdp // cols, fsdp % cols
    q_width, kv_width = query_weight.shape[1], key_weight.shape[1]
    heads_local = q_width // HD // parts
    flat_in = inputs.reshape(tokens, width)
    grad_out = cotangent.reshape(tokens, width)

    qkv_shard = jnp.concatenate([query_weight, key_weight, value_weight], axis=1)
    qkv_weight, z_end, y_end = gather_rows(qkv_shard, half_of(qkv_shard, core), core, z, y)
    out_start = after(half_of(output_weight, core), z_end)
    out_weight, z_end, _ = gather_rows(output_weight, out_start, core, z, y)

    gains = jnp.stack([gain_attn, gain_ffn])
    gain_full = jnp.zeros((2, width), BF)
    for j, piece in enumerate(ring_gather(gains, z_next, LINE)):
        for k, sub in enumerate(ring_gather(piece, y_next, cols)):
            at = (((z - j) % LINE) * cols + (y - k) % cols) * gains.shape[1]
            gain_full = lax.dynamic_update_slice(gain_full, sub, (0, at))
    gain_one = gain_full[:1].astype(F32)
    gain_two = gain_full[1:].astype(F32)
    positions = seq * local_len + jnp.arange(local_len)
    cos_table, sin_table = rope_tables(positions, kv_width // HD)

    grad_parts = ring_gather(after(grad_out, z_end), z_next, LINE)
    wide = []
    for weight in (gate_weight, up_weight, down_weight):
        piece = half_of(half_of(weight, side, 0), core)
        full, y_end = gather_columns(weight, after(piece, y_end), core, side, y)
        wide.append(full)
    gate_all, up_all, down_all = wide

    acts_one, *sent = project_in(seq, flat_in, gain_one, qkv_weight, cos_table, sin_table, parts)
    packs = exchange(sent)
    *mixed_sent, log_totals = attend_forward(seq, packs, heads_local, kv_local)
    mixed_flat, residual, acts_two = project_out(
        seq, exchange(mixed_sent), flat_in, gain_two, out_weight
    )

    acts_parts = ring_gather(acts_two, z_next, LINE)
    done = [
        feed_forward(a, g, gate_all, up_all, down_all) for a, g in zip(acts_parts, grad_parts)
    ]
    hidden, grad_gate, grad_up, ffn_parts, grad_terms = [list(v) for v in zip(*done)]

    def line_sum(terms):
        total = terms[1]
        for j in range(2, LINE):
            total = (terms[j].astype(F32) + z_next(total).astype(F32)).astype(BF)
        return z_next(total)

    grad_recv = line_sum(grad_terms)
    grad_res, grad_res_low, grad_gain_two, *grad_sent = middle_back(
        seq, (grad_recv, grad_terms[0]), residual, grad_out, gain_two, out_weight, parts
    )
    grad_packs = exchange(grad_sent)
    ffn_parts[1] = after(ffn_parts[1], grad_recv)
    ffn_recv = line_sum(ffn_parts)
    outputs = (residual + ffn_recv.astype(F32) + ffn_parts[0].astype(F32)).astype(BF)

    d_down = scatter_columns(hidden, grad_parts, core, y)
    d_gate = scatter_columns(grad_gate, acts_parts, core, y)
    d_up = scatter_columns(grad_up, acts_parts, core, y)
    d_out = scatter_rows(mixed_flat, grad_res_low, core, z, y, [width])

    back_sent = attend_backward(seq, log_totals, packs, grad_packs, heads_local, kv_local)
    grad_qkv = unpack(seq, exchange(back_sent), cos_table, sin_table)
    d_qkv = scatter_rows(acts_one, grad_qkv, core, z, y, [q_width, kv_width, kv_width])
    grad_inputs, grad_gain_one = inner_back(grad_qkv, qkv_weight, flat_in, gain_one, grad_res)
    gain_sums = all_sum(jnp.concatenate([grad_gain_one, grad_gain_two], axis=0))
    rows = gain_attn.shape[0]
    gain_sums = lax.dynamic_slice_in_dim(gain_sums, fsdp * rows, rows, 1)
    return (
        outputs.reshape(inputs.shape),
        grad_inputs.reshape(inputs.shape),
        d_qkv[0],
        d_qkv[1],
        d_qkv[2],
        d_out[0],
        d_gate[0],
        d_up[0],
        d_down[0],
        gain_sums[0],
        gain_sums[1],
    )


def solution(mesh):
    token_spec, row_spec, gain_spec = P("fsdp", "seq", None), P("fsdp", None), P("fsdp")
    return jax.shard_map(
        shards,
        mesh=mesh,
        in_specs=(token_spec,) + (row_spec,) * 7 + (gain_spec,) * 2 + (token_spec,),
        out_specs=(token_spec,) * 2 + (row_spec,) * 7 + (gain_spec,) * 2,
        check_vma=False,
    )
```

```python
import functools

import jax
import jax.numpy as jnp
from jax import lax
from jax.experimental import pallas as pl
from jax.experimental.pallas import tpu as pltpu
from jax.sharding import PartitionSpec as P

KVH = 8
HD = 64
BLOCK = 256
LINE = 4

EPSILON = 1e-05
THETA = 500000.0
LOG2E = 1.4426950408889634

BF = jnp.bfloat16
F32 = jnp.float32


def after(value, *others):
    return lax.optimization_barrier((value,) + others)[0]


def columns():
    return lax.axis_size("fsdp") // LINE


def z_next(value):
    cols = columns()
    count = lax.axis_size("fsdp")
    return lax.ppermute(value, "fsdp", [(i, (i + cols) % count) for i in range(count)])


def y_next(value):
    cols = columns()
    count = lax.axis_size("fsdp")
    return lax.ppermute(
        value, "fsdp", [(i, i // cols * cols + (i + 1) % cols) for i in range(count)]
    )


def seq_swap(value, bit):
    return lax.ppermute(value, "seq", [(i, i ^ bit) for i in range(lax.axis_size("seq"))])


def core_swap(value):
    return seq_swap(value, 1)


def x_swap(value):
    return seq_swap(value, 2)


def ring_gather(value, step, count):
    pieces = [value]
    for _ in range(count - 1):
        pieces.append(step(pieces[-1]))
    return pieces


def ring_scatter(part_of, step, count):
    total = None
    for j in list(range(1, count)) + [0]:
        total = part_of(j) if total is None else part_of(j) + total.astype(F32)
        if j:
            total = step(total.astype(BF))
    return total


def all_sum(value):
    bit = 1
    while bit < lax.axis_size("seq"):
        value = value + seq_swap(value, bit)
        bit *= 2
    count = lax.axis_size("fsdp")
    bit = 1
    while bit < count:
        value = value + lax.ppermute(value, "fsdp", [(i, i ^ bit) for i in range(count)])
        bit *= 2
    return value


def dot_nt(a, b):
    return lax.dot_general(a, b, (((1,), (1,)), ((), ())), preferred_element_type=F32)

def dot_nn(a, b):
    return jnp.dot(a, b, preferred_element_type=F32)


def attend_forward_kernel(parts, heads, kv, seq_ref, *refs):
    packs, outs = refs[:parts], refs[parts : 2 * parts]
    lse_ref, q_s, k_s, vt_s, o_s = refs[2 * parts :]
    tokens = packs[0].shape[0]
    seq = seq_ref[0]
    group = heads // kv
    for k in range(parts):
        rows = pl.ds(pl.multiple_of((seq ^ k) * tokens, tokens), tokens)
        q_s[rows, :] = packs[k][:, : heads * HD]
        for g in range(kv):
            lane = (heads + g) * HD
            k_s[g, rows, :] = packs[k][:, lane : lane + HD]
            lane = (heads + kv + g) * HD
            vt_s[g, :, rows] = packs[k][:, lane : lane + HD].T
    full = parts * tokens
    for g in range(kv):
        for i in range(full // BLOCK):
            keys = (i + 1) * BLOCK
            rows = slice(i * BLOCK, keys)
            for pair in range(group // 2):
                halves = []
                for h in (g * group + 2 * pair, g * group + 2 * pair + 1):
                    scores = dot_nt(k_s[g, :keys, :], q_s[rows, h * HD : (h + 1) * HD])
                    scores = scores * (HD**-0.5 * LOG2E)
                    top = jnp.max(scores, axis=0, keepdims=True)
                    powers = jnp.exp2(scores - top)
                    total = jnp.sum(powers, axis=0, keepdims=True)
                    halves.append(dot_nn(vt_s[g, :, :keys], powers.astype(BF)) / total)
                    lse_ref[h : h + 1, rows] = top + jnp.log2(total)
                lane = (g * group + 2 * pair) * HD
                o_s[rows, lane : lane + 2 * HD] = jnp.concatenate(halves, axis=0).T.astype(BF)
    for k in range(parts):
        rows = pl.ds(pl.multiple_of((seq ^ k) * tokens, tokens), tokens)
        outs[k][...] = o_s[rows, :]


def attend_forward(seq, packs, heads, kv):
    parts = len(packs)
    tokens = packs[0].shape[0]
    full = parts * tokens
    vmem = pl.BlockSpec(memory_space=pltpu.VMEM)
    flops = 4 * heads * full * full * HD * 5 // 8
    return pl.pallas_call(
        functools.partial(attend_forward_kernel, parts, heads, kv),
        out_shape=[jax.ShapeDtypeStruct((tokens, heads * HD), BF)] * parts
        + [jax.ShapeDtypeStruct((heads, full), F32)],
        in_specs=[pl.BlockSpec(memory_space=pltpu.SMEM)] + [vmem] * parts,
        out_specs=[vmem] * (parts + 1),
        scratch_shapes=[
            pltpu.VMEM((full, heads * HD), BF),
            pltpu.VMEM((kv, full, HD), BF),
            pltpu.VMEM((kv, HD, full), BF),
            pltpu.VMEM((full, heads * HD), BF),
        ],
        compiler_params=pltpu.CompilerParams(vmem_limit_bytes=48 * 2**20),
        cost_estimate=pl.CostEstimate(flops=flops * 4, bytes_accessed=4 * 2**20, transcendentals=heads * full * full * 5 // 8),
        name="attend_forward",
    )(seq.reshape(1), *packs)


def attend_backward_kernel(parts, heads, kv, seq_ref, lse_ref, *refs):
    packs, grads, outs = refs[:parts], refs[parts : 2 * parts], refs[2 * parts : 3 * parts]
    q_s, k_s, kt_s, v_s, g_s, dq_s, dk_s, dv_s = refs[3 * parts :]
    tokens = packs[0].shape[0]
    seq = seq_ref[0]
    group = heads // kv
    for k in range(parts):
        rows = pl.ds(pl.multiple_of((seq ^ k) * tokens, tokens), tokens)
        q_s[rows, :] = packs[k][:, : heads * HD]
        g_s[rows, :] = grads[k][...]
        for g in range(kv):
            lane = (heads + g) * HD
            k_s[g, rows, :] = packs[k][:, lane : lane + HD]
            kt_s[g, :, rows] = packs[k][:, lane : lane + HD].T
            lane = (heads + kv + g) * HD
            v_s[g, rows, :] = packs[k][:, lane : lane + HD]
    full = parts * tokens
    dk_s[...] = jnp.zeros_like(dk_s)
    dv_s[...] = jnp.zeros_like(dv_s)
    for g in range(kv):
        for i in range(full // BLOCK):
            keys = (i + 1) * BLOCK
            rows = slice(i * BLOCK, keys)
            for pair in range(group // 2):
                halves = []
                for h in (g * group + 2 * pair, g * group + 2 * pair + 1):
                    query = q_s[rows, h * HD : (h + 1) * HD]
                    grad = g_s[rows, h * HD : (h + 1) * HD]
                    scores = dot_nt(k_s[g, :keys, :], query) * (HD**-0.5 * LOG2E)
                    probs = jnp.exp2(scores - lse_ref[h : h + 1, rows])
                    grad_probs = dot_nt(v_s[g, :keys, :], grad)
                    inner = jnp.sum(probs * grad_probs, axis=0, keepdims=True)
                    grad_scores = (probs * (grad_probs - inner)).astype(BF)
                    dv_s[g, :keys, :] += dot_nn(probs.astype(BF), grad)
                    dk_s[g, :keys, :] += dot_nn(grad_scores, query)
                    halves.append(dot_nn(kt_s[g, :, :keys], grad_scores) * HD**-0.5)
                lane = (g * group + 2 * pair) * HD
                dq_s[rows, lane : lane + 2 * HD] = jnp.concatenate(halves, axis=0).T.astype(BF)
    for k in range(parts):
        rows = pl.ds(pl.multiple_of((seq ^ k) * tokens, tokens), tokens)
        outs[k][:, : heads * HD] = dq_s[rows, :]
        for g in range(kv):
            lane = (heads + g) * HD
            outs[k][:, lane : lane + HD] = (dk_s[g, rows, :] * HD**-0.5).astype(BF)
            lane = (heads + kv + g) * HD
            outs[k][:, lane : lane + HD] = dv_s[g, rows, :].astype(BF)


def attend_backward(seq, lse, packs, grads, heads, kv):
    parts = len(packs)
    tokens = packs[0].shape[0]
    full = parts * tokens
    vmem = pl.BlockSpec(memory_space=pltpu.VMEM)
    flops = 10 * heads * full * full * HD * 5 // 8
    return pl.pallas_call(
        functools.partial(attend_backward_kernel, parts, heads, kv),
        out_shape=[jax.ShapeDtypeStruct(packs[0].shape, BF)] * parts,
        in_specs=[pl.BlockSpec(memory_space=pltpu.SMEM)] + [vmem] * (2 * parts + 1),
        out_specs=[vmem] * parts,
        scratch_shapes=[
            pltpu.VMEM((full, heads * HD), BF),
            pltpu.VMEM((kv, full, HD), BF),
            pltpu.VMEM((kv, HD, full), BF),
            pltpu.VMEM((kv, full, HD), BF),
            pltpu.VMEM((full, heads * HD), BF),
            pltpu.VMEM((full, heads * HD), BF),
            pltpu.VMEM((kv, full, HD), F32),
            pltpu.VMEM((kv, full, HD), F32),
        ],
        compiler_params=pltpu.CompilerParams(vmem_limit_bytes=48 * 2**20),
        cost_estimate=pl.CostEstimate(flops=flops * 4, bytes_accessed=8 * 2**20, transcendentals=heads * full * full * 5 // 8),
        name="attend_backward",
    )(seq.reshape(1), lse, *packs, *grads)


def smem():
    return pl.BlockSpec(memory_space=pltpu.SMEM)


def params(mib=56):
    return pltpu.CompilerParams(vmem_limit_bytes=mib * 2**20)


def cost(flops, moved):
    return pl.CostEstimate(flops=flops, bytes_accessed=moved, transcendentals=0)


def place(full, shape, pieces, offsets, taken=None):
    count = len(pieces)
    given = [] if full is None else [full]

    def kernel(at_ref, *refs):
        sources, target, sems = refs[len(given) : -2], refs[-2], refs[-1]
        copies = []
        for i, source in enumerate(sources):
            rows, width = source.shape
            rows = taken or rows
            row = pl.multiple_of(at_ref[2 * i], rows)
            column = pl.multiple_of(at_ref[2 * i + 1], width)
            spot = target.at[pl.ds(row, rows), pl.ds(column, width)]
            copies.append(pltpu.make_async_copy(source.at[pl.ds(0, rows), :], spot, sems.at[i]))
            copies[-1].start()
        for copy in copies:
            copy.wait()

    hbm = pl.BlockSpec(memory_space=pl.ANY)
    moved = 2 * sum(piece.size * 2 for piece in pieces)
    return pl.pallas_call(
        kernel,
        out_shape=jax.ShapeDtypeStruct(shape, pieces[0].dtype),
        in_specs=[smem()] + [hbm] * (len(given) + count),
        out_specs=hbm,
        scratch_shapes=[pltpu.SemaphoreType.DMA((count,))],
        input_output_aliases={1: 0} if given else {},
        compiler_params=params(16),
        cost_estimate=cost(0, moved),
        name="place",
    )(jnp.stack([jnp.int32(v) for pair in offsets for v in pair]), *given, *pieces)


def turn(values, cos_table, sin_table):
    width = values.shape[1]
    lane = lax.broadcasted_iota(jnp.int32, values.shape, 1)
    swapped = jnp.where(
        lane % HD < HD // 2,
        pltpu.roll(values, width - HD // 2, 1),
        pltpu.roll(values, HD // 2, 1),
    )
    return values * cos_table + swapped * sin_table


def project_in(seq, inputs, gain, weight, cos_table, sin_table, parts):
    tokens, width = inputs.shape
    tile = cos_table.shape[1]
    each = tile // parts
    pack = tile + 2 * each

    def kernel(seq_ref, in_ref, gain_ref, w_ref, cos_ref, sin_ref, acts_ref, *packs):
        step = pl.program_id(0)

        @pl.when(step == 0)
        def _():
            values = in_ref[...].astype(F32)
            scale = lax.rsqrt(jnp.mean(values * values, axis=-1, keepdims=True) + EPSILON)
            acts_ref[...] = (values * scale * gain_ref[...]).astype(BF)

        rows = dot_nn(acts_ref[...], w_ref[...])
        turned = jnp.where(
            step == parts + 1, rows, turn(rows, cos_ref[...], sin_ref[...])
        ).astype(BF)
        seq_now = seq_ref[0]
        for k in range(parts):

            @pl.when((seq_now ^ k) == step)
            def _():
                packs[k][:, :tile] = turned

            for d in range(parts):
                for which in range(2):

                    @pl.when(((seq_now ^ k) == d) & (step == parts + which))
                    def _():
                        lane = tile + which * each
                        packs[k][:, lane : lane + each] = turned[:, d * each : (d + 1) * each]

    def whole(shape):
        return pl.BlockSpec(shape, lambda n: (0,) * len(shape))

    return pl.pallas_call(
        kernel,
        grid=(parts + 2,),
        out_shape=[jax.ShapeDtypeStruct((tokens, width), BF)]
        + [jax.ShapeDtypeStruct((tokens, pack), BF)] * parts,
        in_specs=[
            smem(),
            whole((tokens, width)),
            whole((1, width)),
            pl.BlockSpec((width, tile), lambda n: (0, n)),
            whole((tokens, tile)),
            whole((tokens, tile)),
        ],
        out_specs=[whole((tokens, width))] + [whole((tokens, pack))] * parts,
        compiler_params=params(),
        cost_estimate=cost(2 * tokens * width * tile * (parts + 2), 2 * width * tile * (parts + 2)),
        name="project_in",
    )(seq.reshape(1), inputs, gain, weight, cos_table, sin_table)


def project_out(seq, mixed, inputs, gain, weight):
    parts = len(mixed)
    tokens, width = inputs.shape
    each = mixed[0].shape[1]
    tile = width // parts

    def kernel(seq_ref, *refs):
        parts_in, (in_ref, gain_ref, w_ref, flat_ref, res_ref, acts_ref) = refs[:parts], refs[parts:]
        step = pl.program_id(0)

        @pl.when(step == 0)
        def _():
            for k in range(parts):
                lane = pl.multiple_of((seq_ref[0] ^ k) * each, each)
                flat_ref[:, pl.ds(lane, each)] = parts_in[k][...]

        lanes = pl.ds(pl.multiple_of(step * tile, tile), tile)
        res_ref[:, lanes] = in_ref[:, lanes].astype(F32) + dot_nn(flat_ref[...], w_ref[...])

        @pl.when(step == parts - 1)
        def _():
            values = res_ref[...]
            scale = lax.rsqrt(jnp.mean(values * values, axis=-1, keepdims=True) + EPSILON)
            acts_ref[...] = (values * scale * gain_ref[...]).astype(BF)

    def whole(shape):
        return pl.BlockSpec(shape, lambda n: (0,) * len(shape))

    return pl.pallas_call(
        kernel,
        grid=(parts,),
        out_shape=[
            jax.ShapeDtypeStruct((tokens, parts * each), BF),
            jax.ShapeDtypeStruct((tokens, width), F32),
            jax.ShapeDtypeStruct((tokens, width), BF),
        ],
        in_specs=[smem()]
        + [whole((tokens, each))] * parts
        + [
            whole((tokens, width)),
            whole((1, width)),
            pl.BlockSpec((parts * each, tile), lambda n: (0, n)),
        ],
        out_specs=[whole((tokens, parts * each)), whole((tokens, width)), whole((tokens, width))],
        compiler_params=params(),
        cost_estimate=cost(2 * tokens * width * parts * each, 2 * width * parts * each),
        name="project_out",
    )(seq.reshape(1), *mixed, inputs, gain, weight)


def feed_forward(acts, grads, gate, up, down, begun=None):
    tokens, width = acts.shape
    hidden = gate.shape[0]
    tile = 256
    steps = hidden // tile
    kind = F32 if begun is None else BF
    begun = [] if begun is None else list(begun)

    def kernel(a_ref, c_ref, g_ref, u_ref, d_ref, *refs):
        starts, (h_ref, gg_ref, gu_ref, o_ref, ga_ref, o_s, ga_s) = refs[:-7], refs[-7:]
        step = pl.program_id(0)

        @pl.when(step == 0)
        def _():
            if starts:
                o_s[...] = starts[0][...]
                ga_s[...] = starts[1][...]
            else:
                o_s[...] = jnp.zeros_like(o_s)
                ga_s[...] = jnp.zeros_like(ga_s)

        gate_act = dot_nt(a_ref[...], g_ref[...])
        up_act = dot_nt(a_ref[...], u_ref[...])
        grad_hidden = dot_nt(c_ref[...], d_ref[...])
        sigma = jax.nn.sigmoid(gate_act)
        silu = gate_act * sigma
        low = (silu * up_act).astype(BF)
        grad_gate = (grad_hidden * up_act * (sigma * (1.0 + gate_act * (1.0 - sigma)))).astype(BF)
        grad_up = (grad_hidden * silu).astype(BF)
        h_ref[...] = low
        gg_ref[...] = grad_gate
        gu_ref[...] = grad_up
        o_s[...] += dot_nn(low, d_ref[...])
        ga_s[...] += dot_nn(grad_gate, g_ref[...]) + dot_nn(grad_up, u_ref[...])

        @pl.when(step == steps - 1)
        def _():
            o_ref[...] = o_s[...].astype(kind)
            ga_ref[...] = ga_s[...].astype(kind)

    whole = pl.BlockSpec((tokens, width), lambda n: (0, 0))
    rows = pl.BlockSpec((tile, width), lambda n: (n, 0))
    lanes = pl.BlockSpec((tokens, tile), lambda n: (0, n))
    return pl.pallas_call(
        kernel,
        grid=(steps,),
        out_shape=[jax.ShapeDtypeStruct((tokens, hidden), BF)] * 3
        + [jax.ShapeDtypeStruct((tokens, width), kind)] * 2,
        in_specs=[whole, whole, rows, rows, rows] + [whole] * len(begun),
        out_specs=[lanes] * 3 + [whole] * 2,
        scratch_shapes=[pltpu.VMEM((tokens, width), F32)] * 2,
        compiler_params=params(),
        cost_estimate=cost(12 * tokens * width * hidden, 6 * width * hidden),
        name="feed_forward",
    )(acts, grads, gate, up, down, *begun)


def middle_back(seq, terms, residual, grad_out, gain, weight, parts):
    tokens, width = residual.shape
    tile = weight.shape[0] // parts

    def kernel(seq_ref, t0_ref, t1_ref, res_ref, go_ref, gain_ref, w_ref, gr_ref, low_ref, gg_ref, *outs):
        step = pl.program_id(0)

        @pl.when(step == 0)
        def _():
            grad = t0_ref[...].astype(F32) + t1_ref[...].astype(F32)
            values = res_ref[...]
            scale = lax.rsqrt(jnp.mean(values * values, axis=-1, keepdims=True) + EPSILON)
            weighted = grad * gain_ref[...]
            inner = jnp.mean(weighted * values, axis=-1, keepdims=True)
            result = go_ref[...].astype(F32) + scale * weighted - values * (scale**3 * inner)
            gr_ref[...] = result
            low_ref[...] = result.astype(BF)
            gg_ref[...] = jnp.sum(grad * values * scale, axis=0, keepdims=True)

        part = dot_nt(low_ref[...], w_ref[...]).astype(BF)
        for k in range(parts):

            @pl.when((seq_ref[0] ^ k) == step)
            def _():
                outs[k][...] = part

    def whole(shape):
        return pl.BlockSpec(shape, lambda n: (0,) * len(shape))

    full, row = whole((tokens, width)), whole((1, width))
    return pl.pallas_call(
        kernel,
        grid=(parts,),
        out_shape=[
            jax.ShapeDtypeStruct((tokens, width), F32),
            jax.ShapeDtypeStruct((tokens, width), BF),
            jax.ShapeDtypeStruct((1, width), F32),
        ]
        + [jax.ShapeDtypeStruct((tokens, tile), BF)] * parts,
        in_specs=[smem(), full, full, full, full, row, pl.BlockSpec((tile, width), lambda n: (n, 0))],
        out_specs=[full, full, row] + [whole((tokens, tile))] * parts,
        compiler_params=params(),
        cost_estimate=cost(2 * tokens * width * tile * parts, 2 * width * tile * parts + 8 * tokens * width),
        name="middle_back",
    )(seq.reshape(1), terms[0], terms[1], residual, grad_out, gain, weight)


def unpack(seq, packs, cos_table, sin_table):
    parts = len(packs)
    tokens, tile = cos_table.shape
    each = tile // parts

    def kernel(seq_ref, *refs):
        ins, (cos_ref, sin_ref, out_ref) = refs[:parts], refs[parts:]
        for k in range(parts):
            at = seq_ref[0] ^ k
            queries = turn(ins[k][:, :tile].astype(F32), cos_ref[...], -sin_ref[...])
            out_ref[:, pl.ds(pl.multiple_of(at * tile, tile), tile)] = queries.astype(BF)
            keys = turn(
                ins[k][:, tile : tile + each].astype(F32), cos_ref[:, :each], -sin_ref[:, :each]
            )
            lane = pl.multiple_of(parts * tile + at * each, each)
            out_ref[:, pl.ds(lane, each)] = keys.astype(BF)
            lane = pl.multiple_of((parts + 1) * tile + at * each, each)
            out_ref[:, pl.ds(lane, each)] = ins[k][:, tile + each :]

    vmem = pl.BlockSpec(memory_space=pltpu.VMEM)
    return pl.pallas_call(
        kernel,
        out_shape=jax.ShapeDtypeStruct((tokens, (parts + 2) * tile), BF),
        in_specs=[smem()] + [vmem] * (parts + 2),
        out_specs=vmem,
        compiler_params=params(),
        cost_estimate=cost(0, 6 * 2**20),
        name="unpack",
    )(seq.reshape(1), *packs, cos_table, sin_table)


def inner_back(grad_qkv, weight, inputs, gain, grad_res):
    tokens, width = inputs.shape
    tile = 512
    steps = width // tile

    def kernel(gq_ref, w_ref, in_ref, gain_ref, gr_ref, out_ref, gg_ref, grad_s):
        step = pl.program_id(0)
        grad_s[:, pl.ds(pl.multiple_of(step * tile, tile), tile)] = dot_nt(gq_ref[...], w_ref[...])

        @pl.when(step == steps - 1)
        def _():
            grad = grad_s[...]
            values = in_ref[...].astype(F32)
            scale = lax.rsqrt(jnp.mean(values * values, axis=-1, keepdims=True) + EPSILON)
            weighted = grad * gain_ref[...]
            inner = jnp.mean(weighted * values, axis=-1, keepdims=True)
            result = gr_ref[...] + scale * weighted - values * (scale**3 * inner)
            out_ref[...] = result.astype(BF)
            gg_ref[...] = jnp.sum(grad * values * scale, axis=0, keepdims=True)

    def whole(shape):
        return pl.BlockSpec(shape, lambda n: (0,) * len(shape))

    full, row = whole((tokens, width)), whole((1, width))
    return pl.pallas_call(
        kernel,
        grid=(steps,),
        out_shape=[jax.ShapeDtypeStruct((tokens, width), BF), jax.ShapeDtypeStruct((1, width), F32)],
        in_specs=[
            whole(grad_qkv.shape),
            pl.BlockSpec((tile, weight.shape[1]), lambda n: (n, 0)),
            full,
            row,
            full,
        ],
        out_specs=[full, row],
        scratch_shapes=[pltpu.VMEM((tokens, width), F32)],
        compiler_params=params(),
        cost_estimate=cost(2 * tokens * weight.size, 2 * weight.size),
        name="inner_back",
    )(grad_qkv, weight, inputs, gain, grad_res)


def weight_grad(left, right, rows, blocks, half, adds=()):
    count = len(left)
    tokens = left[0].shape[0]
    width = right[0].shape[1] // 2
    tile = min(rows, 512)
    steps = rows // tile
    total_rows = rows * len(blocks)

    def kernel(at_ref, *refs):
        lefts, rights, extra, out = refs[:count], refs[count : 2 * count], refs[2 * count : -1], refs[-1]
        total = None
        for l_ref, r_ref in zip(lefts, rights):
            term = lax.dot_general(
                l_ref[...], r_ref[...], (((0,), (0,)), ((), ())), preferred_element_type=F32
            )
            total = term if total is None else total + term
        for ref in extra:
            total = total + ref[...].astype(F32)
        out[...] = total.astype(BF)

    rows_spec = pl.BlockSpec((tile, width), lambda n, at: (n, 0))
    spec = pltpu.PrefetchScalarGridSpec(
        num_scalar_prefetch=1,
        grid=(steps * len(blocks),),
        in_specs=[pl.BlockSpec((tokens, tile), lambda n, at: (0, at[1 + n]))] * count
        + [pl.BlockSpec((tokens, width), lambda n, at: (0, at[0]))] * count
        + [rows_spec] * len(adds),
        out_specs=rows_spec,
    )
    at = [jnp.int32(half)]
    for block in blocks:
        at += [jnp.int32(block) * steps + i for i in range(steps)]
    return pl.pallas_call(
        kernel,
        grid_spec=spec,
        out_shape=jax.ShapeDtypeStruct((total_rows, width), BF),
        compiler_params=params(),
        cost_estimate=cost(
            2 * tokens * count * total_rows * width, 2 * (tokens * count + total_rows) * width
        ),
        name="weight_grad",
    )(jnp.stack(at), *left, *right, *adds)


def join(core, mine, other, widths):
    rows, half = mine.shape
    tile = min(rows, 256)

    def kernel(core_ref, mine_ref, other_ref, *refs):
        outs, full = refs[:-1], refs[-1]
        target = outs[0] if len(outs) == 1 else full
        at = pl.multiple_of(core_ref[0] * half, half)
        target[:, pl.ds(at, half)] = mine_ref[...].astype(F32)
        at = pl.multiple_of((1 - core_ref[0]) * half, half)
        target[:, pl.ds(at, half)] = other_ref[...].astype(F32)
        if len(outs) > 1:
            lane = 0
            for out in outs:
                out[...] = full[:, lane : lane + out.shape[1]]
                lane += out.shape[1]

    def block(width):
        return pl.BlockSpec((tile, width), lambda n: (n, 0))

    return pl.pallas_call(
        kernel,
        grid=(rows // tile,),
        out_shape=[jax.ShapeDtypeStruct((rows, width), F32) for width in widths],
        in_specs=[smem(), block(half), block(half)],
        out_specs=[block(width) for width in widths],
        scratch_shapes=[pltpu.VMEM((tile, 2 * half) if len(widths) > 1 else (8, 128), F32)],
        compiler_params=params(),
        cost_estimate=cost(0, rows * half * 12),
        name="join",
    )(core.reshape(1), mine, other)
def half_of(array, which, axis=1):
    size = array.shape[axis] // 2
    return lax.dynamic_slice_in_dim(array, which * size, size, axis)


def after_all(values, *others):
    return list(lax.optimization_barrier(tuple(values) + others)[: len(values)])


def gather_rows(shard, start, first, core, z, y):
    cols = columns()
    rows, width = shard.shape
    half = width // 2
    shape = (rows * LINE * cols, width)
    full = None
    pieces = [start]
    table = []
    last = first
    for j in range(LINE):
        if j + 1 < LINE:
            pieces.append(z_next(pieces[j]))
        subs = [pieces[j]]
        for k in range(1, cols):
            sent = subs[-1] if last is None else after(subs[-1], last)
            subs.append(y_next(sent))
            last = subs[-1]
        placed, offsets = [], []
        for k, sub in enumerate(subs):
            row = (((z - j) % LINE) * cols + (y - k) % cols) * rows
            if j == 0 and k == 0:
                placed.append(shard)
                offsets.append((row, 0))
                continue
            placed += [sub, core_swap(sub)]
            offsets += [(row, core * half), (row, (1 - core) * half)]
        table.append(subs)
        full = place(full, shape, placed, offsets, rows)
    return full, table, pieces[-1], last


def gather_others(shards_in, first, core, side):
    cols = columns()
    rows, width = shards_in[0].shape
    half, part = width // 2, rows // 2
    sent, moved = list(first), []
    for shard in shards_in:
        piece = half_of(half_of(shard, side, 0), core)
        subs = []
        for k in range(1, cols):
            piece = y_next(after(piece, sent[-2]))
            sent.append(piece)
            subs.append(piece)
        moved.append(subs)
    fulls = []
    for subs in moved:
        placed, offsets = [], []
        for k, sub in enumerate(subs):
            crossed = x_swap(sub)
            for piece, at in ((sub, side), (crossed, 1 - side)):
                row = k * rows + at * part
                placed += [piece, core_swap(piece)]
                offsets += [(row, core * half), (row, (1 - core) * half)]
        fulls.append(place(None, (rows * (cols - 1), width), placed, offsets))
    return fulls


def finish_sum(low, core, widths):
    whole = (low.astype(F32) + x_swap(low).astype(F32)).astype(BF)
    return join(core, whole, core_swap(whole), widths)


def scatter_rows(left, right, core, z, y, widths):
    cols = columns()
    rows = left.shape[1] // LINE
    each = rows // cols
    order = list(range(1, LINE)) + [0]
    blocks = [(z - j) % LINE for j in order]
    sent = core_swap(weight_grad([left], [right], rows, blocks, 1 - core))
    kept = weight_grad([left], [right], rows, blocks, core, [sent])

    def in_line(j):
        base = order.index(j) * rows

        def at(k):
            start = base + (y - k) % cols * each
            return lax.dynamic_slice_in_dim(kept, start, each, 0).astype(F32)

        return ring_scatter(at, y_next, cols)

    return finish_sum(ring_scatter(in_line, z_next, LINE).astype(BF), core, widths)


def scatter_hidden(own, others, right, core):
    cols = columns()
    rows, far_rows = own[0].shape[1], others[0].shape[1]
    far_sent = core_swap(weight_grad(others, right, far_rows, [0], 1 - core))
    own_sent = core_swap(weight_grad(own, right, rows, [0], 1 - core))
    far = weight_grad(others, right, far_rows, [0], core, [far_sent])
    total = y_next(far[:rows])
    for k in range(1, cols - 1):
        term = far[k * rows : (k + 1) * rows]
        total = y_next((total.astype(F32) + term.astype(F32)).astype(BF))
    low = weight_grad(own, right, rows, [0], core, [own_sent, total])
    return finish_sum(low, core, [2 * low.shape[1]])


def rope_tables(positions, repeat):
    frequency = THETA ** (-(jnp.arange(HD // 2, dtype=F32) * 2.0) / HD)
    angles = positions.astype(F32)[:, None] * frequency[None, :]
    cos, sin = jnp.cos(angles), jnp.sin(angles)
    return (
        jnp.tile(jnp.concatenate([cos, cos], axis=1), (1, repeat)),
        jnp.tile(jnp.concatenate([-sin, sin], axis=1), (1, repeat)),
    )


def exchange(packs):
    return [packs[0]] + [seq_swap(packs[k], k) for k in range(1, len(packs))]


def shards(
    inputs,
    query_weight,
    key_weight,
    value_weight,
    output_weight,
    gate_weight,
    up_weight,
    down_weight,
    gain_attn,
    gain_ffn,
    cotangent,
):
    seq_count, local_len, width = inputs.shape
    assert seq_count == 1
    tokens = local_len
    parts = lax.axis_size("seq")
    kv_local = KVH // parts
    cols = columns()
    seq = lax.axis_index("seq")
    core, side = seq % 2, seq // 2
    fsdp = lax.axis_index("fsdp")
    z, y = fsdp // cols, fsdp % cols
    q_width, kv_width = query_weight.shape[1], key_weight.shape[1]
    heads_local = q_width // HD // parts
    flat_in = inputs.reshape(tokens, width)
    grad_out = cotangent.reshape(tokens, width)

    qkv_shard = jnp.concatenate([query_weight, key_weight, value_weight], axis=1)
    rows = qkv_shard.shape[0]
    gains = jnp.concatenate([gain_attn, gain_ffn]).reshape(1, 2 * rows)
    start = half_of(qkv_shard, core)
    start = jnp.concatenate([start, jnp.pad(gains, ((0, 15), (0, start.shape[1] - 2 * rows)))], axis=0)
    qkv_weight, table, z_end, y_end = gather_rows(qkv_shard, start, None, core, z, y)
    gain_full = jnp.zeros((2, width), BF)
    for j, subs in enumerate(table):
        for k, sub in enumerate(subs):
            at = (((z - j) % LINE) * cols + (y - k) % cols) * rows
            pair = sub[rows, : 2 * rows].reshape(2, rows)
            gain_full = lax.dynamic_update_slice(gain_full, pair, (0, at))
    gain_one = gain_full[:1].astype(F32)
    gain_two = gain_full[1:].astype(F32)
    positions = seq * local_len + jnp.arange(local_len)
    cos_table, sin_table = rope_tables(positions, kv_width // HD)

    out_start = after(half_of(output_weight, core), z_end)
    out_weight, table, z_end, y_end = gather_rows(output_weight, out_start, y_end, core, z, y)
    grad_parts = ring_gather(after(grad_out, z_end), z_next, LINE)
    own = (gate_weight, up_weight, down_weight)
    far = gather_others(own, (table[-2][-1], y_end), core, side)

    acts_one, *sent = project_in(seq, flat_in, gain_one, qkv_weight, cos_table, sin_table, parts)
    packs = exchange(sent)
    *mixed_sent, log_totals = attend_forward(seq, packs, heads_local, kv_local)
    mixed_flat, residual, acts_two = project_out(
        seq, exchange(mixed_sent), flat_in, gain_two, out_weight
    )

    acts_parts = ring_gather(acts_two, z_next, LINE)
    near_done = [feed_forward(a, g, *own) for a, g in zip(acts_parts, grad_parts)]
    far_done = [None] * LINE
    for j in list(range(1, LINE)) + [0]:
        far_done[j] = feed_forward(acts_parts[j], grad_parts[j], *far, near_done[j][3:])
    ffn_parts, grad_terms = [d[3] for d in far_done], [d[4] for d in far_done]

    def line_sum(terms):
        total = terms[1]
        for j in range(2, LINE):
            total = (terms[j].astype(F32) + z_next(total).astype(F32)).astype(BF)
        return z_next(total)

    grad_recv = line_sum(grad_terms)
    grad_res, grad_res_low, grad_gain_two, *grad_sent = middle_back(
        seq, (grad_recv, grad_terms[0]), residual, grad_out, gain_two, out_weight, parts
    )
    grad_packs = exchange(grad_sent)
    ffn_parts[1] = after(ffn_parts[1], grad_recv)
    ffn_recv = line_sum(ffn_parts)
    outputs = (residual + ffn_recv.astype(F32) + ffn_parts[0].astype(F32)).astype(BF)

    def hidden_grad(which, right):
        return scatter_hidden([d[which] for d in near_done], [d[which] for d in far_done], right, core)

    d_down = hidden_grad(0, grad_parts)
    d_gate = hidden_grad(1, acts_parts)
    d_up = hidden_grad(2, acts_parts)
    d_out = scatter_rows(mixed_flat, grad_res_low, core, z, y, [width])

    back_sent = attend_backward(seq, log_totals, packs, grad_packs, heads_local, kv_local)
    grad_qkv = unpack(seq, exchange(back_sent), cos_table, sin_table)
    d_qkv = scatter_rows(acts_one, grad_qkv, core, z, y, [q_width, kv_width, kv_width])
    grad_inputs, grad_gain_one = inner_back(grad_qkv, qkv_weight, flat_in, gain_one, grad_res)
    gain_sums = all_sum(jnp.concatenate([grad_gain_one, grad_gain_two], axis=0))
    rows = gain_attn.shape[0]
    gain_sums = lax.dynamic_slice_in_dim(gain_sums, fsdp * rows, rows, 1)
    return (
        outputs.reshape(inputs.shape),
        grad_inputs.reshape(inputs.shape),
        d_qkv[0],
        d_qkv[1],
        d_qkv[2],
        d_out[0],
        d_gate[0],
        d_up[0],
        d_down[0],
        gain_sums[0],
        gain_sums[1],
    )


def solution(mesh):
    token_spec, row_spec, gain_spec = P("fsdp", "seq", None), P("fsdp", None), P("fsdp")
    return jax.shard_map(
        shards,
        mesh=mesh,
        in_specs=(token_spec,) + (row_spec,) * 7 + (gain_spec,) * 2 + (token_spec,),
        out_specs=(token_spec,) * 2 + (row_spec,) * 7 + (gain_spec,) * 2,
        check_vma=False,
    )
```

```python
import functools

import jax
import jax.numpy as jnp
from jax import lax
from jax.experimental import pallas as pl
from jax.experimental.pallas import tpu as pltpu
from jax.sharding import PartitionSpec as P

KVH = 8
HD = 64
BLOCK = 256
LINE = 4

EPSILON = 1e-05
THETA = 500000.0
LOG2E = 1.4426950408889634

BF = jnp.bfloat16
F32 = jnp.float32


def after(value, *others):
    return lax.optimization_barrier((value,) + others)[0]


def columns():
    return lax.axis_size("fsdp") // LINE


def z_next(value):
    cols = columns()
    count = lax.axis_size("fsdp")
    return lax.ppermute(value, "fsdp", [(i, (i + cols) % count) for i in range(count)])


def y_next(value):
    cols = columns()
    count = lax.axis_size("fsdp")
    return lax.ppermute(
        value, "fsdp", [(i, i // cols * cols + (i + 1) % cols) for i in range(count)]
    )


def seq_swap(value, bit):
    return lax.ppermute(value, "seq", [(i, i ^ bit) for i in range(lax.axis_size("seq"))])


def core_swap(value):
    return seq_swap(value, 1)


def x_swap(value):
    return seq_swap(value, 2)


def ring_gather(value, step, count):
    pieces = [value]
    for _ in range(count - 1):
        pieces.append(step(pieces[-1]))
    return pieces


def ring_scatter(part_of, step, count):
    total = None
    for j in list(range(1, count)) + [0]:
        total = part_of(j) if total is None else part_of(j) + total.astype(F32)
        if j:
            total = step(total.astype(BF))
    return total


def all_sum(value):
    bit = 1
    while bit < lax.axis_size("seq"):
        value = value + seq_swap(value, bit)
        bit *= 2
    count = lax.axis_size("fsdp")
    bit = 1
    while bit < count:
        value = value + lax.ppermute(value, "fsdp", [(i, i ^ bit) for i in range(count)])
        bit *= 2
    return value


def dot_nt(a, b):
    return lax.dot_general(a, b, (((1,), (1,)), ((), ())), preferred_element_type=F32)

def dot_nn(a, b):
    return jnp.dot(a, b, preferred_element_type=F32)


def attend_forward_kernel(parts, heads, kv, seq_ref, *refs):
    packs, outs = refs[:parts], refs[parts : 2 * parts]
    lse_ref, q_s, k_s, vt_s, o_s = refs[2 * parts :]
    tokens = packs[0].shape[0]
    seq = seq_ref[0]
    group = heads // kv
    for k in range(parts):
        rows = pl.ds(pl.multiple_of((seq ^ k) * tokens, tokens), tokens)
        q_s[rows, :] = packs[k][:, : heads * HD]
        for g in range(kv):
            lane = (heads + g) * HD
            k_s[g, rows, :] = packs[k][:, lane : lane + HD]
            lane = (heads + kv + g) * HD
            vt_s[g, :, rows] = packs[k][:, lane : lane + HD].T
    full = parts * tokens
    for g in range(kv):
        for i in range(full // BLOCK):
            keys = (i + 1) * BLOCK
            rows = slice(i * BLOCK, keys)
            for pair in range(group // 2):
                halves = []
                for h in (g * group + 2 * pair, g * group + 2 * pair + 1):
                    scores = dot_nt(k_s[g, :keys, :], q_s[rows, h * HD : (h + 1) * HD])
                    scores = scores * (HD**-0.5 * LOG2E)
                    top = jnp.max(scores, axis=0, keepdims=True)
                    powers = jnp.exp2(scores - top)
                    total = jnp.sum(powers, axis=0, keepdims=True)
                    halves.append(dot_nn(vt_s[g, :, :keys], powers.astype(BF)) / total)
                    lse_ref[h : h + 1, rows] = top + jnp.log2(total)
                lane = (g * group + 2 * pair) * HD
                o_s[rows, lane : lane + 2 * HD] = jnp.concatenate(halves, axis=0).T.astype(BF)
    for k in range(parts):
        rows = pl.ds(pl.multiple_of((seq ^ k) * tokens, tokens), tokens)
        outs[k][...] = o_s[rows, :]


def attend_forward(seq, packs, heads, kv):
    parts = len(packs)
    tokens = packs[0].shape[0]
    full = parts * tokens
    vmem = pl.BlockSpec(memory_space=pltpu.VMEM)
    flops = 4 * heads * full * full * HD * 5 // 8
    return pl.pallas_call(
        functools.partial(attend_forward_kernel, parts, heads, kv),
        out_shape=[jax.ShapeDtypeStruct((tokens, heads * HD), BF)] * parts
        + [jax.ShapeDtypeStruct((heads, full), F32)],
        in_specs=[pl.BlockSpec(memory_space=pltpu.SMEM)] + [vmem] * parts,
        out_specs=[vmem] * (parts + 1),
        scratch_shapes=[
            pltpu.VMEM((full, heads * HD), BF),
            pltpu.VMEM((kv, full, HD), BF),
            pltpu.VMEM((kv, HD, full), BF),
            pltpu.VMEM((full, heads * HD), BF),
        ],
        compiler_params=pltpu.CompilerParams(vmem_limit_bytes=48 * 2**20),
        cost_estimate=pl.CostEstimate(flops=flops * 4, bytes_accessed=4 * 2**20, transcendentals=heads * full * full * 5 // 8),
        name="attend_forward",
    )(seq.reshape(1), *packs)


def attend_backward_kernel(parts, heads, kv, seq_ref, lse_ref, *refs):
    packs, grads, outs = refs[:parts], refs[parts : 2 * parts], refs[2 * parts : 3 * parts]
    q_s, k_s, kt_s, v_s, g_s, dq_s, dk_s, dv_s = refs[3 * parts :]
    tokens = packs[0].shape[0]
    seq = seq_ref[0]
    group = heads // kv
    for k in range(parts):
        rows = pl.ds(pl.multiple_of((seq ^ k) * tokens, tokens), tokens)
        q_s[rows, :] = packs[k][:, : heads * HD]
        g_s[rows, :] = grads[k][...]
        for g in range(kv):
            lane = (heads + g) * HD
            k_s[g, rows, :] = packs[k][:, lane : lane + HD]
            kt_s[g, :, rows] = packs[k][:, lane : lane + HD].T
            lane = (heads + kv + g) * HD
            v_s[g, rows, :] = packs[k][:, lane : lane + HD]
    full = parts * tokens
    dk_s[...] = jnp.zeros_like(dk_s)
    dv_s[...] = jnp.zeros_like(dv_s)
    for g in range(kv):
        for i in range(full // BLOCK):
            keys = (i + 1) * BLOCK
            rows = slice(i * BLOCK, keys)
            for pair in range(group // 2):
                halves = []
                for h in (g * group + 2 * pair, g * group + 2 * pair + 1):
                    query = q_s[rows, h * HD : (h + 1) * HD]
                    grad = g_s[rows, h * HD : (h + 1) * HD]
                    scores = dot_nt(k_s[g, :keys, :], query) * (HD**-0.5 * LOG2E)
                    probs = jnp.exp2(scores - lse_ref[h : h + 1, rows])
                    grad_probs = dot_nt(v_s[g, :keys, :], grad)
                    inner = jnp.sum(probs * grad_probs, axis=0, keepdims=True)
                    grad_scores = (probs * (grad_probs - inner)).astype(BF)
                    dv_s[g, :keys, :] += dot_nn(probs.astype(BF), grad)
                    dk_s[g, :keys, :] += dot_nn(grad_scores, query)
                    halves.append(dot_nn(kt_s[g, :, :keys], grad_scores) * HD**-0.5)
                lane = (g * group + 2 * pair) * HD
                dq_s[rows, lane : lane + 2 * HD] = jnp.concatenate(halves, axis=0).T.astype(BF)
    for k in range(parts):
        rows = pl.ds(pl.multiple_of((seq ^ k) * tokens, tokens), tokens)
        outs[k][:, : heads * HD] = dq_s[rows, :]
        for g in range(kv):
            lane = (heads + g) * HD
            outs[k][:, lane : lane + HD] = (dk_s[g, rows, :] * HD**-0.5).astype(BF)
            lane = (heads + kv + g) * HD
            outs[k][:, lane : lane + HD] = dv_s[g, rows, :].astype(BF)


def attend_backward(seq, lse, packs, grads, heads, kv):
    parts = len(packs)
    tokens = packs[0].shape[0]
    full = parts * tokens
    vmem = pl.BlockSpec(memory_space=pltpu.VMEM)
    flops = 10 * heads * full * full * HD * 5 // 8
    return pl.pallas_call(
        functools.partial(attend_backward_kernel, parts, heads, kv),
        out_shape=[jax.ShapeDtypeStruct(packs[0].shape, BF)] * parts,
        in_specs=[pl.BlockSpec(memory_space=pltpu.SMEM)] + [vmem] * (2 * parts + 1),
        out_specs=[vmem] * parts,
        scratch_shapes=[
            pltpu.VMEM((full, heads * HD), BF),
            pltpu.VMEM((kv, full, HD), BF),
            pltpu.VMEM((kv, HD, full), BF),
            pltpu.VMEM((kv, full, HD), BF),
            pltpu.VMEM((full, heads * HD), BF),
            pltpu.VMEM((full, heads * HD), BF),
            pltpu.VMEM((kv, full, HD), F32),
            pltpu.VMEM((kv, full, HD), F32),
        ],
        compiler_params=pltpu.CompilerParams(vmem_limit_bytes=48 * 2**20),
        cost_estimate=pl.CostEstimate(flops=flops * 4, bytes_accessed=8 * 2**20, transcendentals=heads * full * full * 5 // 8),
        name="attend_backward",
    )(seq.reshape(1), lse, *packs, *grads)


def smem():
    return pl.BlockSpec(memory_space=pltpu.SMEM)


def params(mib=56):
    return pltpu.CompilerParams(vmem_limit_bytes=mib * 2**20)


def cost(flops, moved):
    return pl.CostEstimate(flops=flops, bytes_accessed=moved, transcendentals=0)


def place(shape, pieces, offsets):
    count = len(pieces)

    def kernel(at_ref, *refs):
        sources, target, sems = refs[:-2], refs[-2], refs[-1]
        copies = []
        for i, source in enumerate(sources):
            rows, width = source.shape
            row = pl.multiple_of(at_ref[2 * i], rows)
            column = pl.multiple_of(at_ref[2 * i + 1], width)
            spot = target.at[pl.ds(row, rows), pl.ds(column, width)]
            copies.append(pltpu.make_async_copy(source, spot, sems.at[i]))
            copies[-1].start()
        for copy in copies:
            copy.wait()

    moved = 2 * sum(piece.size * 2 for piece in pieces)
    return pl.pallas_call(
        kernel,
        out_shape=jax.ShapeDtypeStruct(shape, pieces[0].dtype),
        in_specs=[smem()] + [pl.BlockSpec(memory_space=pl.ANY)] * count,
        out_specs=pl.BlockSpec(memory_space=pltpu.HBM),
        scratch_shapes=[pltpu.SemaphoreType.DMA((count,))],
        compiler_params=params(16),
        cost_estimate=cost(0, moved),
        name="place",
    )(jnp.stack([jnp.int32(v) for pair in offsets for v in pair]), *pieces)


def turn(values, cos_table, sin_table):
    width = values.shape[1]
    lane = lax.broadcasted_iota(jnp.int32, values.shape, 1)
    swapped = jnp.where(
        lane % HD < HD // 2,
        pltpu.roll(values, width - HD // 2, 1),
        pltpu.roll(values, HD // 2, 1),
    )
    return values * cos_table + swapped * sin_table


def whole(shape):
    return pl.BlockSpec(shape, lambda n: (0,) * len(shape))


def project_in(seq, z, inputs, gain, groups, cos_table, sin_table, parts):
    tokens, width = inputs.shape
    tile = cos_table.shape[1]
    each = tile // parts
    pack = tile + 2 * each
    count = len(groups)
    depth = width // count

    def kernel(at_ref, in_ref, gain_ref, *refs):
        w_refs, (cos_ref, sin_ref, acts_ref), packs = refs[:count], refs[count : count + 3], refs[count + 3 :]
        step = pl.program_id(0)

        @pl.when(step == 0)
        def _():
            values = in_ref[...].astype(F32)
            scale = lax.rsqrt(jnp.mean(values * values, axis=-1, keepdims=True) + EPSILON)
            acts_ref[...] = (values * scale * gain_ref[...]).astype(BF)

        rows = None
        for j in range(count):
            lanes = pl.ds(pl.multiple_of((at_ref[1] + count - j) % count * depth, depth), depth)
            term = dot_nn(acts_ref[:, lanes], w_refs[j][...])
            rows = term if rows is None else rows + term
        turned = jnp.where(
            step == parts + 1, rows, turn(rows, cos_ref[...], sin_ref[...])
        ).astype(BF)
        seq_now = at_ref[0]
        for k in range(parts):

            @pl.when((seq_now ^ k) == step)
            def _():
                packs[k][:, :tile] = turned

            for d in range(parts):
                for which in range(2):

                    @pl.when(((seq_now ^ k) == d) & (step == parts + which))
                    def _():
                        lane = tile + which * each
                        packs[k][:, lane : lane + each] = turned[:, d * each : (d + 1) * each]

    return pl.pallas_call(
        kernel,
        grid=(parts + 2,),
        out_shape=[jax.ShapeDtypeStruct((tokens, width), BF)]
        + [jax.ShapeDtypeStruct((tokens, pack), BF)] * parts,
        in_specs=[smem(), whole((tokens, width)), whole((1, width))]
        + [pl.BlockSpec((depth, tile), lambda n: (0, n))] * count
        + [whole((tokens, tile))] * 2,
        out_specs=[whole((tokens, width))] + [whole((tokens, pack))] * parts,
        compiler_params=params(),
        cost_estimate=cost(2 * tokens * width * tile * (parts + 2), 2 * width * tile * (parts + 2)),
        name="project_in",
    )(jnp.stack([seq, z]), inputs, gain, *groups, cos_table, sin_table)


def project_out(seq, z, mixed, inputs, gain, groups):
    parts = len(mixed)
    tokens, width = inputs.shape
    each = mixed[0].shape[1]
    tile = width // parts
    count = len(groups)
    depth = parts * each // count

    def kernel(at_ref, *refs):
        parts_in, (in_ref, gain_ref) = refs[:parts], refs[parts : parts + 2]
        w_refs, (flat_ref, res_ref, acts_ref) = refs[parts + 2 : -3], refs[-3:]
        step = pl.program_id(0)

        @pl.when(step == 0)
        def _():
            for k in range(parts):
                lane = pl.multiple_of((at_ref[0] ^ k) * each, each)
                flat_ref[:, pl.ds(lane, each)] = parts_in[k][...]

        lanes = pl.ds(pl.multiple_of(step * tile, tile), tile)
        total = in_ref[:, lanes].astype(F32)
        for j in range(count):
            rows = pl.ds(pl.multiple_of((at_ref[1] + count - j) % count * depth, depth), depth)
            total = total + dot_nn(flat_ref[:, rows], w_refs[j][...])
        res_ref[:, lanes] = total

        @pl.when(step == parts - 1)
        def _():
            values = res_ref[...]
            scale = lax.rsqrt(jnp.mean(values * values, axis=-1, keepdims=True) + EPSILON)
            acts_ref[...] = (values * scale * gain_ref[...]).astype(BF)

    return pl.pallas_call(
        kernel,
        grid=(parts,),
        out_shape=[
            jax.ShapeDtypeStruct((tokens, parts * each), BF),
            jax.ShapeDtypeStruct((tokens, width), F32),
            jax.ShapeDtypeStruct((tokens, width), BF),
        ],
        in_specs=[smem()]
        + [whole((tokens, each))] * parts
        + [whole((tokens, width)), whole((1, width))]
        + [pl.BlockSpec((depth, tile), lambda n: (0, n))] * count,
        out_specs=[whole((tokens, parts * each)), whole((tokens, width)), whole((tokens, width))],
        compiler_params=params(),
        cost_estimate=cost(2 * tokens * width * parts * each, 2 * width * parts * each),
        name="project_out",
    )(jnp.stack([seq, z]), *mixed, inputs, gain, *groups)


def feed_forward(acts, grads, gate, up, down, begun=None):
    tokens, width = acts.shape
    hidden = gate.shape[0]
    tile = 256
    steps = hidden // tile
    kind = F32 if begun is None else BF
    begun = [] if begun is None else list(begun)

    def kernel(a_ref, c_ref, g_ref, u_ref, d_ref, *refs):
        starts, (h_ref, gg_ref, gu_ref, o_ref, ga_ref, o_s, ga_s) = refs[:-7], refs[-7:]
        step = pl.program_id(0)

        @pl.when(step == 0)
        def _():
            if starts:
                o_s[...] = starts[0][...]
                ga_s[...] = starts[1][...]
            else:
                o_s[...] = jnp.zeros_like(o_s)
                ga_s[...] = jnp.zeros_like(ga_s)

        gate_act = dot_nt(a_ref[...], g_ref[...])
        up_act = dot_nt(a_ref[...], u_ref[...])
        grad_hidden = dot_nt(c_ref[...], d_ref[...])
        sigma = jax.nn.sigmoid(gate_act)
        silu = gate_act * sigma
        low = (silu * up_act).astype(BF)
        grad_gate = (grad_hidden * up_act * (sigma * (1.0 + gate_act * (1.0 - sigma)))).astype(BF)
        grad_up = (grad_hidden * silu).astype(BF)
        h_ref[...] = low
        gg_ref[...] = grad_gate
        gu_ref[...] = grad_up
        o_s[...] += dot_nn(low, d_ref[...])
        ga_s[...] += dot_nn(grad_gate, g_ref[...]) + dot_nn(grad_up, u_ref[...])

        @pl.when(step == steps - 1)
        def _():
            o_ref[...] = o_s[...].astype(kind)
            ga_ref[...] = ga_s[...].astype(kind)

    whole = pl.BlockSpec((tokens, width), lambda n: (0, 0))
    rows = pl.BlockSpec((tile, width), lambda n: (n, 0))
    lanes = pl.BlockSpec((tokens, tile), lambda n: (0, n))
    return pl.pallas_call(
        kernel,
        grid=(steps,),
        out_shape=[jax.ShapeDtypeStruct((tokens, hidden), BF)] * 3
        + [jax.ShapeDtypeStruct((tokens, width), kind)] * 2,
        in_specs=[whole, whole, rows, rows, rows] + [whole] * len(begun),
        out_specs=[lanes] * 3 + [whole] * 2,
        scratch_shapes=[pltpu.VMEM((tokens, width), F32)] * 2,
        compiler_params=params(),
        cost_estimate=cost(12 * tokens * width * hidden, 6 * width * hidden),
        name="feed_forward",
    )(acts, grads, gate, up, down, *begun)


def middle_back(seq, z, terms, residual, grad_out, gain, groups, parts):
    tokens, width = residual.shape
    tile = groups[0].shape[0]
    count = len(groups)
    assert count == parts

    def kernel(at_ref, t0_ref, t1_ref, res_ref, go_ref, gain_ref, *refs):
        w_refs, (gr_ref, low_ref, gg_ref), outs = refs[:count], refs[count : count + 3], refs[count + 3 :]
        grad = t0_ref[...].astype(F32) + t1_ref[...].astype(F32)
        values = res_ref[...]
        scale = lax.rsqrt(jnp.mean(values * values, axis=-1, keepdims=True) + EPSILON)
        weighted = grad * gain_ref[...]
        inner = jnp.mean(weighted * values, axis=-1, keepdims=True)
        result = go_ref[...].astype(F32) + scale * weighted - values * (scale**3 * inner)
        gr_ref[...] = result
        low_ref[...] = result.astype(BF)
        gg_ref[...] = jnp.sum(grad * values * scale, axis=0, keepdims=True)
        for j in range(count):
            part = dot_nt(low_ref[...], w_refs[j][...]).astype(BF)
            at = ((at_ref[1] + count - j) % count) ^ at_ref[0]
            for k in range(parts):

                @pl.when(at == k)
                def _():
                    outs[k][...] = part

    vmem = pl.BlockSpec(memory_space=pltpu.VMEM)
    return pl.pallas_call(
        kernel,
        out_shape=[
            jax.ShapeDtypeStruct((tokens, width), F32),
            jax.ShapeDtypeStruct((tokens, width), BF),
            jax.ShapeDtypeStruct((1, width), F32),
        ]
        + [jax.ShapeDtypeStruct((tokens, tile), BF)] * parts,
        in_specs=[smem()] + [vmem] * (5 + count),
        out_specs=[vmem] * (3 + parts),
        compiler_params=params(),
        cost_estimate=cost(2 * tokens * width * tile * parts, 2 * width * tile * parts + 8 * tokens * width),
        name="middle_back",
    )(jnp.stack([seq, z]), terms[0], terms[1], residual, grad_out, gain, *groups)


def unpack(seq, packs, cos_table, sin_table):
    parts = len(packs)
    tokens, tile = cos_table.shape
    each = tile // parts

    def kernel(seq_ref, *refs):
        ins, (cos_ref, sin_ref, out_ref) = refs[:parts], refs[parts:]
        for k in range(parts):
            at = seq_ref[0] ^ k
            queries = turn(ins[k][:, :tile].astype(F32), cos_ref[...], -sin_ref[...])
            out_ref[:, pl.ds(pl.multiple_of(at * tile, tile), tile)] = queries.astype(BF)
            keys = turn(
                ins[k][:, tile : tile + each].astype(F32), cos_ref[:, :each], -sin_ref[:, :each]
            )
            lane = pl.multiple_of(parts * tile + at * each, each)
            out_ref[:, pl.ds(lane, each)] = keys.astype(BF)
            lane = pl.multiple_of((parts + 1) * tile + at * each, each)
            out_ref[:, pl.ds(lane, each)] = ins[k][:, tile + each :]

    vmem = pl.BlockSpec(memory_space=pltpu.VMEM)
    return pl.pallas_call(
        kernel,
        out_shape=jax.ShapeDtypeStruct((tokens, (parts + 2) * tile), BF),
        in_specs=[smem()] + [vmem] * (parts + 2),
        out_specs=vmem,
        compiler_params=params(),
        cost_estimate=cost(0, 6 * 2**20),
        name="unpack",
    )(seq.reshape(1), *packs, cos_table, sin_table)


def inner_back(z, grad_qkv, groups, inputs, gain, grad_res):
    tokens, width = inputs.shape
    count = len(groups)
    depth = width // count

    def kernel(at_ref, gq_ref, *refs):
        w_refs, (in_ref, gain_ref, gr_ref, out_ref, gg_ref, grad_s) = refs[:count], refs[count:]
        for j in range(count):
            lanes = pl.ds(pl.multiple_of((at_ref[0] + count - j) % count * depth, depth), depth)
            grad_s[:, lanes] = dot_nt(gq_ref[...], w_refs[j][...])
        grad = grad_s[...]
        values = in_ref[...].astype(F32)
        scale = lax.rsqrt(jnp.mean(values * values, axis=-1, keepdims=True) + EPSILON)
        weighted = grad * gain_ref[...]
        inner = jnp.mean(weighted * values, axis=-1, keepdims=True)
        result = gr_ref[...] + scale * weighted - values * (scale**3 * inner)
        out_ref[...] = result.astype(BF)
        gg_ref[...] = jnp.sum(grad * values * scale, axis=0, keepdims=True)

    vmem = pl.BlockSpec(memory_space=pltpu.VMEM)
    return pl.pallas_call(
        kernel,
        out_shape=[jax.ShapeDtypeStruct((tokens, width), BF), jax.ShapeDtypeStruct((1, width), F32)],
        in_specs=[smem()] + [vmem] * (4 + count),
        out_specs=[vmem] * 2,
        scratch_shapes=[pltpu.VMEM((tokens, width), F32)],
        compiler_params=params(),
        cost_estimate=cost(2 * tokens * groups[0].size * count, 2 * groups[0].size * count),
        name="inner_back",
    )(z.reshape(1), grad_qkv, *groups, inputs, gain, grad_res)


def weight_grad(left, right, rows, blocks, half, adds=()):
    count = len(left)
    tokens = left[0].shape[0]
    width = right[0].shape[1] // 2
    tile = min(rows, 512)
    steps = rows // tile
    total_rows = rows * len(blocks)

    def kernel(at_ref, *refs):
        lefts, rights, extra, out = refs[:count], refs[count : 2 * count], refs[2 * count : -1], refs[-1]
        total = None
        for l_ref, r_ref in zip(lefts, rights):
            term = lax.dot_general(
                l_ref[...], r_ref[...], (((0,), (0,)), ((), ())), preferred_element_type=F32
            )
            total = term if total is None else total + term
        for ref in extra:
            total = total + ref[...].astype(F32)
        out[...] = total.astype(BF)

    rows_spec = pl.BlockSpec((tile, width), lambda n, at: (n, 0))
    spec = pltpu.PrefetchScalarGridSpec(
        num_scalar_prefetch=1,
        grid=(steps * len(blocks),),
        in_specs=[pl.BlockSpec((tokens, tile), lambda n, at: (0, at[1 + n]))] * count
        + [pl.BlockSpec((tokens, width), lambda n, at: (0, at[0]))] * count
        + [rows_spec] * len(adds),
        out_specs=rows_spec,
    )
    at = [jnp.int32(half)]
    for block in blocks:
        at += [jnp.int32(block) * steps + i for i in range(steps)]
    return pl.pallas_call(
        kernel,
        grid_spec=spec,
        out_shape=jax.ShapeDtypeStruct((total_rows, width), BF),
        compiler_params=params(),
        cost_estimate=cost(
            2 * tokens * count * total_rows * width, 2 * (tokens * count + total_rows) * width
        ),
        name="weight_grad",
    )(jnp.stack(at), *left, *right, *adds)


def row_grads(left, right, blocks, half, added, y, cuts):
    tokens = left.shape[0]
    width = right.shape[1] // 2
    rows = left.shape[1] // LINE
    each = rows // cuts
    count = len(blocks)

    def kernel(at_ref, l_ref, r_ref, add_ref, *refs):
        outs, total_s = refs[:-1], refs[-1]
        total = lax.dot_general(
            l_ref[...], r_ref[...], (((0,), (0,)), ((), ())), preferred_element_type=F32
        )
        total_s[...] = (total + add_ref[...].astype(F32)).astype(BF)
        for j in range(count):

            @pl.when(pl.program_id(0) == j)
            def _():
                for k in range(cuts):
                    start = pl.multiple_of((at_ref[1] + cuts - k) % cuts * each, each)
                    outs[j * cuts + k][...] = total_s[pl.ds(start, each), :]

    spec = pltpu.PrefetchScalarGridSpec(
        num_scalar_prefetch=1,
        grid=(count,),
        in_specs=[
            pl.BlockSpec((tokens, rows), lambda n, at: (0, at[2 + n])),
            pl.BlockSpec((tokens, width), lambda n, at: (0, at[0])),
            pl.BlockSpec((rows, width), lambda n, at: (n, 0)),
        ],
        out_specs=[pl.BlockSpec((each, width), lambda n, at: (0, 0))] * (count * cuts),
        scratch_shapes=[pltpu.VMEM((rows, width), BF)],
    )
    at = jnp.stack([jnp.int32(half), jnp.int32(y)] + [jnp.int32(b) for b in blocks])
    outs = pl.pallas_call(
        kernel,
        grid_spec=spec,
        out_shape=[jax.ShapeDtypeStruct((each, width), BF)] * (count * cuts),
        compiler_params=params(),
        cost_estimate=cost(2 * tokens * count * rows * width, 6 * count * rows * width),
        name="row_grads",
    )(at, left, right, added)
    return [outs[j * cuts : (j + 1) * cuts] for j in range(count)]


def join(core, mine, other, widths):
    rows, half = mine.shape
    tile = min(rows, 256)

    def kernel(core_ref, mine_ref, other_ref, *refs):
        outs, full = refs[:-1], refs[-1]
        target = outs[0] if len(outs) == 1 else full
        at = pl.multiple_of(core_ref[0] * half, half)
        target[:, pl.ds(at, half)] = mine_ref[...].astype(F32)
        at = pl.multiple_of((1 - core_ref[0]) * half, half)
        target[:, pl.ds(at, half)] = other_ref[...].astype(F32)
        if len(outs) > 1:
            lane = 0
            for out in outs:
                out[...] = full[:, lane : lane + out.shape[1]]
                lane += out.shape[1]

    def block(width):
        return pl.BlockSpec((tile, width), lambda n: (n, 0))

    return pl.pallas_call(
        kernel,
        grid=(rows // tile,),
        out_shape=[jax.ShapeDtypeStruct((rows, width), F32) for width in widths],
        in_specs=[smem(), block(half), block(half)],
        out_specs=[block(width) for width in widths],
        scratch_shapes=[pltpu.VMEM((tile, 2 * half) if len(widths) > 1 else (8, 128), F32)],
        compiler_params=params(),
        cost_estimate=cost(0, rows * half * 12),
        name="join",
    )(core.reshape(1), mine, other)
def half_of(array, which, axis=1):
    size = array.shape[axis] // 2
    return lax.dynamic_slice_in_dim(array, which * size, size, axis)


class Order:
    def __init__(self):
        self.marks = ()

    def tie(self, *values):
        if self.marks:
            values = lax.optimization_barrier(tuple(values) + self.marks)[: len(values)]
        return values[0] if len(values) == 1 else list(values)

    def done(self, *values):
        self.marks = tuple(values)


def y_hops(value):
    return ring_gather(value, y_next, columns())[1:]


def add_low(left, right):
    return (left.astype(F32) + right.astype(F32)).astype(BF)


def finish_sum(low, core, widths):
    total = add_low(low, x_swap(low))
    return join(core, total, core_swap(total), widths)


def rope_tables(positions, repeat):
    frequency = THETA ** (-(jnp.arange(HD // 2, dtype=F32) * 2.0) / HD)
    angles = positions.astype(F32)[:, None] * frequency[None, :]
    cos, sin = jnp.cos(angles), jnp.sin(angles)
    return (
        jnp.tile(jnp.concatenate([cos, cos], axis=1), (1, repeat)),
        jnp.tile(jnp.concatenate([-sin, sin], axis=1), (1, repeat)),
    )


def exchange(packs):
    return [packs[0]] + [seq_swap(packs[k], k) for k in range(1, len(packs))]


def shards(
    inputs,
    query_weight,
    key_weight,
    value_weight,
    output_weight,
    gate_weight,
    up_weight,
    down_weight,
    gain_attn,
    gain_ffn,
    cotangent,
):
    seq_count, local_len, width = inputs.shape
    assert seq_count == 1
    tokens = local_len
    parts = lax.axis_size("seq")
    kv_local = KVH // parts
    cols = columns()
    seq = lax.axis_index("seq")
    core, side = seq % 2, seq // 2
    fsdp = lax.axis_index("fsdp")
    z, y = fsdp // cols, fsdp % cols
    q_width, kv_width = query_weight.shape[1], key_weight.shape[1]
    heads_local = q_width // HD // parts
    flat_in = inputs.reshape(tokens, width)
    grad_out = cotangent.reshape(tokens, width)

    qkv_shard = jnp.concatenate([query_weight, key_weight, value_weight], axis=1)
    rows = qkv_shard.shape[0]
    part, half = rows // 2, qkv_shard.shape[1] // 2
    positions = seq * local_len + jnp.arange(local_len)
    cos_table, sin_table = rope_tables(positions, kv_width // HD)
    order = Order()

    def group_of(j, quarters, crossed):
        placed, offsets = [], []
        for k in range(cols):
            row = (y - k) % cols * rows
            for piece, at in ((quarters[k], side), (crossed[k], 1 - side)):
                placed += [piece, core_swap(piece)]
                offsets += [
                    (row + at * part, core * half),
                    (row + at * part, (1 - core) * half),
                ]
        return place((rows * cols, 2 * half), placed, offsets)

    def group_of_halves(halves, width, own):
        placed, offsets = [], []
        for k, piece in enumerate(halves):
            row = (y - k) % cols * rows
            if k == 0 and own is not None:
                placed.append(own)
                offsets.append((row, 0))
            else:
                placed += [piece, core_swap(piece)]
                offsets += [(row, core * width), (row, (1 - core) * width)]
        return place((rows * cols, 2 * width), placed, offsets)

    quarter = half_of(half_of(qkv_shard, side, 0), core)
    out_half = half_of(output_weight, core)
    out_width = width // 2
    gains = jnp.pad(jnp.stack([gain_attn, gain_ffn]), ((0, 14), (0, 0)))
    line_q, line_g, cross = [quarter], [gains], [None]
    beside = [y_hops(half_of(qkv_shard, core))]
    beside_cross = [None]
    beside_g = [y_hops(gains)]
    line_q.append(z_next(quarter))
    line_g.append(z_next(gains))
    cross.append(x_swap(line_q[1]))
    line_q.append(z_next(line_q[1]))
    order.done(beside[0][-1], cross[1], line_q[2], line_g[1], beside_g[0][-1])
    line_o = [out_half]
    groups = []
    for j in range(1, LINE):
        here, there, g = order.tie(line_q[j], cross[j], line_g[j])
        beside.append(y_hops(here))
        beside_cross.append(y_hops(there))
        beside_g.append(y_hops(g))
        marks = [beside[j][-1], beside_cross[j][-1], beside_g[j][-1]]
        if j + 1 < LINE:
            ahead = order.tie(line_q[j + 1])
            cross.append(x_swap(ahead))
            marks.append(cross[j + 1])
            line_g.append(z_next(g))
            marks.append(line_g[j + 1])
        if j + 2 < LINE:
            line_q.append(z_next(ahead))
            marks.append(line_q[j + 2])
        line_o.append(z_next(order.tie(line_o[j - 1])))
        marks.append(line_o[j])
        if j == 1:
            groups.append(group_of_halves([None] + beside[0], half, qkv_shard))
        else:
            groups.append(
                group_of(j - 1, [line_q[j - 1]] + beside[j - 1], [cross[j - 1]] + beside_cross[j - 1])
            )
        marks.append(groups[-1])
        order.done(*marks)
    last = LINE - 1
    groups.append(group_of(last, [line_q[last]] + beside[last], [cross[last]] + beside_cross[last]))
    gain_full = jnp.zeros((2, width), BF)
    for j in range(LINE):
        for k, g in enumerate([line_g[j]] + beside_g[j]):
            at = (((z - j) % LINE) * cols + (y - k) % cols) * rows
            gain_full = lax.dynamic_update_slice(gain_full, g[:2], (0, at))
    gain_one = gain_full[:1].astype(F32)
    gain_two = gain_full[1:].astype(F32)

    grad_parts = [grad_out, z_next(order.tie(grad_out))]
    beside_o = [y_hops(order.tie(line_o[0])), y_hops(order.tie(line_o[1]))]
    acts_one, *sent = project_in(
        seq, z, flat_in, gain_one, groups, cos_table, sin_table, parts
    )
    order.done(*sent)
    sent = order.tie(*sent)
    packs = exchange(sent)
    order.done(*packs, beside_o[0][-1], beside_o[1][-1], grad_parts[1])
    grad_parts.append(z_next(order.tie(grad_parts[1])))
    beside_o += [y_hops(order.tie(line_o[2])), y_hops(order.tie(line_o[3]))]
    *mixed_sent, log_totals = attend_forward(seq, order.tie(*packs), heads_local, kv_local)
    out_groups = [
        group_of_halves([line_o[j]] + beside_o[j], out_width, output_weight if j == 0 else None)
        for j in range(LINE)
    ]
    order.done(*mixed_sent)
    own = (gate_weight, up_weight, down_weight)
    starts = [half_of(half_of(weight, side, 0), core) for weight in own]
    mixed = exchange(order.tie(*mixed_sent))
    order.done(*mixed, *out_groups, grad_parts[2])
    far_y = [y_hops(order.tie(starts[0]))]
    grad_parts.append(z_next(order.tie(grad_parts[2])))
    mixed_flat, residual, acts_two = project_out(
        seq, z, order.tie(*mixed), flat_in, gain_two, out_groups
    )
    order.done(acts_two)

    far_rows = gate_weight.shape[0]

    def far_x(pieces):
        return [x_swap(p) for p in pieces]

    def far_place(pieces, crossed):
        placed, offsets = [], []
        for k in range(cols - 1):
            for piece, at in ((pieces[k], side), (crossed[k], 1 - side)):
                row = k * far_rows + at * (far_rows // 2)
                placed += [piece, core_swap(piece)]
                offsets += [(row, core * out_width), (row, (1 - core) * out_width)]
        return place((far_rows * (cols - 1), width), placed, offsets)

    acts_parts = [acts_two]
    far_c = []
    far = []
    near_done = []
    for j in range(LINE - 1):
        acts_parts.append(z_next(order.tie(acts_parts[j])))
        if j < 2:
            far_y.append(y_hops(order.tie(starts[j + 1])))
        pieces = order.tie(*far_y[j], far_y[j][-1])[:-1]
        far_c.append(far_x(pieces))
        if j:
            far.append(far_place(far_y[j - 1], far_c[j - 1]))
        near_done.append(feed_forward(order.tie(acts_parts[j]), grad_parts[j], *own))
        marks = [acts_parts[j + 1], far_c[j][-1], near_done[j][3]]
        if j == 0:
            marks.append(grad_parts[3])
        if j < 2:
            marks.append(far_y[j + 1][-1])
        order.done(*marks, *far)
    far.append(far_place(far_y[2], far_c[2]))
    near_done.append(feed_forward(order.tie(acts_parts[3]), grad_parts[3], *own))
    order.done(near_done[3][3], *far)

    far_done = [None] * LINE

    def run_far(j):
        far_done[j] = feed_forward(order.tie(acts_parts[j]), grad_parts[j], *far, near_done[j][3:])
        return far_done[j]

    order.done(run_far(1)[4])
    passed = z_next(order.tie(far_done[1][4]))
    run_far(2)
    run_far(0)
    order.done(passed, far_done[2][4], far_done[0][4])
    passed = z_next(order.tie(add_low(passed, far_done[2][4])))
    run_far(3)

    def grads_of(done, which):
        return [d[which] for d in done]

    rights = (grad_parts, acts_parts, acts_parts)
    far_size = far_rows * (cols - 1)
    far_sent = [None] * 3
    far_kept = [None] * 3
    far_total = [None] * 3

    def send_far(i):
        term = weight_grad(grads_of(far_done, i), rights[i], far_size, [0], 1 - core)
        far_sent[i] = core_swap(term)
        return term

    def keep_far(i):
        kept = weight_grad(grads_of(far_done, i), rights[i], far_size, [0], core, [far_sent[i]])
        total = y_next(kept[:far_rows])
        for k in range(1, cols - 1):
            total = y_next(add_low(total, kept[k * far_rows : (k + 1) * far_rows]))
        far_total[i] = total
        return kept

    marks = [send_far(0)]
    order.done(passed, far_done[3][4], *marks)
    passed = z_next(order.tie(add_low(passed, far_done[3][4])))
    marks = [keep_far(0), send_far(1), send_far(2)]
    order.done(passed, *marks)

    ffn_parts = [d[3] for d in far_done]
    ffn_sum = z_next(order.tie(ffn_parts[1]))
    grad_res, grad_res_low, grad_gain_two, *grad_sent = middle_back(
        seq, z, order.tie(passed, far_done[0][4]), residual, grad_out, gain_two, out_groups, parts
    )
    order.done(*grad_sent)
    grad_packs = exchange(order.tie(*grad_sent))
    marks = [keep_far(1), keep_far(2)]
    order.done(*grad_packs, ffn_sum, *marks)
    ffn_sum = z_next(order.tie(add_low(ffn_sum, ffn_parts[2])))
    back_sent = attend_backward(
        seq, log_totals, packs, order.tie(*grad_packs), heads_local, kv_local
    )
    order.done(*back_sent)
    back_packs = exchange(order.tie(*back_sent))
    own_sent = []
    marks = []
    for i in range(3):
        term = weight_grad(order.tie(*grads_of(near_done, i)), rights[i], far_rows, [0], 1 - core)
        own_sent.append(core_swap(term))
        marks.append(term)
    line_order = list(range(1, LINE)) + [0]
    blocks = [(z - j) % LINE for j in line_order]
    line_rows = rows * cols
    out_sent = weight_grad([mixed_flat], [grad_res_low], line_rows, blocks, 1 - core)
    out_recv = core_swap(out_sent)
    order.done(*back_packs, *marks, out_sent, ffn_sum, far_total[0])

    def keep_own(i):
        low = weight_grad(
            grads_of(near_done, i), rights[i], far_rows, [0], core, [own_sent[i], far_total[i]]
        )
        return finish_sum(low, core, [width])[0]

    ffn_sum = z_next(order.tie(add_low(ffn_sum, ffn_parts[3])))
    grad_qkv = unpack(seq, order.tie(*back_packs), cos_table, sin_table)
    term = weight_grad([acts_one], [grad_qkv], line_rows, blocks, 1 - core)
    qkv_recv = core_swap(term)
    d_down = keep_own(0)
    out_terms = row_grads(mixed_flat, grad_res_low, blocks, core, out_recv, y, 1)
    total = out_terms[0][0]
    for j in range(1, LINE):
        total = add_low(z_next(total), out_terms[j][0])
    pieces = [
        lax.dynamic_slice_in_dim(total, (y - k) % cols * rows, rows, 0) for k in range(cols)
    ]
    total = None
    for k in list(range(1, cols)) + [0]:
        total = pieces[k] if total is None else add_low(y_next(total), pieces[k])
    d_out = finish_sum(total, core, [width])

    qkv_terms = row_grads(acts_one, grad_qkv, blocks, core, qkv_recv, y, cols)
    passed = None
    for terms in qkv_terms:
        total = None
        for k in list(range(1, cols)) + [0]:
            total = terms[k] if total is None else add_low(y_next(total), terms[k])
        passed = total if passed is None else add_low(z_next(passed), total)
    d_qkv = finish_sum(passed, core, [q_width, kv_width, kv_width])
    d_gate = keep_own(1)
    d_up = keep_own(2)

    outputs = (residual + ffn_sum.astype(F32) + ffn_parts[0].astype(F32)).astype(BF)
    grad_inputs, grad_gain_one = inner_back(z, grad_qkv, groups, flat_in, gain_one, grad_res)
    gain_sums = all_sum(jnp.concatenate([grad_gain_one, grad_gain_two], axis=0))
    gain_sums = lax.dynamic_slice_in_dim(gain_sums, fsdp * rows, rows, 1)
    return (
        outputs.reshape(inputs.shape),
        grad_inputs.reshape(inputs.shape),
        d_qkv[0],
        d_qkv[1],
        d_qkv[2],
        d_out[0],
        d_gate,
        d_up,
        d_down,
        gain_sums[0],
        gain_sums[1],
    )


def solution(mesh):
    token_spec, row_spec, gain_spec = P("fsdp", "seq", None), P("fsdp", None), P("fsdp")
    return jax.shard_map(
        shards,
        mesh=mesh,
        in_specs=(token_spec,) + (row_spec,) * 7 + (gain_spec,) * 2 + (token_spec,),
        out_specs=(token_spec,) * 2 + (row_spec,) * 7 + (gain_spec,) * 2,
        check_vma=False,
    )
```

```python
import functools

import jax
import jax.numpy as jnp
from jax import lax
from jax.experimental import pallas as pl
from jax.experimental.pallas import tpu as pltpu
from jax.sharding import PartitionSpec as P

KVH = 8
HD = 64
BLOCK = 256
LINE = 4

EPSILON = 1e-05
THETA = 500000.0
LOG2E = 1.4426950408889634

BF = jnp.bfloat16
F32 = jnp.float32


def after(value, *others):
    return lax.optimization_barrier((value,) + others)[0]


def columns():
    return lax.axis_size("fsdp") // LINE


def z_next(value):
    cols = columns()
    count = lax.axis_size("fsdp")
    return lax.ppermute(value, "fsdp", [(i, (i + cols) % count) for i in range(count)])


def y_next(value):
    cols = columns()
    count = lax.axis_size("fsdp")
    return lax.ppermute(
        value, "fsdp", [(i, i // cols * cols + (i + 1) % cols) for i in range(count)]
    )


def seq_swap(value, bit):
    return lax.ppermute(value, "seq", [(i, i ^ bit) for i in range(lax.axis_size("seq"))])


def core_swap(value):
    return seq_swap(value, 1)


def x_swap(value):
    return seq_swap(value, 2)


def ring_gather(value, step, count):
    pieces = [value]
    for _ in range(count - 1):
        pieces.append(step(pieces[-1]))
    return pieces


def ring_scatter(part_of, step, count):
    total = None
    for j in list(range(1, count)) + [0]:
        total = part_of(j) if total is None else part_of(j) + total.astype(F32)
        if j:
            total = step(total.astype(BF))
    return total


def all_sum(value):
    bit = 1
    while bit < lax.axis_size("seq"):
        value = value + seq_swap(value, bit)
        bit *= 2
    count = lax.axis_size("fsdp")
    bit = 1
    while bit < count:
        value = value + lax.ppermute(value, "fsdp", [(i, i ^ bit) for i in range(count)])
        bit *= 2
    return value


def dot_nt(a, b):
    return lax.dot_general(a, b, (((1,), (1,)), ((), ())), preferred_element_type=F32)

def dot_nn(a, b):
    return jnp.dot(a, b, preferred_element_type=F32)


def attend_forward_kernel(parts, heads, kv, seq_ref, *refs):
    packs, outs = refs[:parts], refs[parts : 2 * parts]
    lse_ref, q_s, k_s, vt_s, o_s = refs[2 * parts :]
    tokens = packs[0].shape[0]
    seq = seq_ref[0]
    group = heads // kv
    for k in range(parts):
        rows = pl.ds(pl.multiple_of((seq ^ k) * tokens, tokens), tokens)
        q_s[rows, :] = packs[k][:, : heads * HD]
        for g in range(kv):
            lane = (heads + g) * HD
            k_s[g, rows, :] = packs[k][:, lane : lane + HD]
            lane = (heads + kv + g) * HD
            vt_s[g, :, rows] = packs[k][:, lane : lane + HD].T
    full = parts * tokens
    for g in range(kv):
        for i in range(full // BLOCK):
            keys = (i + 1) * BLOCK
            rows = slice(i * BLOCK, keys)
            for pair in range(group // 2):
                halves = []
                for h in (g * group + 2 * pair, g * group + 2 * pair + 1):
                    scores = dot_nt(k_s[g, :keys, :], q_s[rows, h * HD : (h + 1) * HD])
                    scores = scores * (HD**-0.5 * LOG2E)
                    top = jnp.max(scores, axis=0, keepdims=True)
                    powers = jnp.exp2(scores - top)
                    total = jnp.sum(powers, axis=0, keepdims=True)
                    halves.append(dot_nn(vt_s[g, :, :keys], powers.astype(BF)) / total)
                    lse_ref[h : h + 1, rows] = top + jnp.log2(total)
                lane = (g * group + 2 * pair) * HD
                o_s[rows, lane : lane + 2 * HD] = jnp.concatenate(halves, axis=0).T.astype(BF)
    for k in range(parts):
        rows = pl.ds(pl.multiple_of((seq ^ k) * tokens, tokens), tokens)
        outs[k][...] = o_s[rows, :]


def attend_forward(seq, packs, heads, kv):
    parts = len(packs)
    tokens = packs[0].shape[0]
    full = parts * tokens
    vmem = pl.BlockSpec(memory_space=pltpu.VMEM)
    flops = 4 * heads * full * full * HD * 5 // 8
    return pl.pallas_call(
        functools.partial(attend_forward_kernel, parts, heads, kv),
        out_shape=[jax.ShapeDtypeStruct((tokens, heads * HD), BF)] * parts
        + [jax.ShapeDtypeStruct((heads, full), F32)],
        in_specs=[pl.BlockSpec(memory_space=pltpu.SMEM)] + [vmem] * parts,
        out_specs=[vmem] * (parts + 1),
        scratch_shapes=[
            pltpu.VMEM((full, heads * HD), BF),
            pltpu.VMEM((kv, full, HD), BF),
            pltpu.VMEM((kv, HD, full), BF),
            pltpu.VMEM((full, heads * HD), BF),
        ],
        compiler_params=pltpu.CompilerParams(vmem_limit_bytes=48 * 2**20),
        cost_estimate=cost(flops * 4, 4 * 2**20),
        name="attend_forward",
    )(seq.reshape(1), *packs)


def attend_backward_kernel(parts, heads, kv, seq_ref, lse_ref, *refs):
    packs, grads, outs = refs[:parts], refs[parts : 2 * parts], refs[2 * parts : 3 * parts]
    q_s, k_s, kt_s, v_s, g_s, dq_s, dk_s, dv_s = refs[3 * parts :]
    tokens = packs[0].shape[0]
    seq = seq_ref[0]
    group = heads // kv
    for k in range(parts):
        rows = pl.ds(pl.multiple_of((seq ^ k) * tokens, tokens), tokens)
        q_s[rows, :] = packs[k][:, : heads * HD]
        g_s[rows, :] = grads[k][...]
        for g in range(kv):
            lane = (heads + g) * HD
            k_s[g, rows, :] = packs[k][:, lane : lane + HD]
            kt_s[g, :, rows] = packs[k][:, lane : lane + HD].T
            lane = (heads + kv + g) * HD
            v_s[g, rows, :] = packs[k][:, lane : lane + HD]
    full = parts * tokens
    dk_s[...] = jnp.zeros_like(dk_s)
    dv_s[...] = jnp.zeros_like(dv_s)
    for g in range(kv):
        for i in range(full // BLOCK):
            keys = (i + 1) * BLOCK
            rows = slice(i * BLOCK, keys)
            for pair in range(group // 2):
                halves = []
                for h in (g * group + 2 * pair, g * group + 2 * pair + 1):
                    query = q_s[rows, h * HD : (h + 1) * HD]
                    grad = g_s[rows, h * HD : (h + 1) * HD]
                    scores = dot_nt(k_s[g, :keys, :], query) * (HD**-0.5 * LOG2E)
                    probs = jnp.exp2(scores - lse_ref[h : h + 1, rows])
                    grad_probs = dot_nt(v_s[g, :keys, :], grad)
                    inner = jnp.sum(probs * grad_probs, axis=0, keepdims=True)
                    grad_scores = (probs * (grad_probs - inner)).astype(BF)
                    dv_s[g, :keys, :] += dot_nn(probs.astype(BF), grad)
                    dk_s[g, :keys, :] += dot_nn(grad_scores, query)
                    halves.append(dot_nn(kt_s[g, :, :keys], grad_scores) * HD**-0.5)
                lane = (g * group + 2 * pair) * HD
                dq_s[rows, lane : lane + 2 * HD] = jnp.concatenate(halves, axis=0).T.astype(BF)
    for k in range(parts):
        rows = pl.ds(pl.multiple_of((seq ^ k) * tokens, tokens), tokens)
        outs[k][:, : heads * HD] = dq_s[rows, :]
        for g in range(kv):
            lane = (heads + g) * HD
            outs[k][:, lane : lane + HD] = (dk_s[g, rows, :] * HD**-0.5).astype(BF)
            lane = (heads + kv + g) * HD
            outs[k][:, lane : lane + HD] = dv_s[g, rows, :].astype(BF)


def attend_backward(seq, lse, packs, grads, heads, kv):
    parts = len(packs)
    tokens = packs[0].shape[0]
    full = parts * tokens
    vmem = pl.BlockSpec(memory_space=pltpu.VMEM)
    flops = 10 * heads * full * full * HD * 5 // 8
    return pl.pallas_call(
        functools.partial(attend_backward_kernel, parts, heads, kv),
        out_shape=[jax.ShapeDtypeStruct(packs[0].shape, BF)] * parts,
        in_specs=[pl.BlockSpec(memory_space=pltpu.SMEM)] + [vmem] * (2 * parts + 1),
        out_specs=[vmem] * parts,
        scratch_shapes=[
            pltpu.VMEM((full, heads * HD), BF),
            pltpu.VMEM((kv, full, HD), BF),
            pltpu.VMEM((kv, HD, full), BF),
            pltpu.VMEM((kv, full, HD), BF),
            pltpu.VMEM((full, heads * HD), BF),
            pltpu.VMEM((full, heads * HD), BF),
            pltpu.VMEM((kv, full, HD), F32),
            pltpu.VMEM((kv, full, HD), F32),
        ],
        compiler_params=pltpu.CompilerParams(vmem_limit_bytes=48 * 2**20),
        cost_estimate=cost(flops * 4, 8 * 2**20),
        name="attend_backward",
    )(seq.reshape(1), lse, *packs, *grads)


def smem():
    return pl.BlockSpec(memory_space=pltpu.SMEM)


def params(mib=56):
    return pltpu.CompilerParams(vmem_limit_bytes=mib * 2**20)


def cost(flops, moved):
    return pl.CostEstimate(flops=flops // 8, bytes_accessed=moved // 8, transcendentals=0)


def place(shape, pieces, offsets):
    count = len(pieces)

    def kernel(at_ref, *refs):
        sources, target, sems = refs[:-2], refs[-2], refs[-1]
        copies = []
        for i, source in enumerate(sources):
            rows, width = source.shape
            row = pl.multiple_of(at_ref[2 * i], rows)
            column = pl.multiple_of(at_ref[2 * i + 1], width)
            spot = target.at[pl.ds(row, rows), pl.ds(column, width)]
            copies.append(pltpu.make_async_copy(source, spot, sems.at[i]))
            copies[-1].start()
        for copy in copies:
            copy.wait()

    moved = 2 * sum(piece.size * 2 for piece in pieces)
    return pl.pallas_call(
        kernel,
        out_shape=jax.ShapeDtypeStruct(shape, pieces[0].dtype),
        in_specs=[smem()] + [pl.BlockSpec(memory_space=pl.ANY)] * count,
        out_specs=pl.BlockSpec(memory_space=pltpu.HBM),
        scratch_shapes=[pltpu.SemaphoreType.DMA((count,))],
        compiler_params=params(16),
        cost_estimate=cost(0, moved),
        name="place",
    )(jnp.stack([jnp.int32(v) for pair in offsets for v in pair]), *pieces)


def turn(values, cos_table, sin_table):
    width = values.shape[1]
    lane = lax.broadcasted_iota(jnp.int32, values.shape, 1)
    swapped = jnp.where(
        lane % HD < HD // 2,
        pltpu.roll(values, width - HD // 2, 1),
        pltpu.roll(values, HD // 2, 1),
    )
    return values * cos_table + swapped * sin_table


def whole(shape):
    return pl.BlockSpec(shape, lambda n: (0,) * len(shape))


def project_in(seq, z, inputs, gain, groups, cos_table, sin_table, parts):
    tokens, width = inputs.shape
    tile = cos_table.shape[1]
    each = tile // parts
    pack = tile + 2 * each
    count = len(groups)
    depth = width // count

    def kernel(at_ref, in_ref, gain_ref, *refs):
        w_refs, (cos_ref, sin_ref, acts_ref), packs = refs[:count], refs[count : count + 3], refs[count + 3 :]
        step = pl.program_id(0)

        @pl.when(step == 0)
        def _():
            values = in_ref[...].astype(F32)
            scale = lax.rsqrt(jnp.mean(values * values, axis=-1, keepdims=True) + EPSILON)
            acts_ref[...] = (values * scale * gain_ref[...]).astype(BF)

        rows = None
        for j in range(count):
            lanes = pl.ds(pl.multiple_of((at_ref[1] + count - j) % count * depth, depth), depth)
            term = dot_nn(acts_ref[:, lanes], w_refs[j][...])
            rows = term if rows is None else rows + term
        turned = jnp.where(
            step == parts + 1, rows, turn(rows, cos_ref[...], sin_ref[...])
        ).astype(BF)
        seq_now = at_ref[0]
        for k in range(parts):

            @pl.when((seq_now ^ k) == step)
            def _():
                packs[k][:, :tile] = turned

            for d in range(parts):
                for which in range(2):

                    @pl.when(((seq_now ^ k) == d) & (step == parts + which))
                    def _():
                        lane = tile + which * each
                        packs[k][:, lane : lane + each] = turned[:, d * each : (d + 1) * each]

    return pl.pallas_call(
        kernel,
        grid=(parts + 2,),
        out_shape=[jax.ShapeDtypeStruct((tokens, width), BF)]
        + [jax.ShapeDtypeStruct((tokens, pack), BF)] * parts,
        in_specs=[smem(), whole((tokens, width)), whole((1, width))]
        + [pl.BlockSpec((depth, tile), lambda n: (0, n))] * count
        + [whole((tokens, tile))] * 2,
        out_specs=[whole((tokens, width))] + [whole((tokens, pack))] * parts,
        compiler_params=params(),
        cost_estimate=cost(2 * tokens * width * tile * (parts + 2), 2 * width * tile * (parts + 2)),
        name="project_in",
    )(jnp.stack([seq, z]), inputs, gain, *groups, cos_table, sin_table)


def project_out(seq, z, mixed, inputs, gain, groups):
    parts = len(mixed)
    tokens, width = inputs.shape
    each = mixed[0].shape[1]
    tile = width // parts
    count = len(groups)
    depth = parts * each // count

    def kernel(at_ref, *refs):
        parts_in, (in_ref, gain_ref) = refs[:parts], refs[parts : parts + 2]
        w_refs, (flat_ref, res_ref, acts_ref) = refs[parts + 2 : -3], refs[-3:]
        step = pl.program_id(0)

        @pl.when(step == 0)
        def _():
            for k in range(parts):
                lane = pl.multiple_of((at_ref[0] ^ k) * each, each)
                flat_ref[:, pl.ds(lane, each)] = parts_in[k][...]

        lanes = pl.ds(pl.multiple_of(step * tile, tile), tile)
        total = in_ref[:, lanes].astype(F32)
        for j in range(count):
            rows = pl.ds(pl.multiple_of((at_ref[1] + count - j) % count * depth, depth), depth)
            total = total + dot_nn(flat_ref[:, rows], w_refs[j][...])
        res_ref[:, lanes] = total

        @pl.when(step == parts - 1)
        def _():
            values = res_ref[...]
            scale = lax.rsqrt(jnp.mean(values * values, axis=-1, keepdims=True) + EPSILON)
            acts_ref[...] = (values * scale * gain_ref[...]).astype(BF)

    return pl.pallas_call(
        kernel,
        grid=(parts,),
        out_shape=[
            jax.ShapeDtypeStruct((tokens, parts * each), BF),
            jax.ShapeDtypeStruct((tokens, width), F32),
            jax.ShapeDtypeStruct((tokens, width), BF),
        ],
        in_specs=[smem()]
        + [whole((tokens, each))] * parts
        + [whole((tokens, width)), whole((1, width))]
        + [pl.BlockSpec((depth, tile), lambda n: (0, n))] * count,
        out_specs=[whole((tokens, parts * each)), whole((tokens, width)), whole((tokens, width))],
        compiler_params=params(),
        cost_estimate=cost(2 * tokens * width * parts * each, 2 * width * parts * each),
        name="project_out",
    )(jnp.stack([seq, z]), *mixed, inputs, gain, *groups)


def feed_forward(acts, grads, gate, up, down, begun=None):
    tokens, width = acts.shape
    hidden = gate.shape[0]
    tile = 256
    steps = hidden // tile
    kind = F32 if begun is None else BF
    begun = [] if begun is None else list(begun)

    def kernel(a_ref, c_ref, g_ref, u_ref, d_ref, *refs):
        starts, (h_ref, gg_ref, gu_ref, o_ref, ga_ref, o_s, ga_s) = refs[:-7], refs[-7:]
        step = pl.program_id(0)

        @pl.when(step == 0)
        def _():
            if starts:
                o_s[...] = starts[0][...]
                ga_s[...] = starts[1][...]
            else:
                o_s[...] = jnp.zeros_like(o_s)
                ga_s[...] = jnp.zeros_like(ga_s)

        gate_act = dot_nt(a_ref[...], g_ref[...])
        up_act = dot_nt(a_ref[...], u_ref[...])
        grad_hidden = dot_nt(c_ref[...], d_ref[...])
        sigma = jax.nn.sigmoid(gate_act)
        silu = gate_act * sigma
        low = (silu * up_act).astype(BF)
        grad_gate = (grad_hidden * up_act * (sigma * (1.0 + gate_act * (1.0 - sigma)))).astype(BF)
        grad_up = (grad_hidden * silu).astype(BF)
        h_ref[...] = low
        gg_ref[...] = grad_gate
        gu_ref[...] = grad_up
        o_s[...] += dot_nn(low, d_ref[...])
        ga_s[...] += dot_nn(grad_gate, g_ref[...]) + dot_nn(grad_up, u_ref[...])

        @pl.when(step == steps - 1)
        def _():
            o_ref[...] = o_s[...].astype(kind)
            ga_ref[...] = ga_s[...].astype(kind)

    whole = pl.BlockSpec((tokens, width), lambda n: (0, 0))
    rows = pl.BlockSpec((tile, width), lambda n: (n, 0))
    lanes = pl.BlockSpec((tokens, tile), lambda n: (0, n))
    return pl.pallas_call(
        kernel,
        grid=(steps,),
        out_shape=[jax.ShapeDtypeStruct((tokens, hidden), BF)] * 3
        + [jax.ShapeDtypeStruct((tokens, width), kind)] * 2,
        in_specs=[whole, whole, rows, rows, rows] + [whole] * len(begun),
        out_specs=[lanes] * 3 + [whole] * 2,
        scratch_shapes=[pltpu.VMEM((tokens, width), F32)] * 2,
        compiler_params=params(),
        cost_estimate=cost(12 * tokens * width * hidden, 6 * width * hidden),
        name="feed_forward",
    )(acts, grads, gate, up, down, *begun)


def middle_back(seq, z, terms, residual, grad_out, gain, groups, parts):
    tokens, width = residual.shape
    tile = groups[0].shape[0]
    count = len(groups)
    assert count == parts

    def kernel(at_ref, t0_ref, t1_ref, res_ref, go_ref, gain_ref, *refs):
        w_refs, (gr_ref, low_ref, gg_ref), outs = refs[:count], refs[count : count + 3], refs[count + 3 :]
        grad = t0_ref[...].astype(F32) + t1_ref[...].astype(F32)
        values = res_ref[...]
        scale = lax.rsqrt(jnp.mean(values * values, axis=-1, keepdims=True) + EPSILON)
        weighted = grad * gain_ref[...]
        inner = jnp.mean(weighted * values, axis=-1, keepdims=True)
        result = go_ref[...].astype(F32) + scale * weighted - values * (scale**3 * inner)
        gr_ref[...] = result
        low_ref[...] = result.astype(BF)
        gg_ref[...] = jnp.sum(grad * values * scale, axis=0, keepdims=True)
        for j in range(count):
            part = dot_nt(low_ref[...], w_refs[j][...]).astype(BF)
            at = ((at_ref[1] + count - j) % count) ^ at_ref[0]
            for k in range(parts):

                @pl.when(at == k)
                def _():
                    outs[k][...] = part

    vmem = pl.BlockSpec(memory_space=pltpu.VMEM)
    return pl.pallas_call(
        kernel,
        out_shape=[
            jax.ShapeDtypeStruct((tokens, width), F32),
            jax.ShapeDtypeStruct((tokens, width), BF),
            jax.ShapeDtypeStruct((1, width), F32),
        ]
        + [jax.ShapeDtypeStruct((tokens, tile), BF)] * parts,
        in_specs=[smem()] + [vmem] * (5 + count),
        out_specs=[vmem] * (3 + parts),
        compiler_params=params(),
        cost_estimate=cost(2 * tokens * width * tile * parts, 2 * width * tile * parts + 8 * tokens * width),
        name="middle_back",
    )(jnp.stack([seq, z]), terms[0], terms[1], residual, grad_out, gain, *groups)


def unpack(seq, packs, cos_table, sin_table):
    parts = len(packs)
    tokens, tile = cos_table.shape
    each = tile // parts

    def kernel(seq_ref, *refs):
        ins, (cos_ref, sin_ref, out_ref) = refs[:parts], refs[parts:]
        for k in range(parts):
            at = seq_ref[0] ^ k
            queries = turn(ins[k][:, :tile].astype(F32), cos_ref[...], -sin_ref[...])
            out_ref[:, pl.ds(pl.multiple_of(at * tile, tile), tile)] = queries.astype(BF)
            keys = turn(
                ins[k][:, tile : tile + each].astype(F32), cos_ref[:, :each], -sin_ref[:, :each]
            )
            lane = pl.multiple_of(parts * tile + at * each, each)
            out_ref[:, pl.ds(lane, each)] = keys.astype(BF)
            lane = pl.multiple_of((parts + 1) * tile + at * each, each)
            out_ref[:, pl.ds(lane, each)] = ins[k][:, tile + each :]

    vmem = pl.BlockSpec(memory_space=pltpu.VMEM)
    return pl.pallas_call(
        kernel,
        out_shape=jax.ShapeDtypeStruct((tokens, (parts + 2) * tile), BF),
        in_specs=[smem()] + [vmem] * (parts + 2),
        out_specs=vmem,
        compiler_params=params(),
        cost_estimate=cost(0, 6 * 2**20),
        name="unpack",
    )(seq.reshape(1), *packs, cos_table, sin_table)


def inner_back(z, grad_qkv, groups, inputs, gain, grad_res):
    tokens, width = inputs.shape
    count = len(groups)
    depth = width // count

    def kernel(at_ref, gq_ref, *refs):
        w_refs, (in_ref, gain_ref, gr_ref, out_ref, gg_ref, grad_s) = refs[:count], refs[count:]
        for j in range(count):
            lanes = pl.ds(pl.multiple_of((at_ref[0] + count - j) % count * depth, depth), depth)
            grad_s[:, lanes] = dot_nt(gq_ref[...], w_refs[j][...])
        grad = grad_s[...]
        values = in_ref[...].astype(F32)
        scale = lax.rsqrt(jnp.mean(values * values, axis=-1, keepdims=True) + EPSILON)
        weighted = grad * gain_ref[...]
        inner = jnp.mean(weighted * values, axis=-1, keepdims=True)
        result = gr_ref[...] + scale * weighted - values * (scale**3 * inner)
        out_ref[...] = result.astype(BF)
        gg_ref[...] = jnp.sum(grad * values * scale, axis=0, keepdims=True)

    vmem = pl.BlockSpec(memory_space=pltpu.VMEM)
    return pl.pallas_call(
        kernel,
        out_shape=[jax.ShapeDtypeStruct((tokens, width), BF), jax.ShapeDtypeStruct((1, width), F32)],
        in_specs=[smem()] + [vmem] * (4 + count),
        out_specs=[vmem] * 2,
        scratch_shapes=[pltpu.VMEM((tokens, width), F32)],
        compiler_params=params(),
        cost_estimate=cost(2 * tokens * groups[0].size * count, 2 * groups[0].size * count),
        name="inner_back",
    )(z.reshape(1), grad_qkv, *groups, inputs, gain, grad_res)


def weight_grad(left, right, rows, blocks, half, adds=()):
    count = len(left)
    tokens = left[0].shape[0]
    width = right[0].shape[1] // 2
    tile = min(rows, 512)
    steps = rows // tile
    total_rows = rows * len(blocks)

    def kernel(at_ref, *refs):
        lefts, rights, extra, out = refs[:count], refs[count : 2 * count], refs[2 * count : -1], refs[-1]
        total = None
        for l_ref, r_ref in zip(lefts, rights):
            term = lax.dot_general(
                l_ref[...], r_ref[...], (((0,), (0,)), ((), ())), preferred_element_type=F32
            )
            total = term if total is None else total + term
        for ref in extra:
            total = total + ref[...].astype(F32)
        out[...] = total.astype(BF)

    rows_spec = pl.BlockSpec((tile, width), lambda n, at: (n, 0))
    spec = pltpu.PrefetchScalarGridSpec(
        num_scalar_prefetch=1,
        grid=(steps * len(blocks),),
        in_specs=[pl.BlockSpec((tokens, tile), lambda n, at: (0, at[1 + n]))] * count
        + [pl.BlockSpec((tokens, width), lambda n, at: (0, at[0]))] * count
        + [rows_spec] * len(adds),
        out_specs=rows_spec,
    )
    at = [jnp.int32(half)]
    for block in blocks:
        at += [jnp.int32(block) * steps + i for i in range(steps)]
    return pl.pallas_call(
        kernel,
        grid_spec=spec,
        out_shape=jax.ShapeDtypeStruct((total_rows, width), BF),
        compiler_params=params(),
        cost_estimate=cost(
            2 * tokens * count * total_rows * width, 2 * (tokens * count + total_rows) * width
        ),
        name="weight_grad",
    )(jnp.stack(at), *left, *right, *adds)


def row_grads(left, right, blocks, half, added, y, cuts):
    tokens = left.shape[0]
    width = right.shape[1] // 2
    rows = left.shape[1] // LINE
    each = rows // cuts
    count = len(blocks)

    def kernel(at_ref, l_ref, r_ref, add_ref, *refs):
        outs, total_s = refs[:-1], refs[-1]
        total = lax.dot_general(
            l_ref[...], r_ref[...], (((0,), (0,)), ((), ())), preferred_element_type=F32
        )
        total_s[...] = (total + add_ref[...].astype(F32)).astype(BF)
        for j in range(count):

            @pl.when(pl.program_id(0) == j)
            def _():
                for k in range(cuts):
                    start = pl.multiple_of((at_ref[1] + cuts - k) % cuts * each, each)
                    outs[j * cuts + k][...] = total_s[pl.ds(start, each), :]

    spec = pltpu.PrefetchScalarGridSpec(
        num_scalar_prefetch=1,
        grid=(count,),
        in_specs=[
            pl.BlockSpec((tokens, rows), lambda n, at: (0, at[2 + n])),
            pl.BlockSpec((tokens, width), lambda n, at: (0, at[0])),
            pl.BlockSpec((rows, width), lambda n, at: (n, 0)),
        ],
        out_specs=[pl.BlockSpec((each, width), lambda n, at: (0, 0))] * (count * cuts),
        scratch_shapes=[pltpu.VMEM((rows, width), BF)],
    )
    at = jnp.stack([jnp.int32(half), jnp.int32(y)] + [jnp.int32(b) for b in blocks])
    outs = pl.pallas_call(
        kernel,
        grid_spec=spec,
        out_shape=[jax.ShapeDtypeStruct((each, width), BF)] * (count * cuts),
        compiler_params=params(),
        cost_estimate=cost(2 * tokens * count * rows * width, 6 * count * rows * width),
        name="row_grads",
    )(at, left, right, added)
    return [outs[j * cuts : (j + 1) * cuts] for j in range(count)]


def join(core, mine, other, widths):
    rows, half = mine.shape
    tile = min(rows, 256)

    def kernel(core_ref, mine_ref, other_ref, *refs):
        outs, full = refs[:-1], refs[-1]
        target = outs[0] if len(outs) == 1 else full
        at = pl.multiple_of(core_ref[0] * half, half)
        target[:, pl.ds(at, half)] = mine_ref[...].astype(F32)
        at = pl.multiple_of((1 - core_ref[0]) * half, half)
        target[:, pl.ds(at, half)] = other_ref[...].astype(F32)
        if len(outs) > 1:
            lane = 0
            for out in outs:
                out[...] = full[:, lane : lane + out.shape[1]]
                lane += out.shape[1]

    def block(width):
        return pl.BlockSpec((tile, width), lambda n: (n, 0))

    return pl.pallas_call(
        kernel,
        grid=(rows // tile,),
        out_shape=[jax.ShapeDtypeStruct((rows, width), F32) for width in widths],
        in_specs=[smem(), block(half), block(half)],
        out_specs=[block(width) for width in widths],
        scratch_shapes=[pltpu.VMEM((tile, 2 * half) if len(widths) > 1 else (8, 128), F32)],
        compiler_params=params(),
        cost_estimate=cost(0, rows * half * 12),
        name="join",
    )(core.reshape(1), mine, other)
def half_of(array, which, axis=1):
    size = array.shape[axis] // 2
    return lax.dynamic_slice_in_dim(array, which * size, size, axis)


class Order:
    def __init__(self):
        self.marks = ()

    def tie(self, *values):
        if self.marks:
            values = lax.optimization_barrier(tuple(values) + self.marks)[: len(values)]
        return values[0] if len(values) == 1 else list(values)

    def done(self, *values):
        self.marks = tuple(values)


def y_hops(value):
    return ring_gather(value, y_next, columns())[1:]


def add_low(left, right):
    return (left.astype(F32) + right.astype(F32)).astype(BF)


def finish_sum(low, core, widths):
    total = add_low(low, x_swap(low))
    return join(core, total, core_swap(total), widths)


def rope_tables(positions, repeat):
    frequency = THETA ** (-(jnp.arange(HD // 2, dtype=F32) * 2.0) / HD)
    angles = positions.astype(F32)[:, None] * frequency[None, :]
    cos, sin = jnp.cos(angles), jnp.sin(angles)
    return (
        jnp.tile(jnp.concatenate([cos, cos], axis=1), (1, repeat)),
        jnp.tile(jnp.concatenate([-sin, sin], axis=1), (1, repeat)),
    )


def exchange(packs):
    return [packs[0]] + [seq_swap(packs[k], k) for k in range(1, len(packs))]


def shards(
    inputs,
    query_weight,
    key_weight,
    value_weight,
    output_weight,
    gate_weight,
    up_weight,
    down_weight,
    gain_attn,
    gain_ffn,
    cotangent,
):
    seq_count, local_len, width = inputs.shape
    assert seq_count == 1
    tokens = local_len
    parts = lax.axis_size("seq")
    kv_local = KVH // parts
    cols = columns()
    seq = lax.axis_index("seq")
    core, side = seq % 2, seq // 2
    fsdp = lax.axis_index("fsdp")
    z, y = fsdp // cols, fsdp % cols
    q_width, kv_width = query_weight.shape[1], key_weight.shape[1]
    heads_local = q_width // HD // parts
    flat_in = inputs.reshape(tokens, width)
    grad_out = cotangent.reshape(tokens, width)

    qkv_shard = jnp.concatenate([query_weight, key_weight, value_weight], axis=1)
    rows = qkv_shard.shape[0]
    part, half = rows // 2, qkv_shard.shape[1] // 2
    positions = seq * local_len + jnp.arange(local_len)
    cos_table, sin_table = rope_tables(positions, kv_width // HD)
    order = Order()

    def swapped(pieces):
        return [core_swap(p) for p in pieces]

    def place_halves(pieces, others, whole_first=None):
        each = pieces[-1].shape[1]
        placed, offsets = [], []
        for k, (piece, other) in enumerate(zip(pieces, others)):
            row = (y - k) % cols * rows
            if k == 0 and whole_first is not None:
                placed.append(whole_first)
                offsets.append((row, 0))
            else:
                placed += [piece, other]
                offsets += [(row, core * each), (row, (1 - core) * each)]
        return place((rows * cols, 2 * each), placed, offsets)

    def place_quarters(pieces, others, sides, count, size, first):
        each = pieces[0].shape[1]
        placed, offsets = [], []
        for i, (piece, other) in enumerate(zip(pieces, others)):
            k, at = i // 2, sides[i % 2]
            row = first(k) * size + at * (size // 2)
            placed += [piece, other]
            offsets += [(row, core * each), (row, (1 - core) * each)]
        return place((size * count, 2 * each), placed, offsets)

    def line_row(k):
        return (y - k) % cols

    qkv_half = half_of(qkv_shard, core)
    out_half = half_of(output_weight, core)
    gains = jnp.pad(jnp.stack([gain_attn, gain_ffn]), ((0, 14), (0, 0)))
    line, beside, line_g = [qkv_half], [], [gains]
    other_line, other_beside, groups = [None], [], []
    for j in range(LINE):
        here = order.tie(line[j]) if j else line[j]
        beside.append(y_hops(here))
        marks = list(beside[j])
        if j + 1 < LINE:
            line.append(z_next(here))
            line_g.append(z_next(order.tie(line_g[j]) if j else line_g[j]))
            marks += [line[j + 1], line_g[j + 1]]
        if j:
            other_beside.append(swapped(order.tie(*beside[j - 1], here)[:-1]))
            other_line.append(core_swap(here))
            marks += other_beside[j - 1]
        if j > 1:
            i = j - 2
            groups.append(
                place_halves(
                    [line[i]] + beside[i], [other_line[i]] + other_beside[i], None if i else qkv_shard
                )
            )
            marks.append(groups[i])
        if j == LINE - 1:
            line_o = [out_half, z_next(order.tie(out_half))]
            gains_near = jnp.concatenate(line_g, axis=0)
            gains_far = y_hops(gains_near)
            marks += [line_o[1]] + gains_far
        order.done(*marks)

    j = LINE - 1
    line_o.append(z_next(order.tie(line_o[1])))
    grad_parts = [grad_out, z_next(order.tie(grad_out))]
    beside_o = [y_hops(order.tie(line_o[0])), y_hops(order.tie(line_o[1]))]
    other_beside.append(swapped(order.tie(*beside[j], line_o[1])[:-1]))
    for i in (j - 1, j):
        groups.append(place_halves([line[i]] + beside[i], [other_line[i]] + other_beside[i]))
    gain_full = jnp.zeros((2, width), BF)
    for j in range(LINE):
        for k, g in enumerate([gains_near] + gains_far):
            at = (((z - j) % LINE) * cols + (y - k) % cols) * rows
            gain_full = lax.dynamic_update_slice(gain_full, g[16 * j : 16 * j + 2], (0, at))
    gain_one = gain_full[:1].astype(F32)
    gain_two = gain_full[1:].astype(F32)
    acts_one, *sent = project_in(seq, z, flat_in, gain_one, groups, cos_table, sin_table, parts)
    order.done(*sent, line_o[2], *beside_o[0])

    def out_group(j):
        hops = order.tie(line_o[j], *beside_o[j])
        if j == 0:
            return place_halves([None] + hops[1:], [None] + swapped(hops[1:]), output_weight)
        return place_halves(hops, swapped(hops))

    packs = exchange(order.tie(*sent))
    line_o.append(z_next(order.tie(line_o[2])))
    order.done(*packs, line_o[3], *beside_o[1], grad_parts[1])

    beside_o += [y_hops(order.tie(line_o[2])), y_hops(order.tie(line_o[3]))]
    grad_parts.append(z_next(order.tie(grad_parts[1])))
    out_groups = [out_group(0), out_group(1)]
    *mixed_sent, log_totals = attend_forward(seq, order.tie(*packs), heads_local, kv_local)
    order.done(*mixed_sent, *beside_o[2], *beside_o[3], grad_parts[2], *out_groups)

    mixed = exchange(order.tie(*mixed_sent))
    grad_parts.append(z_next(order.tie(grad_parts[2])))
    out_groups += [out_group(2), out_group(3)]
    order.done(*mixed, *out_groups)

    own = (gate_weight, up_weight, down_weight)
    starts = [half_of(half_of(weight, side, 0), core) for weight in own]
    far_y = [y_hops(order.tie(starts[0]))]
    mixed_flat, residual, acts_two = project_out(
        seq, z, order.tie(*mixed), flat_in, gain_two, out_groups
    )
    order.done(acts_two, grad_parts[3])

    far_rows = gate_weight.shape[0]

    def far_place(i):
        pieces = []
        for k in range(cols - 1):
            pieces += [far_y[i][k], far_c[i][k]]
        pieces = order.tie(*pieces)
        return place_quarters(
            pieces, swapped(pieces), (side, 1 - side), cols - 1, far_rows, lambda k: k
        )

    acts_parts, far_c, far, near_done = [acts_two], [], [], []

    def run_near(j):
        near_done.append(feed_forward(order.tie(acts_parts[j]), grad_parts[j], *own))
        return near_done[j][3]

    for j in range(LINE - 1):
        acts_parts.append(z_next(order.tie(acts_parts[j])))
        marks = [acts_parts[j + 1]]
        if j == 0:
            marks += far_y[0]
            far_y.append(y_hops(order.tie(starts[1])))
        else:
            far_c.append([x_swap(p) for p in order.tie(*far_y[j - 1], acts_parts[j])[:-1]])
            marks += far_y[j] + far_c[j - 1]
            if j == 1:
                far_y.append(y_hops(order.tie(starts[2])))
            else:
                far.append(far_place(0))
                marks.append(far[0])
        order.done(*marks, run_near(j))

    far_c.append([x_swap(p) for p in order.tie(*far_y[2], acts_parts[3])[:-1]])
    far.append(far_place(1))
    order.done(run_near(3), *far_c[2], far[1])
    far.append(far_place(2))
    far_done = [None] * LINE

    def run_far(j):
        far_done[j] = feed_forward(order.tie(acts_parts[j]), grad_parts[j], *far, near_done[j][3:])
        return far_done[j][4]

    order.done(run_far(1))

    passed = z_next(order.tie(far_done[1][4]))
    order.done(passed, run_far(2))
    passed = z_next(order.tie(add_low(passed, far_done[2][4])))
    first = run_far(3)
    order.done(passed, first, run_far(0))
    passed = z_next(order.tie(add_low(passed, far_done[3][4])))

    rights = (grad_parts, acts_parts, acts_parts)
    far_size = far_rows * (cols - 1)
    far_sent, far_total, own_sent = [None] * 3, [None] * 3, [None] * 3

    def of(done, which):
        return order.tie(*[d[which] for d in done])

    def send_far(i):
        far_sent[i] = weight_grad(of(far_done, i), rights[i], far_size, [0], 1 - core)
        return far_sent[i]

    def keep_far(i):
        return weight_grad(of(far_done, i), rights[i], far_size, [0], core, [far_sent[i]])

    def pass_far(i, kept):
        kept = order.tie(kept)
        total = y_next(kept[:far_rows])
        for k in range(1, cols - 1):
            total = y_next(add_low(total, kept[k * far_rows : (k + 1) * far_rows]))
        far_total[i] = total

    def send_own(i):
        own_sent[i] = weight_grad(of(near_done, i), rights[i], far_rows, [0], 1 - core)
        return own_sent[i]

    def keep_own(i):
        return weight_grad(
            of(near_done, i), rights[i], far_rows, [0], core, [own_sent[i], far_total[i]]
        )

    marks = [send_far(0), send_far(1), send_far(2)]
    order.done(passed, *marks)

    far_sent = [core_swap(order.tie(term)) for term in far_sent]
    ffn_parts = [d[3] for d in far_done]
    ffn_sum = z_next(order.tie(ffn_parts[1]))
    grad_res, grad_res_low, grad_gain_two, *grad_sent = middle_back(
        seq, z, order.tie(passed, far_done[0][4]), residual, grad_out, gain_two, out_groups, parts
    )
    order.done(*grad_sent, *far_sent)

    grad_packs = exchange(order.tie(*grad_sent))
    kept = [keep_far(0), keep_far(1)]
    order.done(*grad_packs, ffn_sum, *kept)

    pass_far(0, kept[0])
    pass_far(1, kept[1])
    ffn_sum = z_next(order.tie(add_low(ffn_sum, ffn_parts[2])))
    back_sent = attend_backward(
        seq, log_totals, packs, order.tie(*grad_packs), heads_local, kv_local
    )
    order.done(*back_sent)

    back_packs = exchange(order.tie(*back_sent))
    kept = [keep_far(2), send_own(0), send_own(1), send_own(2)]
    order.done(*back_packs, *kept, far_total[0], ffn_sum)

    pass_far(2, kept[0])
    own_sent = [core_swap(term) for term in order.tie(*own_sent)]
    ffn_sum = z_next(order.tie(add_low(ffn_sum, ffn_parts[3])))
    grad_qkv = unpack(seq, order.tie(*back_packs), cos_table, sin_table)
    line_order = list(range(1, LINE)) + [0]
    blocks = [(z - j) % LINE for j in line_order]
    line_rows = rows * cols
    qkv_sent = weight_grad([acts_one], [grad_qkv], line_rows, blocks, 1 - core)
    order.done(qkv_sent, own_sent[0])

    qkv_recv = core_swap(order.tie(qkv_sent))
    out_left, out_right = order.tie(mixed_flat, grad_res_low)
    low_down = keep_own(0)
    out_sent = weight_grad([out_left], [out_right], line_rows, blocks, 1 - core)
    order.done(qkv_recv, low_down, out_sent, far_total[1], own_sent[1])

    cross_w = [x_swap(order.tie(low_down))]
    out_recv = core_swap(order.tie(out_sent))
    qkv_terms = row_grads(acts_one, grad_qkv, blocks, core, order.tie(qkv_recv), y, cols)
    low_gate = keep_own(1)
    order.done(low_gate, ffn_sum, *[t for terms in qkv_terms for t in terms])
    hops = []
    for terms in qkv_terms:
        terms = order.tie(*terms)
        total = None
        for k in list(range(1, cols)) + [0]:
            total = terms[k] if total is None else add_low(y_next(total), terms[k])
        hops.append(total)
    out_terms = row_grads(mixed_flat, grad_res_low, blocks, core, order.tie(out_recv), y, 1)
    order.done(hops[0], *[t for terms in out_terms for t in terms])

    def summed(low, crossed):
        total = add_low(low, crossed)
        return total, core_swap(total)

    passed = z_next(order.tie(hops[0]))
    cross_w.append(x_swap(order.tie(low_gate)))
    low_up = keep_own(2)
    order.done(passed, low_up, hops[1])
    passed = z_next(order.tie(add_low(passed, hops[1])))
    cross_w.append(x_swap(order.tie(low_up)))
    total = order.tie(out_terms[0][0])
    for j in range(1, LINE):
        total = add_low(z_next(total), out_terms[j][0])
    pieces = [
        lax.dynamic_slice_in_dim(total, (y - k) % cols * rows, rows, 0) for k in range(cols)
    ]
    total = None
    for k in list(range(1, cols)) + [0]:
        total = pieces[k] if total is None else add_low(y_next(total), pieces[k])
    d_out = finish_sum(total, core, [width])
    for i in (2, 3):
        passed = add_low(passed, hops[i])
        if i < 3:
            passed = z_next(passed)
    d_qkv = finish_sum(passed, core, [q_width, kv_width, kv_width])
    d_down, d_gate, d_up = [
        join(core, *summed(low, crossed), [width])[0]
        for low, crossed in zip((low_down, low_gate, low_up), cross_w)
    ]

    outputs = (residual + ffn_sum.astype(F32) + ffn_parts[0].astype(F32)).astype(BF)
    grad_inputs, grad_gain_one = inner_back(z, grad_qkv, groups, flat_in, gain_one, grad_res)
    gain_sums = all_sum(jnp.concatenate([grad_gain_one, grad_gain_two], axis=0))
    gain_sums = lax.dynamic_slice_in_dim(gain_sums, fsdp * rows, rows, 1)
    return (
        outputs.reshape(inputs.shape),
        grad_inputs.reshape(inputs.shape),
        d_qkv[0],
        d_qkv[1],
        d_qkv[2],
        d_out[0],
        d_gate,
        d_up,
        d_down,
        gain_sums[0],
        gain_sums[1],
    )


def solution(mesh):
    token_spec, row_spec, gain_spec = P("fsdp", "seq", None), P("fsdp", None), P("fsdp")
    return jax.shard_map(
        shards,
        mesh=mesh,
        in_specs=(token_spec,) + (row_spec,) * 7 + (gain_spec,) * 2 + (token_spec,),
        out_specs=(token_spec,) * 2 + (row_spec,) * 7 + (gain_spec,) * 2,
        check_vma=False,
    )
```

```python
import functools

import jax
import jax.numpy as jnp
from jax import lax
from jax.experimental import pallas as pl
from jax.experimental.pallas import tpu as pltpu
from jax.sharding import PartitionSpec as P

KVH = 8
HD = 64
BLOCK = 256
LINE = 4

EPSILON = 1e-05
THETA = 500000.0
LOG2E = 1.4426950408889634

BF = jnp.bfloat16
F32 = jnp.float32


def after(value, *others):
    return lax.optimization_barrier((value,) + others)[0]


def columns():
    return lax.axis_size("fsdp") // LINE


def z_next(value):
    cols = columns()
    count = lax.axis_size("fsdp")
    return lax.ppermute(value, "fsdp", [(i, (i + cols) % count) for i in range(count)])


def y_next(value):
    cols = columns()
    count = lax.axis_size("fsdp")
    return lax.ppermute(
        value, "fsdp", [(i, i // cols * cols + (i + 1) % cols) for i in range(count)]
    )


def seq_swap(value, bit):
    return lax.ppermute(value, "seq", [(i, i ^ bit) for i in range(lax.axis_size("seq"))])


def core_swap(value):
    return seq_swap(value, 1)


def x_swap(value):
    return seq_swap(value, 2)


def ring_gather(value, step, count):
    pieces = [value]
    for _ in range(count - 1):
        pieces.append(step(pieces[-1]))
    return pieces


def ring_scatter(part_of, step, count):
    total = None
    for j in list(range(1, count)) + [0]:
        total = part_of(j) if total is None else part_of(j) + total.astype(F32)
        if j:
            total = step(total.astype(BF))
    return total


def all_sum(value):
    bit = 1
    while bit < lax.axis_size("seq"):
        value = value + seq_swap(value, bit)
        bit *= 2
    count = lax.axis_size("fsdp")
    bit = 1
    while bit < count:
        value = value + lax.ppermute(value, "fsdp", [(i, i ^ bit) for i in range(count)])
        bit *= 2
    return value


def dot_nt(a, b):
    return lax.dot_general(a, b, (((1,), (1,)), ((), ())), preferred_element_type=F32)

def dot_nn(a, b):
    return jnp.dot(a, b, preferred_element_type=F32)


def attend_forward_kernel(parts, heads, kv, seq_ref, *refs):
    packs, outs = refs[:parts], refs[parts : 2 * parts]
    lse_ref, q_s, k_s, vt_s, o_s = refs[2 * parts :]
    tokens = packs[0].shape[0]
    seq = seq_ref[0]
    group = heads // kv
    for k in range(parts):
        rows = pl.ds(pl.multiple_of((seq ^ k) * tokens, tokens), tokens)
        q_s[rows, :] = packs[k][:, : heads * HD]
        for g in range(kv):
            lane = (heads + g) * HD
            k_s[g, rows, :] = packs[k][:, lane : lane + HD]
            lane = (heads + kv + g) * HD
            vt_s[g, :, rows] = packs[k][:, lane : lane + HD].T
    full = parts * tokens
    for g in range(kv):
        for i in range(full // BLOCK):
            keys = (i + 1) * BLOCK
            rows = slice(i * BLOCK, keys)
            for pair in range(group // 2):
                halves = []
                for h in (g * group + 2 * pair, g * group + 2 * pair + 1):
                    scores = dot_nt(k_s[g, :keys, :], q_s[rows, h * HD : (h + 1) * HD])
                    scores = scores * (HD**-0.5 * LOG2E)
                    top = jnp.max(scores, axis=0, keepdims=True)
                    powers = jnp.exp2(scores - top)
                    total = jnp.sum(powers, axis=0, keepdims=True)
                    halves.append(dot_nn(vt_s[g, :, :keys], powers.astype(BF)) / total)
                    lse_ref[h : h + 1, rows] = top + jnp.log2(total)
                lane = (g * group + 2 * pair) * HD
                o_s[rows, lane : lane + 2 * HD] = jnp.concatenate(halves, axis=0).T.astype(BF)
    for k in range(parts):
        rows = pl.ds(pl.multiple_of((seq ^ k) * tokens, tokens), tokens)
        outs[k][...] = o_s[rows, :]


def attend_forward(seq, packs, heads, kv):
    parts = len(packs)
    tokens = packs[0].shape[0]
    full = parts * tokens
    vmem = pl.BlockSpec(memory_space=pltpu.VMEM)
    flops = 4 * heads * full * full * HD * 5 // 8
    return pl.pallas_call(
        functools.partial(attend_forward_kernel, parts, heads, kv),
        out_shape=[jax.ShapeDtypeStruct((tokens, heads * HD), BF)] * parts
        + [jax.ShapeDtypeStruct((heads, full), F32)],
        in_specs=[pl.BlockSpec(memory_space=pltpu.SMEM)] + [vmem] * parts,
        out_specs=[vmem] * (parts + 1),
        scratch_shapes=[
            pltpu.VMEM((full, heads * HD), BF),
            pltpu.VMEM((kv, full, HD), BF),
            pltpu.VMEM((kv, HD, full), BF),
            pltpu.VMEM((full, heads * HD), BF),
        ],
        compiler_params=pltpu.CompilerParams(vmem_limit_bytes=48 * 2**20),
        cost_estimate=cost(flops * 4, 4 * 2**20),
        name="attend_forward",
    )(seq.reshape(1), *packs)


def attend_backward_kernel(parts, heads, kv, seq_ref, lse_ref, *refs):
    packs, grads, outs = refs[:parts], refs[parts : 2 * parts], refs[2 * parts : 3 * parts]
    q_s, k_s, kt_s, v_s, g_s, dq_s, dk_s, dv_s = refs[3 * parts :]
    tokens = packs[0].shape[0]
    seq = seq_ref[0]
    group = heads // kv
    for k in range(parts):
        rows = pl.ds(pl.multiple_of((seq ^ k) * tokens, tokens), tokens)
        q_s[rows, :] = packs[k][:, : heads * HD]
        g_s[rows, :] = grads[k][...]
        for g in range(kv):
            lane = (heads + g) * HD
            k_s[g, rows, :] = packs[k][:, lane : lane + HD]
            kt_s[g, :, rows] = packs[k][:, lane : lane + HD].T
            lane = (heads + kv + g) * HD
            v_s[g, rows, :] = packs[k][:, lane : lane + HD]
    full = parts * tokens
    dk_s[...] = jnp.zeros_like(dk_s)
    dv_s[...] = jnp.zeros_like(dv_s)
    for g in range(kv):
        for i in range(full // BLOCK):
            keys = (i + 1) * BLOCK
            rows = slice(i * BLOCK, keys)
            for pair in range(group // 2):
                halves = []
                for h in (g * group + 2 * pair, g * group + 2 * pair + 1):
                    query = q_s[rows, h * HD : (h + 1) * HD]
                    grad = g_s[rows, h * HD : (h + 1) * HD]
                    scores = dot_nt(k_s[g, :keys, :], query) * (HD**-0.5 * LOG2E)
                    probs = jnp.exp2(scores - lse_ref[h : h + 1, rows])
                    grad_probs = dot_nt(v_s[g, :keys, :], grad)
                    inner = jnp.sum(probs * grad_probs, axis=0, keepdims=True)
                    grad_scores = (probs * (grad_probs - inner)).astype(BF)
                    dv_s[g, :keys, :] += dot_nn(probs.astype(BF), grad)
                    dk_s[g, :keys, :] += dot_nn(grad_scores, query)
                    halves.append(dot_nn(kt_s[g, :, :keys], grad_scores) * HD**-0.5)
                lane = (g * group + 2 * pair) * HD
                dq_s[rows, lane : lane + 2 * HD] = jnp.concatenate(halves, axis=0).T.astype(BF)
    for k in range(parts):
        rows = pl.ds(pl.multiple_of((seq ^ k) * tokens, tokens), tokens)
        outs[k][:, : heads * HD] = dq_s[rows, :]
        for g in range(kv):
            lane = (heads + g) * HD
            outs[k][:, lane : lane + HD] = (dk_s[g, rows, :] * HD**-0.5).astype(BF)
            lane = (heads + kv + g) * HD
            outs[k][:, lane : lane + HD] = dv_s[g, rows, :].astype(BF)


def attend_backward(seq, lse, packs, grads, heads, kv):
    parts = len(packs)
    tokens = packs[0].shape[0]
    full = parts * tokens
    vmem = pl.BlockSpec(memory_space=pltpu.VMEM)
    flops = 10 * heads * full * full * HD * 5 // 8
    return pl.pallas_call(
        functools.partial(attend_backward_kernel, parts, heads, kv),
        out_shape=[jax.ShapeDtypeStruct(packs[0].shape, BF)] * parts,
        in_specs=[pl.BlockSpec(memory_space=pltpu.SMEM)] + [vmem] * (2 * parts + 1),
        out_specs=[vmem] * parts,
        scratch_shapes=[
            pltpu.VMEM((full, heads * HD), BF),
            pltpu.VMEM((kv, full, HD), BF),
            pltpu.VMEM((kv, HD, full), BF),
            pltpu.VMEM((kv, full, HD), BF),
            pltpu.VMEM((full, heads * HD), BF),
            pltpu.VMEM((full, heads * HD), BF),
            pltpu.VMEM((kv, full, HD), F32),
            pltpu.VMEM((kv, full, HD), F32),
        ],
        compiler_params=pltpu.CompilerParams(vmem_limit_bytes=48 * 2**20),
        cost_estimate=cost(flops * 4, 8 * 2**20),
        name="attend_backward",
    )(seq.reshape(1), lse, *packs, *grads)


def smem():
    return pl.BlockSpec(memory_space=pltpu.SMEM)


def params(mib=56):
    return pltpu.CompilerParams(vmem_limit_bytes=mib * 2**20)


def cost(flops, moved):
    return pl.CostEstimate(flops=flops // 8, bytes_accessed=moved // 8, transcendentals=0)


def place(shape, pieces, offsets):
    count = len(pieces)

    def kernel(at_ref, *refs):
        sources, target, sems = refs[:-2], refs[-2], refs[-1]
        copies = []
        for i, source in enumerate(sources):
            rows, width = source.shape
            row = pl.multiple_of(at_ref[2 * i], rows)
            column = pl.multiple_of(at_ref[2 * i + 1], width)
            spot = target.at[pl.ds(row, rows), pl.ds(column, width)]
            copies.append(pltpu.make_async_copy(source, spot, sems.at[i]))
            copies[-1].start()
        for copy in copies:
            copy.wait()

    moved = 2 * sum(piece.size * 2 for piece in pieces)
    return pl.pallas_call(
        kernel,
        out_shape=jax.ShapeDtypeStruct(shape, pieces[0].dtype),
        in_specs=[smem()] + [pl.BlockSpec(memory_space=pl.ANY)] * count,
        out_specs=pl.BlockSpec(memory_space=pltpu.HBM),
        scratch_shapes=[pltpu.SemaphoreType.DMA((count,))],
        compiler_params=params(16),
        cost_estimate=cost(0, moved),
        name="place",
    )(jnp.stack([jnp.int32(v) for pair in offsets for v in pair]), *pieces)


def turn(values, cos_table, sin_table):
    width = values.shape[1]
    lane = lax.broadcasted_iota(jnp.int32, values.shape, 1)
    swapped = jnp.where(
        lane % HD < HD // 2,
        pltpu.roll(values, width - HD // 2, 1),
        pltpu.roll(values, HD // 2, 1),
    )
    return values * cos_table + swapped * sin_table


def whole(shape):
    return pl.BlockSpec(shape, lambda n: (0,) * len(shape))


def project_in(seq, z, inputs, gain, groups, cos_table, sin_table, parts):
    tokens, width = inputs.shape
    tile = cos_table.shape[1]
    each = tile // parts
    pack = tile + 2 * each
    count = len(groups)
    depth = width // count

    def kernel(at_ref, in_ref, gain_ref, *refs):
        w_refs, (cos_ref, sin_ref, acts_ref), packs = refs[:count], refs[count : count + 3], refs[count + 3 :]
        step = pl.program_id(0)

        @pl.when(step == 0)
        def _():
            values = in_ref[...].astype(F32)
            scale = lax.rsqrt(jnp.mean(values * values, axis=-1, keepdims=True) + EPSILON)
            acts_ref[...] = (values * scale * gain_ref[...]).astype(BF)

        rows = None
        for j in range(count):
            lanes = pl.ds(pl.multiple_of((at_ref[1] + count - j) % count * depth, depth), depth)
            term = dot_nn(acts_ref[:, lanes], w_refs[j][...])
            rows = term if rows is None else rows + term
        turned = jnp.where(
            step == parts + 1, rows, turn(rows, cos_ref[...], sin_ref[...])
        ).astype(BF)
        seq_now = at_ref[0]
        for k in range(parts):

            @pl.when((seq_now ^ k) == step)
            def _():
                packs[k][:, :tile] = turned

            for d in range(parts):
                for which in range(2):

                    @pl.when(((seq_now ^ k) == d) & (step == parts + which))
                    def _():
                        lane = tile + which * each
                        packs[k][:, lane : lane + each] = turned[:, d * each : (d + 1) * each]

    return pl.pallas_call(
        kernel,
        grid=(parts + 2,),
        out_shape=[jax.ShapeDtypeStruct((tokens, width), BF)]
        + [jax.ShapeDtypeStruct((tokens, pack), BF)] * parts,
        in_specs=[smem(), whole((tokens, width)), whole((1, width))]
        + [pl.BlockSpec((depth, tile), lambda n: (0, n))] * count
        + [whole((tokens, tile))] * 2,
        out_specs=[whole((tokens, width))] + [whole((tokens, pack))] * parts,
        compiler_params=params(),
        cost_estimate=cost(2 * tokens * width * tile * (parts + 2), 2 * width * tile * (parts + 2)),
        name="project_in",
    )(jnp.stack([seq, z]), inputs, gain, *groups, cos_table, sin_table)


def project_out(seq, z, mixed, inputs, gain, groups):
    parts = len(mixed)
    tokens, width = inputs.shape
    each = mixed[0].shape[1]
    tile = width // parts
    count = len(groups)
    depth = parts * each // count

    def kernel(at_ref, *refs):
        parts_in, (in_ref, gain_ref) = refs[:parts], refs[parts : parts + 2]
        w_refs, (flat_ref, res_ref, acts_ref) = refs[parts + 2 : -3], refs[-3:]
        step = pl.program_id(0)

        @pl.when(step == 0)
        def _():
            for k in range(parts):
                lane = pl.multiple_of((at_ref[0] ^ k) * each, each)
                flat_ref[:, pl.ds(lane, each)] = parts_in[k][...]

        lanes = pl.ds(pl.multiple_of(step * tile, tile), tile)
        total = in_ref[:, lanes].astype(F32)
        for j in range(count):
            rows = pl.ds(pl.multiple_of((at_ref[1] + count - j) % count * depth, depth), depth)
            total = total + dot_nn(flat_ref[:, rows], w_refs[j][...])
        res_ref[:, lanes] = total

        @pl.when(step == parts - 1)
        def _():
            values = res_ref[...]
            scale = lax.rsqrt(jnp.mean(values * values, axis=-1, keepdims=True) + EPSILON)
            acts_ref[...] = (values * scale * gain_ref[...]).astype(BF)

    return pl.pallas_call(
        kernel,
        grid=(parts,),
        out_shape=[
            jax.ShapeDtypeStruct((tokens, parts * each), BF),
            jax.ShapeDtypeStruct((tokens, width), F32),
            jax.ShapeDtypeStruct((tokens, width), BF),
        ],
        in_specs=[smem()]
        + [whole((tokens, each))] * parts
        + [whole((tokens, width)), whole((1, width))]
        + [pl.BlockSpec((depth, tile), lambda n: (0, n))] * count,
        out_specs=[whole((tokens, parts * each)), whole((tokens, width)), whole((tokens, width))],
        compiler_params=params(),
        cost_estimate=cost(2 * tokens * width * parts * each, 2 * width * parts * each),
        name="project_out",
    )(jnp.stack([seq, z]), *mixed, inputs, gain, *groups)


def feed_forward(acts, grads, gate, up, down, begun=None):
    tokens, width = acts.shape
    hidden = gate.shape[0]
    tile = 256
    steps = hidden // tile
    kind = F32 if begun is None else BF
    begun = [] if begun is None else list(begun)

    def kernel(a_ref, c_ref, g_ref, u_ref, d_ref, *refs):
        starts, (h_ref, gg_ref, gu_ref, o_ref, ga_ref, o_s, ga_s) = refs[:-7], refs[-7:]
        step = pl.program_id(0)

        @pl.when(step == 0)
        def _():
            if starts:
                o_s[...] = starts[0][...]
                ga_s[...] = starts[1][...]
            else:
                o_s[...] = jnp.zeros_like(o_s)
                ga_s[...] = jnp.zeros_like(ga_s)

        gate_act = dot_nt(a_ref[...], g_ref[...])
        up_act = dot_nt(a_ref[...], u_ref[...])
        grad_hidden = dot_nt(c_ref[...], d_ref[...])
        sigma = jax.nn.sigmoid(gate_act)
        silu = gate_act * sigma
        low = (silu * up_act).astype(BF)
        grad_gate = (grad_hidden * up_act * (sigma * (1.0 + gate_act * (1.0 - sigma)))).astype(BF)
        grad_up = (grad_hidden * silu).astype(BF)
        h_ref[...] = low
        gg_ref[...] = grad_gate
        gu_ref[...] = grad_up
        o_s[...] += dot_nn(low, d_ref[...])
        ga_s[...] += dot_nn(grad_gate, g_ref[...]) + dot_nn(grad_up, u_ref[...])

        @pl.when(step == steps - 1)
        def _():
            o_ref[...] = o_s[...].astype(kind)
            ga_ref[...] = ga_s[...].astype(kind)

    whole = pl.BlockSpec((tokens, width), lambda n: (0, 0))
    rows = pl.BlockSpec((tile, width), lambda n: (n, 0))
    lanes = pl.BlockSpec((tokens, tile), lambda n: (0, n))
    return pl.pallas_call(
        kernel,
        grid=(steps,),
        out_shape=[jax.ShapeDtypeStruct((tokens, hidden), BF)] * 3
        + [jax.ShapeDtypeStruct((tokens, width), kind)] * 2,
        in_specs=[whole, whole, rows, rows, rows] + [whole] * len(begun),
        out_specs=[lanes] * 3 + [whole] * 2,
        scratch_shapes=[pltpu.VMEM((tokens, width), F32)] * 2,
        compiler_params=params(),
        cost_estimate=cost(12 * tokens * width * hidden, 6 * width * hidden),
        name="feed_forward",
    )(acts, grads, gate, up, down, *begun)


def middle_back(seq, z, terms, residual, grad_out, gain, groups, parts):
    tokens, width = residual.shape
    tile = groups[0].shape[0]
    count = len(groups)
    assert count == parts

    def kernel(at_ref, t0_ref, t1_ref, res_ref, go_ref, gain_ref, *refs):
        w_refs, (gr_ref, low_ref, gg_ref), outs = refs[:count], refs[count : count + 3], refs[count + 3 :]
        grad = t0_ref[...].astype(F32) + t1_ref[...].astype(F32)
        values = res_ref[...]
        scale = lax.rsqrt(jnp.mean(values * values, axis=-1, keepdims=True) + EPSILON)
        weighted = grad * gain_ref[...]
        inner = jnp.mean(weighted * values, axis=-1, keepdims=True)
        result = go_ref[...].astype(F32) + scale * weighted - values * (scale**3 * inner)
        gr_ref[...] = result
        low_ref[...] = result.astype(BF)
        gg_ref[...] = jnp.sum(grad * values * scale, axis=0, keepdims=True)
        for j in range(count):
            part = dot_nt(low_ref[...], w_refs[j][...]).astype(BF)
            at = ((at_ref[1] + count - j) % count) ^ at_ref[0]
            for k in range(parts):

                @pl.when(at == k)
                def _():
                    outs[k][...] = part

    vmem = pl.BlockSpec(memory_space=pltpu.VMEM)
    return pl.pallas_call(
        kernel,
        out_shape=[
            jax.ShapeDtypeStruct((tokens, width), F32),
            jax.ShapeDtypeStruct((tokens, width), BF),
            jax.ShapeDtypeStruct((1, width), F32),
        ]
        + [jax.ShapeDtypeStruct((tokens, tile), BF)] * parts,
        in_specs=[smem()] + [vmem] * (5 + count),
        out_specs=[vmem] * (3 + parts),
        compiler_params=params(),
        cost_estimate=cost(2 * tokens * width * tile * parts, 2 * width * tile * parts + 8 * tokens * width),
        name="middle_back",
    )(jnp.stack([seq, z]), terms[0], terms[1], residual, grad_out, gain, *groups)


def unpack(seq, packs, cos_table, sin_table):
    parts = len(packs)
    tokens, tile = cos_table.shape
    each = tile // parts

    def kernel(seq_ref, *refs):
        ins, (cos_ref, sin_ref, out_ref) = refs[:parts], refs[parts:]
        for k in range(parts):
            at = seq_ref[0] ^ k
            queries = turn(ins[k][:, :tile].astype(F32), cos_ref[...], -sin_ref[...])
            out_ref[:, pl.ds(pl.multiple_of(at * tile, tile), tile)] = queries.astype(BF)
            keys = turn(
                ins[k][:, tile : tile + each].astype(F32), cos_ref[:, :each], -sin_ref[:, :each]
            )
            lane = pl.multiple_of(parts * tile + at * each, each)
            out_ref[:, pl.ds(lane, each)] = keys.astype(BF)
            lane = pl.multiple_of((parts + 1) * tile + at * each, each)
            out_ref[:, pl.ds(lane, each)] = ins[k][:, tile + each :]

    vmem = pl.BlockSpec(memory_space=pltpu.VMEM)
    return pl.pallas_call(
        kernel,
        out_shape=jax.ShapeDtypeStruct((tokens, (parts + 2) * tile), BF),
        in_specs=[smem()] + [vmem] * (parts + 2),
        out_specs=vmem,
        compiler_params=params(),
        cost_estimate=cost(0, 6 * 2**20),
        name="unpack",
    )(seq.reshape(1), *packs, cos_table, sin_table)


def inner_back(z, grad_qkv, groups, inputs, gain, grad_res):
    tokens, width = inputs.shape
    count = len(groups)
    depth = width // count

    def kernel(at_ref, gq_ref, *refs):
        w_refs, (in_ref, gain_ref, gr_ref, out_ref, gg_ref, grad_s) = refs[:count], refs[count:]
        for j in range(count):
            lanes = pl.ds(pl.multiple_of((at_ref[0] + count - j) % count * depth, depth), depth)
            grad_s[:, lanes] = dot_nt(gq_ref[...], w_refs[j][...])
        grad = grad_s[...]
        values = in_ref[...].astype(F32)
        scale = lax.rsqrt(jnp.mean(values * values, axis=-1, keepdims=True) + EPSILON)
        weighted = grad * gain_ref[...]
        inner = jnp.mean(weighted * values, axis=-1, keepdims=True)
        result = gr_ref[...] + scale * weighted - values * (scale**3 * inner)
        out_ref[...] = result.astype(BF)
        gg_ref[...] = jnp.sum(grad * values * scale, axis=0, keepdims=True)

    vmem = pl.BlockSpec(memory_space=pltpu.VMEM)
    return pl.pallas_call(
        kernel,
        out_shape=[jax.ShapeDtypeStruct((tokens, width), BF), jax.ShapeDtypeStruct((1, width), F32)],
        in_specs=[smem()] + [vmem] * (4 + count),
        out_specs=[vmem] * 2,
        scratch_shapes=[pltpu.VMEM((tokens, width), F32)],
        compiler_params=params(),
        cost_estimate=cost(2 * tokens * groups[0].size * count, 2 * groups[0].size * count),
        name="inner_back",
    )(z.reshape(1), grad_qkv, *groups, inputs, gain, grad_res)


def weight_grad(left, right, rows, blocks, half, adds=()):
    count = len(left)
    tokens = left[0].shape[0]
    width = right[0].shape[1] // 2
    tile = min(rows, 512)
    steps = rows // tile
    total_rows = rows * len(blocks)

    def kernel(at_ref, *refs):
        lefts, rights, extra, out = refs[:count], refs[count : 2 * count], refs[2 * count : -1], refs[-1]
        total = None
        for l_ref, r_ref in zip(lefts, rights):
            term = lax.dot_general(
                l_ref[...], r_ref[...], (((0,), (0,)), ((), ())), preferred_element_type=F32
            )
            total = term if total is None else total + term
        for ref in extra:
            total = total + ref[...].astype(F32)
        out[...] = total.astype(BF)

    rows_spec = pl.BlockSpec((tile, width), lambda n, at: (n, 0))
    spec = pltpu.PrefetchScalarGridSpec(
        num_scalar_prefetch=1,
        grid=(steps * len(blocks),),
        in_specs=[pl.BlockSpec((tokens, tile), lambda n, at: (0, at[1 + n]))] * count
        + [pl.BlockSpec((tokens, width), lambda n, at: (0, at[0]))] * count
        + [rows_spec] * len(adds),
        out_specs=rows_spec,
    )
    at = [jnp.int32(half)]
    for block in blocks:
        at += [jnp.int32(block) * steps + i for i in range(steps)]
    return pl.pallas_call(
        kernel,
        grid_spec=spec,
        out_shape=jax.ShapeDtypeStruct((total_rows, width), BF),
        compiler_params=params(),
        cost_estimate=cost(
            2 * tokens * count * total_rows * width, 2 * (tokens * count + total_rows) * width
        ),
        name="weight_grad",
    )(jnp.stack(at), *left, *right, *adds)


def row_grads(left, right, blocks, half, added, y, cuts):
    tokens = left.shape[0]
    width = right.shape[1] // 2
    rows = left.shape[1] // LINE
    each = rows // cuts
    count = len(blocks)

    def kernel(at_ref, l_ref, r_ref, add_ref, *refs):
        outs, total_s = refs[:-1], refs[-1]
        total = lax.dot_general(
            l_ref[...], r_ref[...], (((0,), (0,)), ((), ())), preferred_element_type=F32
        )
        total_s[...] = (total + add_ref[...].astype(F32)).astype(BF)
        for j in range(count):

            @pl.when(pl.program_id(0) == j)
            def _():
                for k in range(cuts):
                    start = pl.multiple_of((at_ref[1] + cuts - k) % cuts * each, each)
                    outs[j * cuts + k][...] = total_s[pl.ds(start, each), :]

    spec = pltpu.PrefetchScalarGridSpec(
        num_scalar_prefetch=1,
        grid=(count,),
        in_specs=[
            pl.BlockSpec((tokens, rows), lambda n, at: (0, at[2 + n])),
            pl.BlockSpec((tokens, width), lambda n, at: (0, at[0])),
            pl.BlockSpec((rows, width), lambda n, at: (n, 0)),
        ],
        out_specs=[pl.BlockSpec((each, width), lambda n, at: (0, 0))] * (count * cuts),
        scratch_shapes=[pltpu.VMEM((rows, width), BF)],
    )
    at = jnp.stack([jnp.int32(half), jnp.int32(y)] + [jnp.int32(b) for b in blocks])
    outs = pl.pallas_call(
        kernel,
        grid_spec=spec,
        out_shape=[jax.ShapeDtypeStruct((each, width), BF)] * (count * cuts),
        compiler_params=params(),
        cost_estimate=cost(2 * tokens * count * rows * width, 6 * count * rows * width),
        name="row_grads",
    )(at, left, right, added)
    return [outs[j * cuts : (j + 1) * cuts] for j in range(count)]


def join(core, mine, other, widths):
    rows, half = mine.shape
    tile = min(rows, 256)

    def kernel(core_ref, mine_ref, other_ref, *refs):
        outs, full = refs[:-1], refs[-1]
        target = outs[0] if len(outs) == 1 else full
        at = pl.multiple_of(core_ref[0] * half, half)
        target[:, pl.ds(at, half)] = mine_ref[...].astype(F32)
        at = pl.multiple_of((1 - core_ref[0]) * half, half)
        target[:, pl.ds(at, half)] = other_ref[...].astype(F32)
        if len(outs) > 1:
            lane = 0
            for out in outs:
                out[...] = full[:, lane : lane + out.shape[1]]
                lane += out.shape[1]

    def block(width):
        return pl.BlockSpec((tile, width), lambda n: (n, 0))

    return pl.pallas_call(
        kernel,
        grid=(rows // tile,),
        out_shape=[jax.ShapeDtypeStruct((rows, width), F32) for width in widths],
        in_specs=[smem(), block(half), block(half)],
        out_specs=[block(width) for width in widths],
        scratch_shapes=[pltpu.VMEM((tile, 2 * half) if len(widths) > 1 else (8, 128), F32)],
        compiler_params=params(),
        cost_estimate=cost(0, rows * half * 12),
        name="join",
    )(core.reshape(1), mine, other)
def half_of(array, which, axis=1):
    size = array.shape[axis] // 2
    return lax.dynamic_slice_in_dim(array, which * size, size, axis)


def join_halves(core, top, bottom):
    rows, half = top[0].shape
    tile = min(rows, 256)
    steps = rows // tile

    def kernel(core_ref, a_ref, b_ref, c_ref, d_ref, out):
        mine = pl.multiple_of(core_ref[0] * half, half)
        other = pl.multiple_of((1 - core_ref[0]) * half, half)
        upper = pl.program_id(0) < steps

        @pl.when(upper)
        def _():
            out[:, pl.ds(mine, half)] = a_ref[...].astype(F32)
            out[:, pl.ds(other, half)] = b_ref[...].astype(F32)

        @pl.when(jnp.logical_not(upper))
        def _():
            out[:, pl.ds(mine, half)] = c_ref[...].astype(F32)
            out[:, pl.ds(other, half)] = d_ref[...].astype(F32)

    first = pl.BlockSpec((tile, half), lambda n: (jnp.minimum(n, steps - 1), 0))
    second = pl.BlockSpec((tile, half), lambda n: (jnp.maximum(n - steps, 0), 0))
    return pl.pallas_call(
        kernel,
        grid=(2 * steps,),
        out_shape=jax.ShapeDtypeStruct((2 * rows, 2 * half), F32),
        in_specs=[smem(), first, first, second, second],
        out_specs=pl.BlockSpec((tile, 2 * half), lambda n: (n, 0)),
        compiler_params=params(),
        cost_estimate=cost(0, rows * half * 24),
        name="join_halves",
    )(core.reshape(1), *top, *bottom)


class Order:
    def __init__(self):
        self.marks = ()

    def tie(self, *values):
        if self.marks:
            values = lax.optimization_barrier(tuple(values) + self.marks)[: len(values)]
        return values[0] if len(values) == 1 else list(values)

    def done(self, *values):
        self.marks = tuple(values)


def y_hops(value):
    return ring_gather(value, y_next, columns())[1:]


def add_low(left, right):
    return (left.astype(F32) + right.astype(F32)).astype(BF)


def finish_sum(low, core, widths):
    total = add_low(low, x_swap(low))
    return join(core, total, core_swap(total), widths)


def rope_tables(positions, repeat):
    frequency = THETA ** (-(jnp.arange(HD // 2, dtype=F32) * 2.0) / HD)
    angles = positions.astype(F32)[:, None] * frequency[None, :]
    cos, sin = jnp.cos(angles), jnp.sin(angles)
    return (
        jnp.tile(jnp.concatenate([cos, cos], axis=1), (1, repeat)),
        jnp.tile(jnp.concatenate([-sin, sin], axis=1), (1, repeat)),
    )


def exchange(packs):
    return [packs[0]] + [seq_swap(packs[k], k) for k in range(1, len(packs))]


def shards(
    inputs,
    query_weight,
    key_weight,
    value_weight,
    output_weight,
    gate_weight,
    up_weight,
    down_weight,
    gain_attn,
    gain_ffn,
    cotangent,
):
    seq_count, local_len, width = inputs.shape
    assert seq_count == 1
    tokens = local_len
    parts = lax.axis_size("seq")
    kv_local = KVH // parts
    cols = columns()
    seq = lax.axis_index("seq")
    core, side = seq % 2, seq // 2
    fsdp = lax.axis_index("fsdp")
    z, y = fsdp // cols, fsdp % cols
    q_width, kv_width = query_weight.shape[1], key_weight.shape[1]
    heads_local = q_width // HD // parts
    flat_in = inputs.reshape(tokens, width)
    grad_out = cotangent.reshape(tokens, width)

    qkv_shard = jnp.concatenate([query_weight, key_weight, value_weight], axis=1)
    rows = qkv_shard.shape[0]
    part, half = rows // 2, qkv_shard.shape[1] // 2
    positions = seq * local_len + jnp.arange(local_len)
    cos_table, sin_table = rope_tables(positions, kv_width // HD)
    order = Order()

    def swapped(pieces):
        return [core_swap(p) for p in pieces]

    def place_halves(pieces, others, whole_first=None):
        each = pieces[-1].shape[1]
        placed, offsets = [], []
        for k, (piece, other) in enumerate(zip(pieces, others)):
            row = (y - k) % cols * rows
            if k == 0 and whole_first is not None:
                placed.append(whole_first)
                offsets.append((row, 0))
            else:
                placed += [piece, other]
                offsets += [(row, core * each), (row, (1 - core) * each)]
        return place((rows * cols, 2 * each), placed, offsets)

    def place_quarters(pieces, others, sides, count, size, first):
        each = pieces[0].shape[1]
        placed, offsets = [], []
        for i, (piece, other) in enumerate(zip(pieces, others)):
            k, at = i // 2, sides[i % 2]
            row = first(k) * size + at * (size // 2)
            placed += [piece, other]
            offsets += [(row, core * each), (row, (1 - core) * each)]
        return place((size * count, 2 * each), placed, offsets)

    def line_row(k):
        return (y - k) % cols

    own = (gate_weight, up_weight, down_weight)
    far_rows = gate_weight.shape[0]
    far_part = far_rows // 4
    far_y, far_x = {}, {}

    def far_start(i, h):
        at = side * 2 * far_part + h * far_part
        return lax.dynamic_slice(own[i], (at, core * out_width), (far_part, out_width))

    out_width = width // 2
    far_starts = {(i, h): far_start(i, h) for i in range(3) for h in range(2)}

    def far_along_y(i, h):
        start = order.tie(far_starts[i, h]) if order.marks else far_starts[i, h]
        far_y[i, h] = y_hops(start)
        return far_y[i, h]

    def far_along_x(i, h):
        pieces = order.tie(*far_y[i, h], far_y[i, h][0])[:-1]
        far_x[i, h] = [x_swap(p) for p in pieces]
        return far_x[i, h]

    gains = jnp.concatenate([gain_attn, gain_ffn]).reshape(1, 2 * rows)
    start = half_of(qkv_shard, core)
    start = jnp.concatenate([start, jnp.pad(gains, ((0, 15), (0, half - 2 * rows)))], axis=0)
    out_half = half_of(output_weight, core)

    def quarter_of(piece):
        return lax.dynamic_slice_in_dim(piece, side * part, part, 0)

    def line_group(i):
        here = order.tie(line[i])
        placed, offsets = [], []
        row = y * rows
        if i:
            placed += [here[:rows], core_swap(here[:rows])]
            offsets += [(row, core * half), (row, (1 - core) * half)]
        else:
            placed.append(qkv_shard)
            offsets.append((row, 0))
        for k in range(1, cols):
            row = (y - k) % cols * rows
            if i < LINE - 1:
                for piece, at in ((beside[i][k - 1], side), (crossed[i][k - 1], 1 - side)):
                    piece = order.tie(piece)
                    placed += [piece, core_swap(piece)]
                    offsets += [
                        (row + at * part, core * half),
                        (row + at * part, (1 - core) * half),
                    ]
            else:
                piece = order.tie(beside[i][k - 1])
                placed += [piece, core_swap(piece)]
                offsets += [(row, core * half), (row, (1 - core) * half)]
        return place((rows * cols, 2 * half), placed, offsets)

    line, beside, crossed, groups = [start], [], [], []
    for j in range(LINE):
        here = order.tie(line[j]) if j else line[j]
        if j + 1 < LINE:
            line.append(z_next(here))
            beside.append(y_hops(quarter_of(here)))
            marks = [line[j + 1]] + beside[j] + far_along_y(j // 2, j % 2)
        else:
            beside.append(y_hops(here[:rows]))
            line_o = [out_half, z_next(order.tie(out_half))]
            gains_near = jnp.concatenate([p[rows:, : 2 * rows] for p in line], axis=0)
            gains_far = y_hops(order.tie(gains_near))
            marks = beside[j] + [line_o[1]]
        if j:
            pieces = order.tie(*beside[j - 1], here)[:-1]
            crossed.append([x_swap(p) for p in pieces])
            marks += crossed[j - 1]
        if j > 1:
            marks += far_along_x(0, j - 2)
            groups.append(line_group(j - 2))
            marks.append(groups[-1])
        order.done(*marks)

    line_o.append(z_next(order.tie(line_o[1])))
    grad_parts = [grad_out, z_next(order.tie(grad_out))]
    beside_o = [y_hops(order.tie(line_o[0])), y_hops(order.tie(line_o[1]))]
    groups += [line_group(LINE - 2), line_group(LINE - 1)]
    marks = far_along_x(1, 0)
    gain_full = jnp.zeros((2, width), BF)
    for j in range(LINE):
        for k, g in enumerate([gains_near] + gains_far):
            at = (((z - j) % LINE) * cols + (y - k) % cols) * rows
            pair = g[16 * j].reshape(2, rows)
            gain_full = lax.dynamic_update_slice(gain_full, pair, (0, at))
    gain_one = gain_full[:1].astype(F32)
    gain_two = gain_full[1:].astype(F32)
    acts_one, *sent = project_in(seq, z, flat_in, gain_one, groups, cos_table, sin_table, parts)
    order.done(*sent, line_o[2], *beside_o[0], *marks)

    def out_group(j):
        hops = order.tie(line_o[j], *beside_o[j])
        if j == 0:
            return place_halves([None] + hops[1:], [None] + swapped(hops[1:]), output_weight)
        return place_halves(hops, swapped(hops))

    packs = exchange(order.tie(*sent))
    line_o.append(z_next(order.tie(line_o[2])))
    order.done(*packs, line_o[3], *beside_o[1], grad_parts[1])

    beside_o += [y_hops(order.tie(line_o[2])), y_hops(order.tie(line_o[3]))]
    grad_parts.append(z_next(order.tie(grad_parts[1])))
    out_groups = [out_group(0), out_group(1)]
    *mixed_sent, log_totals = attend_forward(seq, order.tie(*packs), heads_local, kv_local)
    order.done(*mixed_sent, *beside_o[2], *beside_o[3], grad_parts[2], *out_groups)

    mixed = exchange(order.tie(*mixed_sent))
    grad_parts.append(z_next(order.tie(grad_parts[2])))
    out_groups += [out_group(2), out_group(3)]
    order.done(*mixed, *out_groups)

    marks = far_along_y(1, 1)
    mixed_flat, residual, acts_two = project_out(
        seq, z, order.tie(*mixed), flat_in, gain_two, out_groups
    )
    order.done(acts_two, grad_parts[3], *marks)

    def far_place(i):
        placed, offsets = [], []
        for k in range(cols - 1):
            for h in range(2):
                pieces = order.tie(far_y[i, h][k], far_x[i, h][k])
                for piece, at in zip(pieces, (side, 1 - side)):
                    row = k * far_rows + at * 2 * far_part + h * far_part
                    placed += [piece, core_swap(piece)]
                    offsets += [(row, core * out_width), (row, (1 - core) * out_width)]
        return place((far_rows * (cols - 1), width), placed, offsets)

    acts_parts, far, near_done, far_done = [acts_two], [], [], [None] * LINE

    def run_near(j):
        near_done.append(feed_forward(order.tie(acts_parts[j]), grad_parts[j], *own))
        return near_done[j][3]

    def run_far(j):
        far_done[j] = feed_forward(order.tie(acts_parts[j]), grad_parts[j], *far, near_done[j][3:])
        return far_done[j][4]

    acts_parts.append(z_next(order.tie(acts_parts[0])))
    marks = far_along_y(2, 0) + far_along_y(2, 1) + far_along_x(1, 1)
    far.append(far_place(0))
    order.done(acts_parts[1], *marks, *far, run_near(0))
    acts_parts.append(z_next(order.tie(acts_parts[1])))
    marks = far_along_x(2, 0) + far_along_x(2, 1)
    far.append(far_place(1))
    order.done(acts_parts[2], *marks, *far, run_near(1))
    acts_parts.append(z_next(order.tie(acts_parts[2])))
    far.append(far_place(2))
    marks = [run_near(2), run_far(1)]
    order.done(acts_parts[3], *marks)

    passed = z_next(order.tie(far_done[1][4]))
    marks = [run_near(3), run_far(2)]
    order.done(passed, *marks)
    passed = z_next(order.tie(add_low(passed, far_done[2][4])))
    marks = [run_far(3), run_far(0)]
    order.done(passed, *marks)
    passed = z_next(order.tie(add_low(passed, far_done[3][4])))

    rights = (grad_parts, acts_parts, acts_parts)
    far_size = far_rows * (cols - 1)
    far_sent, far_total, own_sent = [None] * 3, {}, [None] * 3

    def of(done, which):
        return order.tie(*[d[which] for d in done])

    def send_far(i):
        far_sent[i] = weight_grad(of(far_done, i), rights[i], far_size, [0], 1 - core)
        return far_sent[i]

    def keep_far(i):
        return weight_grad(of(far_done, i), rights[i], far_size, [0], core, [far_sent[i]])

    def pass_far(i, kept, h):
        size = far_rows // 2
        kept = order.tie(kept)
        total = y_next(kept[h * size : (h + 1) * size])
        for k in range(1, cols - 1):
            start = k * far_rows + h * size
            total = y_next(add_low(total, kept[start : start + size]))
        far_total[i, h] = total
        return total

    def send_own(i):
        own_sent[i] = weight_grad(of(near_done, i), rights[i], far_rows, [0], 1 - core)
        return own_sent[i]

    def keep_own(i):
        return weight_grad(of(near_done, i), rights[i], far_rows, [0], core, [own_sent[i]])

    marks = [send_far(0), send_far(1), send_far(2), send_own(0)]
    order.done(passed, *marks)

    far_sent = [core_swap(order.tie(term)) for term in far_sent]
    ffn_parts = [d[3] for d in far_done]
    ffn_sum = z_next(order.tie(ffn_parts[1]))
    grad_res, grad_res_low, grad_gain_two, *grad_sent = middle_back(
        seq, z, order.tie(passed, far_done[0][4]), residual, grad_out, gain_two, out_groups, parts
    )
    order.done(*grad_sent, *far_sent)

    grad_packs = exchange(order.tie(*grad_sent))
    kept = [keep_far(0), keep_far(1)]
    order.done(*grad_packs, ffn_sum, *kept)

    marks = [pass_far(0, kept[0], 0)]
    ffn_sum = z_next(order.tie(add_low(ffn_sum, ffn_parts[2])))
    back_sent = attend_backward(
        seq, log_totals, packs, order.tie(*grad_packs), heads_local, kv_local
    )
    order.done(*back_sent, *marks)

    back_packs = exchange(order.tie(*back_sent))
    own_sent[0] = core_swap(order.tie(own_sent[0]))
    marks = [pass_far(0, kept[0], 1), keep_far(2), send_own(1), keep_own(0)]
    own_low = [marks[3]]
    kept.append(marks[1])
    order.done(*back_packs, *marks, ffn_sum)

    size = far_rows // 2
    sums = {}

    def along_x(i, h):
        low = add_low(order.tie(own_low[i])[h * size : (h + 1) * size], far_total[i, h])
        return low, x_swap(low)

    def finish(i, h):
        low, crossed = order.tie(*sums[i, h])
        total = add_low(low, crossed)
        sums[i, h] = (total, core_swap(total))
        return sums[i, h][1]

    marks = [pass_far(1, kept[1], 0)]
    sums[0, 0] = along_x(0, 0)
    ffn_sum = z_next(order.tie(add_low(ffn_sum, ffn_parts[3])))
    grad_qkv = unpack(seq, order.tie(*back_packs), cos_table, sin_table)
    line_order = list(range(1, LINE)) + [0]
    blocks = [(z - j) % LINE for j in line_order]
    line_rows = rows * cols
    qkv_sent = weight_grad([acts_one], [grad_qkv], line_rows, blocks, 1 - core)
    out_left, out_right = order.tie(mixed_flat, grad_res_low)
    out_sent = weight_grad([out_left], [out_right], line_rows, blocks, 1 - core)
    order.done(qkv_sent, out_sent, sums[0, 0][1], *marks)

    qkv_recv = core_swap(order.tie(qkv_sent))
    own_sent[1] = core_swap(order.tie(own_sent[1]))
    marks = [pass_far(1, kept[1], 1), send_own(2)]
    sums[0, 1] = along_x(0, 1)
    own_low.append(keep_own(1))
    marks += [own_low[1], sums[0, 1][1], finish(0, 0)]
    order.done(qkv_recv, ffn_sum, *marks)

    qkv_terms = row_grads(acts_one, grad_qkv, blocks, core, order.tie(qkv_recv), y, cols)
    out_recv = core_swap(order.tie(out_sent))
    own_sent[2] = core_swap(order.tie(own_sent[2]))
    own_low.append(keep_own(2))
    marks = [pass_far(2, kept[2], 0), own_low[2], finish(0, 1)]
    sums[1, 0] = along_x(1, 0)
    order.done(*[t for terms in qkv_terms for t in terms], out_recv, sums[1, 0][1], *marks)

    def along_y(terms):
        terms = order.tie(*terms, terms[0])[:-1]
        total = None
        for k in list(range(1, cols)) + [0]:
            total = terms[k] if total is None else add_low(y_next(total), terms[k])
        return total

    hops = [along_y(qkv_terms[0])]
    sums[1, 1] = along_x(1, 1)
    out_terms = row_grads(mixed_flat, grad_res_low, blocks, core, order.tie(out_recv), y, 1)
    grad_inputs, grad_gain_one = inner_back(z, order.tie(grad_qkv), groups, flat_in, gain_one, grad_res)
    order.done(hops[0], sums[1, 1][1], finish(1, 0), *[t[0] for t in out_terms])
    passed = z_next(order.tie(hops[0]))
    out_total = z_next(order.tie(out_terms[0][0]))
    hops.append(along_y(qkv_terms[1]))
    sums[2, 0] = along_x(2, 0)
    order.done(passed, hops[1], out_total, sums[2, 0][1], finish(1, 1))
    passed = z_next(order.tie(add_low(passed, hops[1])))
    out_total = z_next(order.tie(add_low(out_total, out_terms[1][0])))
    hops.append(along_y(qkv_terms[2]))
    marks = [pass_far(2, kept[2], 1)]
    order.done(passed, hops[2], out_total, finish(2, 0), *marks)
    passed = z_next(order.tie(add_low(passed, hops[2])))
    out_total = z_next(order.tie(add_low(out_total, out_terms[2][0])))
    hops.append(along_y(qkv_terms[3]))
    sums[2, 1] = along_x(2, 1)
    order.done(passed, hops[3], out_total, sums[2, 1][1])
    d_qkv = finish_sum(order.tie(add_low(passed, hops[3])), core, [q_width, kv_width, kv_width])
    out_total = order.tie(add_low(out_total, out_terms[3][0]))
    finish(2, 1)
    pieces = [
        lax.dynamic_slice_in_dim(out_total, (y - k) % cols * rows, rows, 0) for k in range(cols)
    ]
    total = None
    for k in list(range(1, cols)) + [0]:
        total = pieces[k] if total is None else add_low(y_next(total), pieces[k])
    d_out = finish_sum(total, core, [width])
    d_down, d_gate, d_up = [join_halves(core, sums[i, 0], sums[i, 1]) for i in range(3)]

    outputs = (residual + ffn_sum.astype(F32) + ffn_parts[0].astype(F32)).astype(BF)
    gain_sums = all_sum(jnp.concatenate([grad_gain_one, grad_gain_two], axis=0))
    gain_sums = lax.dynamic_slice_in_dim(gain_sums, fsdp * rows, rows, 1)
    return (
        outputs.reshape(inputs.shape),
        grad_inputs.reshape(inputs.shape),
        d_qkv[0],
        d_qkv[1],
        d_qkv[2],
        d_out[0],
        d_gate,
        d_up,
        d_down,
        gain_sums[0],
        gain_sums[1],
    )


def solution(mesh):
    token_spec, row_spec, gain_spec = P("fsdp", "seq", None), P("fsdp", None), P("fsdp")
    return jax.shard_map(
        shards,
        mesh=mesh,
        in_specs=(token_spec,) + (row_spec,) * 7 + (gain_spec,) * 2 + (token_spec,),
        out_specs=(token_spec,) * 2 + (row_spec,) * 7 + (gain_spec,) * 2,
        check_vma=False,
    )
```

```python
import functools

import jax
import jax.numpy as jnp
from jax import lax
from jax.experimental import pallas as pl
from jax.experimental.pallas import tpu as pltpu
from jax.sharding import PartitionSpec as P

KVH = 8
HD = 64
BLOCK = 256
LINE = 4

EPSILON = 1e-05
THETA = 500000.0
LOG2E = 1.4426950408889634

BF = jnp.bfloat16
F32 = jnp.float32


def after(value, *others):
    return lax.optimization_barrier((value,) + others)[0]


def columns():
    return lax.axis_size("fsdp") // LINE


def z_next(value):
    cols = columns()
    count = lax.axis_size("fsdp")
    return lax.ppermute(value, "fsdp", [(i, (i + cols) % count) for i in range(count)])


def y_next(value):
    cols = columns()
    count = lax.axis_size("fsdp")
    return lax.ppermute(
        value, "fsdp", [(i, i // cols * cols + (i + 1) % cols) for i in range(count)]
    )


def seq_swap(value, bit):
    return lax.ppermute(value, "seq", [(i, i ^ bit) for i in range(lax.axis_size("seq"))])


def core_swap(value):
    return seq_swap(value, 1)


def x_swap(value):
    return seq_swap(value, 2)


def ring_gather(value, step, count):
    pieces = [value]
    for _ in range(count - 1):
        pieces.append(step(pieces[-1]))
    return pieces


def ring_scatter(part_of, step, count):
    total = None
    for j in list(range(1, count)) + [0]:
        total = part_of(j) if total is None else part_of(j) + total.astype(F32)
        if j:
            total = step(total.astype(BF))
    return total


def sum_steps():
    steps = []
    bit = 1
    while bit < lax.axis_size("seq"):
        steps.append(functools.partial(seq_swap, bit=bit))
        bit *= 2
    count = lax.axis_size("fsdp")
    bit = 1
    while bit < count:
        pairs = [(i, i ^ bit) for i in range(count)]
        steps.append(functools.partial(lax.ppermute, axis_name="fsdp", perm=pairs))
        bit *= 2
    return steps


def dot_nt(a, b):
    return lax.dot_general(a, b, (((1,), (1,)), ((), ())), preferred_element_type=F32)

def dot_nn(a, b):
    return jnp.dot(a, b, preferred_element_type=F32)


def attend_forward_kernel(parts, heads, kv, seq_ref, *refs):
    packs, outs = refs[:parts], refs[parts : 2 * parts]
    lse_ref, q_s, k_s, vt_s, o_s = refs[2 * parts :]
    tokens = packs[0].shape[0]
    seq = seq_ref[0]
    group = heads // kv
    for k in range(parts):
        rows = pl.ds(pl.multiple_of((seq ^ k) * tokens, tokens), tokens)
        q_s[rows, :] = packs[k][:, : heads * HD]
        for g in range(kv):
            lane = (heads + g) * HD
            k_s[g, rows, :] = packs[k][:, lane : lane + HD]
            lane = (heads + kv + g) * HD
            vt_s[g, :, rows] = packs[k][:, lane : lane + HD].T
    full = parts * tokens
    for g in range(kv):
        for i in range(full // BLOCK):
            keys = (i + 1) * BLOCK
            rows = slice(i * BLOCK, keys)
            for pair in range(group // 2):
                halves = []
                for h in (g * group + 2 * pair, g * group + 2 * pair + 1):
                    scores = dot_nt(k_s[g, :keys, :], q_s[rows, h * HD : (h + 1) * HD])
                    scores = scores * (HD**-0.5 * LOG2E)
                    top = jnp.max(scores, axis=0, keepdims=True)
                    powers = jnp.exp2(scores - top)
                    total = jnp.sum(powers, axis=0, keepdims=True)
                    halves.append(dot_nn(vt_s[g, :, :keys], powers.astype(BF)) / total)
                    lse_ref[h : h + 1, rows] = top + jnp.log2(total)
                lane = (g * group + 2 * pair) * HD
                o_s[rows, lane : lane + 2 * HD] = jnp.concatenate(halves, axis=0).T.astype(BF)
    for k in range(parts):
        rows = pl.ds(pl.multiple_of((seq ^ k) * tokens, tokens), tokens)
        outs[k][...] = o_s[rows, :]


def attend_forward(seq, packs, heads, kv):
    parts = len(packs)
    tokens = packs[0].shape[0]
    full = parts * tokens
    vmem = pl.BlockSpec(memory_space=pltpu.VMEM)
    flops = 4 * heads * full * full * HD * 5 // 8
    return pl.pallas_call(
        functools.partial(attend_forward_kernel, parts, heads, kv),
        out_shape=[jax.ShapeDtypeStruct((tokens, heads * HD), BF)] * parts
        + [jax.ShapeDtypeStruct((heads, full), F32)],
        in_specs=[pl.BlockSpec(memory_space=pltpu.SMEM)] + [vmem] * parts,
        out_specs=[vmem] * (parts + 1),
        scratch_shapes=[
            pltpu.VMEM((full, heads * HD), BF),
            pltpu.VMEM((kv, full, HD), BF),
            pltpu.VMEM((kv, HD, full), BF),
            pltpu.VMEM((full, heads * HD), BF),
        ],
        compiler_params=pltpu.CompilerParams(vmem_limit_bytes=48 * 2**20),
        cost_estimate=cost(flops * 4, 4 * 2**20),
        name="attend_forward",
    )(seq.reshape(1), *packs)


def attend_backward_kernel(parts, heads, kv, seq_ref, lse_ref, *refs):
    packs, grads, outs = refs[:parts], refs[parts : 2 * parts], refs[2 * parts : 3 * parts]
    q_s, k_s, kt_s, v_s, g_s, dq_s, dk_s, dv_s = refs[3 * parts :]
    tokens = packs[0].shape[0]
    seq = seq_ref[0]
    group = heads // kv
    for k in range(parts):
        rows = pl.ds(pl.multiple_of((seq ^ k) * tokens, tokens), tokens)
        q_s[rows, :] = packs[k][:, : heads * HD]
        g_s[rows, :] = grads[k][...]
        for g in range(kv):
            lane = (heads + g) * HD
            k_s[g, rows, :] = packs[k][:, lane : lane + HD]
            kt_s[g, :, rows] = packs[k][:, lane : lane + HD].T
            lane = (heads + kv + g) * HD
            v_s[g, rows, :] = packs[k][:, lane : lane + HD]
    full = parts * tokens
    dk_s[...] = jnp.zeros_like(dk_s)
    dv_s[...] = jnp.zeros_like(dv_s)
    for g in range(kv):
        for i in range(full // BLOCK):
            keys = (i + 1) * BLOCK
            rows = slice(i * BLOCK, keys)
            for pair in range(group // 2):
                halves = []
                for h in (g * group + 2 * pair, g * group + 2 * pair + 1):
                    query = q_s[rows, h * HD : (h + 1) * HD]
                    grad = g_s[rows, h * HD : (h + 1) * HD]
                    scores = dot_nt(k_s[g, :keys, :], query) * (HD**-0.5 * LOG2E)
                    probs = jnp.exp2(scores - lse_ref[h : h + 1, rows])
                    grad_probs = dot_nt(v_s[g, :keys, :], grad)
                    inner = jnp.sum(probs * grad_probs, axis=0, keepdims=True)
                    grad_scores = (probs * (grad_probs - inner)).astype(BF)
                    dv_s[g, :keys, :] += dot_nn(probs.astype(BF), grad)
                    dk_s[g, :keys, :] += dot_nn(grad_scores, query)
                    halves.append(dot_nn(kt_s[g, :, :keys], grad_scores) * HD**-0.5)
                lane = (g * group + 2 * pair) * HD
                dq_s[rows, lane : lane + 2 * HD] = jnp.concatenate(halves, axis=0).T.astype(BF)
    for k in range(parts):
        rows = pl.ds(pl.multiple_of((seq ^ k) * tokens, tokens), tokens)
        outs[k][:, : heads * HD] = dq_s[rows, :]
        for g in range(kv):
            lane = (heads + g) * HD
            outs[k][:, lane : lane + HD] = (dk_s[g, rows, :] * HD**-0.5).astype(BF)
            lane = (heads + kv + g) * HD
            outs[k][:, lane : lane + HD] = dv_s[g, rows, :].astype(BF)


def attend_backward(seq, lse, packs, grads, heads, kv):
    parts = len(packs)
    tokens = packs[0].shape[0]
    full = parts * tokens
    vmem = pl.BlockSpec(memory_space=pltpu.VMEM)
    flops = 10 * heads * full * full * HD * 5 // 8
    return pl.pallas_call(
        functools.partial(attend_backward_kernel, parts, heads, kv),
        out_shape=[jax.ShapeDtypeStruct(packs[0].shape, BF)] * parts,
        in_specs=[pl.BlockSpec(memory_space=pltpu.SMEM)] + [vmem] * (2 * parts + 1),
        out_specs=[vmem] * parts,
        scratch_shapes=[
            pltpu.VMEM((full, heads * HD), BF),
            pltpu.VMEM((kv, full, HD), BF),
            pltpu.VMEM((kv, HD, full), BF),
            pltpu.VMEM((kv, full, HD), BF),
            pltpu.VMEM((full, heads * HD), BF),
            pltpu.VMEM((full, heads * HD), BF),
            pltpu.VMEM((kv, full, HD), F32),
            pltpu.VMEM((kv, full, HD), F32),
        ],
        compiler_params=pltpu.CompilerParams(vmem_limit_bytes=48 * 2**20),
        cost_estimate=cost(flops * 4, 8 * 2**20),
        name="attend_backward",
    )(seq.reshape(1), lse, *packs, *grads)


def smem():
    return pl.BlockSpec(memory_space=pltpu.SMEM)


def params(mib=56):
    return pltpu.CompilerParams(vmem_limit_bytes=mib * 2**20)


def cost(flops, moved):
    return pl.CostEstimate(flops=flops // 8, bytes_accessed=moved // 8, transcendentals=0)


def place(shape, pieces, offsets, most=None):
    count = len(pieces)

    def kernel(at_ref, *refs):
        sources, target, sems = refs[:-2], refs[-2], refs[-1]
        copies = []
        for i, source in enumerate(sources):
            rows, width = source.shape
            rows = min(rows, most or rows)
            row = pl.multiple_of(at_ref[2 * i], rows)
            column = pl.multiple_of(at_ref[2 * i + 1], width)
            spot = target.at[pl.ds(row, rows), pl.ds(column, width)]
            copies.append(pltpu.make_async_copy(source.at[pl.ds(0, rows), :], spot, sems.at[i]))
            copies[-1].start()
        for copy in copies:
            copy.wait()

    moved = 2 * sum(piece.size * 2 for piece in pieces)
    return pl.pallas_call(
        kernel,
        out_shape=jax.ShapeDtypeStruct(shape, pieces[0].dtype),
        in_specs=[smem()] + [pl.BlockSpec(memory_space=pl.ANY)] * count,
        out_specs=pl.BlockSpec(memory_space=pltpu.HBM),
        scratch_shapes=[pltpu.SemaphoreType.DMA((count,))],
        compiler_params=params(16),
        cost_estimate=cost(0, moved),
        name="place",
    )(jnp.stack([jnp.int32(v) for pair in offsets for v in pair]), *pieces)


def turn(values, cos_table, sin_table):
    width = values.shape[1]
    lane = lax.broadcasted_iota(jnp.int32, values.shape, 1)
    swapped = jnp.where(
        lane % HD < HD // 2,
        pltpu.roll(values, width - HD // 2, 1),
        pltpu.roll(values, HD // 2, 1),
    )
    return values * cos_table + swapped * sin_table


def whole(shape):
    return pl.BlockSpec(shape, lambda n: (0,) * len(shape))


def project_in(seq, z, inputs, gain, groups, cos_table, sin_table, parts):
    tokens, width = inputs.shape
    tile = cos_table.shape[1]
    each = tile // parts
    pack = tile + 2 * each
    count = len(groups)
    depth = width // count

    def kernel(at_ref, in_ref, gain_ref, *refs):
        w_refs, (cos_ref, sin_ref, acts_ref), packs = refs[:count], refs[count : count + 3], refs[count + 3 :]
        step = pl.program_id(0)

        @pl.when(step == 0)
        def _():
            values = in_ref[...].astype(F32)
            scale = lax.rsqrt(jnp.mean(values * values, axis=-1, keepdims=True) + EPSILON)
            acts_ref[...] = (values * scale * gain_ref[...]).astype(BF)

        rows = None
        for j in range(count):
            lanes = pl.ds(pl.multiple_of((at_ref[1] + count - j) % count * depth, depth), depth)
            term = dot_nn(acts_ref[:, lanes], w_refs[j][...])
            rows = term if rows is None else rows + term
        turned = jnp.where(
            step == parts + 1, rows, turn(rows, cos_ref[...], sin_ref[...])
        ).astype(BF)
        seq_now = at_ref[0]
        for k in range(parts):

            @pl.when((seq_now ^ k) == step)
            def _():
                packs[k][:, :tile] = turned

            for d in range(parts):
                for which in range(2):

                    @pl.when(((seq_now ^ k) == d) & (step == parts + which))
                    def _():
                        lane = tile + which * each
                        packs[k][:, lane : lane + each] = turned[:, d * each : (d + 1) * each]

    return pl.pallas_call(
        kernel,
        grid=(parts + 2,),
        out_shape=[jax.ShapeDtypeStruct((tokens, width), BF)]
        + [jax.ShapeDtypeStruct((tokens, pack), BF)] * parts,
        in_specs=[smem(), whole((tokens, width)), whole((1, width))]
        + [pl.BlockSpec((depth, tile), lambda n: (0, n))] * count
        + [whole((tokens, tile))] * 2,
        out_specs=[whole((tokens, width))] + [whole((tokens, pack))] * parts,
        compiler_params=params(),
        cost_estimate=cost(2 * tokens * width * tile * (parts + 2), 2 * width * tile * (parts + 2)),
        name="project_in",
    )(jnp.stack([seq, z]), inputs, gain, *groups, cos_table, sin_table)


def project_out(seq, z, mixed, inputs, gain, groups):
    parts = len(mixed)
    tokens, width = inputs.shape
    each = mixed[0].shape[1]
    tile = width // parts
    count = len(groups)
    depth = parts * each // count

    def kernel(at_ref, *refs):
        parts_in, (in_ref, gain_ref) = refs[:parts], refs[parts : parts + 2]
        w_refs, (flat_ref, res_ref, acts_ref) = refs[parts + 2 : -3], refs[-3:]
        step = pl.program_id(0)

        @pl.when(step == 0)
        def _():
            for k in range(parts):
                lane = pl.multiple_of((at_ref[0] ^ k) * each, each)
                flat_ref[:, pl.ds(lane, each)] = parts_in[k][...]

        lanes = pl.ds(pl.multiple_of(step * tile, tile), tile)
        total = in_ref[:, lanes].astype(F32)
        for j in range(count):
            rows = pl.ds(pl.multiple_of((at_ref[1] + count - j) % count * depth, depth), depth)
            total = total + dot_nn(flat_ref[:, rows], w_refs[j][...])
        res_ref[:, lanes] = total

        @pl.when(step == parts - 1)
        def _():
            values = res_ref[...]
            scale = lax.rsqrt(jnp.mean(values * values, axis=-1, keepdims=True) + EPSILON)
            acts_ref[...] = (values * scale * gain_ref[...]).astype(BF)

    return pl.pallas_call(
        kernel,
        grid=(parts,),
        out_shape=[
            jax.ShapeDtypeStruct((tokens, parts * each), BF),
            jax.ShapeDtypeStruct((tokens, width), F32),
            jax.ShapeDtypeStruct((tokens, width), BF),
        ],
        in_specs=[smem()]
        + [whole((tokens, each))] * parts
        + [whole((tokens, width)), whole((1, width))]
        + [pl.BlockSpec((depth, tile), lambda n: (0, n))] * count,
        out_specs=[whole((tokens, parts * each)), whole((tokens, width)), whole((tokens, width))],
        compiler_params=params(),
        cost_estimate=cost(2 * tokens * width * parts * each, 2 * width * parts * each),
        name="project_out",
    )(jnp.stack([seq, z]), *mixed, inputs, gain, *groups)


def feed_forward(acts, grads, gate, up, down, begun=None):
    tokens, width = acts.shape
    hidden = gate.shape[0]
    tile = 256
    steps = hidden // tile
    kind = F32 if begun is None else BF
    begun = [] if begun is None else list(begun)

    def kernel(a_ref, c_ref, g_ref, u_ref, d_ref, *refs):
        starts, (h_ref, gg_ref, gu_ref, o_ref, ga_ref, o_s, ga_s) = refs[:-7], refs[-7:]
        step = pl.program_id(0)

        @pl.when(step == 0)
        def _():
            if starts:
                o_s[...] = starts[0][...]
                ga_s[...] = starts[1][...]
            else:
                o_s[...] = jnp.zeros_like(o_s)
                ga_s[...] = jnp.zeros_like(ga_s)

        gate_act = dot_nt(a_ref[...], g_ref[...])
        up_act = dot_nt(a_ref[...], u_ref[...])
        grad_hidden = dot_nt(c_ref[...], d_ref[...])
        sigma = jax.nn.sigmoid(gate_act)
        silu = gate_act * sigma
        low = (silu * up_act).astype(BF)
        grad_gate = (grad_hidden * up_act * (sigma * (1.0 + gate_act * (1.0 - sigma)))).astype(BF)
        grad_up = (grad_hidden * silu).astype(BF)
        h_ref[...] = low
        gg_ref[...] = grad_gate
        gu_ref[...] = grad_up
        o_s[...] += dot_nn(low, d_ref[...])
        ga_s[...] += dot_nn(grad_gate, g_ref[...]) + dot_nn(grad_up, u_ref[...])

        @pl.when(step == steps - 1)
        def _():
            o_ref[...] = o_s[...].astype(kind)
            ga_ref[...] = ga_s[...].astype(kind)

    whole = pl.BlockSpec((tokens, width), lambda n: (0, 0))
    rows = pl.BlockSpec((tile, width), lambda n: (n, 0))
    lanes = pl.BlockSpec((tokens, tile), lambda n: (0, n))
    return pl.pallas_call(
        kernel,
        grid=(steps,),
        out_shape=[jax.ShapeDtypeStruct((tokens, hidden), BF)] * 3
        + [jax.ShapeDtypeStruct((tokens, width), kind)] * 2,
        in_specs=[whole, whole, rows, rows, rows] + [whole] * len(begun),
        out_specs=[lanes] * 3 + [whole] * 2,
        scratch_shapes=[pltpu.VMEM((tokens, width), F32)] * 2,
        compiler_params=params(),
        cost_estimate=cost(12 * tokens * width * hidden, 6 * width * hidden),
        name="feed_forward",
    )(acts, grads, gate, up, down, *begun)


def middle_back(seq, z, terms, residual, grad_out, gain, groups, parts):
    tokens, width = residual.shape
    tile = groups[0].shape[0]
    count = len(groups)
    assert count == parts

    def kernel(at_ref, t0_ref, t1_ref, res_ref, go_ref, gain_ref, *refs):
        w_refs, (gr_ref, low_ref, gg_ref), outs = refs[:count], refs[count : count + 3], refs[count + 3 :]
        grad = t0_ref[...].astype(F32) + t1_ref[...].astype(F32)
        values = res_ref[...]
        scale = lax.rsqrt(jnp.mean(values * values, axis=-1, keepdims=True) + EPSILON)
        weighted = grad * gain_ref[...]
        inner = jnp.mean(weighted * values, axis=-1, keepdims=True)
        result = go_ref[...].astype(F32) + scale * weighted - values * (scale**3 * inner)
        gr_ref[...] = result
        low_ref[...] = result.astype(BF)
        gg_ref[...] = jnp.sum(grad * values * scale, axis=0, keepdims=True)
        for j in range(count):
            part = dot_nt(low_ref[...], w_refs[j][...]).astype(BF)
            at = ((at_ref[1] + count - j) % count) ^ at_ref[0]
            for k in range(parts):

                @pl.when(at == k)
                def _():
                    outs[k][...] = part

    vmem = pl.BlockSpec(memory_space=pltpu.VMEM)
    return pl.pallas_call(
        kernel,
        out_shape=[
            jax.ShapeDtypeStruct((tokens, width), F32),
            jax.ShapeDtypeStruct((tokens, width), BF),
            jax.ShapeDtypeStruct((1, width), F32),
        ]
        + [jax.ShapeDtypeStruct((tokens, tile), BF)] * parts,
        in_specs=[smem()] + [vmem] * (5 + count),
        out_specs=[vmem] * (3 + parts),
        compiler_params=params(),
        cost_estimate=cost(2 * tokens * width * tile * parts, 2 * width * tile * parts + 8 * tokens * width),
        name="middle_back",
    )(jnp.stack([seq, z]), terms[0], terms[1], residual, grad_out, gain, *groups)


def unpack(seq, packs, cos_table, sin_table):
    parts = len(packs)
    tokens, tile = cos_table.shape
    each = tile // parts

    def kernel(seq_ref, *refs):
        ins, (cos_ref, sin_ref, out_ref) = refs[:parts], refs[parts:]
        for k in range(parts):
            at = seq_ref[0] ^ k
            queries = turn(ins[k][:, :tile].astype(F32), cos_ref[...], -sin_ref[...])
            out_ref[:, pl.ds(pl.multiple_of(at * tile, tile), tile)] = queries.astype(BF)
            keys = turn(
                ins[k][:, tile : tile + each].astype(F32), cos_ref[:, :each], -sin_ref[:, :each]
            )
            lane = pl.multiple_of(parts * tile + at * each, each)
            out_ref[:, pl.ds(lane, each)] = keys.astype(BF)
            lane = pl.multiple_of((parts + 1) * tile + at * each, each)
            out_ref[:, pl.ds(lane, each)] = ins[k][:, tile + each :]

    vmem = pl.BlockSpec(memory_space=pltpu.VMEM)
    return pl.pallas_call(
        kernel,
        out_shape=jax.ShapeDtypeStruct((tokens, (parts + 2) * tile), BF),
        in_specs=[smem()] + [vmem] * (parts + 2),
        out_specs=vmem,
        compiler_params=params(),
        cost_estimate=cost(0, 6 * 2**20),
        name="unpack",
    )(seq.reshape(1), *packs, cos_table, sin_table)


def inner_back(z, grad_qkv, groups, inputs, gain, grad_res):
    tokens, width = inputs.shape
    count = len(groups)
    depth = width // count

    def kernel(at_ref, gq_ref, *refs):
        w_refs, (in_ref, gain_ref, gr_ref, out_ref, gg_ref, grad_s) = refs[:count], refs[count:]
        for j in range(count):
            lanes = pl.ds(pl.multiple_of((at_ref[0] + count - j) % count * depth, depth), depth)
            grad_s[:, lanes] = dot_nt(gq_ref[...], w_refs[j][...])
        grad = grad_s[...]
        values = in_ref[...].astype(F32)
        scale = lax.rsqrt(jnp.mean(values * values, axis=-1, keepdims=True) + EPSILON)
        weighted = grad * gain_ref[...]
        inner = jnp.mean(weighted * values, axis=-1, keepdims=True)
        result = gr_ref[...] + scale * weighted - values * (scale**3 * inner)
        out_ref[...] = result.astype(BF)
        gg_ref[...] = jnp.sum(grad * values * scale, axis=0, keepdims=True)

    vmem = pl.BlockSpec(memory_space=pltpu.VMEM)
    return pl.pallas_call(
        kernel,
        out_shape=[jax.ShapeDtypeStruct((tokens, width), BF), jax.ShapeDtypeStruct((1, width), F32)],
        in_specs=[smem()] + [vmem] * (4 + count),
        out_specs=[vmem] * 2,
        scratch_shapes=[pltpu.VMEM((tokens, width), F32)],
        compiler_params=params(),
        cost_estimate=cost(2 * tokens * groups[0].size * count, 2 * groups[0].size * count),
        name="inner_back",
    )(z.reshape(1), grad_qkv, *groups, inputs, gain, grad_res)


def weight_grad(left, right, rows, blocks, half, adds=()):
    count = len(left)
    tokens = left[0].shape[0]
    width = right[0].shape[1] // 2
    tile = min(rows, 512)
    steps = rows // tile
    total_rows = rows * len(blocks)

    def kernel(at_ref, *refs):
        lefts, rights, extra, out = refs[:count], refs[count : 2 * count], refs[2 * count : -1], refs[-1]
        total = None
        for l_ref, r_ref in zip(lefts, rights):
            term = lax.dot_general(
                l_ref[...], r_ref[...], (((0,), (0,)), ((), ())), preferred_element_type=F32
            )
            total = term if total is None else total + term
        for ref in extra:
            total = total + ref[...].astype(F32)
        out[...] = total.astype(BF)

    rows_spec = pl.BlockSpec((tile, width), lambda n, at: (n, 0))
    spec = pltpu.PrefetchScalarGridSpec(
        num_scalar_prefetch=1,
        grid=(steps * len(blocks),),
        in_specs=[pl.BlockSpec((tokens, tile), lambda n, at: (0, at[1 + n]))] * count
        + [pl.BlockSpec((tokens, width), lambda n, at: (0, at[0]))] * count
        + [rows_spec] * len(adds),
        out_specs=rows_spec,
    )
    at = [jnp.int32(half)]
    for block in blocks:
        at += [jnp.int32(block) * steps + i for i in range(steps)]
    return pl.pallas_call(
        kernel,
        grid_spec=spec,
        out_shape=jax.ShapeDtypeStruct((total_rows, width), BF),
        compiler_params=params(),
        cost_estimate=cost(
            2 * tokens * count * total_rows * width, 2 * (tokens * count + total_rows) * width
        ),
        name="weight_grad",
    )(jnp.stack(at), *left, *right, *adds)


def row_grads(left, right, blocks, half, added, y, cuts):
    tokens = left.shape[0]
    width = right.shape[1] // 2
    rows = left.shape[1] // LINE
    each = rows // cuts
    count = len(blocks)

    def kernel(at_ref, l_ref, r_ref, add_ref, *refs):
        outs, total_s = refs[:-1], refs[-1]
        total = lax.dot_general(
            l_ref[...], r_ref[...], (((0,), (0,)), ((), ())), preferred_element_type=F32
        )
        total_s[...] = (total + add_ref[...].astype(F32)).astype(BF)
        for j in range(count):

            @pl.when(pl.program_id(0) == j)
            def _():
                for k in range(cuts):
                    start = pl.multiple_of((at_ref[1] + cuts - k) % cuts * each, each)
                    outs[j * cuts + k][...] = total_s[pl.ds(start, each), :]

    spec = pltpu.PrefetchScalarGridSpec(
        num_scalar_prefetch=1,
        grid=(count,),
        in_specs=[
            pl.BlockSpec((tokens, rows), lambda n, at: (0, at[2 + n])),
            pl.BlockSpec((tokens, width), lambda n, at: (0, at[0])),
            pl.BlockSpec((rows, width), lambda n, at: (n, 0)),
        ],
        out_specs=[pl.BlockSpec((each, width), lambda n, at: (0, 0))] * (count * cuts),
        scratch_shapes=[pltpu.VMEM((rows, width), BF)],
    )
    at = jnp.stack([jnp.int32(half), jnp.int32(y)] + [jnp.int32(b) for b in blocks])
    outs = pl.pallas_call(
        kernel,
        grid_spec=spec,
        out_shape=[jax.ShapeDtypeStruct((each, width), BF)] * (count * cuts),
        compiler_params=params(),
        cost_estimate=cost(2 * tokens * count * rows * width, 6 * count * rows * width),
        name="row_grads",
    )(at, left, right, added)
    return [outs[j * cuts : (j + 1) * cuts] for j in range(count)]


def join(core, mine, other, widths):
    rows, half = mine.shape
    tile = min(rows, 256)

    def kernel(core_ref, mine_ref, other_ref, *refs):
        outs, full = refs[:-1], refs[-1]
        target = outs[0] if len(outs) == 1 else full
        at = pl.multiple_of(core_ref[0] * half, half)
        target[:, pl.ds(at, half)] = mine_ref[...].astype(F32)
        at = pl.multiple_of((1 - core_ref[0]) * half, half)
        target[:, pl.ds(at, half)] = other_ref[...].astype(F32)
        if len(outs) > 1:
            lane = 0
            for out in outs:
                out[...] = full[:, lane : lane + out.shape[1]]
                lane += out.shape[1]

    def block(width):
        return pl.BlockSpec((tile, width), lambda n: (n, 0))

    return pl.pallas_call(
        kernel,
        grid=(rows // tile,),
        out_shape=[jax.ShapeDtypeStruct((rows, width), F32) for width in widths],
        in_specs=[smem(), block(half), block(half)],
        out_specs=[block(width) for width in widths],
        scratch_shapes=[pltpu.VMEM((tile, 2 * half) if len(widths) > 1 else (8, 128), F32)],
        compiler_params=params(),
        cost_estimate=cost(0, rows * half * 12),
        name="join",
    )(core.reshape(1), mine, other)
def half_of(array, which, axis=1):
    size = array.shape[axis] // 2
    return lax.dynamic_slice_in_dim(array, which * size, size, axis)


def join_halves(core, top, bottom):
    rows, half = top[0].shape
    tile = min(rows, 256)
    steps = rows // tile

    def kernel(core_ref, a_ref, b_ref, c_ref, d_ref, out):
        mine = pl.multiple_of(core_ref[0] * half, half)
        other = pl.multiple_of((1 - core_ref[0]) * half, half)
        upper = pl.program_id(0) < steps

        @pl.when(upper)
        def _():
            out[:, pl.ds(mine, half)] = a_ref[...].astype(F32)
            out[:, pl.ds(other, half)] = b_ref[...].astype(F32)

        @pl.when(jnp.logical_not(upper))
        def _():
            out[:, pl.ds(mine, half)] = c_ref[...].astype(F32)
            out[:, pl.ds(other, half)] = d_ref[...].astype(F32)

    first = pl.BlockSpec((tile, half), lambda n: (jnp.minimum(n, steps - 1), 0))
    second = pl.BlockSpec((tile, half), lambda n: (jnp.maximum(n - steps, 0), 0))
    return pl.pallas_call(
        kernel,
        grid=(2 * steps,),
        out_shape=jax.ShapeDtypeStruct((2 * rows, 2 * half), F32),
        in_specs=[smem(), first, first, second, second],
        out_specs=pl.BlockSpec((tile, 2 * half), lambda n: (n, 0)),
        compiler_params=params(),
        cost_estimate=cost(0, rows * half * 24),
        name="join_halves",
    )(core.reshape(1), *top, *bottom)


class Order:
    def __init__(self):
        self.marks = ()

    def tie(self, *values):
        if self.marks:
            values = lax.optimization_barrier(tuple(values) + self.marks)[: len(values)]
        return values[0] if len(values) == 1 else list(values)

    def done(self, *values):
        self.marks = tuple(values)


def y_hops(value):
    return ring_gather(value, y_next, columns())[1:]


def add_low(left, right):
    return (left.astype(F32) + right.astype(F32)).astype(BF)


def rope_tables(positions, repeat):
    frequency = THETA ** (-(jnp.arange(HD // 2, dtype=F32) * 2.0) / HD)
    angles = positions.astype(F32)[:, None] * frequency[None, :]
    cos, sin = jnp.cos(angles), jnp.sin(angles)
    return (
        jnp.tile(jnp.concatenate([cos, cos], axis=1), (1, repeat)),
        jnp.tile(jnp.concatenate([-sin, sin], axis=1), (1, repeat)),
    )


def exchange(packs):
    return [packs[0]] + [seq_swap(packs[k], k) for k in range(1, len(packs))]


def shards(
    inputs,
    query_weight,
    key_weight,
    value_weight,
    output_weight,
    gate_weight,
    up_weight,
    down_weight,
    gain_attn,
    gain_ffn,
    cotangent,
):
    seq_count, local_len, width = inputs.shape
    assert seq_count == 1
    tokens = local_len
    parts = lax.axis_size("seq")
    kv_local = KVH // parts
    cols = columns()
    seq = lax.axis_index("seq")
    core, side = seq % 2, seq // 2
    fsdp = lax.axis_index("fsdp")
    z, y = fsdp // cols, fsdp % cols
    q_width, kv_width = query_weight.shape[1], key_weight.shape[1]
    heads_local = q_width // HD // parts
    flat_in = inputs.reshape(tokens, width)
    grad_out = cotangent.reshape(tokens, width)

    qkv_shard = jnp.concatenate([query_weight, key_weight, value_weight], axis=1)
    rows = qkv_shard.shape[0]
    part, half = rows // 2, qkv_shard.shape[1] // 2
    positions = seq * local_len + jnp.arange(local_len)
    cos_table, sin_table = rope_tables(positions, kv_width // HD)
    order = Order()

    def swapped(pieces):
        return [core_swap(p) for p in pieces]

    def place_halves(pieces, others, whole_first=None):
        each = pieces[-1].shape[1]
        placed, offsets = [], []
        for k, (piece, other) in enumerate(zip(pieces, others)):
            row = (y - k) % cols * rows
            if k == 0 and whole_first is not None:
                placed.append(whole_first)
                offsets.append((row, 0))
            else:
                placed += [piece, other]
                offsets += [(row, core * each), (row, (1 - core) * each)]
        return place((rows * cols, 2 * each), placed, offsets)

    def place_quarters(pieces, others, sides, count, size, first):
        each = pieces[0].shape[1]
        placed, offsets = [], []
        for i, (piece, other) in enumerate(zip(pieces, others)):
            k, at = i // 2, sides[i % 2]
            row = first(k) * size + at * (size // 2)
            placed += [piece, other]
            offsets += [(row, core * each), (row, (1 - core) * each)]
        return place((size * count, 2 * each), placed, offsets)

    def line_row(k):
        return (y - k) % cols

    own = (gate_weight, up_weight, down_weight)
    far_rows = gate_weight.shape[0]
    far_part = far_rows // 4
    far_y, far_x = {}, {}

    def far_start(i, h):
        at = side * 2 * far_part + h * far_part
        return lax.dynamic_slice(own[i], (at, core * out_width), (far_part, out_width))

    out_width = width // 2
    far_starts = {(i, h): far_start(i, h) for i in range(3) for h in range(2)}

    def far_along_y(i, h):
        start = order.tie(far_starts[i, h]) if order.marks else far_starts[i, h]
        far_y[i, h] = y_hops(start)
        return far_y[i, h]

    def far_along_x(i, h):
        pieces = order.tie(*far_y[i, h], far_y[i, h][0])[:-1]
        far_x[i, h] = [x_swap(p) for p in pieces]
        return far_x[i, h]

    gains = jnp.concatenate([gain_attn, gain_ffn]).reshape(1, 2 * rows)
    start = half_of(qkv_shard, core)
    start = jnp.concatenate([start, jnp.pad(gains, ((0, 15), (0, half - 2 * rows)))], axis=0)
    out_half = half_of(output_weight, core)

    def quarter_of(piece):
        return lax.dynamic_slice_in_dim(piece, side * part, part, 0)

    def line_group(i):
        here = order.tie(line[i])
        placed, offsets = [], []
        row = y * rows
        if i:
            placed += [here, core_swap(here)]
            offsets += [(row, core * half), (row, (1 - core) * half)]
        else:
            placed.append(qkv_shard)
            offsets.append((row, 0))
        for k in range(1, cols):
            row = (y - k) % cols * rows
            if i < LINE - 1:
                for piece, at in ((beside[i][k - 1], side), (crossed[i][k - 1], 1 - side)):
                    piece = order.tie(piece)
                    placed += [piece, core_swap(piece)]
                    offsets += [
                        (row + at * part, core * half),
                        (row + at * part, (1 - core) * half),
                    ]
            else:
                piece = order.tie(beside[i][k - 1])
                placed += [piece, core_swap(piece)]
                offsets += [(row, core * half), (row, (1 - core) * half)]
        return place((rows * cols, 2 * half), placed, offsets, rows)

    line, beside, crossed, groups = [start], [], [], []
    for j in range(LINE):
        here = order.tie(line[j]) if j else line[j]
        if j + 1 < LINE:
            line.append(z_next(here))
            beside.append(y_hops(quarter_of(here)))
            marks = [line[j + 1]] + beside[j] + far_along_y(j // 2, j % 2)
        else:
            beside.append(y_hops(here))
            line_o = [out_half, z_next(order.tie(out_half))]
            gains_near = jnp.concatenate([p[rows:, : 2 * rows] for p in line[:j]], axis=0)
            gains_far = y_hops(order.tie(gains_near))
            marks = beside[j] + [line_o[1]]
        if j:
            pieces = order.tie(*beside[j - 1], here)[:-1]
            crossed.append([x_swap(p) for p in pieces])
            marks += crossed[j - 1]
        if j > 1:
            marks += far_along_x(0, j - 2)
            groups.append(line_group(j - 2))
            marks.append(groups[-1])
        if j == 0:
            marks += [cos_table, sin_table]
        order.done(*marks)

    line_o.append(z_next(order.tie(line_o[1])))
    grad_parts = [grad_out, z_next(order.tie(grad_out))]
    beside_o = [y_hops(order.tie(line_o[0])), y_hops(order.tie(line_o[1]))]
    groups += [line_group(LINE - 2), line_group(LINE - 1)]
    marks = far_along_x(1, 0)
    gain_full = jnp.zeros((2, width), BF)
    for j in range(LINE):
        for k in range(cols):
            if j == LINE - 1:
                g = line[j][rows] if k == 0 else beside[j][k - 1][rows]
                pair = g[: 2 * rows].reshape(2, rows)
            else:
                g = gains_near if k == 0 else gains_far[k - 1]
                pair = g[16 * j].reshape(2, rows)
            at = (((z - j) % LINE) * cols + (y - k) % cols) * rows
            gain_full = lax.dynamic_update_slice(gain_full, pair, (0, at))
    gain_one = gain_full[:1].astype(F32)
    gain_two = gain_full[1:].astype(F32)
    acts_one, *sent = project_in(seq, z, flat_in, gain_one, groups, cos_table, sin_table, parts)
    order.done(*sent, line_o[2], *beside_o[0], *marks)

    def out_group(j):
        hops = order.tie(line_o[j], *beside_o[j])
        if j == 0:
            return place_halves([None] + hops[1:], [None] + swapped(hops[1:]), output_weight)
        return place_halves(hops, swapped(hops))

    packs = exchange(order.tie(*sent))
    line_o.append(z_next(order.tie(line_o[2])))
    order.done(*packs, line_o[3], *beside_o[1])

    beside_o += [y_hops(order.tie(line_o[2])), y_hops(order.tie(line_o[3]))]
    grad_parts.append(z_next(order.tie(grad_parts[1])))
    out_groups = [out_group(0), out_group(1)]
    *mixed_sent, log_totals = attend_forward(seq, order.tie(*packs), heads_local, kv_local)
    order.done(*mixed_sent, *beside_o[2], *beside_o[3], grad_parts[2], *out_groups)

    mixed = exchange(order.tie(*mixed_sent))
    grad_parts.append(z_next(order.tie(grad_parts[2])))
    out_groups += [out_group(2), out_group(3)]
    order.done(*mixed, *out_groups)

    marks = far_along_y(1, 1)
    mixed_flat, residual, acts_two = project_out(
        seq, z, order.tie(*mixed), flat_in, gain_two, out_groups
    )
    order.done(acts_two, grad_parts[3], *marks)

    def far_place(i):
        placed, offsets = [], []
        for k in range(cols - 1):
            for h in range(2):
                pieces = order.tie(far_y[i, h][k], far_x[i, h][k])
                for piece, at in zip(pieces, (side, 1 - side)):
                    row = k * far_rows + at * 2 * far_part + h * far_part
                    placed += [piece, core_swap(piece)]
                    offsets += [(row, core * out_width), (row, (1 - core) * out_width)]
        return place((far_rows * (cols - 1), width), placed, offsets)

    acts_parts, far, near_done, far_done = [acts_two], [], [], [None] * LINE

    def run_near(j):
        near_done.append(feed_forward(order.tie(acts_parts[j]), grad_parts[j], *own))
        return near_done[j][3]

    def run_far(j):
        far_done[j] = feed_forward(order.tie(acts_parts[j]), grad_parts[j], *far, near_done[j][3:])
        return far_done[j][4]

    acts_parts.append(z_next(order.tie(acts_parts[0])))
    marks = far_along_y(2, 0) + far_along_y(2, 1) + far_along_x(1, 1)
    far.append(far_place(0))
    order.done(acts_parts[1], *marks, *far, run_near(0))
    acts_parts.append(z_next(order.tie(acts_parts[1])))
    marks = far_along_x(2, 0) + far_along_x(2, 1)
    far.append(far_place(1))
    order.done(acts_parts[2], *marks, *far, run_near(1))
    acts_parts.append(z_next(order.tie(acts_parts[2])))
    far.append(far_place(2))
    marks = [run_near(2), run_far(1)]
    order.done(acts_parts[3], *marks)

    passed = z_next(order.tie(far_done[1][4]))
    marks = [run_near(3), run_far(2)]
    order.done(passed, *marks)
    passed = z_next(order.tie(add_low(passed, far_done[2][4])))
    marks = [run_far(3), run_far(0)]
    order.done(passed, *marks)
    passed = z_next(order.tie(add_low(passed, far_done[3][4])))

    rights = (grad_parts, acts_parts, acts_parts)
    far_size = far_rows * (cols - 1)
    far_sent, far_total, own_sent = [None] * 3, {}, [None] * 3

    def of(done, which):
        return order.tie(*[d[which] for d in done])

    def send_far(i):
        far_sent[i] = weight_grad(of(far_done, i), rights[i], far_size, [0], 1 - core)
        return far_sent[i]

    def keep_far(i):
        return weight_grad(of(far_done, i), rights[i], far_size, [0], core, [far_sent[i]])

    def pass_far(i, kept, h):
        size = far_rows // 2
        kept = order.tie(kept)
        total = y_next(kept[h * size : (h + 1) * size])
        for k in range(1, cols - 1):
            start = k * far_rows + h * size
            total = y_next(add_low(total, kept[start : start + size]))
        far_total[i, h] = total
        return total

    def send_own(i):
        own_sent[i] = weight_grad(of(near_done, i), rights[i], far_rows, [0], 1 - core)
        return own_sent[i]

    def keep_own(i):
        return weight_grad(of(near_done, i), rights[i], far_rows, [0], core, [own_sent[i]])

    marks = [send_far(0), send_far(1), send_far(2), send_own(0)]
    order.done(passed, *marks)

    far_sent = [core_swap(order.tie(term)) for term in far_sent]
    ffn_parts = [d[3] for d in far_done]
    ffn_sum = z_next(order.tie(ffn_parts[1]))
    grad_res, grad_res_low, grad_gain_two, *grad_sent = middle_back(
        seq, z, order.tie(passed, far_done[0][4]), residual, grad_out, gain_two, out_groups, parts
    )
    order.done(*grad_sent, *far_sent)

    grad_packs = exchange(order.tie(*grad_sent))
    kept = [keep_far(0), keep_far(1)]
    order.done(*grad_packs, ffn_sum, *kept)

    marks = [pass_far(0, kept[0], 0)]
    ffn_sum = z_next(order.tie(add_low(ffn_sum, ffn_parts[2])))
    back_sent = attend_backward(
        seq, log_totals, packs, order.tie(*grad_packs), heads_local, kv_local
    )
    order.done(*back_sent, *marks)

    line_order = list(range(1, LINE)) + [0]
    blocks = [(z - j) % LINE for j in line_order]
    line_rows = rows * cols
    back_packs = exchange(order.tie(*back_sent))
    own_sent[0] = core_swap(order.tie(own_sent[0]))
    out_left, out_right = order.tie(mixed_flat, grad_res_low)
    out_sent = weight_grad([out_left], [out_right], line_rows, blocks, 1 - core)
    marks = [pass_far(0, kept[0], 1), keep_far(2), keep_own(0), out_sent]
    own_low = [marks[2]]
    kept.append(marks[1])
    order.done(*back_packs, *marks, ffn_sum)

    size = far_rows // 2
    sums = {}

    def along_x(i, h):
        low = add_low(order.tie(own_low[i])[h * size : (h + 1) * size], far_total[i, h])
        sums[i, h] = (low, x_swap(low))
        return sums[i, h][1]

    def finish(i, h):
        low, crossed = order.tie(*sums[i, h])
        total = add_low(low, crossed)
        sums[i, h] = (total, core_swap(total))
        return sums[i, h][1]

    def joined(i):
        pairs = order.tie(*sums[i, 0], *sums[i, 1])
        return join_halves(core, pairs[:2], pairs[2:])

    def along_y(terms):
        terms = order.tie(*terms, terms[0])[:-1]
        total = None
        for k in list(range(1, cols)) + [0]:
            total = terms[k] if total is None else add_low(y_next(total), terms[k])
        return total

    marks = [pass_far(1, kept[1], 0), along_x(0, 0)]
    out_recv = core_swap(order.tie(out_sent))
    ffn_sum = z_next(order.tie(add_low(ffn_sum, ffn_parts[3])))
    grad_qkv = unpack(seq, order.tie(*back_packs), cos_table, sin_table)
    qkv_sent = weight_grad([acts_one], [grad_qkv], line_rows, blocks, 1 - core)
    marks.append(send_own(1))
    order.done(qkv_sent, out_recv, *marks)

    qkv_recv = core_swap(order.tie(qkv_sent))
    own_sent[1] = core_swap(order.tie(own_sent[1]))
    out_terms = row_grads(out_left, out_right, blocks, core, order.tie(out_recv), y, 1)
    out_terms = [t[0] for t in out_terms]
    marks = [pass_far(1, kept[1], 1), send_own(2), along_x(0, 1), finish(0, 0)]
    order.done(qkv_recv, ffn_sum, own_sent[1], *out_terms, *marks)

    out_total = z_next(order.tie(out_terms[0]))
    qkv_terms = row_grads(acts_one, grad_qkv, blocks, core, order.tie(qkv_recv), y, cols)
    own_sent[2] = core_swap(order.tie(own_sent[2]))
    own_low.append(keep_own(1))
    marks = [pass_far(2, kept[2], 0), own_low[1], finish(0, 1), own_sent[2]]
    order.done(*[t for terms in qkv_terms for t in terms], out_total, *marks)

    out_total = z_next(order.tie(add_low(out_total, out_terms[1])))
    hops = [along_y(qkv_terms[0])]
    own_low.append(keep_own(2))
    d_down = joined(0)
    order.done(hops[0], out_total, own_low[2], d_down, along_x(1, 0))

    passed = z_next(order.tie(hops[0]))
    out_total = z_next(order.tie(add_low(out_total, out_terms[2])))
    hops.append(along_y(qkv_terms[1]))
    grad_inputs, grad_gain_one = inner_back(z, order.tie(grad_qkv), groups, flat_in, gain_one, grad_res)
    marks = [pass_far(2, kept[2], 1), along_x(1, 1), finish(1, 0), grad_inputs]
    order.done(passed, hops[1], out_total, *marks)

    passed = z_next(order.tie(add_low(passed, hops[1])))
    hops.append(along_y(qkv_terms[2]))
    out_total = order.tie(add_low(out_total, out_terms[3]))
    pieces = [
        lax.dynamic_slice_in_dim(out_total, (y - k) % cols * rows, rows, 0) for k in range(cols)
    ]
    out_low = along_y(pieces)
    gain_sums = jnp.concatenate([grad_gain_one, grad_gain_two], axis=0)
    steps = sum_steps()
    gain_sums = gain_sums + steps[0](order.tie(gain_sums))
    marks = [along_x(2, 0), finish(1, 1), gain_sums]
    order.done(passed, hops[2], out_low, *marks)

    passed = z_next(order.tie(add_low(passed, hops[2])))
    hops.append(along_y(qkv_terms[3]))
    out_cross = x_swap(order.tie(out_low))
    gain_sums = gain_sums + steps[1](order.tie(gain_sums))
    outputs = (residual + ffn_sum.astype(F32) + order.tie(ffn_parts[0]).astype(F32)).astype(BF)
    d_gate = joined(1)
    marks = [along_x(2, 1), finish(2, 0), d_gate, outputs, gain_sums]
    order.done(passed, hops[3], out_cross, *marks)

    low = order.tie(add_low(passed, hops[3]))
    crossed = x_swap(low)
    finish(2, 1)
    d_up = joined(2)
    out_low = add_low(out_low, order.tie(out_cross))
    d_out = join(core, out_low, core_swap(out_low), [width])
    gain_sums = order.tie(gain_sums)
    for step in steps[2:-1]:
        gain_sums = gain_sums + step(gain_sums)
    order.done(crossed, d_up, d_out[0], gain_sums)
    gain_sums = gain_sums + steps[-1](order.tie(gain_sums))
    total = add_low(low, crossed)
    d_qkv = join(core, total, core_swap(total), [q_width, kv_width, kv_width])

    gain_sums = lax.dynamic_slice_in_dim(gain_sums, fsdp * rows, rows, 1)
    return (
        outputs.reshape(inputs.shape),
        grad_inputs.reshape(inputs.shape),
        d_qkv[0],
        d_qkv[1],
        d_qkv[2],
        d_out[0],
        d_gate,
        d_up,
        d_down,
        gain_sums[0],
        gain_sums[1],
    )


def solution(mesh):
    token_spec, row_spec, gain_spec = P("fsdp", "seq", None), P("fsdp", None), P("fsdp")
    return jax.shard_map(
        shards,
        mesh=mesh,
        in_specs=(token_spec,) + (row_spec,) * 7 + (gain_spec,) * 2 + (token_spec,),
        out_specs=(token_spec,) * 2 + (row_spec,) * 7 + (gain_spec,) * 2,
        check_vma=False,
    )
```

```python
import functools

import jax
import jax.numpy as jnp
from jax import lax
from jax.experimental import pallas as pl
from jax.experimental.pallas import tpu as pltpu
from jax.sharding import PartitionSpec as P

KVH = 8
HD = 64
BLOCK = 256
LINE = 4

EPSILON = 1e-05
THETA = 500000.0
LOG2E = 1.4426950408889634

BF = jnp.bfloat16
F32 = jnp.float32


def after(value, *others):
    return lax.optimization_barrier((value,) + others)[0]


def columns():
    return lax.axis_size("fsdp") // LINE


def z_next(value):
    cols = columns()
    count = lax.axis_size("fsdp")
    return lax.ppermute(value, "fsdp", [(i, (i + cols) % count) for i in range(count)])


def y_next(value):
    cols = columns()
    count = lax.axis_size("fsdp")
    return lax.ppermute(
        value, "fsdp", [(i, i // cols * cols + (i + 1) % cols) for i in range(count)]
    )


def seq_swap(value, bit):
    return lax.ppermute(value, "seq", [(i, i ^ bit) for i in range(lax.axis_size("seq"))])


def core_swap(value):
    return seq_swap(value, 1)


def x_swap(value):
    return seq_swap(value, 2)


def ring_gather(value, step, count):
    pieces = [value]
    for _ in range(count - 1):
        pieces.append(step(pieces[-1]))
    return pieces


def ring_scatter(part_of, step, count):
    total = None
    for j in list(range(1, count)) + [0]:
        total = part_of(j) if total is None else part_of(j) + total.astype(F32)
        if j:
            total = step(total.astype(BF))
    return total


def sum_steps():
    steps = []
    bit = 1
    while bit < lax.axis_size("seq"):
        steps.append(functools.partial(seq_swap, bit=bit))
        bit *= 2
    count = lax.axis_size("fsdp")
    bit = 1
    while bit < count:
        pairs = [(i, i ^ bit) for i in range(count)]
        steps.append(functools.partial(lax.ppermute, axis_name="fsdp", perm=pairs))
        bit *= 2
    return steps


def dot_nt(a, b):
    return lax.dot_general(a, b, (((1,), (1,)), ((), ())), preferred_element_type=F32)

def dot_nn(a, b):
    return jnp.dot(a, b, preferred_element_type=F32)


def attend_forward_kernel(parts, heads, kv, seq_ref, *refs):
    packs, outs = refs[:parts], refs[parts : 2 * parts]
    lse_ref, q_s, k_s, vt_s, o_s = refs[2 * parts :]
    tokens = packs[0].shape[0]
    seq = seq_ref[0]
    group = heads // kv
    for k in range(parts):
        rows = pl.ds(pl.multiple_of((seq ^ k) * tokens, tokens), tokens)
        q_s[rows, :] = packs[k][:, : heads * HD]
        for g in range(kv):
            lane = (heads + g) * HD
            k_s[g, rows, :] = packs[k][:, lane : lane + HD]
            lane = (heads + kv + g) * HD
            vt_s[g, :, rows] = packs[k][:, lane : lane + HD].T
    full = parts * tokens
    for g in range(kv):
        for i in range(full // BLOCK):
            keys = (i + 1) * BLOCK
            rows = slice(i * BLOCK, keys)
            for pair in range(group // 2):
                halves = []
                for h in (g * group + 2 * pair, g * group + 2 * pair + 1):
                    scores = dot_nt(k_s[g, :keys, :], q_s[rows, h * HD : (h + 1) * HD])
                    scores = scores * (HD**-0.5 * LOG2E)
                    top = jnp.max(scores, axis=0, keepdims=True)
                    powers = jnp.exp2(scores - top)
                    total = jnp.sum(powers, axis=0, keepdims=True)
                    halves.append(dot_nn(vt_s[g, :, :keys], powers.astype(BF)) / total)
                    lse_ref[h : h + 1, rows] = top + jnp.log2(total)
                lane = (g * group + 2 * pair) * HD
                o_s[rows, lane : lane + 2 * HD] = jnp.concatenate(halves, axis=0).T.astype(BF)
    for k in range(parts):
        rows = pl.ds(pl.multiple_of((seq ^ k) * tokens, tokens), tokens)
        outs[k][...] = o_s[rows, :]


def attend_forward(seq, packs, heads, kv):
    parts = len(packs)
    tokens = packs[0].shape[0]
    full = parts * tokens
    vmem = pl.BlockSpec(memory_space=pltpu.VMEM)
    flops = 4 * heads * full * full * HD * 5 // 8
    return pl.pallas_call(
        functools.partial(attend_forward_kernel, parts, heads, kv),
        out_shape=[jax.ShapeDtypeStruct((tokens, heads * HD), BF)] * parts
        + [jax.ShapeDtypeStruct((heads, full), F32)],
        in_specs=[pl.BlockSpec(memory_space=pltpu.SMEM)] + [vmem] * parts,
        out_specs=[vmem] * (parts + 1),
        scratch_shapes=[
            pltpu.VMEM((full, heads * HD), BF),
            pltpu.VMEM((kv, full, HD), BF),
            pltpu.VMEM((kv, HD, full), BF),
            pltpu.VMEM((full, heads * HD), BF),
        ],
        compiler_params=pltpu.CompilerParams(vmem_limit_bytes=48 * 2**20),
        cost_estimate=cost(flops * 4, 4 * 2**20),
        name="attend_forward",
    )(seq.reshape(1), *packs)


def attend_backward_kernel(parts, heads, kv, seq_ref, lse_ref, *refs):
    packs, grads, outs = refs[:parts], refs[parts : 2 * parts], refs[2 * parts : 3 * parts]
    q_s, k_s, kt_s, v_s, g_s, dq_s, dk_s, dv_s = refs[3 * parts :]
    tokens = packs[0].shape[0]
    seq = seq_ref[0]
    group = heads // kv
    for k in range(parts):
        rows = pl.ds(pl.multiple_of((seq ^ k) * tokens, tokens), tokens)
        q_s[rows, :] = packs[k][:, : heads * HD]
        g_s[rows, :] = grads[k][...]
        for g in range(kv):
            lane = (heads + g) * HD
            k_s[g, rows, :] = packs[k][:, lane : lane + HD]
            kt_s[g, :, rows] = packs[k][:, lane : lane + HD].T
            lane = (heads + kv + g) * HD
            v_s[g, rows, :] = packs[k][:, lane : lane + HD]
    full = parts * tokens
    dk_s[...] = jnp.zeros_like(dk_s)
    dv_s[...] = jnp.zeros_like(dv_s)
    for g in range(kv):
        for i in range(full // BLOCK):
            keys = (i + 1) * BLOCK
            rows = slice(i * BLOCK, keys)
            for pair in range(group // 2):
                halves = []
                for h in (g * group + 2 * pair, g * group + 2 * pair + 1):
                    query = q_s[rows, h * HD : (h + 1) * HD]
                    grad = g_s[rows, h * HD : (h + 1) * HD]
                    scores = dot_nt(k_s[g, :keys, :], query) * (HD**-0.5 * LOG2E)
                    probs = jnp.exp2(scores - lse_ref[h : h + 1, rows])
                    grad_probs = dot_nt(v_s[g, :keys, :], grad)
                    inner = jnp.sum(probs * grad_probs, axis=0, keepdims=True)
                    grad_scores = (probs * (grad_probs - inner)).astype(BF)
                    dv_s[g, :keys, :] += dot_nn(probs.astype(BF), grad)
                    dk_s[g, :keys, :] += dot_nn(grad_scores, query)
                    halves.append(dot_nn(kt_s[g, :, :keys], grad_scores) * HD**-0.5)
                lane = (g * group + 2 * pair) * HD
                dq_s[rows, lane : lane + 2 * HD] = jnp.concatenate(halves, axis=0).T.astype(BF)
    for k in range(parts):
        rows = pl.ds(pl.multiple_of((seq ^ k) * tokens, tokens), tokens)
        outs[k][:, : heads * HD] = dq_s[rows, :]
        for g in range(kv):
            lane = (heads + g) * HD
            outs[k][:, lane : lane + HD] = (dk_s[g, rows, :] * HD**-0.5).astype(BF)
            lane = (heads + kv + g) * HD
            outs[k][:, lane : lane + HD] = dv_s[g, rows, :].astype(BF)


def attend_backward(seq, lse, packs, grads, heads, kv):
    parts = len(packs)
    tokens = packs[0].shape[0]
    full = parts * tokens
    vmem = pl.BlockSpec(memory_space=pltpu.VMEM)
    flops = 10 * heads * full * full * HD * 5 // 8
    return pl.pallas_call(
        functools.partial(attend_backward_kernel, parts, heads, kv),
        out_shape=[jax.ShapeDtypeStruct(packs[0].shape, BF)] * parts,
        in_specs=[pl.BlockSpec(memory_space=pltpu.SMEM)] + [vmem] * (2 * parts + 1),
        out_specs=[vmem] * parts,
        scratch_shapes=[
            pltpu.VMEM((full, heads * HD), BF),
            pltpu.VMEM((kv, full, HD), BF),
            pltpu.VMEM((kv, HD, full), BF),
            pltpu.VMEM((kv, full, HD), BF),
            pltpu.VMEM((full, heads * HD), BF),
            pltpu.VMEM((full, heads * HD), BF),
            pltpu.VMEM((kv, full, HD), F32),
            pltpu.VMEM((kv, full, HD), F32),
        ],
        compiler_params=pltpu.CompilerParams(vmem_limit_bytes=48 * 2**20),
        cost_estimate=cost(flops * 4, 8 * 2**20),
        name="attend_backward",
    )(seq.reshape(1), lse, *packs, *grads)


def smem():
    return pl.BlockSpec(memory_space=pltpu.SMEM)


def params(mib=56):
    return pltpu.CompilerParams(vmem_limit_bytes=mib * 2**20)


def cost(flops, moved):
    return pl.CostEstimate(flops=flops // 8, bytes_accessed=moved // 8, transcendentals=0)


def place(shape, pieces, offsets, most=None):
    count = len(pieces)

    def kernel(at_ref, *refs):
        sources, target, sems = refs[:-2], refs[-2], refs[-1]
        copies = []
        for i, source in enumerate(sources):
            rows, width = source.shape
            rows = min(rows, most or rows)
            row = pl.multiple_of(at_ref[2 * i], rows)
            column = pl.multiple_of(at_ref[2 * i + 1], width)
            spot = target.at[pl.ds(row, rows), pl.ds(column, width)]
            copies.append(pltpu.make_async_copy(source.at[pl.ds(0, rows), :], spot, sems.at[i]))
            copies[-1].start()
        for copy in copies:
            copy.wait()

    moved = 2 * sum(piece.size * 2 for piece in pieces)
    return pl.pallas_call(
        kernel,
        out_shape=jax.ShapeDtypeStruct(shape, pieces[0].dtype),
        in_specs=[smem()] + [pl.BlockSpec(memory_space=pl.ANY)] * count,
        out_specs=pl.BlockSpec(memory_space=pltpu.HBM),
        scratch_shapes=[pltpu.SemaphoreType.DMA((count,))],
        compiler_params=params(16),
        cost_estimate=cost(0, moved),
        name="place",
    )(jnp.stack([jnp.int32(v) for pair in offsets for v in pair]), *pieces)


def turn(values, cos_table, sin_table):
    width = values.shape[1]
    lane = lax.broadcasted_iota(jnp.int32, values.shape, 1)
    swapped = jnp.where(
        lane % HD < HD // 2,
        pltpu.roll(values, width - HD // 2, 1),
        pltpu.roll(values, HD // 2, 1),
    )
    return values * cos_table + swapped * sin_table


def whole(shape):
    return pl.BlockSpec(shape, lambda n: (0,) * len(shape))


def project_in(seq, z, inputs, gain, groups, cos_table, sin_table, parts):
    tokens, width = inputs.shape
    tile = cos_table.shape[1]
    each = tile // parts
    pack = tile + 2 * each
    count = len(groups)
    depth = width // count

    def kernel(at_ref, in_ref, gain_ref, *refs):
        w_refs, (cos_ref, sin_ref, acts_ref), packs = refs[:count], refs[count : count + 3], refs[count + 3 :]
        step = pl.program_id(0)

        @pl.when(step == 0)
        def _():
            values = in_ref[...].astype(F32)
            scale = lax.rsqrt(jnp.mean(values * values, axis=-1, keepdims=True) + EPSILON)
            acts_ref[...] = (values * scale * gain_ref[...]).astype(BF)

        rows = None
        for j in range(count):
            lanes = pl.ds(pl.multiple_of((at_ref[1] + count - j) % count * depth, depth), depth)
            term = dot_nn(acts_ref[:, lanes], w_refs[j][...])
            rows = term if rows is None else rows + term
        turned = jnp.where(
            step == parts + 1, rows, turn(rows, cos_ref[...], sin_ref[...])
        ).astype(BF)
        seq_now = at_ref[0]
        for k in range(parts):

            @pl.when((seq_now ^ k) == step)
            def _():
                packs[k][:, :tile] = turned

            for d in range(parts):
                for which in range(2):

                    @pl.when(((seq_now ^ k) == d) & (step == parts + which))
                    def _():
                        lane = tile + which * each
                        packs[k][:, lane : lane + each] = turned[:, d * each : (d + 1) * each]

    return pl.pallas_call(
        kernel,
        grid=(parts + 2,),
        out_shape=[jax.ShapeDtypeStruct((tokens, width), BF)]
        + [jax.ShapeDtypeStruct((tokens, pack), BF)] * parts,
        in_specs=[smem(), whole((tokens, width)), whole((1, width))]
        + [pl.BlockSpec((depth, tile), lambda n: (0, n))] * count
        + [whole((tokens, tile))] * 2,
        out_specs=[whole((tokens, width))] + [whole((tokens, pack))] * parts,
        compiler_params=params(),
        cost_estimate=cost(2 * tokens * width * tile * (parts + 2), 2 * width * tile * (parts + 2)),
        name="project_in",
    )(jnp.stack([seq, z]), inputs, gain, *groups, cos_table, sin_table)


def project_out(seq, z, mixed, inputs, gain, groups):
    parts = len(mixed)
    tokens, width = inputs.shape
    each = mixed[0].shape[1]
    tile = width // parts
    count = len(groups)
    depth = parts * each // count

    def kernel(at_ref, *refs):
        parts_in, (in_ref, gain_ref) = refs[:parts], refs[parts : parts + 2]
        w_refs, (flat_ref, res_ref, acts_ref) = refs[parts + 2 : -3], refs[-3:]
        step = pl.program_id(0)

        @pl.when(step == 0)
        def _():
            for k in range(parts):
                lane = pl.multiple_of((at_ref[0] ^ k) * each, each)
                flat_ref[:, pl.ds(lane, each)] = parts_in[k][...]

        lanes = pl.ds(pl.multiple_of(step * tile, tile), tile)
        total = in_ref[:, lanes].astype(F32)
        for j in range(count):
            rows = pl.ds(pl.multiple_of((at_ref[1] + count - j) % count * depth, depth), depth)
            total = total + dot_nn(flat_ref[:, rows], w_refs[j][...])
        res_ref[:, lanes] = total

        @pl.when(step == parts - 1)
        def _():
            values = res_ref[...]
            scale = lax.rsqrt(jnp.mean(values * values, axis=-1, keepdims=True) + EPSILON)
            acts_ref[...] = (values * scale * gain_ref[...]).astype(BF)

    return pl.pallas_call(
        kernel,
        grid=(parts,),
        out_shape=[
            jax.ShapeDtypeStruct((tokens, parts * each), BF),
            jax.ShapeDtypeStruct((tokens, width), F32),
            jax.ShapeDtypeStruct((tokens, width), BF),
        ],
        in_specs=[smem()]
        + [whole((tokens, each))] * parts
        + [whole((tokens, width)), whole((1, width))]
        + [pl.BlockSpec((depth, tile), lambda n: (0, n))] * count,
        out_specs=[whole((tokens, parts * each)), whole((tokens, width)), whole((tokens, width))],
        compiler_params=params(),
        cost_estimate=cost(2 * tokens * width * parts * each, 2 * width * parts * each),
        name="project_out",
    )(jnp.stack([seq, z]), *mixed, inputs, gain, *groups)


def feed_forward(acts, grads, gate, up, down, begun=None):
    tokens, width = acts.shape
    hidden = gate.shape[0]
    tile = 256
    steps = hidden // tile
    kind = F32 if begun is None else BF
    begun = [] if begun is None else list(begun)

    def kernel(a_ref, c_ref, g_ref, u_ref, d_ref, *refs):
        starts, (h_ref, gg_ref, gu_ref, o_ref, ga_ref, o_s, ga_s) = refs[:-7], refs[-7:]
        step = pl.program_id(0)

        @pl.when(step == 0)
        def _():
            if starts:
                o_s[...] = starts[0][...]
                ga_s[...] = starts[1][...]
            else:
                o_s[...] = jnp.zeros_like(o_s)
                ga_s[...] = jnp.zeros_like(ga_s)

        gate_act = dot_nt(a_ref[...], g_ref[...])
        up_act = dot_nt(a_ref[...], u_ref[...])
        grad_hidden = dot_nt(c_ref[...], d_ref[...])
        sigma = jax.nn.sigmoid(gate_act)
        silu = gate_act * sigma
        low = (silu * up_act).astype(BF)
        grad_gate = (grad_hidden * up_act * (sigma * (1.0 + gate_act * (1.0 - sigma)))).astype(BF)
        grad_up = (grad_hidden * silu).astype(BF)
        h_ref[...] = low
        gg_ref[...] = grad_gate
        gu_ref[...] = grad_up
        o_s[...] += dot_nn(low, d_ref[...])
        ga_s[...] += dot_nn(grad_gate, g_ref[...]) + dot_nn(grad_up, u_ref[...])

        @pl.when(step == steps - 1)
        def _():
            o_ref[...] = o_s[...].astype(kind)
            ga_ref[...] = ga_s[...].astype(kind)

    whole = pl.BlockSpec((tokens, width), lambda n: (0, 0))
    rows = pl.BlockSpec((tile, width), lambda n: (n, 0))
    lanes = pl.BlockSpec((tokens, tile), lambda n: (0, n))
    return pl.pallas_call(
        kernel,
        grid=(steps,),
        out_shape=[jax.ShapeDtypeStruct((tokens, hidden), BF)] * 3
        + [jax.ShapeDtypeStruct((tokens, width), kind)] * 2,
        in_specs=[whole, whole, rows, rows, rows] + [whole] * len(begun),
        out_specs=[lanes] * 3 + [whole] * 2,
        scratch_shapes=[pltpu.VMEM((tokens, width), F32)] * 2,
        compiler_params=params(),
        cost_estimate=cost(12 * tokens * width * hidden, 6 * width * hidden),
        name="feed_forward",
    )(acts, grads, gate, up, down, *begun)


def middle_back(seq, z, terms, residual, grad_out, gain, groups, parts):
    tokens, width = residual.shape
    tile = groups[0].shape[0]
    count = len(groups)
    assert count == parts

    def kernel(at_ref, t0_ref, t1_ref, res_ref, go_ref, gain_ref, *refs):
        w_refs, (gr_ref, low_ref, gg_ref), outs = refs[:count], refs[count : count + 3], refs[count + 3 :]
        grad = t0_ref[...].astype(F32) + t1_ref[...].astype(F32)
        values = res_ref[...]
        scale = lax.rsqrt(jnp.mean(values * values, axis=-1, keepdims=True) + EPSILON)
        weighted = grad * gain_ref[...]
        inner = jnp.mean(weighted * values, axis=-1, keepdims=True)
        result = go_ref[...].astype(F32) + scale * weighted - values * (scale**3 * inner)
        gr_ref[...] = result
        low_ref[...] = result.astype(BF)
        gg_ref[...] = jnp.sum(grad * values * scale, axis=0, keepdims=True)
        for j in range(count):
            part = dot_nt(low_ref[...], w_refs[j][...]).astype(BF)
            at = ((at_ref[1] + count - j) % count) ^ at_ref[0]
            for k in range(parts):

                @pl.when(at == k)
                def _():
                    outs[k][...] = part

    vmem = pl.BlockSpec(memory_space=pltpu.VMEM)
    return pl.pallas_call(
        kernel,
        out_shape=[
            jax.ShapeDtypeStruct((tokens, width), F32),
            jax.ShapeDtypeStruct((tokens, width), BF),
            jax.ShapeDtypeStruct((1, width), F32),
        ]
        + [jax.ShapeDtypeStruct((tokens, tile), BF)] * parts,
        in_specs=[smem()] + [vmem] * (5 + count),
        out_specs=[vmem] * (3 + parts),
        compiler_params=params(),
        cost_estimate=cost(2 * tokens * width * tile * parts, 2 * width * tile * parts + 8 * tokens * width),
        name="middle_back",
    )(jnp.stack([seq, z]), terms[0], terms[1], residual, grad_out, gain, *groups)


def unpack(seq, packs, cos_table, sin_table):
    parts = len(packs)
    tokens, tile = cos_table.shape
    each = tile // parts

    def kernel(seq_ref, *refs):
        ins, (cos_ref, sin_ref, out_ref) = refs[:parts], refs[parts:]
        for k in range(parts):
            at = seq_ref[0] ^ k
            queries = turn(ins[k][:, :tile].astype(F32), cos_ref[...], -sin_ref[...])
            out_ref[:, pl.ds(pl.multiple_of(at * tile, tile), tile)] = queries.astype(BF)
            keys = turn(
                ins[k][:, tile : tile + each].astype(F32), cos_ref[:, :each], -sin_ref[:, :each]
            )
            lane = pl.multiple_of(parts * tile + at * each, each)
            out_ref[:, pl.ds(lane, each)] = keys.astype(BF)
            lane = pl.multiple_of((parts + 1) * tile + at * each, each)
            out_ref[:, pl.ds(lane, each)] = ins[k][:, tile + each :]

    vmem = pl.BlockSpec(memory_space=pltpu.VMEM)
    return pl.pallas_call(
        kernel,
        out_shape=jax.ShapeDtypeStruct((tokens, (parts + 2) * tile), BF),
        in_specs=[smem()] + [vmem] * (parts + 2),
        out_specs=vmem,
        compiler_params=params(),
        cost_estimate=cost(0, 6 * 2**20),
        name="unpack",
    )(seq.reshape(1), *packs, cos_table, sin_table)


def inner_back(z, grad_qkv, groups, inputs, gain, grad_res):
    tokens, width = inputs.shape
    count = len(groups)
    depth = width // count

    def kernel(at_ref, gq_ref, *refs):
        w_refs, (in_ref, gain_ref, gr_ref, out_ref, gg_ref, grad_s) = refs[:count], refs[count:]
        for j in range(count):
            lanes = pl.ds(pl.multiple_of((at_ref[0] + count - j) % count * depth, depth), depth)
            grad_s[:, lanes] = dot_nt(gq_ref[...], w_refs[j][...])
        grad = grad_s[...]
        values = in_ref[...].astype(F32)
        scale = lax.rsqrt(jnp.mean(values * values, axis=-1, keepdims=True) + EPSILON)
        weighted = grad * gain_ref[...]
        inner = jnp.mean(weighted * values, axis=-1, keepdims=True)
        result = gr_ref[...] + scale * weighted - values * (scale**3 * inner)
        out_ref[...] = result.astype(BF)
        gg_ref[...] = jnp.sum(grad * values * scale, axis=0, keepdims=True)

    vmem = pl.BlockSpec(memory_space=pltpu.VMEM)
    return pl.pallas_call(
        kernel,
        out_shape=[jax.ShapeDtypeStruct((tokens, width), BF), jax.ShapeDtypeStruct((1, width), F32)],
        in_specs=[smem()] + [vmem] * (4 + count),
        out_specs=[vmem] * 2,
        scratch_shapes=[pltpu.VMEM((tokens, width), F32)],
        compiler_params=params(),
        cost_estimate=cost(2 * tokens * groups[0].size * count, 2 * groups[0].size * count),
        name="inner_back",
    )(z.reshape(1), grad_qkv, *groups, inputs, gain, grad_res)


def weight_grad(left, right, rows, blocks, half, adds=()):
    count = len(left)
    tokens = left[0].shape[0]
    width = right[0].shape[1] // 2
    tile = min(rows, 512)
    steps = rows // tile
    total_rows = rows * len(blocks)

    def kernel(at_ref, *refs):
        lefts, rights, extra, out = refs[:count], refs[count : 2 * count], refs[2 * count : -1], refs[-1]
        total = None
        for l_ref, r_ref in zip(lefts, rights):
            term = lax.dot_general(
                l_ref[...], r_ref[...], (((0,), (0,)), ((), ())), preferred_element_type=F32
            )
            total = term if total is None else total + term
        for ref in extra:
            total = total + ref[...].astype(F32)
        out[...] = total.astype(BF)

    rows_spec = pl.BlockSpec((tile, width), lambda n, at: (n, 0))
    spec = pltpu.PrefetchScalarGridSpec(
        num_scalar_prefetch=1,
        grid=(steps * len(blocks),),
        in_specs=[pl.BlockSpec((tokens, tile), lambda n, at: (0, at[1 + n]))] * count
        + [pl.BlockSpec((tokens, width), lambda n, at: (0, at[0]))] * count
        + [rows_spec] * len(adds),
        out_specs=rows_spec,
    )
    at = [jnp.int32(half)]
    for block in blocks:
        at += [jnp.int32(block) * steps + i for i in range(steps)]
    return pl.pallas_call(
        kernel,
        grid_spec=spec,
        out_shape=jax.ShapeDtypeStruct((total_rows, width), BF),
        compiler_params=params(),
        cost_estimate=cost(
            2 * tokens * count * total_rows * width, 2 * (tokens * count + total_rows) * width
        ),
        name="weight_grad",
    )(jnp.stack(at), *left, *right, *adds)


def row_grads(left, right, blocks, half, added, y, cuts):
    tokens = left.shape[0]
    width = right.shape[1] // 2
    rows = left.shape[1] // LINE
    each = rows // cuts
    count = len(blocks)

    def kernel(at_ref, l_ref, r_ref, add_ref, *refs):
        outs, total_s = refs[:-1], refs[-1]
        total = lax.dot_general(
            l_ref[...], r_ref[...], (((0,), (0,)), ((), ())), preferred_element_type=F32
        )
        total_s[...] = (total + add_ref[...].astype(F32)).astype(BF)
        for j in range(count):

            @pl.when(pl.program_id(0) == j)
            def _():
                for k in range(cuts):
                    start = pl.multiple_of((at_ref[1] + cuts - k) % cuts * each, each)
                    outs[j * cuts + k][...] = total_s[pl.ds(start, each), :]

    spec = pltpu.PrefetchScalarGridSpec(
        num_scalar_prefetch=1,
        grid=(count,),
        in_specs=[
            pl.BlockSpec((tokens, rows), lambda n, at: (0, at[2 + n])),
            pl.BlockSpec((tokens, width), lambda n, at: (0, at[0])),
            pl.BlockSpec((rows, width), lambda n, at: (n, 0)),
        ],
        out_specs=[pl.BlockSpec((each, width), lambda n, at: (0, 0))] * (count * cuts),
        scratch_shapes=[pltpu.VMEM((rows, width), BF)],
    )
    at = jnp.stack([jnp.int32(half), jnp.int32(y)] + [jnp.int32(b) for b in blocks])
    outs = pl.pallas_call(
        kernel,
        grid_spec=spec,
        out_shape=[jax.ShapeDtypeStruct((each, width), BF)] * (count * cuts),
        compiler_params=params(),
        cost_estimate=cost(2 * tokens * count * rows * width, 6 * count * rows * width),
        name="row_grads",
    )(at, left, right, added)
    return [outs[j * cuts : (j + 1) * cuts] for j in range(count)]


def join(core, mine, other, widths):
    rows, half = mine.shape
    tile = min(rows, 256)

    def kernel(core_ref, mine_ref, other_ref, *refs):
        outs, full = refs[:-1], refs[-1]
        target = outs[0] if len(outs) == 1 else full
        at = pl.multiple_of(core_ref[0] * half, half)
        target[:, pl.ds(at, half)] = mine_ref[...].astype(F32)
        at = pl.multiple_of((1 - core_ref[0]) * half, half)
        target[:, pl.ds(at, half)] = other_ref[...].astype(F32)
        if len(outs) > 1:
            lane = 0
            for out in outs:
                out[...] = full[:, lane : lane + out.shape[1]]
                lane += out.shape[1]

    def block(width):
        return pl.BlockSpec((tile, width), lambda n: (n, 0))

    return pl.pallas_call(
        kernel,
        grid=(rows // tile,),
        out_shape=[jax.ShapeDtypeStruct((rows, width), F32) for width in widths],
        in_specs=[smem(), block(half), block(half)],
        out_specs=[block(width) for width in widths],
        scratch_shapes=[pltpu.VMEM((tile, 2 * half) if len(widths) > 1 else (8, 128), F32)],
        compiler_params=params(),
        cost_estimate=cost(0, rows * half * 12),
        name="join",
    )(core.reshape(1), mine, other)
def half_of(array, which, axis=1):
    size = array.shape[axis] // 2
    return lax.dynamic_slice_in_dim(array, which * size, size, axis)


def join_halves(core, top, bottom):
    rows, half = top[0].shape
    tile = min(rows, 256)
    steps = rows // tile

    def kernel(core_ref, a_ref, b_ref, c_ref, d_ref, out):
        mine = pl.multiple_of(core_ref[0] * half, half)
        other = pl.multiple_of((1 - core_ref[0]) * half, half)
        upper = pl.program_id(0) < steps

        @pl.when(upper)
        def _():
            out[:, pl.ds(mine, half)] = a_ref[...].astype(F32)
            out[:, pl.ds(other, half)] = b_ref[...].astype(F32)

        @pl.when(jnp.logical_not(upper))
        def _():
            out[:, pl.ds(mine, half)] = c_ref[...].astype(F32)
            out[:, pl.ds(other, half)] = d_ref[...].astype(F32)

    first = pl.BlockSpec((tile, half), lambda n: (jnp.minimum(n, steps - 1), 0))
    second = pl.BlockSpec((tile, half), lambda n: (jnp.maximum(n - steps, 0), 0))
    return pl.pallas_call(
        kernel,
        grid=(2 * steps,),
        out_shape=jax.ShapeDtypeStruct((2 * rows, 2 * half), F32),
        in_specs=[smem(), first, first, second, second],
        out_specs=pl.BlockSpec((tile, 2 * half), lambda n: (n, 0)),
        compiler_params=params(),
        cost_estimate=cost(0, rows * half * 24),
        name="join_halves",
    )(core.reshape(1), *top, *bottom)


class Order:
    def __init__(self):
        self.marks = ()

    def tie(self, *values):
        if self.marks:
            values = lax.optimization_barrier(tuple(values) + self.marks)[: len(values)]
        return values[0] if len(values) == 1 else list(values)

    def done(self, *values):
        self.marks = tuple(values)


def y_hops(value):
    return ring_gather(value, y_next, columns())[1:]


def add_low(left, right):
    return (left.astype(F32) + right.astype(F32)).astype(BF)


def rope_tables(positions, repeat):
    frequency = THETA ** (-(jnp.arange(HD // 2, dtype=F32) * 2.0) / HD)
    angles = positions.astype(F32)[:, None] * frequency[None, :]
    cos, sin = jnp.cos(angles), jnp.sin(angles)
    return (
        jnp.tile(jnp.concatenate([cos, cos], axis=1), (1, repeat)),
        jnp.tile(jnp.concatenate([-sin, sin], axis=1), (1, repeat)),
    )


def exchange(packs):
    return [packs[0]] + [seq_swap(packs[k], k) for k in range(1, len(packs))]


def shards(
    inputs,
    query_weight,
    key_weight,
    value_weight,
    output_weight,
    gate_weight,
    up_weight,
    down_weight,
    gain_attn,
    gain_ffn,
    cotangent,
):
    seq_count, local_len, width = inputs.shape
    assert seq_count == 1
    tokens = local_len
    parts = lax.axis_size("seq")
    kv_local = KVH // parts
    cols = columns()
    seq = lax.axis_index("seq")
    core, side = seq % 2, seq // 2
    fsdp = lax.axis_index("fsdp")
    z, y = fsdp // cols, fsdp % cols
    q_width, kv_width = query_weight.shape[1], key_weight.shape[1]
    heads_local = q_width // HD // parts
    flat_in = inputs.reshape(tokens, width)
    grad_out = cotangent.reshape(tokens, width)

    qkv_shard = jnp.concatenate([query_weight, key_weight, value_weight], axis=1)
    rows = qkv_shard.shape[0]
    part, half = rows // 2, qkv_shard.shape[1] // 2
    positions = seq * local_len + jnp.arange(local_len)
    cos_table, sin_table = rope_tables(positions, kv_width // HD)
    order = Order()

    def swapped(pieces):
        return [core_swap(p) for p in pieces]

    def place_halves(pieces, others, whole_first=None):
        each = pieces[-1].shape[1]
        placed, offsets = [], []
        for k, (piece, other) in enumerate(zip(pieces, others)):
            row = (y - k) % cols * rows
            if k == 0 and whole_first is not None:
                placed.append(whole_first)
                offsets.append((row, 0))
            else:
                placed += [piece, other]
                offsets += [(row, core * each), (row, (1 - core) * each)]
        return place((rows * cols, 2 * each), placed, offsets)

    def place_quarters(pieces, others, sides, count, size, first):
        each = pieces[0].shape[1]
        placed, offsets = [], []
        for i, (piece, other) in enumerate(zip(pieces, others)):
            k, at = i // 2, sides[i % 2]
            row = first(k) * size + at * (size // 2)
            placed += [piece, other]
            offsets += [(row, core * each), (row, (1 - core) * each)]
        return place((size * count, 2 * each), placed, offsets)

    def line_row(k):
        return (y - k) % cols

    own = (gate_weight, up_weight, down_weight)
    far_rows = gate_weight.shape[0]
    far_part = far_rows // 4
    far_y, far_x = {}, {}

    def far_start(i, h):
        at = side * 2 * far_part + h * far_part
        return lax.dynamic_slice(own[i], (at, core * out_width), (far_part, out_width))

    out_width = width // 2
    far_starts = {(i, h): far_start(i, h) for i in range(3) for h in range(2)}

    def far_along_y(i, h):
        start = order.tie(far_starts[i, h]) if order.marks else far_starts[i, h]
        far_y[i, h] = y_hops(start)
        return far_y[i, h]

    def far_along_x(i, h):
        pieces = order.tie(*far_y[i, h], far_y[i, h][0])[:-1]
        far_x[i, h] = [x_swap(p) for p in pieces]
        return far_x[i, h]

    gains = jnp.concatenate([gain_attn, gain_ffn]).reshape(1, 2 * rows)
    start = half_of(qkv_shard, core)
    start = jnp.concatenate([start, jnp.pad(gains, ((0, 15), (0, half - 2 * rows)))], axis=0)
    out_half = half_of(output_weight, core)

    def quarter_of(piece):
        return lax.dynamic_slice_in_dim(piece, side * part, part, 0)

    def line_group(i):
        here = order.tie(line[i])
        placed, offsets = [], []
        row = y * rows
        if i:
            placed += [here, core_swap(here)]
            offsets += [(row, core * half), (row, (1 - core) * half)]
        else:
            placed.append(qkv_shard)
            offsets.append((row, 0))
        for k in range(1, cols):
            row = (y - k) % cols * rows
            if i < LINE - 1:
                for piece, at in ((beside[i][k - 1], side), (crossed[i][k - 1], 1 - side)):
                    piece = order.tie(piece)
                    placed += [piece, core_swap(piece)]
                    offsets += [
                        (row + at * part, core * half),
                        (row + at * part, (1 - core) * half),
                    ]
            else:
                piece = order.tie(beside[i][k - 1])
                placed += [piece, core_swap(piece)]
                offsets += [(row, core * half), (row, (1 - core) * half)]
        return place((rows * cols, 2 * half), placed, offsets, rows)

    line, beside, crossed, groups = [start], [], [], []
    for j in range(LINE):
        here = order.tie(line[j]) if j else line[j]
        if j + 1 < LINE:
            line.append(z_next(here))
            beside.append(y_hops(quarter_of(here)))
            marks = [line[j + 1]] + beside[j] + far_along_y(j // 2, j % 2)
        else:
            beside.append(y_hops(here))
            line_o = [out_half, z_next(order.tie(out_half))]
            grad_parts = [grad_out, z_next(order.tie(grad_out))]
            gains_near = jnp.concatenate([p[rows:, : 2 * rows] for p in line[:j]], axis=0)
            gains_far = y_hops(order.tie(gains_near))
            marks = beside[j] + [line_o[1]]
        if j:
            pieces = order.tie(*beside[j - 1], here)[:-1]
            crossed.append([x_swap(p) for p in pieces])
            marks += crossed[j - 1]
        if j > 1:
            groups.append(line_group(j - 2))
            marks.append(groups[-1])
        if j == 0:
            marks += [cos_table, sin_table] + list(far_starts.values())
        order.done(*marks)

    line_o.append(z_next(order.tie(line_o[1])))
    beside_o = [y_hops(order.tie(line_o[0])), y_hops(order.tie(line_o[1]))]
    groups += [line_group(LINE - 2), line_group(LINE - 1)]
    marks = far_along_x(0, 0)
    gain_full = jnp.zeros((2, width), BF)
    for j in range(LINE):
        for k in range(cols):
            if j == LINE - 1:
                g = line[j][rows] if k == 0 else beside[j][k - 1][rows]
                pair = g[: 2 * rows].reshape(2, rows)
            else:
                g = gains_near if k == 0 else gains_far[k - 1]
                pair = g[16 * j].reshape(2, rows)
            at = (((z - j) % LINE) * cols + (y - k) % cols) * rows
            gain_full = lax.dynamic_update_slice(gain_full, pair, (0, at))
    gain_one = gain_full[:1].astype(F32)
    gain_two = gain_full[1:].astype(F32)
    acts_one, *sent = project_in(seq, z, flat_in, gain_one, groups, cos_table, sin_table, parts)
    order.done(*sent, line_o[2], *beside_o[0], *beside_o[1], grad_parts[1], *marks)

    def out_group(j):
        hops = order.tie(line_o[j], *beside_o[j])
        if j == 0:
            return place_halves([None] + hops[1:], [None] + swapped(hops[1:]), output_weight)
        return place_halves(hops, swapped(hops))

    packs = exchange(order.tie(*sent))
    line_o.append(z_next(order.tie(line_o[2])))
    beside_o.append(y_hops(order.tie(line_o[2])))
    order.done(*packs, line_o[3], *beside_o[2])

    beside_o.append(y_hops(order.tie(line_o[3])))
    grad_parts.append(z_next(order.tie(grad_parts[1])))
    out_groups = [out_group(0), out_group(1), out_group(2)]
    marks = far_along_x(0, 1) + far_along_x(1, 0)
    *mixed_sent, log_totals = attend_forward(seq, order.tie(*packs), heads_local, kv_local)
    order.done(*mixed_sent, *beside_o[3], grad_parts[2], *out_groups, *marks)

    mixed = exchange(order.tie(*mixed_sent))
    grad_parts.append(z_next(order.tie(grad_parts[2])))
    out_groups.append(out_group(3))
    order.done(*mixed, out_groups[3])

    marks = far_along_y(1, 1)
    mixed_flat, residual, acts_two = project_out(
        seq, z, order.tie(*mixed), flat_in, gain_two, out_groups
    )
    order.done(acts_two, grad_parts[3], *marks)

    def far_place(i):
        placed, offsets = [], []
        for k in range(cols - 1):
            for h in range(2):
                pieces = order.tie(far_y[i, h][k], far_x[i, h][k])
                for piece, at in zip(pieces, (side, 1 - side)):
                    row = k * far_rows + at * 2 * far_part + h * far_part
                    placed += [piece, core_swap(piece)]
                    offsets += [(row, core * out_width), (row, (1 - core) * out_width)]
        return place((far_rows * (cols - 1), width), placed, offsets)

    acts_parts, far, near_done, far_done = [acts_two], [], [], [None] * LINE

    def run_near(j):
        near_done.append(feed_forward(order.tie(acts_parts[j]), grad_parts[j], *own))
        return near_done[j][3]

    def run_far(j):
        far_done[j] = feed_forward(order.tie(acts_parts[j]), grad_parts[j], *far, near_done[j][3:])
        return far_done[j][4]

    acts_parts.append(z_next(order.tie(acts_parts[0])))
    marks = far_along_y(2, 0) + far_along_y(2, 1) + far_along_x(1, 1)
    far.append(far_place(0))
    order.done(acts_parts[1], *marks, *far, run_near(0))
    acts_parts.append(z_next(order.tie(acts_parts[1])))
    marks = far_along_x(2, 0) + far_along_x(2, 1)
    far.append(far_place(1))
    order.done(acts_parts[2], *marks, *far, run_near(1))
    acts_parts.append(z_next(order.tie(acts_parts[2])))
    far.append(far_place(2))
    marks = [run_near(2), run_far(1)]
    order.done(acts_parts[3], *marks)

    passed = z_next(order.tie(far_done[1][4]))
    marks = [run_near(3), run_far(2)]
    order.done(passed, *marks)
    passed = z_next(order.tie(add_low(passed, far_done[2][4])))
    marks = [run_far(3), run_far(0)]
    order.done(passed, *marks)
    passed = z_next(order.tie(add_low(passed, far_done[3][4])))

    rights = (grad_parts, acts_parts, acts_parts)
    far_size = far_rows * (cols - 1)
    far_sent, far_total, own_sent = [None] * 3, {}, [None] * 3

    def of(done, which):
        return order.tie(*[d[which] for d in done])

    def send_far(i):
        far_sent[i] = weight_grad(of(far_done, i), rights[i], far_size, [0], 1 - core)
        return far_sent[i]

    def keep_far(i):
        return weight_grad(of(far_done, i), rights[i], far_size, [0], core, [far_sent[i]])

    def pass_far(i, kept, h, cut=2):
        size = far_rows // cut
        kept = order.tie(kept)
        total = y_next(kept[h * size : (h + 1) * size])
        for k in range(1, cols - 1):
            start = k * far_rows + h * size
            total = y_next(add_low(total, kept[start : start + size]))
        far_total[i, h] = total
        return total

    def send_own(i):
        own_sent[i] = weight_grad(of(near_done, i), rights[i], far_rows, [0], 1 - core)
        return own_sent[i]

    def keep_own(i):
        return weight_grad(of(near_done, i), rights[i], far_rows, [0], core, [own_sent[i]])

    marks = [send_far(0), send_far(1), send_far(2), send_own(0)]
    order.done(passed, *marks)

    far_sent = [core_swap(order.tie(term)) for term in far_sent]
    ffn_parts = [d[3] for d in far_done]
    ffn_sum = z_next(order.tie(ffn_parts[1]))
    grad_res, grad_res_low, grad_gain_two, *grad_sent = middle_back(
        seq, z, order.tie(passed, far_done[0][4]), residual, grad_out, gain_two, out_groups, parts
    )
    order.done(*grad_sent, *far_sent)

    grad_packs = exchange(order.tie(*grad_sent))
    kept = [keep_far(0), keep_far(1)]
    order.done(*grad_packs, ffn_sum, *kept)

    marks = [pass_far(0, kept[0], 0)]
    ffn_sum = z_next(order.tie(add_low(ffn_sum, ffn_parts[2])))
    back_sent = attend_backward(
        seq, log_totals, packs, order.tie(*grad_packs), heads_local, kv_local
    )
    order.done(*back_sent, *marks)

    line_order = list(range(1, LINE)) + [0]
    blocks = [(z - j) % LINE for j in line_order]
    line_rows = rows * cols
    back_packs = exchange(order.tie(*back_sent))
    own_sent[0] = core_swap(order.tie(own_sent[0]))
    out_left, out_right = order.tie(mixed_flat, grad_res_low)
    out_sent = weight_grad([out_left], [out_right], line_rows, blocks, 1 - core)
    marks = [pass_far(0, kept[0], 1), keep_far(2), keep_own(0), out_sent]
    own_low = [marks[2]]
    kept.append(marks[1])
    order.done(*back_packs, *marks, ffn_sum)

    size = far_rows // 2
    sums = {}

    def along_x(i, h):
        low = add_low(order.tie(own_low[i])[h * size : (h + 1) * size], far_total[i, h])
        sums[i, h] = (low, x_swap(low))
        return sums[i, h][1]

    def finish(i, h):
        low, crossed = order.tie(*sums[i, h])
        total = add_low(low, crossed)
        sums[i, h] = (total, core_swap(total))
        return sums[i, h][1]

    def joined(i):
        pairs = order.tie(*sums[i, 0], *sums[i, 1])
        return join_halves(core, pairs[:2], pairs[2:])

    def along_y(terms):
        terms = order.tie(*terms, terms[0])[:-1]
        total = None
        for k in list(range(1, cols)) + [0]:
            total = terms[k] if total is None else add_low(y_next(total), terms[k])
        return total

    marks = [pass_far(1, kept[1], 0), along_x(0, 0)]
    out_recv = core_swap(order.tie(out_sent))
    ffn_sum = z_next(order.tie(add_low(ffn_sum, ffn_parts[3])))
    grad_qkv = unpack(seq, order.tie(*back_packs), cos_table, sin_table)
    qkv_sent = weight_grad([acts_one], [grad_qkv], line_rows, blocks, 1 - core)
    out_terms = row_grads(out_left, out_right, blocks, core, out_recv, y, 1)
    out_terms = [t[0] for t in out_terms]
    order.done(qkv_sent, ffn_sum, *out_terms, *marks)

    qkv_recv = core_swap(order.tie(qkv_sent))
    out_total = z_next(order.tie(out_terms[0]))
    marks = [pass_far(1, kept[1], 1), send_own(1), send_own(2), along_x(0, 1), finish(0, 0)]
    order.done(qkv_recv, out_total, *marks)

    out_total = z_next(order.tie(add_low(out_total, out_terms[1])))
    qkv_terms = row_grads(acts_one, grad_qkv, blocks, core, order.tie(qkv_recv), y, cols)
    own_sent[1] = core_swap(order.tie(own_sent[1]))
    own_low.append(keep_own(1))
    marks = [pass_far(2, kept[2], 0), own_low[1], finish(0, 1)]
    order.done(*[t for terms in qkv_terms for t in terms], out_total, *marks)

    out_total = z_next(order.tie(add_low(out_total, out_terms[2])))
    hops = [along_y(qkv_terms[0])]
    own_sent[2] = core_swap(order.tie(own_sent[2]))
    own_low.append(keep_own(2))
    d_down = joined(0)
    part_one = pass_far(2, kept[2], 2, 4)
    order.done(hops[0], out_total, own_low[2], d_down, part_one, along_x(1, 0))

    passed = z_next(order.tie(hops[0]))
    hops.append(along_y(qkv_terms[1]))
    grad_inputs, grad_gain_one = inner_back(z, order.tie(grad_qkv), groups, flat_in, gain_one, grad_res)
    part_two = pass_far(2, kept[2], 3, 4)
    marks = [part_two, along_x(1, 1), finish(1, 0), grad_inputs]
    order.done(passed, hops[1], *marks)
    far_total[2, 1] = jnp.concatenate([part_one, part_two], axis=0)

    passed = z_next(order.tie(add_low(passed, hops[1])))
    hops.append(along_y(qkv_terms[2]))
    out_total = order.tie(add_low(out_total, out_terms[3]))
    pieces = [
        lax.dynamic_slice_in_dim(out_total, (y - k) % cols * rows, rows, 0) for k in range(cols)
    ]
    out_low = along_y(pieces)
    gain_sums = jnp.concatenate([grad_gain_one, grad_gain_two], axis=0)
    steps = sum_steps()
    gain_sums = order.tie(gain_sums)
    for step in steps[:2]:
        gain_sums = gain_sums + step(gain_sums)
    marks = [along_x(2, 0), finish(1, 1), gain_sums]
    order.done(passed, hops[2], out_low, *marks)

    passed = z_next(order.tie(add_low(passed, hops[2])))
    hops.append(along_y(qkv_terms[3]))
    marks = [along_x(2, 1)]
    out_cross = x_swap(order.tie(out_low))
    outputs = (residual + ffn_sum.astype(F32) + order.tie(ffn_parts[0]).astype(F32)).astype(BF)
    d_gate = joined(1)
    gain_sums = order.tie(gain_sums)
    for step in steps[2:-1]:
        gain_sums = gain_sums + step(gain_sums)
    marks += [finish(2, 0), d_gate, outputs, gain_sums]
    order.done(passed, hops[3], out_cross, *marks)

    low = order.tie(add_low(passed, hops[3]))
    crossed = x_swap(low)
    finish(2, 1)
    d_up = joined(2)
    out_low = add_low(out_low, order.tie(out_cross))
    d_out = join(core, out_low, core_swap(out_low), [width])
    gain_sums = order.tie(gain_sums)
    gain_sums = gain_sums + steps[-1](gain_sums)
    order.done(crossed, d_up, d_out[0], gain_sums)
    total = order.tie(add_low(low, crossed))
    d_qkv = join(core, total, core_swap(total), [q_width, kv_width, kv_width])

    gain_sums = lax.dynamic_slice_in_dim(gain_sums, fsdp * rows, rows, 1)
    return (
        outputs.reshape(inputs.shape),
        grad_inputs.reshape(inputs.shape),
        d_qkv[0],
        d_qkv[1],
        d_qkv[2],
        d_out[0],
        d_gate,
        d_up,
        d_down,
        gain_sums[0],
        gain_sums[1],
    )


def solution(mesh):
    token_spec, row_spec, gain_spec = P("fsdp", "seq", None), P("fsdp", None), P("fsdp")
    return jax.shard_map(
        shards,
        mesh=mesh,
        in_specs=(token_spec,) + (row_spec,) * 7 + (gain_spec,) * 2 + (token_spec,),
        out_specs=(token_spec,) * 2 + (row_spec,) * 7 + (gain_spec,) * 2,
        check_vma=False,
    )
```

```python
import functools

import jax
import jax.numpy as jnp
from jax import lax
from jax.experimental import pallas as pl
from jax.experimental.pallas import tpu as pltpu
from jax.sharding import PartitionSpec as P

KVH = 8
HD = 64
BLOCK = 256
LINE = 4

EPSILON = 1e-05
THETA = 500000.0
LOG2E = 1.4426950408889634

BF = jnp.bfloat16
F32 = jnp.float32


def after(value, *others):
    return lax.optimization_barrier((value,) + others)[0]


def columns():
    return lax.axis_size("fsdp") // LINE


def z_next(value):
    cols = columns()
    count = lax.axis_size("fsdp")
    return lax.ppermute(value, "fsdp", [(i, (i + cols) % count) for i in range(count)])


def y_next(value):
    cols = columns()
    count = lax.axis_size("fsdp")
    return lax.ppermute(
        value, "fsdp", [(i, i // cols * cols + (i + 1) % cols) for i in range(count)]
    )


def seq_swap(value, bit):
    return lax.ppermute(value, "seq", [(i, i ^ bit) for i in range(lax.axis_size("seq"))])


def core_swap(value):
    return seq_swap(value, 1)


def x_swap(value):
    return seq_swap(value, 2)


def ring_gather(value, step, count):
    pieces = [value]
    for _ in range(count - 1):
        pieces.append(step(pieces[-1]))
    return pieces


def ring_scatter(part_of, step, count):
    total = None
    for j in list(range(1, count)) + [0]:
        total = part_of(j) if total is None else part_of(j) + total.astype(F32)
        if j:
            total = step(total.astype(BF))
    return total


def sum_steps():
    steps = []
    bit = 1
    while bit < lax.axis_size("seq"):
        steps.append(functools.partial(seq_swap, bit=bit))
        bit *= 2
    count = lax.axis_size("fsdp")
    bit = 1
    while bit < count:
        pairs = [(i, i ^ bit) for i in range(count)]
        steps.append(functools.partial(lax.ppermute, axis_name="fsdp", perm=pairs))
        bit *= 2
    return steps


def dot_nt(a, b):
    return lax.dot_general(a, b, (((1,), (1,)), ((), ())), preferred_element_type=F32)

def dot_nn(a, b):
    return jnp.dot(a, b, preferred_element_type=F32)


def attend_forward_kernel(parts, heads, kv, seq_ref, *refs):
    packs, outs = refs[:parts], refs[parts : 2 * parts]
    lse_ref, q_s, k_s, vt_s, o_s = refs[2 * parts :]
    tokens = packs[0].shape[0]
    seq = seq_ref[0]
    group = heads // kv
    for k in range(parts):
        rows = pl.ds(pl.multiple_of((seq ^ k) * tokens, tokens), tokens)
        q_s[rows, :] = packs[k][:, : heads * HD]
        for g in range(kv):
            lane = (heads + g) * HD
            k_s[g, rows, :] = packs[k][:, lane : lane + HD]
            lane = (heads + kv + g) * HD
            vt_s[g, :, rows] = packs[k][:, lane : lane + HD].T
    full = parts * tokens
    for g in range(kv):
        for i in range(full // BLOCK):
            keys = (i + 1) * BLOCK
            rows = slice(i * BLOCK, keys)
            for pair in range(group // 2):
                halves = []
                for h in (g * group + 2 * pair, g * group + 2 * pair + 1):
                    scores = dot_nt(k_s[g, :keys, :], q_s[rows, h * HD : (h + 1) * HD])
                    scores = scores * (HD**-0.5 * LOG2E)
                    top = jnp.max(scores, axis=0, keepdims=True)
                    powers = jnp.exp2(scores - top)
                    total = jnp.sum(powers, axis=0, keepdims=True)
                    halves.append(dot_nn(vt_s[g, :, :keys], powers.astype(BF)) / total)
                    lse_ref[h : h + 1, rows] = top + jnp.log2(total)
                lane = (g * group + 2 * pair) * HD
                o_s[rows, lane : lane + 2 * HD] = jnp.concatenate(halves, axis=0).T.astype(BF)
    for k in range(parts):
        rows = pl.ds(pl.multiple_of((seq ^ k) * tokens, tokens), tokens)
        outs[k][...] = o_s[rows, :]


def attend_forward(seq, packs, heads, kv):
    parts = len(packs)
    tokens = packs[0].shape[0]
    full = parts * tokens
    vmem = pl.BlockSpec(memory_space=pltpu.VMEM)
    flops = 4 * heads * full * full * HD * 5 // 8
    return pl.pallas_call(
        functools.partial(attend_forward_kernel, parts, heads, kv),
        out_shape=[jax.ShapeDtypeStruct((tokens, heads * HD), BF)] * parts
        + [jax.ShapeDtypeStruct((heads, full), F32)],
        in_specs=[pl.BlockSpec(memory_space=pltpu.SMEM)] + [vmem] * parts,
        out_specs=[vmem] * (parts + 1),
        scratch_shapes=[
            pltpu.VMEM((full, heads * HD), BF),
            pltpu.VMEM((kv, full, HD), BF),
            pltpu.VMEM((kv, HD, full), BF),
            pltpu.VMEM((full, heads * HD), BF),
        ],
        compiler_params=pltpu.CompilerParams(vmem_limit_bytes=48 * 2**20),
        cost_estimate=cost(flops * 4, 4 * 2**20),
        name="attend_forward",
    )(seq.reshape(1), *packs)


def attend_backward_kernel(parts, heads, kv, seq_ref, lse_ref, *refs):
    packs, grads, outs = refs[:parts], refs[parts : 2 * parts], refs[2 * parts : 3 * parts]
    q_s, k_s, kt_s, v_s, g_s, dq_s, dk_s, dv_s = refs[3 * parts :]
    tokens = packs[0].shape[0]
    seq = seq_ref[0]
    group = heads // kv
    for k in range(parts):
        rows = pl.ds(pl.multiple_of((seq ^ k) * tokens, tokens), tokens)
        q_s[rows, :] = packs[k][:, : heads * HD]
        g_s[rows, :] = grads[k][...]
        for g in range(kv):
            lane = (heads + g) * HD
            k_s[g, rows, :] = packs[k][:, lane : lane + HD]
            kt_s[g, :, rows] = packs[k][:, lane : lane + HD].T
            lane = (heads + kv + g) * HD
            v_s[g, rows, :] = packs[k][:, lane : lane + HD]
    full = parts * tokens
    dk_s[...] = jnp.zeros_like(dk_s)
    dv_s[...] = jnp.zeros_like(dv_s)
    for g in range(kv):
        for i in range(full // BLOCK):
            keys = (i + 1) * BLOCK
            rows = slice(i * BLOCK, keys)
            for pair in range(group // 2):
                halves = []
                for h in (g * group + 2 * pair, g * group + 2 * pair + 1):
                    query = q_s[rows, h * HD : (h + 1) * HD]
                    grad = g_s[rows, h * HD : (h + 1) * HD]
                    scores = dot_nt(k_s[g, :keys, :], query) * (HD**-0.5 * LOG2E)
                    probs = jnp.exp2(scores - lse_ref[h : h + 1, rows])
                    grad_probs = dot_nt(v_s[g, :keys, :], grad)
                    inner = jnp.sum(probs * grad_probs, axis=0, keepdims=True)
                    grad_scores = (probs * (grad_probs - inner)).astype(BF)
                    dv_s[g, :keys, :] += dot_nn(probs.astype(BF), grad)
                    dk_s[g, :keys, :] += dot_nn(grad_scores, query)
                    halves.append(dot_nn(kt_s[g, :, :keys], grad_scores) * HD**-0.5)
                lane = (g * group + 2 * pair) * HD
                dq_s[rows, lane : lane + 2 * HD] = jnp.concatenate(halves, axis=0).T.astype(BF)
    for k in range(parts):
        rows = pl.ds(pl.multiple_of((seq ^ k) * tokens, tokens), tokens)
        outs[k][:, : heads * HD] = dq_s[rows, :]
        for g in range(kv):
            lane = (heads + g) * HD
            outs[k][:, lane : lane + HD] = (dk_s[g, rows, :] * HD**-0.5).astype(BF)
            lane = (heads + kv + g) * HD
            outs[k][:, lane : lane + HD] = dv_s[g, rows, :].astype(BF)


def attend_backward(seq, lse, packs, grads, heads, kv):
    parts = len(packs)
    tokens = packs[0].shape[0]
    full = parts * tokens
    vmem = pl.BlockSpec(memory_space=pltpu.VMEM)
    flops = 10 * heads * full * full * HD * 5 // 8
    return pl.pallas_call(
        functools.partial(attend_backward_kernel, parts, heads, kv),
        out_shape=[jax.ShapeDtypeStruct(packs[0].shape, BF)] * parts,
        in_specs=[pl.BlockSpec(memory_space=pltpu.SMEM)] + [vmem] * (2 * parts + 1),
        out_specs=[vmem] * parts,
        scratch_shapes=[
            pltpu.VMEM((full, heads * HD), BF),
            pltpu.VMEM((kv, full, HD), BF),
            pltpu.VMEM((kv, HD, full), BF),
            pltpu.VMEM((kv, full, HD), BF),
            pltpu.VMEM((full, heads * HD), BF),
            pltpu.VMEM((full, heads * HD), BF),
            pltpu.VMEM((kv, full, HD), F32),
            pltpu.VMEM((kv, full, HD), F32),
        ],
        compiler_params=pltpu.CompilerParams(vmem_limit_bytes=48 * 2**20),
        cost_estimate=cost(flops * 4, 8 * 2**20),
        name="attend_backward",
    )(seq.reshape(1), lse, *packs, *grads)


def smem():
    return pl.BlockSpec(memory_space=pltpu.SMEM)


def params(mib=56):
    return pltpu.CompilerParams(vmem_limit_bytes=mib * 2**20)


def cost(flops, moved):
    return pl.CostEstimate(flops=flops // 8, bytes_accessed=moved // 8, transcendentals=0)


def place(shape, pieces, offsets, most=None):
    count = len(pieces)

    def kernel(at_ref, *refs):
        sources, target, sems = refs[:-2], refs[-2], refs[-1]
        copies = []
        for i, source in enumerate(sources):
            rows, width = source.shape
            rows = min(rows, most or rows)
            row = pl.multiple_of(at_ref[2 * i], rows)
            column = pl.multiple_of(at_ref[2 * i + 1], width)
            spot = target.at[pl.ds(row, rows), pl.ds(column, width)]
            copies.append(pltpu.make_async_copy(source.at[pl.ds(0, rows), :], spot, sems.at[i]))
            copies[-1].start()
        for copy in copies:
            copy.wait()

    moved = 2 * sum(piece.size * 2 for piece in pieces)
    return pl.pallas_call(
        kernel,
        out_shape=jax.ShapeDtypeStruct(shape, pieces[0].dtype),
        in_specs=[smem()] + [pl.BlockSpec(memory_space=pl.ANY)] * count,
        out_specs=pl.BlockSpec(memory_space=pltpu.HBM),
        scratch_shapes=[pltpu.SemaphoreType.DMA((count,))],
        compiler_params=params(16),
        cost_estimate=cost(0, moved),
        name="place",
    )(jnp.stack([jnp.int32(v) for pair in offsets for v in pair]), *pieces)


def turn(values, cos_table, sin_table):
    width = values.shape[1]
    lane = lax.broadcasted_iota(jnp.int32, values.shape, 1)
    swapped = jnp.where(
        lane % HD < HD // 2,
        pltpu.roll(values, width - HD // 2, 1),
        pltpu.roll(values, HD // 2, 1),
    )
    return values * cos_table + swapped * sin_table


def whole(shape):
    return pl.BlockSpec(shape, lambda n: (0,) * len(shape))


def project_in(seq, z, inputs, gain, groups, cos_table, sin_table, parts):
    tokens, width = inputs.shape
    tile = cos_table.shape[1]
    each = tile // parts
    pack = tile + 2 * each
    count = len(groups)
    depth = width // count

    def kernel(at_ref, in_ref, gain_ref, *refs):
        w_refs, (cos_ref, sin_ref, acts_ref), packs = refs[:count], refs[count : count + 3], refs[count + 3 :]
        step = pl.program_id(0)

        @pl.when(step == 0)
        def _():
            values = in_ref[...].astype(F32)
            scale = lax.rsqrt(jnp.mean(values * values, axis=-1, keepdims=True) + EPSILON)
            acts_ref[...] = (values * scale * gain_ref[...]).astype(BF)

        rows = None
        for j in range(count):
            lanes = pl.ds(pl.multiple_of((at_ref[1] + count - j) % count * depth, depth), depth)
            term = dot_nn(acts_ref[:, lanes], w_refs[j][...])
            rows = term if rows is None else rows + term
        turned = jnp.where(
            step == parts + 1, rows, turn(rows, cos_ref[...], sin_ref[...])
        ).astype(BF)
        seq_now = at_ref[0]
        for k in range(parts):

            @pl.when((seq_now ^ k) == step)
            def _():
                packs[k][:, :tile] = turned

            for d in range(parts):
                for which in range(2):

                    @pl.when(((seq_now ^ k) == d) & (step == parts + which))
                    def _():
                        lane = tile + which * each
                        packs[k][:, lane : lane + each] = turned[:, d * each : (d + 1) * each]

    return pl.pallas_call(
        kernel,
        grid=(parts + 2,),
        out_shape=[jax.ShapeDtypeStruct((tokens, width), BF)]
        + [jax.ShapeDtypeStruct((tokens, pack), BF)] * parts,
        in_specs=[smem(), whole((tokens, width)), whole((1, width))]
        + [pl.BlockSpec((depth, tile), lambda n: (0, n))] * count
        + [whole((tokens, tile))] * 2,
        out_specs=[whole((tokens, width))] + [whole((tokens, pack))] * parts,
        compiler_params=params(),
        cost_estimate=cost(2 * tokens * width * tile * (parts + 2), 2 * width * tile * (parts + 2)),
        name="project_in",
    )(jnp.stack([seq, z]), inputs, gain, *groups, cos_table, sin_table)


def project_out(seq, z, mixed, inputs, gain, groups):
    parts = len(mixed)
    tokens, width = inputs.shape
    each = mixed[0].shape[1]
    tile = width // parts
    count = len(groups)
    depth = parts * each // count

    def kernel(at_ref, *refs):
        parts_in, (in_ref, gain_ref) = refs[:parts], refs[parts : parts + 2]
        w_refs, (flat_ref, res_ref, acts_ref) = refs[parts + 2 : -3], refs[-3:]
        step = pl.program_id(0)

        @pl.when(step == 0)
        def _():
            for k in range(parts):
                lane = pl.multiple_of((at_ref[0] ^ k) * each, each)
                flat_ref[:, pl.ds(lane, each)] = parts_in[k][...]

        lanes = pl.ds(pl.multiple_of(step * tile, tile), tile)
        total = in_ref[:, lanes].astype(F32)
        for j in range(count):
            rows = pl.ds(pl.multiple_of((at_ref[1] + count - j) % count * depth, depth), depth)
            total = total + dot_nn(flat_ref[:, rows], w_refs[j][...])
        res_ref[:, lanes] = total

        @pl.when(step == parts - 1)
        def _():
            values = res_ref[...]
            scale = lax.rsqrt(jnp.mean(values * values, axis=-1, keepdims=True) + EPSILON)
            acts_ref[...] = (values * scale * gain_ref[...]).astype(BF)

    return pl.pallas_call(
        kernel,
        grid=(parts,),
        out_shape=[
            jax.ShapeDtypeStruct((tokens, parts * each), BF),
            jax.ShapeDtypeStruct((tokens, width), F32),
            jax.ShapeDtypeStruct((tokens, width), BF),
        ],
        in_specs=[smem()]
        + [whole((tokens, each))] * parts
        + [whole((tokens, width)), whole((1, width))]
        + [pl.BlockSpec((depth, tile), lambda n: (0, n))] * count,
        out_specs=[whole((tokens, parts * each)), whole((tokens, width)), whole((tokens, width))],
        compiler_params=params(),
        cost_estimate=cost(2 * tokens * width * parts * each, 2 * width * parts * each),
        name="project_out",
    )(jnp.stack([seq, z]), *mixed, inputs, gain, *groups)


def feed_forward(acts, grads, gate, up, down, begun=None):
    tokens, width = acts.shape
    hidden = gate.shape[0]
    tile = 256
    steps = hidden // tile
    kind = F32 if begun is None else BF
    begun = [] if begun is None else list(begun)

    def kernel(a_ref, c_ref, g_ref, u_ref, d_ref, *refs):
        starts, (h_ref, gg_ref, gu_ref, o_ref, ga_ref, o_s, ga_s) = refs[:-7], refs[-7:]
        step = pl.program_id(0)

        @pl.when(step == 0)
        def _():
            if starts:
                o_s[...] = starts[0][...]
                ga_s[...] = starts[1][...]
            else:
                o_s[...] = jnp.zeros_like(o_s)
                ga_s[...] = jnp.zeros_like(ga_s)

        gate_act = dot_nt(a_ref[...], g_ref[...])
        up_act = dot_nt(a_ref[...], u_ref[...])
        grad_hidden = dot_nt(c_ref[...], d_ref[...])
        sigma = jax.nn.sigmoid(gate_act)
        silu = gate_act * sigma
        low = (silu * up_act).astype(BF)
        grad_gate = (grad_hidden * up_act * (sigma * (1.0 + gate_act * (1.0 - sigma)))).astype(BF)
        grad_up = (grad_hidden * silu).astype(BF)
        h_ref[...] = low
        gg_ref[...] = grad_gate
        gu_ref[...] = grad_up
        o_s[...] += dot_nn(low, d_ref[...])
        ga_s[...] += dot_nn(grad_gate, g_ref[...]) + dot_nn(grad_up, u_ref[...])

        @pl.when(step == steps - 1)
        def _():
            o_ref[...] = o_s[...].astype(kind)
            ga_ref[...] = ga_s[...].astype(kind)

    whole = pl.BlockSpec((tokens, width), lambda n: (0, 0))
    rows = pl.BlockSpec((tile, width), lambda n: (n, 0))
    lanes = pl.BlockSpec((tokens, tile), lambda n: (0, n))
    return pl.pallas_call(
        kernel,
        grid=(steps,),
        out_shape=[jax.ShapeDtypeStruct((tokens, hidden), BF)] * 3
        + [jax.ShapeDtypeStruct((tokens, width), kind)] * 2,
        in_specs=[whole, whole, rows, rows, rows] + [whole] * len(begun),
        out_specs=[lanes] * 3 + [whole] * 2,
        scratch_shapes=[pltpu.VMEM((tokens, width), F32)] * 2,
        compiler_params=params(),
        cost_estimate=cost(12 * tokens * width * hidden, 6 * width * hidden),
        name="feed_forward",
    )(acts, grads, gate, up, down, *begun)


def middle_back(seq, z, terms, residual, grad_out, gain, groups, parts):
    tokens, width = residual.shape
    tile = groups[0].shape[0]
    count = len(groups)
    assert count == parts

    def kernel(at_ref, t0_ref, t1_ref, res_ref, go_ref, gain_ref, *refs):
        w_refs, (gr_ref, low_ref, gg_ref), outs = refs[:count], refs[count : count + 3], refs[count + 3 :]
        grad = t0_ref[...].astype(F32) + t1_ref[...].astype(F32)
        values = res_ref[...]
        scale = lax.rsqrt(jnp.mean(values * values, axis=-1, keepdims=True) + EPSILON)
        weighted = grad * gain_ref[...]
        inner = jnp.mean(weighted * values, axis=-1, keepdims=True)
        result = go_ref[...].astype(F32) + scale * weighted - values * (scale**3 * inner)
        gr_ref[...] = result
        low_ref[...] = result.astype(BF)
        gg_ref[...] = jnp.sum(grad * values * scale, axis=0, keepdims=True)
        for j in range(count):
            part = dot_nt(low_ref[...], w_refs[j][...]).astype(BF)
            at = ((at_ref[1] + count - j) % count) ^ at_ref[0]
            for k in range(parts):

                @pl.when(at == k)
                def _():
                    outs[k][...] = part

    vmem = pl.BlockSpec(memory_space=pltpu.VMEM)
    return pl.pallas_call(
        kernel,
        out_shape=[
            jax.ShapeDtypeStruct((tokens, width), F32),
            jax.ShapeDtypeStruct((tokens, width), BF),
            jax.ShapeDtypeStruct((1, width), F32),
        ]
        + [jax.ShapeDtypeStruct((tokens, tile), BF)] * parts,
        in_specs=[smem()] + [vmem] * (5 + count),
        out_specs=[vmem] * (3 + parts),
        compiler_params=params(),
        cost_estimate=cost(2 * tokens * width * tile * parts, 2 * width * tile * parts + 8 * tokens * width),
        name="middle_back",
    )(jnp.stack([seq, z]), terms[0], terms[1], residual, grad_out, gain, *groups)


def unpack(seq, packs, cos_table, sin_table):
    parts = len(packs)
    tokens, tile = cos_table.shape
    each = tile // parts

    def kernel(seq_ref, *refs):
        ins, (cos_ref, sin_ref, out_ref) = refs[:parts], refs[parts:]
        for k in range(parts):
            at = seq_ref[0] ^ k
            queries = turn(ins[k][:, :tile].astype(F32), cos_ref[...], -sin_ref[...])
            out_ref[:, pl.ds(pl.multiple_of(at * tile, tile), tile)] = queries.astype(BF)
            keys = turn(
                ins[k][:, tile : tile + each].astype(F32), cos_ref[:, :each], -sin_ref[:, :each]
            )
            lane = pl.multiple_of(parts * tile + at * each, each)
            out_ref[:, pl.ds(lane, each)] = keys.astype(BF)
            lane = pl.multiple_of((parts + 1) * tile + at * each, each)
            out_ref[:, pl.ds(lane, each)] = ins[k][:, tile + each :]

    vmem = pl.BlockSpec(memory_space=pltpu.VMEM)
    return pl.pallas_call(
        kernel,
        out_shape=jax.ShapeDtypeStruct((tokens, (parts + 2) * tile), BF),
        in_specs=[smem()] + [vmem] * (parts + 2),
        out_specs=vmem,
        compiler_params=params(),
        cost_estimate=cost(0, 6 * 2**20),
        name="unpack",
    )(seq.reshape(1), *packs, cos_table, sin_table)


def inner_back(z, grad_qkv, groups, inputs, gain, grad_res):
    tokens, width = inputs.shape
    count = len(groups)
    depth = width // count

    def kernel(at_ref, gq_ref, *refs):
        w_refs, (in_ref, gain_ref, gr_ref, out_ref, gg_ref, grad_s) = refs[:count], refs[count:]
        for j in range(count):
            lanes = pl.ds(pl.multiple_of((at_ref[0] + count - j) % count * depth, depth), depth)
            grad_s[:, lanes] = dot_nt(gq_ref[...], w_refs[j][...])
        grad = grad_s[...]
        values = in_ref[...].astype(F32)
        scale = lax.rsqrt(jnp.mean(values * values, axis=-1, keepdims=True) + EPSILON)
        weighted = grad * gain_ref[...]
        inner = jnp.mean(weighted * values, axis=-1, keepdims=True)
        result = gr_ref[...] + scale * weighted - values * (scale**3 * inner)
        out_ref[...] = result.astype(BF)
        gg_ref[...] = jnp.sum(grad * values * scale, axis=0, keepdims=True)

    vmem = pl.BlockSpec(memory_space=pltpu.VMEM)
    return pl.pallas_call(
        kernel,
        out_shape=[jax.ShapeDtypeStruct((tokens, width), BF), jax.ShapeDtypeStruct((1, width), F32)],
        in_specs=[smem()] + [vmem] * (4 + count),
        out_specs=[vmem] * 2,
        scratch_shapes=[pltpu.VMEM((tokens, width), F32)],
        compiler_params=params(),
        cost_estimate=cost(2 * tokens * groups[0].size * count, 2 * groups[0].size * count),
        name="inner_back",
    )(z.reshape(1), grad_qkv, *groups, inputs, gain, grad_res)


def weight_grad(left, right, rows, blocks, half, adds=()):
    count = len(left)
    tokens = left[0].shape[0]
    width = right[0].shape[1] // 2
    tile = min(rows, 512)
    steps = rows // tile
    total_rows = rows * len(blocks)

    def kernel(at_ref, *refs):
        lefts, rights, extra, out = refs[:count], refs[count : 2 * count], refs[2 * count : -1], refs[-1]
        total = None
        for l_ref, r_ref in zip(lefts, rights):
            term = lax.dot_general(
                l_ref[...], r_ref[...], (((0,), (0,)), ((), ())), preferred_element_type=F32
            )
            total = term if total is None else total + term
        for ref in extra:
            total = total + ref[...].astype(F32)
        out[...] = total.astype(BF)

    rows_spec = pl.BlockSpec((tile, width), lambda n, at: (n, 0))
    spec = pltpu.PrefetchScalarGridSpec(
        num_scalar_prefetch=1,
        grid=(steps * len(blocks),),
        in_specs=[pl.BlockSpec((tokens, tile), lambda n, at: (0, at[1 + n]))] * count
        + [pl.BlockSpec((tokens, width), lambda n, at: (0, at[0]))] * count
        + [rows_spec] * len(adds),
        out_specs=rows_spec,
    )
    at = [jnp.int32(half)]
    for block in blocks:
        at += [jnp.int32(block) * steps + i for i in range(steps)]
    return pl.pallas_call(
        kernel,
        grid_spec=spec,
        out_shape=jax.ShapeDtypeStruct((total_rows, width), BF),
        compiler_params=params(),
        cost_estimate=cost(
            2 * tokens * count * total_rows * width, 2 * (tokens * count + total_rows) * width
        ),
        name="weight_grad",
    )(jnp.stack(at), *left, *right, *adds)


def row_grads(left, right, blocks, half, added, y, cuts):
    tokens = left.shape[0]
    width = right.shape[1] // 2
    rows = left.shape[1] // LINE
    each = rows // cuts
    count = len(blocks)

    def kernel(at_ref, l_ref, r_ref, add_ref, *refs):
        outs, total_s = refs[:-1], refs[-1]
        total = lax.dot_general(
            l_ref[...], r_ref[...], (((0,), (0,)), ((), ())), preferred_element_type=F32
        )
        total_s[...] = (total + add_ref[...].astype(F32)).astype(BF)
        for j in range(count):

            @pl.when(pl.program_id(0) == j)
            def _():
                for k in range(cuts):
                    start = pl.multiple_of((at_ref[1] + cuts - k) % cuts * each, each)
                    outs[j * cuts + k][...] = total_s[pl.ds(start, each), :]

    spec = pltpu.PrefetchScalarGridSpec(
        num_scalar_prefetch=1,
        grid=(count,),
        in_specs=[
            pl.BlockSpec((tokens, rows), lambda n, at: (0, at[2 + n])),
            pl.BlockSpec((tokens, width), lambda n, at: (0, at[0])),
            pl.BlockSpec((rows, width), lambda n, at: (n, 0)),
        ],
        out_specs=[pl.BlockSpec((each, width), lambda n, at: (0, 0))] * (count * cuts),
        scratch_shapes=[pltpu.VMEM((rows, width), BF)],
    )
    at = jnp.stack([jnp.int32(half), jnp.int32(y)] + [jnp.int32(b) for b in blocks])
    outs = pl.pallas_call(
        kernel,
        grid_spec=spec,
        out_shape=[jax.ShapeDtypeStruct((each, width), BF)] * (count * cuts),
        compiler_params=params(),
        cost_estimate=cost(2 * tokens * count * rows * width, 6 * count * rows * width),
        name="row_grads",
    )(at, left, right, added)
    return [outs[j * cuts : (j + 1) * cuts] for j in range(count)]


def join(core, mine, other, widths):
    rows, half = mine.shape
    tile = min(rows, 256)

    def kernel(core_ref, mine_ref, other_ref, *refs):
        outs, full = refs[:-1], refs[-1]
        target = outs[0] if len(outs) == 1 else full
        at = pl.multiple_of(core_ref[0] * half, half)
        target[:, pl.ds(at, half)] = mine_ref[...].astype(F32)
        at = pl.multiple_of((1 - core_ref[0]) * half, half)
        target[:, pl.ds(at, half)] = other_ref[...].astype(F32)
        if len(outs) > 1:
            lane = 0
            for out in outs:
                out[...] = full[:, lane : lane + out.shape[1]]
                lane += out.shape[1]

    def block(width):
        return pl.BlockSpec((tile, width), lambda n: (n, 0))

    return pl.pallas_call(
        kernel,
        grid=(rows // tile,),
        out_shape=[jax.ShapeDtypeStruct((rows, width), F32) for width in widths],
        in_specs=[smem(), block(half), block(half)],
        out_specs=[block(width) for width in widths],
        scratch_shapes=[pltpu.VMEM((tile, 2 * half) if len(widths) > 1 else (8, 128), F32)],
        compiler_params=params(),
        cost_estimate=cost(0, rows * half * 12),
        name="join",
    )(core.reshape(1), mine, other)
def half_of(array, which, axis=1):
    size = array.shape[axis] // 2
    return lax.dynamic_slice_in_dim(array, which * size, size, axis)


def join_halves(core, top, bottom):
    rows, half = top[0].shape
    tile = min(rows, 256)
    steps = rows // tile

    def kernel(core_ref, a_ref, b_ref, c_ref, d_ref, out):
        mine = pl.multiple_of(core_ref[0] * half, half)
        other = pl.multiple_of((1 - core_ref[0]) * half, half)
        upper = pl.program_id(0) < steps

        @pl.when(upper)
        def _():
            out[:, pl.ds(mine, half)] = a_ref[...].astype(F32)
            out[:, pl.ds(other, half)] = b_ref[...].astype(F32)

        @pl.when(jnp.logical_not(upper))
        def _():
            out[:, pl.ds(mine, half)] = c_ref[...].astype(F32)
            out[:, pl.ds(other, half)] = d_ref[...].astype(F32)

    first = pl.BlockSpec((tile, half), lambda n: (jnp.minimum(n, steps - 1), 0))
    second = pl.BlockSpec((tile, half), lambda n: (jnp.maximum(n - steps, 0), 0))
    return pl.pallas_call(
        kernel,
        grid=(2 * steps,),
        out_shape=jax.ShapeDtypeStruct((2 * rows, 2 * half), F32),
        in_specs=[smem(), first, first, second, second],
        out_specs=pl.BlockSpec((tile, 2 * half), lambda n: (n, 0)),
        compiler_params=params(),
        cost_estimate=cost(0, rows * half * 24),
        name="join_halves",
    )(core.reshape(1), *top, *bottom)


class Order:
    def __init__(self):
        self.marks = ()

    def tie(self, *values):
        if self.marks:
            values = lax.optimization_barrier(tuple(values) + self.marks)[: len(values)]
        return values[0] if len(values) == 1 else list(values)

    def done(self, *values):
        self.marks = tuple(values)


def y_hops(value):
    return ring_gather(value, y_next, columns())[1:]


def add_low(left, right):
    return (left.astype(F32) + right.astype(F32)).astype(BF)


def rope_tables(positions, repeat):
    frequency = THETA ** (-(jnp.arange(HD // 2, dtype=F32) * 2.0) / HD)
    angles = positions.astype(F32)[:, None] * frequency[None, :]
    cos, sin = jnp.cos(angles), jnp.sin(angles)
    return (
        jnp.tile(jnp.concatenate([cos, cos], axis=1), (1, repeat)),
        jnp.tile(jnp.concatenate([-sin, sin], axis=1), (1, repeat)),
    )


def exchange(packs):
    return [packs[0]] + [seq_swap(packs[k], k) for k in range(1, len(packs))]


def shards(
    inputs,
    query_weight,
    key_weight,
    value_weight,
    output_weight,
    gate_weight,
    up_weight,
    down_weight,
    gain_attn,
    gain_ffn,
    cotangent,
):
    seq_count, local_len, width = inputs.shape
    assert seq_count == 1
    tokens = local_len
    parts = lax.axis_size("seq")
    kv_local = KVH // parts
    cols = columns()
    seq = lax.axis_index("seq")
    core, side = seq % 2, seq // 2
    fsdp = lax.axis_index("fsdp")
    z, y = fsdp // cols, fsdp % cols
    q_width, kv_width = query_weight.shape[1], key_weight.shape[1]
    heads_local = q_width // HD // parts
    flat_in = inputs.reshape(tokens, width)
    grad_out = cotangent.reshape(tokens, width)

    qkv_shard = jnp.concatenate([query_weight, key_weight, value_weight], axis=1)
    rows = qkv_shard.shape[0]
    part, half = rows // 2, qkv_shard.shape[1] // 2
    positions = seq * local_len + jnp.arange(local_len)
    cos_table, sin_table = rope_tables(positions, kv_width // HD)
    order = Order()

    def swapped(pieces):
        return [core_swap(p) for p in pieces]

    def place_halves(pieces, others, whole_first=None):
        each = pieces[-1].shape[1]
        placed, offsets = [], []
        for k, (piece, other) in enumerate(zip(pieces, others)):
            row = (y - k) % cols * rows
            if k == 0 and whole_first is not None:
                placed.append(whole_first)
                offsets.append((row, 0))
            else:
                placed += [piece, other]
                offsets += [(row, core * each), (row, (1 - core) * each)]
        return place((rows * cols, 2 * each), placed, offsets)

    def place_quarters(pieces, others, sides, count, size, first):
        each = pieces[0].shape[1]
        placed, offsets = [], []
        for i, (piece, other) in enumerate(zip(pieces, others)):
            k, at = i // 2, sides[i % 2]
            row = first(k) * size + at * (size // 2)
            placed += [piece, other]
            offsets += [(row, core * each), (row, (1 - core) * each)]
        return place((size * count, 2 * each), placed, offsets)

    def line_row(k):
        return (y - k) % cols

    own = (gate_weight, up_weight, down_weight)
    far_rows = gate_weight.shape[0]
    far_part = far_rows // 4
    far_y, far_x = {}, {}

    def far_start(i, h):
        at = side * 2 * far_part + h * far_part
        return lax.dynamic_slice(own[i], (at, core * out_width), (far_part, out_width))

    out_width = width // 2
    far_starts = {(i, h): far_start(i, h) for i in range(3) for h in range(2)}

    def far_along_y(i, h):
        start = order.tie(far_starts[i, h]) if order.marks else far_starts[i, h]
        far_y[i, h] = y_hops(start)
        return far_y[i, h]

    def far_along_x(i, h):
        pieces = order.tie(*far_y[i, h], far_y[i, h][0])[:-1]
        far_x[i, h] = [x_swap(p) for p in pieces]
        return far_x[i, h]

    gains = jnp.concatenate([gain_attn, gain_ffn]).reshape(1, 2 * rows)
    start = half_of(qkv_shard, core)
    start = jnp.concatenate([start, jnp.pad(gains, ((0, 15), (0, half - 2 * rows)))], axis=0)
    out_half = half_of(output_weight, core)

    def quarter_of(piece):
        return lax.dynamic_slice_in_dim(piece, side * part, part, 0)

    def line_group(i):
        here = order.tie(line[i])
        placed, offsets = [], []
        row = y * rows
        if i:
            placed += [here, core_swap(here)]
            offsets += [(row, core * half), (row, (1 - core) * half)]
        else:
            placed.append(qkv_shard)
            offsets.append((row, 0))
        for k in range(1, cols):
            row = (y - k) % cols * rows
            if i < LINE - 1:
                for piece, at in ((beside[i][k - 1], side), (crossed[i][k - 1], 1 - side)):
                    piece = order.tie(piece)
                    placed += [piece, core_swap(piece)]
                    offsets += [
                        (row + at * part, core * half),
                        (row + at * part, (1 - core) * half),
                    ]
            else:
                piece = order.tie(beside[i][k - 1])
                placed += [piece, core_swap(piece)]
                offsets += [(row, core * half), (row, (1 - core) * half)]
        return place((rows * cols, 2 * half), placed, offsets, rows)

    line, beside, crossed, groups = [start], [], [], []
    for j in range(LINE):
        here = order.tie(line[j]) if j else line[j]
        if j + 1 < LINE:
            line.append(z_next(here))
            beside.append(y_hops(quarter_of(here)))
            marks = [line[j + 1]] + beside[j] + far_along_y(j // 2, j % 2)
        else:
            beside.append(y_hops(here))
            line_o = [out_half, z_next(order.tie(out_half))]
            grad_parts = [grad_out, z_next(order.tie(grad_out))]
            gains_near = jnp.concatenate([p[rows:, : 2 * rows] for p in line[:j]], axis=0)
            gains_far = y_hops(order.tie(gains_near))
            marks = beside[j] + [line_o[1]]
        if j:
            pieces = order.tie(*beside[j - 1], here)[:-1]
            crossed.append([x_swap(p) for p in pieces])
            marks += crossed[j - 1]
        if j > 1:
            groups.append(line_group(j - 2))
            marks.append(groups[-1])
        if j == 1:
            marks += [cos_table, sin_table] + list(far_starts.values())
        order.done(*marks)

    line_o.append(z_next(order.tie(line_o[1])))
    beside_o = [y_hops(order.tie(line_o[0])), y_hops(order.tie(line_o[1]))]
    groups += [line_group(LINE - 2), line_group(LINE - 1)]
    marks = far_along_x(0, 0)
    gain_full = jnp.zeros((2, width), BF)
    for j in range(LINE):
        for k in range(cols):
            if j == LINE - 1:
                g = line[j][rows] if k == 0 else beside[j][k - 1][rows]
                pair = g[: 2 * rows].reshape(2, rows)
            else:
                g = gains_near if k == 0 else gains_far[k - 1]
                pair = g[16 * j].reshape(2, rows)
            at = (((z - j) % LINE) * cols + (y - k) % cols) * rows
            gain_full = lax.dynamic_update_slice(gain_full, pair, (0, at))
    gain_one = gain_full[:1].astype(F32)
    gain_two = gain_full[1:].astype(F32)
    acts_one, *sent = project_in(seq, z, flat_in, gain_one, groups, cos_table, sin_table, parts)
    order.done(*sent, line_o[2], *beside_o[0], *beside_o[1], grad_parts[1], *marks)

    def out_group(j, *others):
        hops = order.tie(line_o[j], *beside_o[j], *others)[: cols]
        if j == 0:
            return place_halves([None] + hops[1:], [None] + swapped(hops[1:]), output_weight)
        return place_halves(hops, swapped(hops))

    packs = exchange(order.tie(*sent))
    line_o.append(z_next(order.tie(line_o[2])))
    beside_o.append(y_hops(order.tie(line_o[2])))
    out_groups = [out_group(0, line_o[3]), out_group(1, line_o[3])]
    grad_top = [z_next(order.tie(grad_parts[1][: tokens // 2], line_o[3])[0])]
    order.done(*packs, line_o[3], *beside_o[2], *out_groups, grad_top[0])

    beside_o.append(y_hops(order.tie(line_o[3])))
    grad_low = [z_next(order.tie(grad_parts[1])[tokens // 2 :])]
    marks = far_along_x(0, 1) + grad_low
    out_groups.append(out_group(2))
    *mixed_sent, log_totals = attend_forward(seq, order.tie(*packs), heads_local, kv_local)
    order.done(*mixed_sent, *beside_o[3], *marks, out_groups[2])

    mixed = exchange(order.tie(*mixed_sent))
    out_groups.append(out_group(3))
    grad_top.append(z_next(order.tie(grad_top[0])))
    order.done(*mixed, out_groups[3], grad_top[1])

    grad_low.append(z_next(order.tie(grad_low[0])))
    grad_parts += [jnp.concatenate(pair, axis=0) for pair in zip(grad_top, grad_low)]
    marks = far_along_y(1, 1) + far_along_x(1, 0) + [grad_low[1]]
    mixed_flat, residual, acts_two = project_out(
        seq, z, order.tie(*mixed), flat_in, gain_two, out_groups
    )
    order.done(acts_two, *marks)

    def far_place(i):
        placed, offsets = [], []
        for k in range(cols - 1):
            for h in range(2):
                pieces = order.tie(far_y[i, h][k], far_x[i, h][k])
                for piece, at in zip(pieces, (side, 1 - side)):
                    row = k * far_rows + at * 2 * far_part + h * far_part
                    placed += [piece, core_swap(piece)]
                    offsets += [(row, core * out_width), (row, (1 - core) * out_width)]
        return place((far_rows * (cols - 1), width), placed, offsets)

    acts_parts, far, near_done, far_done = [acts_two], [], [], [None] * LINE

    def run_near(j):
        near_done.append(feed_forward(order.tie(acts_parts[j]), grad_parts[j], *own))
        return near_done[j][3]

    def run_far(j):
        far_done[j] = feed_forward(order.tie(acts_parts[j]), grad_parts[j], *far, near_done[j][3:])
        return far_done[j][4]

    acts_parts.append(z_next(order.tie(acts_parts[0])))
    marks = far_along_y(2, 0) + far_along_y(2, 1) + far_along_x(1, 1)
    far.append(far_place(0))
    order.done(acts_parts[1], *marks, *far, run_near(0))
    acts_parts.append(z_next(order.tie(acts_parts[1])))
    marks = far_along_x(2, 0) + far_along_x(2, 1)
    far.append(far_place(1))
    order.done(acts_parts[2], *marks, *far, run_near(1))
    acts_parts.append(z_next(order.tie(acts_parts[2])))
    far.append(far_place(2))
    marks = [run_near(2), run_far(1)]
    order.done(acts_parts[3], *marks)

    passed = z_next(order.tie(far_done[1][4]))
    marks = [run_near(3), run_far(2)]
    order.done(passed, *marks)
    passed = z_next(order.tie(add_low(passed, far_done[2][4])))
    marks = [run_far(3), run_far(0)]
    order.done(passed, *marks)
    passed = z_next(order.tie(add_low(passed, far_done[3][4])))

    rights = (grad_parts, acts_parts, acts_parts)
    far_size = far_rows * (cols - 1)
    far_sent, far_total, own_sent = [None] * 3, {}, [None] * 3

    def of(done, which):
        return order.tie(*[d[which] for d in done])

    def send_far(i):
        far_sent[i] = weight_grad(of(far_done, i), rights[i], far_size, [0], 1 - core)
        return far_sent[i]

    def keep_far(i):
        return weight_grad(of(far_done, i), rights[i], far_size, [0], core, [far_sent[i]])

    def pass_far(i, kept, h):
        size = far_rows // 2
        kept = order.tie(kept)
        total = y_next(kept[h * size : (h + 1) * size])
        for k in range(1, cols - 1):
            start = k * far_rows + h * size
            total = y_next(add_low(total, kept[start : start + size]))
        far_total[i, h] = total
        return total

    def send_own(i):
        own_sent[i] = weight_grad(of(near_done, i), rights[i], far_rows, [0], 1 - core)
        return own_sent[i]

    def keep_own(i):
        return weight_grad(of(near_done, i), rights[i], far_rows, [0], core, [own_sent[i]])

    first = send_far(0)
    far_sent[0] = core_swap(first)
    marks = [send_far(1), send_far(2)]
    kept = [keep_far(0)]
    order.done(passed, *kept, *marks)

    marks = [pass_far(0, kept[0], 0)]
    far_sent[1:] = [core_swap(order.tie(term)) for term in far_sent[1:]]
    ffn_parts = [d[3] for d in far_done]
    ffn_sum = z_next(order.tie(ffn_parts[1]))
    grad_res, grad_res_low, grad_gain_two, *grad_sent = middle_back(
        seq, z, order.tie(passed, far_done[0][4]), residual, grad_out, gain_two, out_groups, parts
    )
    order.done(*grad_sent, *far_sent[1:])

    grad_packs = exchange(order.tie(*grad_sent))
    kept.append(keep_far(1))
    first = send_own(0)
    order.done(*grad_packs, ffn_sum, kept[1], first, *marks)

    marks = [pass_far(0, kept[0], 1)]
    ffn_sum = z_next(order.tie(add_low(ffn_sum, ffn_parts[2])))
    back_sent = attend_backward(
        seq, log_totals, packs, order.tie(*grad_packs), heads_local, kv_local
    )
    order.done(*back_sent, *marks)

    line_order = list(range(1, LINE)) + [0]
    blocks = [(z - j) % LINE for j in line_order]
    line_rows = rows * cols
    back_packs = exchange(order.tie(*back_sent))
    own_sent[0] = core_swap(order.tie(own_sent[0]))
    out_left, out_right = order.tie(mixed_flat, grad_res_low)
    out_sent = weight_grad([out_left], [out_right], line_rows, blocks, 1 - core)
    marks = [pass_far(1, kept[1], 0), keep_far(2), keep_own(0), out_sent]
    own_low = [marks[2]]
    kept.append(marks[1])
    order.done(*back_packs, *marks, ffn_sum)

    size = far_rows // 2
    sums = {}

    def along_x(i, h):
        low = add_low(order.tie(own_low[i])[h * size : (h + 1) * size], far_total[i, h])
        sums[i, h] = (low, x_swap(low))
        return sums[i, h][1]

    def finish(i, h):
        low, crossed = order.tie(*sums[i, h])
        total = add_low(low, crossed)
        sums[i, h] = (total, core_swap(total))
        return sums[i, h][1]

    def joined(i):
        pairs = order.tie(*sums[i, 0], *sums[i, 1])
        return join_halves(core, pairs[:2], pairs[2:])

    def along_y(terms):
        terms = order.tie(*terms, terms[0])[:-1]
        total = None
        for k in list(range(1, cols)) + [0]:
            total = terms[k] if total is None else add_low(y_next(total), terms[k])
        return total

    marks = [pass_far(1, kept[1], 1), along_x(0, 0)]
    out_recv = core_swap(order.tie(out_sent))
    ffn_sum = z_next(order.tie(add_low(ffn_sum, ffn_parts[3])))
    grad_qkv = unpack(seq, order.tie(*back_packs), cos_table, sin_table)
    qkv_sent = weight_grad([acts_one], [grad_qkv], line_rows, blocks, 1 - core)
    out_terms = row_grads(out_left, out_right, blocks, core, out_recv, y, 1)
    out_terms = [t[0] for t in out_terms]
    marks.append(send_own(1))
    order.done(qkv_sent, ffn_sum, *out_terms, *marks)

    qkv_recv = core_swap(order.tie(qkv_sent))
    out_total = z_next(order.tie(out_terms[0]))
    own_sent[1] = core_swap(order.tie(own_sent[1]))
    marks = [pass_far(2, kept[2], 0), send_own(2), along_x(0, 1), finish(0, 0)]
    own_low.append(keep_own(1))
    order.done(qkv_recv, out_total, own_low[1], *marks)

    out_total = z_next(order.tie(add_low(out_total, out_terms[1])))
    qkv_terms = row_grads(acts_one, grad_qkv, blocks, core, order.tie(qkv_recv), y, cols)
    own_sent[2] = core_swap(order.tie(own_sent[2]))
    own_low.append(keep_own(2))
    marks = [pass_far(2, kept[2], 1), along_x(1, 0), own_low[2], finish(0, 1)]
    order.done(*[t for terms in qkv_terms for t in terms], out_total, *marks)

    out_total = z_next(order.tie(add_low(out_total, out_terms[2])))
    hops = [along_y(qkv_terms[0])]
    d_down = joined(0)
    marks = [along_x(1, 1), finish(1, 0)]
    order.done(hops[0], out_total, d_down, *marks)

    passed = z_next(order.tie(hops[0]))
    hops.append(along_y(qkv_terms[1]))
    grad_inputs, grad_gain_one = inner_back(z, order.tie(grad_qkv), groups, flat_in, gain_one, grad_res)
    out_total = order.tie(add_low(out_total, out_terms[3]))
    pieces = [
        lax.dynamic_slice_in_dim(out_total, (y - k) % cols * rows, rows, 0) for k in range(cols)
    ]
    out_low = along_y(pieces)
    marks = [out_low, along_x(2, 0), finish(1, 1), grad_inputs]
    order.done(passed, hops[1], *marks)

    passed = z_next(order.tie(add_low(passed, hops[1])))
    hops.append(along_y(qkv_terms[2]))
    gain_sums = jnp.concatenate([grad_gain_one, grad_gain_two], axis=0)
    steps = sum_steps()
    gain_sums = gain_sums + steps[0](order.tie(gain_sums))
    d_gate = joined(1)
    marks = [along_x(2, 1), finish(2, 0), d_gate, gain_sums]
    order.done(passed, hops[2], *marks)

    passed = z_next(order.tie(add_low(passed, hops[2])))
    hops.append(along_y(qkv_terms[3]))
    out_cross = x_swap(order.tie(out_low))
    outputs = (residual + ffn_sum.astype(F32) + order.tie(ffn_parts[0]).astype(F32)).astype(BF)
    gain_sums = gain_sums + steps[1](order.tie(gain_sums))
    finish(2, 1)
    d_up = joined(2)
    order.done(passed, hops[3], out_cross, d_up, outputs, gain_sums)

    low = order.tie(add_low(passed, hops[3]))
    crossed = x_swap(low)
    out_low = add_low(out_low, order.tie(out_cross))
    d_out = join(core, out_low, core_swap(out_low), [width])
    gain_sums = order.tie(gain_sums)
    for step in steps[2:-1]:
        gain_sums = gain_sums + step(gain_sums)
    order.done(crossed, d_out[0], gain_sums)
    gain_sums = gain_sums + steps[-1](order.tie(gain_sums))
    total = order.tie(add_low(low, crossed))
    d_qkv = join(core, total, core_swap(total), [q_width, kv_width, kv_width])

    gain_sums = lax.dynamic_slice_in_dim(gain_sums, fsdp * rows, rows, 1)
    return (
        outputs.reshape(inputs.shape),
        grad_inputs.reshape(inputs.shape),
        d_qkv[0],
        d_qkv[1],
        d_qkv[2],
        d_out[0],
        d_gate,
        d_up,
        d_down,
        gain_sums[0],
        gain_sums[1],
    )


def solution(mesh):
    token_spec, row_spec, gain_spec = P("fsdp", "seq", None), P("fsdp", None), P("fsdp")
    return jax.shard_map(
        shards,
        mesh=mesh,
        in_specs=(token_spec,) + (row_spec,) * 7 + (gain_spec,) * 2 + (token_spec,),
        out_specs=(token_spec,) * 2 + (row_spec,) * 7 + (gain_spec,) * 2,
        check_vma=False,
    )
```

```python
import functools
import math

import jax
import jax.numpy as jnp
from jax import lax
from jax.experimental import pallas as pl
from jax.experimental.pallas import tpu as pltpu
from jax.sharding import PartitionSpec as P

KVH = 8
HD = 64
BLOCK = 256
LINE = 4

EPSILON = 1e-05
THETA = 500000.0
LOG2E = 1.4426950408889634

BF = jnp.bfloat16
F32 = jnp.float32


def after(value, *others):
    return lax.optimization_barrier((value,) + others)[0]


def columns():
    return lax.axis_size("fsdp") // LINE


def z_next(value):
    cols = columns()
    count = lax.axis_size("fsdp")
    return lax.ppermute(value, "fsdp", [(i, (i + cols) % count) for i in range(count)])


def y_next(value):
    cols = columns()
    count = lax.axis_size("fsdp")
    return lax.ppermute(
        value, "fsdp", [(i, i // cols * cols + (i + 1) % cols) for i in range(count)]
    )


def seq_swap(value, bit):
    return lax.ppermute(value, "seq", [(i, i ^ bit) for i in range(lax.axis_size("seq"))])


def core_swap(value):
    return seq_swap(value, 1)


def x_swap(value):
    return seq_swap(value, 2)


def ring_gather(value, step, count):
    pieces = [value]
    for _ in range(count - 1):
        pieces.append(step(pieces[-1]))
    return pieces


def ring_scatter(part_of, step, count):
    total = None
    for j in list(range(1, count)) + [0]:
        total = part_of(j) if total is None else part_of(j) + total.astype(F32)
        if j:
            total = step(total.astype(BF))
    return total


def sum_steps():
    steps = []
    bit = 1
    while bit < lax.axis_size("seq"):
        steps.append(functools.partial(seq_swap, bit=bit))
        bit *= 2
    count = lax.axis_size("fsdp")
    bit = 1
    while bit < count:
        pairs = [(i, i ^ bit) for i in range(count)]
        steps.append(functools.partial(lax.ppermute, axis_name="fsdp", perm=pairs))
        bit *= 2
    return steps


def dot_nt(a, b):
    return lax.dot_general(a, b, (((1,), (1,)), ((), ())), preferred_element_type=F32)

def dot_nn(a, b):
    return jnp.dot(a, b, preferred_element_type=F32)


def attend_forward_kernel(parts, heads, kv, seq_ref, *refs):
    packs, outs = refs[:parts], refs[parts : 2 * parts]
    lse_ref, q_s, k_s, vt_s, o_s = refs[2 * parts :]
    tokens = packs[0].shape[0]
    seq = seq_ref[0]
    group = heads // kv
    for k in range(parts):
        rows = pl.ds(pl.multiple_of((seq ^ k) * tokens, tokens), tokens)
        q_s[rows, :] = packs[k][:, : heads * HD]
        for g in range(kv):
            lane = (heads + g) * HD
            k_s[g, rows, :] = packs[k][:, lane : lane + HD]
            lane = (heads + kv + g) * HD
            vt_s[g, :, rows] = packs[k][:, lane : lane + HD].T
    full = parts * tokens
    for g in range(kv):
        for i in range(full // BLOCK):
            keys = (i + 1) * BLOCK
            rows = slice(i * BLOCK, keys)
            for pair in range(group // 2):
                halves = []
                for h in (g * group + 2 * pair, g * group + 2 * pair + 1):
                    scores = dot_nt(k_s[g, :keys, :], q_s[rows, h * HD : (h + 1) * HD])
                    scores = scores * (HD**-0.5 * LOG2E)
                    top = jnp.max(scores, axis=0, keepdims=True)
                    powers = jnp.exp2(scores - top)
                    total = jnp.sum(powers, axis=0, keepdims=True)
                    halves.append(dot_nn(vt_s[g, :, :keys], powers.astype(BF)) / total)
                    lse_ref[h : h + 1, rows] = top + jnp.log2(total)
                lane = (g * group + 2 * pair) * HD
                o_s[rows, lane : lane + 2 * HD] = jnp.concatenate(halves, axis=0).T.astype(BF)
    for k in range(parts):
        rows = pl.ds(pl.multiple_of((seq ^ k) * tokens, tokens), tokens)
        outs[k][...] = o_s[rows, :]


def attend_forward(seq, packs, heads, kv):
    parts = len(packs)
    tokens = packs[0].shape[0]
    full = parts * tokens
    vmem = pl.BlockSpec(memory_space=pltpu.VMEM)
    flops = 4 * heads * full * full * HD * 5 // 8
    return pl.pallas_call(
        functools.partial(attend_forward_kernel, parts, heads, kv),
        out_shape=[jax.ShapeDtypeStruct((tokens, heads * HD), BF)] * parts
        + [jax.ShapeDtypeStruct((heads, full), F32)],
        in_specs=[pl.BlockSpec(memory_space=pltpu.SMEM)] + [vmem] * parts,
        out_specs=[vmem] * (parts + 1),
        scratch_shapes=[
            pltpu.VMEM((full, heads * HD), BF),
            pltpu.VMEM((kv, full, HD), BF),
            pltpu.VMEM((kv, HD, full), BF),
            pltpu.VMEM((full, heads * HD), BF),
        ],
        compiler_params=pltpu.CompilerParams(vmem_limit_bytes=48 * 2**20),
        cost_estimate=cost(flops * 4, 4 * 2**20),
        name="attend_forward",
    )(seq.reshape(1), *packs)


def attend_backward_kernel(parts, heads, kv, seq_ref, lse_ref, *refs):
    packs, grads, outs = refs[:parts], refs[parts : 2 * parts], refs[2 * parts : 3 * parts]
    q_s, k_s, kt_s, v_s, g_s, dq_s, dk_s, dv_s = refs[3 * parts :]
    tokens = packs[0].shape[0]
    seq = seq_ref[0]
    group = heads // kv
    for k in range(parts):
        rows = pl.ds(pl.multiple_of((seq ^ k) * tokens, tokens), tokens)
        q_s[rows, :] = packs[k][:, : heads * HD]
        g_s[rows, :] = grads[k][...]
        for g in range(kv):
            lane = (heads + g) * HD
            k_s[g, rows, :] = packs[k][:, lane : lane + HD]
            kt_s[g, :, rows] = packs[k][:, lane : lane + HD].T
            lane = (heads + kv + g) * HD
            v_s[g, rows, :] = packs[k][:, lane : lane + HD]
    full = parts * tokens
    dk_s[...] = jnp.zeros_like(dk_s)
    dv_s[...] = jnp.zeros_like(dv_s)
    for g in range(kv):
        for i in range(full // BLOCK):
            keys = (i + 1) * BLOCK
            rows = slice(i * BLOCK, keys)
            for pair in range(group // 2):
                halves = []
                for h in (g * group + 2 * pair, g * group + 2 * pair + 1):
                    query = q_s[rows, h * HD : (h + 1) * HD]
                    grad = g_s[rows, h * HD : (h + 1) * HD]
                    scores = dot_nt(k_s[g, :keys, :], query) * (HD**-0.5 * LOG2E)
                    probs = jnp.exp2(scores - lse_ref[h : h + 1, rows])
                    grad_probs = dot_nt(v_s[g, :keys, :], grad)
                    inner = jnp.sum(probs * grad_probs, axis=0, keepdims=True)
                    grad_scores = (probs * (grad_probs - inner)).astype(BF)
                    dv_s[g, :keys, :] += dot_nn(probs.astype(BF), grad)
                    dk_s[g, :keys, :] += dot_nn(grad_scores, query)
                    halves.append(dot_nn(kt_s[g, :, :keys], grad_scores) * HD**-0.5)
                lane = (g * group + 2 * pair) * HD
                dq_s[rows, lane : lane + 2 * HD] = jnp.concatenate(halves, axis=0).T.astype(BF)
    for k in range(parts):
        rows = pl.ds(pl.multiple_of((seq ^ k) * tokens, tokens), tokens)
        outs[k][:, : heads * HD] = dq_s[rows, :]
        for g in range(kv):
            lane = (heads + g) * HD
            outs[k][:, lane : lane + HD] = (dk_s[g, rows, :] * HD**-0.5).astype(BF)
            lane = (heads + kv + g) * HD
            outs[k][:, lane : lane + HD] = dv_s[g, rows, :].astype(BF)


def attend_backward(seq, lse, packs, grads, heads, kv):
    parts = len(packs)
    tokens = packs[0].shape[0]
    full = parts * tokens
    vmem = pl.BlockSpec(memory_space=pltpu.VMEM)
    flops = 10 * heads * full * full * HD * 5 // 8
    return pl.pallas_call(
        functools.partial(attend_backward_kernel, parts, heads, kv),
        out_shape=[jax.ShapeDtypeStruct(packs[0].shape, BF)] * parts,
        in_specs=[pl.BlockSpec(memory_space=pltpu.SMEM)] + [vmem] * (2 * parts + 1),
        out_specs=[vmem] * parts,
        scratch_shapes=[
            pltpu.VMEM((full, heads * HD), BF),
            pltpu.VMEM((kv, full, HD), BF),
            pltpu.VMEM((kv, HD, full), BF),
            pltpu.VMEM((kv, full, HD), BF),
            pltpu.VMEM((full, heads * HD), BF),
            pltpu.VMEM((full, heads * HD), BF),
            pltpu.VMEM((kv, full, HD), F32),
            pltpu.VMEM((kv, full, HD), F32),
        ],
        compiler_params=pltpu.CompilerParams(vmem_limit_bytes=48 * 2**20),
        cost_estimate=cost(flops * 4, 8 * 2**20),
        name="attend_backward",
    )(seq.reshape(1), lse, *packs, *grads)


def smem():
    return pl.BlockSpec(memory_space=pltpu.SMEM)


def params(mib=56):
    return pltpu.CompilerParams(vmem_limit_bytes=mib * 2**20)


def cost(flops, moved):
    return pl.CostEstimate(flops=flops // 8, bytes_accessed=moved // 8, transcendentals=0)


def place(shape, pieces, offsets, most=None):
    count = len(pieces)

    def kernel(at_ref, *refs):
        sources, target, sems = refs[:-2], refs[-2], refs[-1]
        copies = []
        for i, source in enumerate(sources):
            rows, width = source.shape
            rows = min(rows, most or rows)
            row = pl.multiple_of(at_ref[2 * i], rows)
            column = pl.multiple_of(at_ref[2 * i + 1], width)
            spot = target.at[pl.ds(row, rows), pl.ds(column, width)]
            copies.append(pltpu.make_async_copy(source.at[pl.ds(0, rows), :], spot, sems.at[i]))
            copies[-1].start()
        for copy in copies:
            copy.wait()

    moved = 2 * sum(piece.size * 2 for piece in pieces)
    return pl.pallas_call(
        kernel,
        out_shape=jax.ShapeDtypeStruct(shape, pieces[0].dtype),
        in_specs=[smem()] + [pl.BlockSpec(memory_space=pl.ANY)] * count,
        out_specs=pl.BlockSpec(memory_space=pltpu.HBM),
        scratch_shapes=[pltpu.SemaphoreType.DMA((count,))],
        compiler_params=params(16),
        cost_estimate=cost(0, moved),
        name="place",
    )(jnp.stack([jnp.int32(v) for pair in offsets for v in pair]), *pieces)


def turn(values, cos_table, sin_table):
    width = values.shape[1]
    lane = lax.broadcasted_iota(jnp.int32, values.shape, 1)
    swapped = jnp.where(
        lane % HD < HD // 2,
        pltpu.roll(values, width - HD // 2, 1),
        pltpu.roll(values, HD // 2, 1),
    )
    return values * cos_table + swapped * sin_table


def whole(shape):
    return pl.BlockSpec(shape, lambda n: (0,) * len(shape))


def project_in(seq, z, inputs, gain, groups, cos_table, sin_table, parts):
    tokens, width = inputs.shape
    tile = cos_table.shape[1]
    each = tile // parts
    pack = tile + 2 * each
    count = len(groups)
    depth = width // count

    def kernel(at_ref, in_ref, gain_ref, *refs):
        w_refs, (cos_ref, sin_ref, acts_ref), packs = refs[:count], refs[count : count + 3], refs[count + 3 :]
        step = pl.program_id(0)

        @pl.when(step == 0)
        def _():
            values = in_ref[...].astype(F32)
            scale = lax.rsqrt(jnp.mean(values * values, axis=-1, keepdims=True) + EPSILON)
            acts_ref[...] = (values * scale * gain_ref[...]).astype(BF)

        rows = None
        for j in range(count):
            lanes = pl.ds(pl.multiple_of((at_ref[1] + count - j) % count * depth, depth), depth)
            term = dot_nn(acts_ref[:, lanes], w_refs[j][...])
            rows = term if rows is None else rows + term
        turned = jnp.where(
            step == parts + 1, rows, turn(rows, cos_ref[...], sin_ref[...])
        ).astype(BF)
        seq_now = at_ref[0]
        for k in range(parts):

            @pl.when((seq_now ^ k) == step)
            def _():
                packs[k][:, :tile] = turned

            for d in range(parts):
                for which in range(2):

                    @pl.when(((seq_now ^ k) == d) & (step == parts + which))
                    def _():
                        lane = tile + which * each
                        packs[k][:, lane : lane + each] = turned[:, d * each : (d + 1) * each]

    return pl.pallas_call(
        kernel,
        grid=(parts + 2,),
        out_shape=[jax.ShapeDtypeStruct((tokens, width), BF)]
        + [jax.ShapeDtypeStruct((tokens, pack), BF)] * parts,
        in_specs=[smem(), whole((tokens, width)), whole((1, width))]
        + [pl.BlockSpec((depth, tile), lambda n: (0, n))] * count
        + [whole((tokens, tile))] * 2,
        out_specs=[whole((tokens, width))] + [whole((tokens, pack))] * parts,
        compiler_params=params(),
        cost_estimate=cost(2 * tokens * width * tile * (parts + 2), 2 * width * tile * (parts + 2)),
        name="project_in",
    )(jnp.stack([seq, z]), inputs, gain, *groups, cos_table, sin_table)


def project_out(seq, z, mixed, inputs, gain, groups):
    parts = len(mixed)
    tokens, width = inputs.shape
    each = mixed[0].shape[1]
    tile = width // parts
    count = len(groups)
    depth = parts * each // count

    def kernel(at_ref, *refs):
        parts_in, (in_ref, gain_ref) = refs[:parts], refs[parts : parts + 2]
        w_refs, (flat_ref, res_ref, acts_ref) = refs[parts + 2 : -3], refs[-3:]
        step = pl.program_id(0)

        @pl.when(step == 0)
        def _():
            for k in range(parts):
                lane = pl.multiple_of((at_ref[0] ^ k) * each, each)
                flat_ref[:, pl.ds(lane, each)] = parts_in[k][...]

        lanes = pl.ds(pl.multiple_of(step * tile, tile), tile)
        total = in_ref[:, lanes].astype(F32)
        for j in range(count):
            rows = pl.ds(pl.multiple_of((at_ref[1] + count - j) % count * depth, depth), depth)
            total = total + dot_nn(flat_ref[:, rows], w_refs[j][...])
        res_ref[:, lanes] = total

        @pl.when(step == parts - 1)
        def _():
            values = res_ref[...]
            scale = lax.rsqrt(jnp.mean(values * values, axis=-1, keepdims=True) + EPSILON)
            acts_ref[...] = (values * scale * gain_ref[...]).astype(BF)

    return pl.pallas_call(
        kernel,
        grid=(parts,),
        out_shape=[
            jax.ShapeDtypeStruct((tokens, parts * each), BF),
            jax.ShapeDtypeStruct((tokens, width), F32),
            jax.ShapeDtypeStruct((tokens, width), BF),
        ],
        in_specs=[smem()]
        + [whole((tokens, each))] * parts
        + [whole((tokens, width)), whole((1, width))]
        + [pl.BlockSpec((depth, tile), lambda n: (0, n))] * count,
        out_specs=[whole((tokens, parts * each)), whole((tokens, width)), whole((tokens, width))],
        compiler_params=params(),
        cost_estimate=cost(2 * tokens * width * parts * each, 2 * width * parts * each),
        name="project_out",
    )(jnp.stack([seq, z]), *mixed, inputs, gain, *groups)


def feed_forward(acts, grads, gate, up, down, begun=None):
    tokens, width = acts.shape
    hidden = gate.shape[0]
    tile = 256
    steps = hidden // tile
    kind = F32 if begun is None else BF
    begun = [] if begun is None else list(begun)

    def kernel(a_ref, c_ref, g_ref, u_ref, d_ref, *refs):
        starts, (h_ref, gg_ref, gu_ref, o_ref, ga_ref, o_s, ga_s) = refs[:-7], refs[-7:]
        step = pl.program_id(0)

        @pl.when(step == 0)
        def _():
            if starts:
                o_s[...] = starts[0][...]
                ga_s[...] = starts[1][...]
            else:
                o_s[...] = jnp.zeros_like(o_s)
                ga_s[...] = jnp.zeros_like(ga_s)

        gate_act = dot_nt(a_ref[...], g_ref[...])
        up_act = dot_nt(a_ref[...], u_ref[...])
        grad_hidden = dot_nt(c_ref[...], d_ref[...])
        sigma = jax.nn.sigmoid(gate_act)
        silu = gate_act * sigma
        low = (silu * up_act).astype(BF)
        grad_gate = (grad_hidden * up_act * (sigma * (1.0 + gate_act * (1.0 - sigma)))).astype(BF)
        grad_up = (grad_hidden * silu).astype(BF)
        h_ref[...] = low
        gg_ref[...] = grad_gate
        gu_ref[...] = grad_up
        o_s[...] += dot_nn(low, d_ref[...])
        ga_s[...] += dot_nn(grad_gate, g_ref[...]) + dot_nn(grad_up, u_ref[...])

        @pl.when(step == steps - 1)
        def _():
            o_ref[...] = o_s[...].astype(kind)
            ga_ref[...] = ga_s[...].astype(kind)

    whole = pl.BlockSpec((tokens, width), lambda n: (0, 0))
    rows = pl.BlockSpec((tile, width), lambda n: (n, 0))
    lanes = pl.BlockSpec((tokens, tile), lambda n: (0, n))
    return pl.pallas_call(
        kernel,
        grid=(steps,),
        out_shape=[jax.ShapeDtypeStruct((tokens, hidden), BF)] * 3
        + [jax.ShapeDtypeStruct((tokens, width), kind)] * 2,
        in_specs=[whole, whole, rows, rows, rows] + [whole] * len(begun),
        out_specs=[lanes] * 3 + [whole] * 2,
        scratch_shapes=[pltpu.VMEM((tokens, width), F32)] * 2,
        compiler_params=params(),
        cost_estimate=cost(12 * tokens * width * hidden, 6 * width * hidden),
        name="feed_forward",
    )(acts, grads, gate, up, down, *begun)


def middle_back(seq, z, terms, residual, grad_out, gain, groups, parts):
    tokens, width = residual.shape
    tile = groups[0].shape[0]
    count = len(groups)
    assert count == parts

    def kernel(at_ref, t0_ref, t1_ref, res_ref, go_ref, gain_ref, *refs):
        w_refs, (gr_ref, low_ref, gg_ref), outs = refs[:count], refs[count : count + 3], refs[count + 3 :]
        grad = t0_ref[...].astype(F32) + t1_ref[...].astype(F32)
        values = res_ref[...]
        scale = lax.rsqrt(jnp.mean(values * values, axis=-1, keepdims=True) + EPSILON)
        weighted = grad * gain_ref[...]
        inner = jnp.mean(weighted * values, axis=-1, keepdims=True)
        result = go_ref[...].astype(F32) + scale * weighted - values * (scale**3 * inner)
        gr_ref[...] = result
        low_ref[...] = result.astype(BF)
        gg_ref[...] = jnp.sum(grad * values * scale, axis=0, keepdims=True)
        for j in range(count):
            part = dot_nt(low_ref[...], w_refs[j][...]).astype(BF)
            at = ((at_ref[1] + count - j) % count) ^ at_ref[0]
            for k in range(parts):

                @pl.when(at == k)
                def _():
                    outs[k][...] = part

    vmem = pl.BlockSpec(memory_space=pltpu.VMEM)
    return pl.pallas_call(
        kernel,
        out_shape=[
            jax.ShapeDtypeStruct((tokens, width), F32),
            jax.ShapeDtypeStruct((tokens, width), BF),
            jax.ShapeDtypeStruct((1, width), F32),
        ]
        + [jax.ShapeDtypeStruct((tokens, tile), BF)] * parts,
        in_specs=[smem()] + [vmem] * (5 + count),
        out_specs=[vmem] * (3 + parts),
        compiler_params=params(),
        cost_estimate=cost(2 * tokens * width * tile * parts, 2 * width * tile * parts + 8 * tokens * width),
        name="middle_back",
    )(jnp.stack([seq, z]), terms[0], terms[1], residual, grad_out, gain, *groups)


def unpack(seq, packs, cos_table, sin_table):
    parts = len(packs)
    tokens, tile = cos_table.shape
    each = tile // parts

    def kernel(seq_ref, *refs):
        ins, (cos_ref, sin_ref, out_ref) = refs[:parts], refs[parts:]
        for k in range(parts):
            at = seq_ref[0] ^ k
            queries = turn(ins[k][:, :tile].astype(F32), cos_ref[...], -sin_ref[...])
            out_ref[:, pl.ds(pl.multiple_of(at * tile, tile), tile)] = queries.astype(BF)
            keys = turn(
                ins[k][:, tile : tile + each].astype(F32), cos_ref[:, :each], -sin_ref[:, :each]
            )
            lane = pl.multiple_of(parts * tile + at * each, each)
            out_ref[:, pl.ds(lane, each)] = keys.astype(BF)
            lane = pl.multiple_of((parts + 1) * tile + at * each, each)
            out_ref[:, pl.ds(lane, each)] = ins[k][:, tile + each :]

    vmem = pl.BlockSpec(memory_space=pltpu.VMEM)
    return pl.pallas_call(
        kernel,
        out_shape=jax.ShapeDtypeStruct((tokens, (parts + 2) * tile), BF),
        in_specs=[smem()] + [vmem] * (parts + 2),
        out_specs=vmem,
        compiler_params=params(),
        cost_estimate=cost(0, 6 * 2**20),
        name="unpack",
    )(seq.reshape(1), *packs, cos_table, sin_table)


def inner_back(z, grad_qkv, groups, inputs, gain, grad_res):
    tokens, width = inputs.shape
    count = len(groups)
    depth = width // count

    def kernel(at_ref, gq_ref, *refs):
        w_refs, (in_ref, gain_ref, gr_ref, out_ref, gg_ref, grad_s) = refs[:count], refs[count:]
        for j in range(count):
            lanes = pl.ds(pl.multiple_of((at_ref[0] + count - j) % count * depth, depth), depth)
            grad_s[:, lanes] = dot_nt(gq_ref[...], w_refs[j][...])
        grad = grad_s[...]
        values = in_ref[...].astype(F32)
        scale = lax.rsqrt(jnp.mean(values * values, axis=-1, keepdims=True) + EPSILON)
        weighted = grad * gain_ref[...]
        inner = jnp.mean(weighted * values, axis=-1, keepdims=True)
        result = gr_ref[...] + scale * weighted - values * (scale**3 * inner)
        out_ref[...] = result.astype(BF)
        gg_ref[...] = jnp.sum(grad * values * scale, axis=0, keepdims=True)

    vmem = pl.BlockSpec(memory_space=pltpu.VMEM)
    return pl.pallas_call(
        kernel,
        out_shape=[jax.ShapeDtypeStruct((tokens, width), BF), jax.ShapeDtypeStruct((1, width), F32)],
        in_specs=[smem()] + [vmem] * (4 + count),
        out_specs=[vmem] * 2,
        scratch_shapes=[pltpu.VMEM((tokens, width), F32)],
        compiler_params=params(),
        cost_estimate=cost(2 * tokens * groups[0].size * count, 2 * groups[0].size * count),
        name="inner_back",
    )(z.reshape(1), grad_qkv, *groups, inputs, gain, grad_res)


def weight_grad(left, right, rows, blocks, half, adds=(), pieces=1):
    count = len(left)
    tokens = left[0].shape[0]
    width = right[0].shape[1] // 2
    total_rows = rows * len(blocks)
    piece = total_rows // pieces
    tile = math.gcd(math.gcd(rows, 512), piece)
    steps = rows // tile
    each = piece // tile

    def kernel(at_ref, *refs):
        lefts, rights = refs[:count], refs[count : 2 * count]
        extra, outs = refs[2 * count : -pieces], refs[-pieces:]
        total = None
        for l_ref, r_ref in zip(lefts, rights):
            term = lax.dot_general(
                l_ref[...], r_ref[...], (((0,), (0,)), ((), ())), preferred_element_type=F32
            )
            total = term if total is None else total + term
        for ref in extra:
            total = total + ref[...].astype(F32)
        total = total.astype(BF)
        for p, out in enumerate(outs):
            if pieces == 1:
                out[...] = total
            else:

                @pl.when(pl.program_id(0) // each == p)
                def _():
                    out[...] = total

    def spec_of(p):
        if pieces == 1:
            return pl.BlockSpec((tile, width), lambda n, at: (n, 0))
        return pl.BlockSpec((tile, width), lambda n, at: (jnp.clip(n - p * each, 0, each - 1), 0))

    spec = pltpu.PrefetchScalarGridSpec(
        num_scalar_prefetch=1,
        grid=(steps * len(blocks),),
        in_specs=[pl.BlockSpec((tokens, tile), lambda n, at: (0, at[1 + n]))] * count
        + [pl.BlockSpec((tokens, width), lambda n, at: (0, at[0]))] * count
        + [pl.BlockSpec((tile, width), lambda n, at: (n, 0))] * len(adds),
        out_specs=[spec_of(p) for p in range(pieces)],
    )
    at = [jnp.int32(half)]
    for block in blocks:
        at += [jnp.int32(block) * steps + i for i in range(steps)]
    outs = pl.pallas_call(
        kernel,
        grid_spec=spec,
        out_shape=[jax.ShapeDtypeStruct((piece, width), BF)] * pieces,
        compiler_params=params(),
        cost_estimate=cost(
            2 * tokens * count * total_rows * width, 2 * (tokens * count + total_rows) * width
        ),
        name="weight_grad",
    )(jnp.stack(at), *left, *right, *adds)
    return outs[0] if pieces == 1 else list(outs)


def row_grads(left, right, blocks, half, added, y, cuts):
    tokens = left.shape[0]
    width = right.shape[1] // 2
    rows = left.shape[1] // LINE
    each = rows // cuts
    count = len(blocks)

    def kernel(at_ref, l_ref, r_ref, add_ref, *refs):
        outs, total_s = refs[:-1], refs[-1]
        total = lax.dot_general(
            l_ref[...], r_ref[...], (((0,), (0,)), ((), ())), preferred_element_type=F32
        )
        total_s[...] = (total + add_ref[...].astype(F32)).astype(BF)
        for j in range(count):

            @pl.when(pl.program_id(0) == j)
            def _():
                for k in range(cuts):
                    start = pl.multiple_of((at_ref[1] + cuts - k) % cuts * each, each)
                    outs[j * cuts + k][...] = total_s[pl.ds(start, each), :]

    spec = pltpu.PrefetchScalarGridSpec(
        num_scalar_prefetch=1,
        grid=(count,),
        in_specs=[
            pl.BlockSpec((tokens, rows), lambda n, at: (0, at[2 + n])),
            pl.BlockSpec((tokens, width), lambda n, at: (0, at[0])),
            pl.BlockSpec((rows, width), lambda n, at: (n, 0)),
        ],
        out_specs=[pl.BlockSpec((each, width), lambda n, at: (0, 0))] * (count * cuts),
        scratch_shapes=[pltpu.VMEM((rows, width), BF)],
    )
    at = jnp.stack([jnp.int32(half), jnp.int32(y)] + [jnp.int32(b) for b in blocks])
    outs = pl.pallas_call(
        kernel,
        grid_spec=spec,
        out_shape=[jax.ShapeDtypeStruct((each, width), BF)] * (count * cuts),
        compiler_params=params(),
        cost_estimate=cost(2 * tokens * count * rows * width, 6 * count * rows * width),
        name="row_grads",
    )(at, left, right, added)
    return [outs[j * cuts : (j + 1) * cuts] for j in range(count)]


def join(core, mine, other, widths):
    rows, half = mine.shape
    tile = min(rows, 256)

    def kernel(core_ref, mine_ref, other_ref, *refs):
        outs, full = refs[:-1], refs[-1]
        target = outs[0] if len(outs) == 1 else full
        at = pl.multiple_of(core_ref[0] * half, half)
        target[:, pl.ds(at, half)] = mine_ref[...].astype(F32)
        at = pl.multiple_of((1 - core_ref[0]) * half, half)
        target[:, pl.ds(at, half)] = other_ref[...].astype(F32)
        if len(outs) > 1:
            lane = 0
            for out in outs:
                out[...] = full[:, lane : lane + out.shape[1]]
                lane += out.shape[1]

    def block(width):
        return pl.BlockSpec((tile, width), lambda n: (n, 0))

    return pl.pallas_call(
        kernel,
        grid=(rows // tile,),
        out_shape=[jax.ShapeDtypeStruct((rows, width), F32) for width in widths],
        in_specs=[smem(), block(half), block(half)],
        out_specs=[block(width) for width in widths],
        scratch_shapes=[pltpu.VMEM((tile, 2 * half) if len(widths) > 1 else (8, 128), F32)],
        compiler_params=params(),
        cost_estimate=cost(0, rows * half * 12),
        name="join",
    )(core.reshape(1), mine, other)
def half_of(array, which, axis=1):
    size = array.shape[axis] // 2
    return lax.dynamic_slice_in_dim(array, which * size, size, axis)


def join_halves(core, top, bottom):
    rows, half = top[0].shape
    tile = min(rows, 256)
    steps = rows // tile

    def kernel(core_ref, a_ref, b_ref, c_ref, d_ref, out):
        mine = pl.multiple_of(core_ref[0] * half, half)
        other = pl.multiple_of((1 - core_ref[0]) * half, half)
        upper = pl.program_id(0) < steps

        @pl.when(upper)
        def _():
            out[:, pl.ds(mine, half)] = a_ref[...].astype(F32)
            out[:, pl.ds(other, half)] = b_ref[...].astype(F32)

        @pl.when(jnp.logical_not(upper))
        def _():
            out[:, pl.ds(mine, half)] = c_ref[...].astype(F32)
            out[:, pl.ds(other, half)] = d_ref[...].astype(F32)

    first = pl.BlockSpec((tile, half), lambda n: (jnp.minimum(n, steps - 1), 0))
    second = pl.BlockSpec((tile, half), lambda n: (jnp.maximum(n - steps, 0), 0))
    return pl.pallas_call(
        kernel,
        grid=(2 * steps,),
        out_shape=jax.ShapeDtypeStruct((2 * rows, 2 * half), F32),
        in_specs=[smem(), first, first, second, second],
        out_specs=pl.BlockSpec((tile, 2 * half), lambda n: (n, 0)),
        compiler_params=params(),
        cost_estimate=cost(0, rows * half * 24),
        name="join_halves",
    )(core.reshape(1), *top, *bottom)


class Order:
    def __init__(self):
        self.marks = ()

    def tie(self, *values):
        if self.marks:
            values = lax.optimization_barrier(tuple(values) + self.marks)[: len(values)]
        return values[0] if len(values) == 1 else list(values)

    def done(self, *values):
        self.marks = tuple(values)


def y_hops(value):
    return ring_gather(value, y_next, columns())[1:]


def add_low(left, right):
    return (left.astype(F32) + right.astype(F32)).astype(BF)


def rope_tables(positions, repeat):
    frequency = THETA ** (-(jnp.arange(HD // 2, dtype=F32) * 2.0) / HD)
    angles = positions.astype(F32)[:, None] * frequency[None, :]
    cos, sin = jnp.cos(angles), jnp.sin(angles)
    return (
        jnp.tile(jnp.concatenate([cos, cos], axis=1), (1, repeat)),
        jnp.tile(jnp.concatenate([-sin, sin], axis=1), (1, repeat)),
    )


def exchange(packs):
    return [packs[0]] + [seq_swap(packs[k], k) for k in range(1, len(packs))]


def shards(
    inputs,
    query_weight,
    key_weight,
    value_weight,
    output_weight,
    gate_weight,
    up_weight,
    down_weight,
    gain_attn,
    gain_ffn,
    cotangent,
):
    seq_count, local_len, width = inputs.shape
    assert seq_count == 1
    tokens = local_len
    parts = lax.axis_size("seq")
    kv_local = KVH // parts
    cols = columns()
    seq = lax.axis_index("seq")
    core, side = seq % 2, seq // 2
    fsdp = lax.axis_index("fsdp")
    z, y = fsdp // cols, fsdp % cols
    q_width, kv_width = query_weight.shape[1], key_weight.shape[1]
    heads_local = q_width // HD // parts
    flat_in = inputs.reshape(tokens, width)
    grad_out = cotangent.reshape(tokens, width)

    qkv_shard = jnp.concatenate([query_weight, key_weight, value_weight], axis=1)
    rows = qkv_shard.shape[0]
    part, half = rows // 2, qkv_shard.shape[1] // 2
    positions = seq * local_len + jnp.arange(local_len)
    cos_table, sin_table = rope_tables(positions, kv_width // HD)
    order = Order()

    def swapped(pieces):
        return [core_swap(p) for p in pieces]

    def place_halves(pieces, others, whole_first=None):
        each = pieces[-1].shape[1]
        placed, offsets = [], []
        for k, (piece, other) in enumerate(zip(pieces, others)):
            row = (y - k) % cols * rows
            if k == 0 and whole_first is not None:
                placed.append(whole_first)
                offsets.append((row, 0))
            else:
                placed += [piece, other]
                offsets += [(row, core * each), (row, (1 - core) * each)]
        return place((rows * cols, 2 * each), placed, offsets)

    def place_quarters(pieces, others, sides, count, size, first):
        each = pieces[0].shape[1]
        placed, offsets = [], []
        for i, (piece, other) in enumerate(zip(pieces, others)):
            k, at = i // 2, sides[i % 2]
            row = first(k) * size + at * (size // 2)
            placed += [piece, other]
            offsets += [(row, core * each), (row, (1 - core) * each)]
        return place((size * count, 2 * each), placed, offsets)

    def line_row(k):
        return (y - k) % cols

    own = (gate_weight, up_weight, down_weight)
    far_rows = gate_weight.shape[0]
    far_part = far_rows // 4
    far_y, far_x = {}, {}

    def far_start(i, h):
        at = side * 2 * far_part + h * far_part
        return lax.dynamic_slice(own[i], (at, core * out_width), (far_part, out_width))

    out_width = width // 2
    far_starts = {(i, h): far_start(i, h) for i in range(3) for h in range(2)}

    def far_along_y(i, h):
        start = order.tie(far_starts[i, h]) if order.marks else far_starts[i, h]
        far_y[i, h] = y_hops(start)
        return far_y[i, h]

    def far_along_x(i, h):
        pieces = order.tie(*far_y[i, h], far_y[i, h][0])[:-1]
        far_x[i, h] = [x_swap(p) for p in pieces]
        return far_x[i, h]

    gains = jnp.concatenate([gain_attn, gain_ffn]).reshape(1, 2 * rows)
    start = half_of(qkv_shard, core)
    start = jnp.concatenate([start, jnp.pad(gains, ((0, 15), (0, half - 2 * rows)))], axis=0)
    out_half = half_of(output_weight, core)

    def quarter_of(piece):
        return lax.dynamic_slice_in_dim(piece, side * part, part, 0)

    def line_group(i):
        here = order.tie(line[i])
        placed, offsets = [], []
        row = y * rows
        if i:
            placed += [here, core_swap(here)]
            offsets += [(row, core * half), (row, (1 - core) * half)]
        else:
            placed.append(qkv_shard)
            offsets.append((row, 0))
        for k in range(1, cols):
            row = (y - k) % cols * rows
            if i < LINE - 1:
                for piece, at in ((beside[i][k - 1], side), (crossed[i][k - 1], 1 - side)):
                    piece = order.tie(piece)
                    placed += [piece, core_swap(piece)]
                    offsets += [
                        (row + at * part, core * half),
                        (row + at * part, (1 - core) * half),
                    ]
            else:
                piece = order.tie(beside[i][k - 1])
                placed += [piece, core_swap(piece)]
                offsets += [(row, core * half), (row, (1 - core) * half)]
        return place((rows * cols, 2 * half), placed, offsets, rows)

    line, beside, crossed, groups = [start], [], [], []
    for j in range(LINE):
        here = order.tie(line[j]) if j else line[j]
        if j + 1 < LINE:
            line.append(z_next(here))
            beside.append(y_hops(quarter_of(here)))
            marks = [line[j + 1]] + beside[j] + far_along_y(j // 2, j % 2)
        else:
            beside.append(y_hops(here))
            line_o = [out_half, z_next(order.tie(out_half))]
            grad_parts = [grad_out, z_next(order.tie(grad_out))]
            gains_near = jnp.concatenate([p[rows:, : 2 * rows] for p in line[:j]], axis=0)
            gains_far = y_hops(order.tie(gains_near))
            marks = beside[j] + [line_o[1]]
        if j:
            pieces = order.tie(*beside[j - 1], here)[:-1]
            crossed.append([x_swap(p) for p in pieces])
            marks += crossed[j - 1]
        if j > 1:
            groups.append(line_group(j - 2))
            marks.append(groups[-1])
        if j == 1:
            marks += [cos_table, sin_table] + list(far_starts.values())
        order.done(*marks)

    line_o.append(z_next(order.tie(line_o[1])))
    beside_o = [y_hops(order.tie(line_o[0])), y_hops(order.tie(line_o[1]))]
    groups += [line_group(LINE - 2), line_group(LINE - 1)]
    marks = far_along_x(0, 0)
    gain_full = jnp.zeros((2, width), BF)
    for j in range(LINE):
        for k in range(cols):
            if j == LINE - 1:
                g = line[j][rows] if k == 0 else beside[j][k - 1][rows]
                pair = g[: 2 * rows].reshape(2, rows)
            else:
                g = gains_near if k == 0 else gains_far[k - 1]
                pair = g[16 * j].reshape(2, rows)
            at = (((z - j) % LINE) * cols + (y - k) % cols) * rows
            gain_full = lax.dynamic_update_slice(gain_full, pair, (0, at))
    gain_one = gain_full[:1].astype(F32)
    gain_two = gain_full[1:].astype(F32)
    acts_one, *sent = project_in(seq, z, flat_in, gain_one, groups, cos_table, sin_table, parts)
    order.done(*sent, line_o[2], *beside_o[0], *beside_o[1], grad_parts[1], *marks)

    def out_group(j, *others):
        hops = order.tie(line_o[j], *beside_o[j], *others)[: cols]
        if j == 0:
            return place_halves([None] + hops[1:], [None] + swapped(hops[1:]), output_weight)
        return place_halves(hops, swapped(hops))

    packs = exchange(order.tie(*sent))
    line_o.append(z_next(order.tie(line_o[2])))
    beside_o.append(y_hops(order.tie(line_o[2])))
    grad_top = [z_next(order.tie(grad_parts[1])[: tokens // 2])]
    order.done(*packs, line_o[3], *beside_o[2], grad_top[0])

    beside_o.append(y_hops(order.tie(line_o[3])))
    grad_low = [z_next(order.tie(grad_parts[1])[tokens // 2 :])]
    marks = grad_low
    out_groups = [out_group(0), out_group(1), out_group(2)]
    *mixed_sent, log_totals = attend_forward(seq, order.tie(*packs), heads_local, kv_local)
    order.done(*mixed_sent, *beside_o[3], *marks, *out_groups)

    mixed = exchange(order.tie(*mixed_sent))
    out_groups.append(out_group(3))
    grad_top.append(z_next(order.tie(grad_top[0])))
    order.done(*mixed, out_groups[3], grad_top[1])

    grad_low.append(z_next(order.tie(grad_low[0])))
    grad_parts += [jnp.concatenate(pair, axis=0) for pair in zip(grad_top, grad_low)]
    marks = far_along_y(1, 1) + far_along_x(0, 1) + [grad_low[1]]
    mixed_flat, residual, acts_two = project_out(
        seq, z, order.tie(*mixed), flat_in, gain_two, out_groups
    )
    order.done(acts_two, *marks)

    def far_place(i):
        placed, offsets = [], []
        for k in range(cols - 1):
            for h in range(2):
                pieces = order.tie(far_y[i, h][k], far_x[i, h][k])
                for piece, at in zip(pieces, (side, 1 - side)):
                    row = k * far_rows + at * 2 * far_part + h * far_part
                    placed += [piece, core_swap(piece)]
                    offsets += [(row, core * out_width), (row, (1 - core) * out_width)]
        return place((far_rows * (cols - 1), width), placed, offsets)

    acts_parts, far, near_done, far_done = [acts_two], [], [], [None] * LINE

    def run_near(j):
        near_done.append(feed_forward(order.tie(acts_parts[j]), grad_parts[j], *own))
        return near_done[j][3]

    def run_far(j):
        far_done[j] = feed_forward(order.tie(acts_parts[j]), grad_parts[j], *far, near_done[j][3:])
        return far_done[j][4]

    acts_parts.append(z_next(order.tie(acts_parts[0])))
    marks = far_along_y(2, 0) + far_along_y(2, 1) + far_along_x(1, 0) + far_along_x(1, 1)
    far.append(far_place(0))
    order.done(acts_parts[1], *marks, *far, run_near(0))
    acts_parts.append(z_next(order.tie(acts_parts[1])))
    marks = far_along_x(2, 0) + far_along_x(2, 1)
    far.append(far_place(1))
    order.done(acts_parts[2], *marks, *far, run_near(1))
    acts_parts.append(z_next(order.tie(acts_parts[2])))
    far.append(far_place(2))
    marks = [run_near(2), run_far(1)]
    order.done(acts_parts[3], *marks)

    passed = z_next(order.tie(far_done[1][4]))
    marks = [run_near(3), run_far(2)]
    order.done(passed, *marks)
    passed = z_next(order.tie(add_low(passed, far_done[2][4])))
    marks = [run_far(3), run_far(0)]
    order.done(passed, *marks)
    passed = z_next(order.tie(add_low(passed, far_done[3][4])))

    rights = (grad_parts, acts_parts, acts_parts)
    far_size = far_rows * (cols - 1)
    far_sent, far_total, own_sent = [None] * 3, {}, [None] * 3

    def of(done, which):
        return order.tie(*[d[which] for d in done])

    def send_far(i):
        far_sent[i] = weight_grad(of(far_done, i), rights[i], far_size, [0], 1 - core)
        return far_sent[i]

    def keep_far(i):
        return weight_grad(
            of(far_done, i), rights[i], far_size, [0], core, [far_sent[i]], 2 * (cols - 1)
        )

    def pass_far(i, kept, h):
        total = y_next(order.tie(kept[h]))
        for k in range(1, cols - 1):
            total = y_next(add_low(total, order.tie(kept[2 * k + h])))
        far_total[i, h] = total
        return total

    def send_own(i):
        own_sent[i] = weight_grad(of(near_done, i), rights[i], far_rows, [0], 1 - core)
        return own_sent[i]

    def keep_own(i):
        return weight_grad(of(near_done, i), rights[i], far_rows, [0], core, [own_sent[i]])

    first = send_far(0)
    far_sent[0] = core_swap(first)
    marks = [send_far(1), send_far(2)]
    kept = [keep_far(0)]
    order.done(passed, *kept[0], *marks)

    marks = [pass_far(0, kept[0], 0)]
    far_sent[1:] = [core_swap(order.tie(term)) for term in far_sent[1:]]
    ffn_parts = [d[3] for d in far_done]
    ffn_sum = z_next(order.tie(ffn_parts[1]))
    grad_res, grad_res_low, grad_gain_two, *grad_sent = middle_back(
        seq, z, order.tie(passed, far_done[0][4]), residual, grad_out, gain_two, out_groups, parts
    )
    order.done(*grad_sent, *far_sent[1:])

    grad_packs = exchange(order.tie(*grad_sent))
    kept.append(keep_far(1))
    first = send_own(0)
    order.done(*grad_packs, ffn_sum, *kept[1], first, *marks)

    marks = [pass_far(0, kept[0], 1)]
    ffn_sum = z_next(order.tie(add_low(ffn_sum, ffn_parts[2])))
    back_sent = attend_backward(
        seq, log_totals, packs, order.tie(*grad_packs), heads_local, kv_local
    )
    order.done(*back_sent, *marks)

    line_order = list(range(1, LINE)) + [0]
    blocks = [(z - j) % LINE for j in line_order]
    line_rows = rows * cols
    back_packs = exchange(order.tie(*back_sent))
    own_sent[0] = core_swap(order.tie(own_sent[0]))
    out_left, out_right = order.tie(mixed_flat, grad_res_low)
    out_sent = weight_grad([out_left], [out_right], line_rows, blocks, 1 - core)
    kept.append(keep_far(2))
    own_low = [keep_own(0)]
    marks = [pass_far(1, kept[1], 0), *kept[2], own_low[0], out_sent]
    order.done(*back_packs, *marks, ffn_sum)

    size = far_rows // 2
    sums = {}

    def along_x(i, h):
        low = add_low(order.tie(own_low[i])[h * size : (h + 1) * size], far_total[i, h])
        sums[i, h] = (low, x_swap(low))
        return sums[i, h][1]

    def finish(i, h):
        low, crossed = order.tie(*sums[i, h])
        total = add_low(low, crossed)
        sums[i, h] = (total, core_swap(total))
        return sums[i, h][1]

    def joined(i):
        pairs = order.tie(*sums[i, 0], *sums[i, 1])
        return join_halves(core, pairs[:2], pairs[2:])

    def along_y(terms):
        terms = order.tie(*terms, terms[0])[:-1]
        total = None
        for k in list(range(1, cols)) + [0]:
            total = terms[k] if total is None else add_low(y_next(total), terms[k])
        return total

    marks = [pass_far(1, kept[1], 1), along_x(0, 0)]
    out_recv = core_swap(order.tie(out_sent))
    ffn_sum = z_next(order.tie(add_low(ffn_sum, ffn_parts[3])))
    grad_qkv = unpack(seq, order.tie(*back_packs), cos_table, sin_table)
    qkv_sent = weight_grad([acts_one], [grad_qkv], line_rows, blocks, 1 - core)
    out_terms = row_grads(out_left, out_right, blocks, core, out_recv, y, 1)
    out_terms = [t[0] for t in out_terms]
    marks.append(send_own(1))
    order.done(qkv_sent, ffn_sum, *out_terms, *marks)

    qkv_recv = core_swap(order.tie(qkv_sent))
    out_total = z_next(order.tie(out_terms[0]))
    own_sent[1] = core_swap(order.tie(own_sent[1]))
    marks = [pass_far(2, kept[2], 0), send_own(2), along_x(0, 1), finish(0, 0)]
    own_low.append(keep_own(1))
    order.done(qkv_recv, out_total, own_low[1], *marks)

    out_total = z_next(order.tie(add_low(out_total, out_terms[1])))
    qkv_terms = row_grads(acts_one, grad_qkv, blocks, core, order.tie(qkv_recv), y, cols)
    own_sent[2] = core_swap(order.tie(own_sent[2]))
    marks = [pass_far(2, kept[2], 1), along_x(1, 0), own_sent[2], finish(0, 1)]
    order.done(*[t for terms in qkv_terms for t in terms], out_total, *marks)

    out_total = z_next(order.tie(add_low(out_total, out_terms[2])))
    hops = [along_y(qkv_terms[0])]
    own_low.append(keep_own(2))
    d_down = joined(0)
    marks = [along_x(1, 1), finish(1, 0)]
    order.done(hops[0], out_total, d_down, own_low[2], *marks)

    passed = z_next(order.tie(hops[0]))
    hops.append(along_y(qkv_terms[1]))
    grad_inputs, grad_gain_one = inner_back(z, order.tie(grad_qkv), groups, flat_in, gain_one, grad_res)
    out_total = order.tie(add_low(out_total, out_terms[3]))
    pieces = [
        lax.dynamic_slice_in_dim(out_total, (y - k) % cols * rows, rows, 0) for k in range(cols)
    ]
    out_low = along_y(pieces)
    marks = [out_low, along_x(2, 0), finish(1, 1), grad_inputs]
    order.done(passed, hops[1], *marks)

    passed = z_next(order.tie(add_low(passed, hops[1])))
    hops.append(along_y(qkv_terms[2]))
    gain_sums = jnp.concatenate([grad_gain_one, grad_gain_two], axis=0)
    steps = sum_steps()
    gain_sums = gain_sums + steps[0](order.tie(gain_sums))
    d_gate = joined(1)
    marks = [along_x(2, 1), finish(2, 0), d_gate, gain_sums]
    order.done(passed, hops[2], *marks)

    passed = z_next(order.tie(add_low(passed, hops[2])))
    hops.append(along_y(qkv_terms[3]))
    out_cross = x_swap(order.tie(out_low))
    outputs = (residual + ffn_sum.astype(F32) + order.tie(ffn_parts[0]).astype(F32)).astype(BF)
    gain_sums = gain_sums + steps[1](order.tie(gain_sums))
    finish(2, 1)
    d_up = joined(2)
    order.done(passed, hops[3], out_cross, d_up, outputs, gain_sums)

    low = order.tie(add_low(passed, hops[3]))
    crossed = x_swap(low)
    out_low = add_low(out_low, order.tie(out_cross))
    d_out = join(core, out_low, core_swap(out_low), [width])
    gain_sums = order.tie(gain_sums)
    for step in steps[2:-1]:
        gain_sums = gain_sums + step(gain_sums)
    order.done(crossed, d_out[0], gain_sums)
    gain_sums = gain_sums + steps[-1](order.tie(gain_sums))
    total = order.tie(add_low(low, crossed))
    d_qkv = join(core, total, core_swap(total), [q_width, kv_width, kv_width])

    gain_sums = lax.dynamic_slice_in_dim(gain_sums, fsdp * rows, rows, 1)
    return (
        outputs.reshape(inputs.shape),
        grad_inputs.reshape(inputs.shape),
        d_qkv[0],
        d_qkv[1],
        d_qkv[2],
        d_out[0],
        d_gate,
        d_up,
        d_down,
        gain_sums[0],
        gain_sums[1],
    )


def solution(mesh):
    token_spec, row_spec, gain_spec = P("fsdp", "seq", None), P("fsdp", None), P("fsdp")
    return jax.shard_map(
        shards,
        mesh=mesh,
        in_specs=(token_spec,) + (row_spec,) * 7 + (gain_spec,) * 2 + (token_spec,),
        out_specs=(token_spec,) * 2 + (row_spec,) * 7 + (gain_spec,) * 2,
        check_vma=False,
    )
```

```python
import functools
import math

import jax
import jax.numpy as jnp
from jax import lax
from jax.experimental import pallas as pl
from jax.experimental.pallas import tpu as pltpu
from jax.sharding import PartitionSpec as P

KVH = 8
HD = 64
BLOCK = 256
LINE = 4

EPSILON = 1e-05
THETA = 500000.0
LOG2E = 1.4426950408889634

BF = jnp.bfloat16
F32 = jnp.float32


def after(value, *others):
    return lax.optimization_barrier((value,) + others)[0]


def columns():
    return lax.axis_size("fsdp") // LINE


def z_next(value):
    cols = columns()
    count = lax.axis_size("fsdp")
    return lax.ppermute(value, "fsdp", [(i, (i + cols) % count) for i in range(count)])


def y_next(value):
    cols = columns()
    count = lax.axis_size("fsdp")
    return lax.ppermute(
        value, "fsdp", [(i, i // cols * cols + (i + 1) % cols) for i in range(count)]
    )


def seq_swap(value, bit):
    return lax.ppermute(value, "seq", [(i, i ^ bit) for i in range(lax.axis_size("seq"))])


def core_swap(value):
    return seq_swap(value, 1)


def x_swap(value):
    return seq_swap(value, 2)


def ring_gather(value, step, count):
    pieces = [value]
    for _ in range(count - 1):
        pieces.append(step(pieces[-1]))
    return pieces


def ring_scatter(part_of, step, count):
    total = None
    for j in list(range(1, count)) + [0]:
        total = part_of(j) if total is None else part_of(j) + total.astype(F32)
        if j:
            total = step(total.astype(BF))
    return total


def sum_steps():
    steps = []
    bit = 1
    while bit < lax.axis_size("seq"):
        steps.append(functools.partial(seq_swap, bit=bit))
        bit *= 2
    count = lax.axis_size("fsdp")
    bit = 1
    while bit < count:
        pairs = [(i, i ^ bit) for i in range(count)]
        steps.append(functools.partial(lax.ppermute, axis_name="fsdp", perm=pairs))
        bit *= 2
    return steps


def dot_nt(a, b):
    return lax.dot_general(a, b, (((1,), (1,)), ((), ())), preferred_element_type=F32)

def dot_nn(a, b):
    return jnp.dot(a, b, preferred_element_type=F32)


def attend_forward_kernel(parts, heads, kv, seq_ref, *refs):
    packs, outs = refs[:parts], refs[parts : 2 * parts]
    lse_ref, q_s, k_s, vt_s, o_s = refs[2 * parts :]
    tokens = packs[0].shape[0]
    seq = seq_ref[0]
    group = heads // kv
    for k in range(parts):
        rows = pl.ds(pl.multiple_of((seq ^ k) * tokens, tokens), tokens)
        q_s[rows, :] = packs[k][:, : heads * HD]
        for g in range(kv):
            lane = (heads + g) * HD
            k_s[g, rows, :] = packs[k][:, lane : lane + HD]
            lane = (heads + kv + g) * HD
            vt_s[g, :, rows] = packs[k][:, lane : lane + HD].T
    full = parts * tokens
    for g in range(kv):
        for i in range(full // BLOCK):
            keys = (i + 1) * BLOCK
            rows = slice(i * BLOCK, keys)
            for pair in range(group // 2):
                halves = []
                for h in (g * group + 2 * pair, g * group + 2 * pair + 1):
                    scores = dot_nt(k_s[g, :keys, :], q_s[rows, h * HD : (h + 1) * HD])
                    scores = scores * (HD**-0.5 * LOG2E)
                    top = jnp.max(scores, axis=0, keepdims=True)
                    powers = jnp.exp2(scores - top)
                    total = jnp.sum(powers, axis=0, keepdims=True)
                    halves.append(dot_nn(vt_s[g, :, :keys], powers.astype(BF)) / total)
                    lse_ref[h : h + 1, rows] = top + jnp.log2(total)
                lane = (g * group + 2 * pair) * HD
                o_s[rows, lane : lane + 2 * HD] = jnp.concatenate(halves, axis=0).T.astype(BF)
    for k in range(parts):
        rows = pl.ds(pl.multiple_of((seq ^ k) * tokens, tokens), tokens)
        outs[k][...] = o_s[rows, :]


def attend_forward(seq, packs, heads, kv):
    parts = len(packs)
    tokens = packs[0].shape[0]
    full = parts * tokens
    vmem = pl.BlockSpec(memory_space=pltpu.VMEM)
    flops = 4 * heads * full * full * HD * 5 // 8
    return pl.pallas_call(
        functools.partial(attend_forward_kernel, parts, heads, kv),
        out_shape=[jax.ShapeDtypeStruct((tokens, heads * HD), BF)] * parts
        + [jax.ShapeDtypeStruct((heads, full), F32)],
        in_specs=[pl.BlockSpec(memory_space=pltpu.SMEM)] + [vmem] * parts,
        out_specs=[vmem] * (parts + 1),
        scratch_shapes=[
            pltpu.VMEM((full, heads * HD), BF),
            pltpu.VMEM((kv, full, HD), BF),
            pltpu.VMEM((kv, HD, full), BF),
            pltpu.VMEM((full, heads * HD), BF),
        ],
        compiler_params=pltpu.CompilerParams(vmem_limit_bytes=48 * 2**20),
        cost_estimate=cost(flops * 4, 4 * 2**20),
        name="attend_forward",
    )(seq.reshape(1), *packs)


def attend_backward_kernel(parts, heads, kv, seq_ref, lse_ref, *refs):
    packs, grads, outs = refs[:parts], refs[parts : 2 * parts], refs[2 * parts : 3 * parts]
    q_s, k_s, kt_s, v_s, g_s, dq_s, dk_s, dv_s = refs[3 * parts :]
    tokens = packs[0].shape[0]
    seq = seq_ref[0]
    group = heads // kv
    for k in range(parts):
        rows = pl.ds(pl.multiple_of((seq ^ k) * tokens, tokens), tokens)
        q_s[rows, :] = packs[k][:, : heads * HD]
        g_s[rows, :] = grads[k][...]
        for g in range(kv):
            lane = (heads + g) * HD
            k_s[g, rows, :] = packs[k][:, lane : lane + HD]
            kt_s[g, :, rows] = packs[k][:, lane : lane + HD].T
            lane = (heads + kv + g) * HD
            v_s[g, rows, :] = packs[k][:, lane : lane + HD]
    full = parts * tokens
    dk_s[...] = jnp.zeros_like(dk_s)
    dv_s[...] = jnp.zeros_like(dv_s)
    for g in range(kv):
        for i in range(full // BLOCK):
            keys = (i + 1) * BLOCK
            rows = slice(i * BLOCK, keys)
            for pair in range(group // 2):
                halves = []
                for h in (g * group + 2 * pair, g * group + 2 * pair + 1):
                    query = q_s[rows, h * HD : (h + 1) * HD]
                    grad = g_s[rows, h * HD : (h + 1) * HD]
                    scores = dot_nt(k_s[g, :keys, :], query) * (HD**-0.5 * LOG2E)
                    probs = jnp.exp2(scores - lse_ref[h : h + 1, rows])
                    grad_probs = dot_nt(v_s[g, :keys, :], grad)
                    inner = jnp.sum(probs * grad_probs, axis=0, keepdims=True)
                    grad_scores = (probs * (grad_probs - inner)).astype(BF)
                    dv_s[g, :keys, :] += dot_nn(probs.astype(BF), grad)
                    dk_s[g, :keys, :] += dot_nn(grad_scores, query)
                    halves.append(dot_nn(kt_s[g, :, :keys], grad_scores) * HD**-0.5)
                lane = (g * group + 2 * pair) * HD
                dq_s[rows, lane : lane + 2 * HD] = jnp.concatenate(halves, axis=0).T.astype(BF)
    for k in range(parts):
        rows = pl.ds(pl.multiple_of((seq ^ k) * tokens, tokens), tokens)
        outs[k][:, : heads * HD] = dq_s[rows, :]
        for g in range(kv):
            lane = (heads + g) * HD
            outs[k][:, lane : lane + HD] = (dk_s[g, rows, :] * HD**-0.5).astype(BF)
            lane = (heads + kv + g) * HD
            outs[k][:, lane : lane + HD] = dv_s[g, rows, :].astype(BF)


def attend_backward(seq, lse, packs, grads, heads, kv):
    parts = len(packs)
    tokens = packs[0].shape[0]
    full = parts * tokens
    vmem = pl.BlockSpec(memory_space=pltpu.VMEM)
    flops = 10 * heads * full * full * HD * 5 // 8
    return pl.pallas_call(
        functools.partial(attend_backward_kernel, parts, heads, kv),
        out_shape=[jax.ShapeDtypeStruct(packs[0].shape, BF)] * parts,
        in_specs=[pl.BlockSpec(memory_space=pltpu.SMEM)] + [vmem] * (2 * parts + 1),
        out_specs=[vmem] * parts,
        scratch_shapes=[
            pltpu.VMEM((full, heads * HD), BF),
            pltpu.VMEM((kv, full, HD), BF),
            pltpu.VMEM((kv, HD, full), BF),
            pltpu.VMEM((kv, full, HD), BF),
            pltpu.VMEM((full, heads * HD), BF),
            pltpu.VMEM((full, heads * HD), BF),
            pltpu.VMEM((kv, full, HD), F32),
            pltpu.VMEM((kv, full, HD), F32),
        ],
        compiler_params=pltpu.CompilerParams(vmem_limit_bytes=48 * 2**20),
        cost_estimate=cost(flops * 4, 8 * 2**20),
        name="attend_backward",
    )(seq.reshape(1), lse, *packs, *grads)


def smem():
    return pl.BlockSpec(memory_space=pltpu.SMEM)


def params(mib=56):
    return pltpu.CompilerParams(vmem_limit_bytes=mib * 2**20)


def cost(flops, moved):
    return pl.CostEstimate(flops=flops // 8, bytes_accessed=moved // 8, transcendentals=0)


def place(shape, pieces, offsets, most=None):
    count = len(pieces)

    def kernel(at_ref, *refs):
        sources, target, sems = refs[:-2], refs[-2], refs[-1]
        copies = []
        for i, source in enumerate(sources):
            rows, width = source.shape
            rows = min(rows, most or rows)
            row = pl.multiple_of(at_ref[2 * i], rows)
            column = pl.multiple_of(at_ref[2 * i + 1], width)
            spot = target.at[pl.ds(row, rows), pl.ds(column, width)]
            copies.append(pltpu.make_async_copy(source.at[pl.ds(0, rows), :], spot, sems.at[i]))
            copies[-1].start()
        for copy in copies:
            copy.wait()

    moved = 2 * sum(piece.size * 2 for piece in pieces)
    return pl.pallas_call(
        kernel,
        out_shape=jax.ShapeDtypeStruct(shape, pieces[0].dtype),
        in_specs=[smem()] + [pl.BlockSpec(memory_space=pl.ANY)] * count,
        out_specs=pl.BlockSpec(memory_space=pltpu.HBM),
        scratch_shapes=[pltpu.SemaphoreType.DMA((count,))],
        compiler_params=params(16),
        cost_estimate=cost(0, moved),
        name="place",
    )(jnp.stack([jnp.int32(v) for pair in offsets for v in pair]), *pieces)


def turn(values, cos_table, sin_table):
    width = values.shape[1]
    lane = lax.broadcasted_iota(jnp.int32, values.shape, 1)
    swapped = jnp.where(
        lane % HD < HD // 2,
        pltpu.roll(values, width - HD // 2, 1),
        pltpu.roll(values, HD // 2, 1),
    )
    return values * cos_table + swapped * sin_table


def whole(shape):
    return pl.BlockSpec(shape, lambda n: (0,) * len(shape))


def project_in(seq, z, inputs, gain, groups, cos_table, sin_table, parts):
    tokens, width = inputs.shape
    tile = cos_table.shape[1]
    each = tile // parts
    pack = tile + 2 * each
    count = len(groups)
    depth = width // count

    def kernel(at_ref, in_ref, gain_ref, *refs):
        w_refs, (cos_ref, sin_ref, acts_ref), packs = refs[:count], refs[count : count + 3], refs[count + 3 :]
        step = pl.program_id(0)

        @pl.when(step == 0)
        def _():
            values = in_ref[...].astype(F32)
            scale = lax.rsqrt(jnp.mean(values * values, axis=-1, keepdims=True) + EPSILON)
            acts_ref[...] = (values * scale * gain_ref[...]).astype(BF)

        rows = None
        for j in range(count):
            lanes = pl.ds(pl.multiple_of((at_ref[1] + count - j) % count * depth, depth), depth)
            term = dot_nn(acts_ref[:, lanes], w_refs[j][...])
            rows = term if rows is None else rows + term
        turned = jnp.where(
            step == parts + 1, rows, turn(rows, cos_ref[...], sin_ref[...])
        ).astype(BF)
        seq_now = at_ref[0]
        for k in range(parts):

            @pl.when((seq_now ^ k) == step)
            def _():
                packs[k][:, :tile] = turned

            for d in range(parts):
                for which in range(2):

                    @pl.when(((seq_now ^ k) == d) & (step == parts + which))
                    def _():
                        lane = tile + which * each
                        packs[k][:, lane : lane + each] = turned[:, d * each : (d + 1) * each]

    return pl.pallas_call(
        kernel,
        grid=(parts + 2,),
        out_shape=[jax.ShapeDtypeStruct((tokens, width), BF)]
        + [jax.ShapeDtypeStruct((tokens, pack), BF)] * parts,
        in_specs=[smem(), whole((tokens, width)), whole((1, width))]
        + [pl.BlockSpec((depth, tile), lambda n: (0, n))] * count
        + [whole((tokens, tile))] * 2,
        out_specs=[whole((tokens, width))] + [whole((tokens, pack))] * parts,
        compiler_params=params(),
        cost_estimate=cost(2 * tokens * width * tile * (parts + 2), 2 * width * tile * (parts + 2)),
        name="project_in",
    )(jnp.stack([seq, z]), inputs, gain, *groups, cos_table, sin_table)


def project_out(seq, z, mixed, inputs, gain, groups):
    parts = len(mixed)
    tokens, width = inputs.shape
    each = mixed[0].shape[1]
    tile = width // parts
    count = len(groups)
    depth = parts * each // count

    def kernel(at_ref, *refs):
        parts_in, (in_ref, gain_ref) = refs[:parts], refs[parts : parts + 2]
        w_refs, (flat_ref, res_ref, acts_ref) = refs[parts + 2 : -3], refs[-3:]
        step = pl.program_id(0)

        @pl.when(step == 0)
        def _():
            for k in range(parts):
                lane = pl.multiple_of((at_ref[0] ^ k) * each, each)
                flat_ref[:, pl.ds(lane, each)] = parts_in[k][...]

        lanes = pl.ds(pl.multiple_of(step * tile, tile), tile)
        total = in_ref[:, lanes].astype(F32)
        for j in range(count):
            rows = pl.ds(pl.multiple_of((at_ref[1] + count - j) % count * depth, depth), depth)
            total = total + dot_nn(flat_ref[:, rows], w_refs[j][...])
        res_ref[:, lanes] = total

        @pl.when(step == parts - 1)
        def _():
            values = res_ref[...]
            scale = lax.rsqrt(jnp.mean(values * values, axis=-1, keepdims=True) + EPSILON)
            acts_ref[...] = (values * scale * gain_ref[...]).astype(BF)

    return pl.pallas_call(
        kernel,
        grid=(parts,),
        out_shape=[
            jax.ShapeDtypeStruct((tokens, parts * each), BF),
            jax.ShapeDtypeStruct((tokens, width), F32),
            jax.ShapeDtypeStruct((tokens, width), BF),
        ],
        in_specs=[smem()]
        + [whole((tokens, each))] * parts
        + [whole((tokens, width)), whole((1, width))]
        + [pl.BlockSpec((depth, tile), lambda n: (0, n))] * count,
        out_specs=[whole((tokens, parts * each)), whole((tokens, width)), whole((tokens, width))],
        compiler_params=params(),
        cost_estimate=cost(2 * tokens * width * parts * each, 2 * width * parts * each),
        name="project_out",
    )(jnp.stack([seq, z]), *mixed, inputs, gain, *groups)


def feed_forward(acts, grads, gate, up, down, begun=None):
    tokens, width = acts.shape
    hidden = gate.shape[0]
    tile = 256
    steps = hidden // tile
    kind = F32 if begun is None else BF
    begun = [] if begun is None else list(begun)

    def kernel(a_ref, c_ref, g_ref, u_ref, d_ref, *refs):
        starts, (h_ref, gg_ref, gu_ref, o_ref, ga_ref, o_s, ga_s) = refs[:-7], refs[-7:]
        step = pl.program_id(0)

        @pl.when(step == 0)
        def _():
            if starts:
                o_s[...] = starts[0][...]
                ga_s[...] = starts[1][...]
            else:
                o_s[...] = jnp.zeros_like(o_s)
                ga_s[...] = jnp.zeros_like(ga_s)

        gate_act = dot_nt(a_ref[...], g_ref[...])
        up_act = dot_nt(a_ref[...], u_ref[...])
        grad_hidden = dot_nt(c_ref[...], d_ref[...])
        sigma = jax.nn.sigmoid(gate_act)
        silu = gate_act * sigma
        low = (silu * up_act).astype(BF)
        grad_gate = (grad_hidden * up_act * (sigma * (1.0 + gate_act * (1.0 - sigma)))).astype(BF)
        grad_up = (grad_hidden * silu).astype(BF)
        h_ref[...] = low
        gg_ref[...] = grad_gate
        gu_ref[...] = grad_up
        o_s[...] += dot_nn(low, d_ref[...])
        ga_s[...] += dot_nn(grad_gate, g_ref[...]) + dot_nn(grad_up, u_ref[...])

        @pl.when(step == steps - 1)
        def _():
            o_ref[...] = o_s[...].astype(kind)
            ga_ref[...] = ga_s[...].astype(kind)

    whole = pl.BlockSpec((tokens, width), lambda n: (0, 0))
    rows = pl.BlockSpec((tile, width), lambda n: (n, 0))
    lanes = pl.BlockSpec((tokens, tile), lambda n: (0, n))
    return pl.pallas_call(
        kernel,
        grid=(steps,),
        out_shape=[jax.ShapeDtypeStruct((tokens, hidden), BF)] * 3
        + [jax.ShapeDtypeStruct((tokens, width), kind)] * 2,
        in_specs=[whole, whole, rows, rows, rows] + [whole] * len(begun),
        out_specs=[lanes] * 3 + [whole] * 2,
        scratch_shapes=[pltpu.VMEM((tokens, width), F32)] * 2,
        compiler_params=params(),
        cost_estimate=cost(12 * tokens * width * hidden, 6 * width * hidden),
        name="feed_forward",
    )(acts, grads, gate, up, down, *begun)


def middle_back(seq, z, terms, residual, grad_out, gain, groups, parts):
    tokens, width = residual.shape
    tile = groups[0].shape[0]
    count = len(groups)
    assert count == parts

    def kernel(at_ref, t0_ref, t1_ref, res_ref, go_ref, gain_ref, *refs):
        w_refs, (gr_ref, low_ref, gg_ref), outs = refs[:count], refs[count : count + 3], refs[count + 3 :]
        grad = t0_ref[...].astype(F32) + t1_ref[...].astype(F32)
        values = res_ref[...]
        scale = lax.rsqrt(jnp.mean(values * values, axis=-1, keepdims=True) + EPSILON)
        weighted = grad * gain_ref[...]
        inner = jnp.mean(weighted * values, axis=-1, keepdims=True)
        result = go_ref[...].astype(F32) + scale * weighted - values * (scale**3 * inner)
        gr_ref[...] = result
        low_ref[...] = result.astype(BF)
        gg_ref[...] = jnp.sum(grad * values * scale, axis=0, keepdims=True)
        for j in range(count):
            part = dot_nt(low_ref[...], w_refs[j][...]).astype(BF)
            at = ((at_ref[1] + count - j) % count) ^ at_ref[0]
            for k in range(parts):

                @pl.when(at == k)
                def _():
                    outs[k][...] = part

    vmem = pl.BlockSpec(memory_space=pltpu.VMEM)
    return pl.pallas_call(
        kernel,
        out_shape=[
            jax.ShapeDtypeStruct((tokens, width), F32),
            jax.ShapeDtypeStruct((tokens, width), BF),
            jax.ShapeDtypeStruct((1, width), F32),
        ]
        + [jax.ShapeDtypeStruct((tokens, tile), BF)] * parts,
        in_specs=[smem()] + [vmem] * (5 + count),
        out_specs=[vmem] * (3 + parts),
        compiler_params=params(),
        cost_estimate=cost(2 * tokens * width * tile * parts, 2 * width * tile * parts + 8 * tokens * width),
        name="middle_back",
    )(jnp.stack([seq, z]), terms[0], terms[1], residual, grad_out, gain, *groups)


def unpack(seq, packs, cos_table, sin_table):
    parts = len(packs)
    tokens, tile = cos_table.shape
    each = tile // parts

    def kernel(seq_ref, *refs):
        ins, (cos_ref, sin_ref, out_ref) = refs[:parts], refs[parts:]
        for k in range(parts):
            at = seq_ref[0] ^ k
            queries = turn(ins[k][:, :tile].astype(F32), cos_ref[...], -sin_ref[...])
            out_ref[:, pl.ds(pl.multiple_of(at * tile, tile), tile)] = queries.astype(BF)
            keys = turn(
                ins[k][:, tile : tile + each].astype(F32), cos_ref[:, :each], -sin_ref[:, :each]
            )
            lane = pl.multiple_of(parts * tile + at * each, each)
            out_ref[:, pl.ds(lane, each)] = keys.astype(BF)
            lane = pl.multiple_of((parts + 1) * tile + at * each, each)
            out_ref[:, pl.ds(lane, each)] = ins[k][:, tile + each :]

    vmem = pl.BlockSpec(memory_space=pltpu.VMEM)
    return pl.pallas_call(
        kernel,
        out_shape=jax.ShapeDtypeStruct((tokens, (parts + 2) * tile), BF),
        in_specs=[smem()] + [vmem] * (parts + 2),
        out_specs=vmem,
        compiler_params=params(),
        cost_estimate=cost(0, 6 * 2**20),
        name="unpack",
    )(seq.reshape(1), *packs, cos_table, sin_table)


def inner_back(z, grad_qkv, groups, inputs, gain, grad_res):
    tokens, width = inputs.shape
    count = len(groups)
    depth = width // count

    def kernel(at_ref, gq_ref, *refs):
        w_refs, (in_ref, gain_ref, gr_ref, out_ref, gg_ref, grad_s) = refs[:count], refs[count:]
        for j in range(count):
            lanes = pl.ds(pl.multiple_of((at_ref[0] + count - j) % count * depth, depth), depth)
            grad_s[:, lanes] = dot_nt(gq_ref[...], w_refs[j][...])
        grad = grad_s[...]
        values = in_ref[...].astype(F32)
        scale = lax.rsqrt(jnp.mean(values * values, axis=-1, keepdims=True) + EPSILON)
        weighted = grad * gain_ref[...]
        inner = jnp.mean(weighted * values, axis=-1, keepdims=True)
        result = gr_ref[...] + scale * weighted - values * (scale**3 * inner)
        out_ref[...] = result.astype(BF)
        gg_ref[...] = jnp.sum(grad * values * scale, axis=0, keepdims=True)

    vmem = pl.BlockSpec(memory_space=pltpu.VMEM)
    return pl.pallas_call(
        kernel,
        out_shape=[jax.ShapeDtypeStruct((tokens, width), BF), jax.ShapeDtypeStruct((1, width), F32)],
        in_specs=[smem()] + [vmem] * (4 + count),
        out_specs=[vmem] * 2,
        scratch_shapes=[pltpu.VMEM((tokens, width), F32)],
        compiler_params=params(),
        cost_estimate=cost(2 * tokens * groups[0].size * count, 2 * groups[0].size * count),
        name="inner_back",
    )(z.reshape(1), grad_qkv, *groups, inputs, gain, grad_res)


def weight_grad(left, right, rows, blocks, half, adds=(), pieces=1):
    count = len(left)
    tokens = left[0].shape[0]
    width = right[0].shape[1] // 2
    total_rows = rows * len(blocks)
    piece = total_rows // pieces
    tile = math.gcd(math.gcd(rows, 512), piece)
    steps = rows // tile
    each = piece // tile

    def kernel(at_ref, *refs):
        lefts, rights = refs[:count], refs[count : 2 * count]
        extra, outs = refs[2 * count : -pieces], refs[-pieces:]
        total = None
        for l_ref, r_ref in zip(lefts, rights):
            term = lax.dot_general(
                l_ref[...], r_ref[...], (((0,), (0,)), ((), ())), preferred_element_type=F32
            )
            total = term if total is None else total + term
        for ref in extra:
            total = total + ref[...].astype(F32)
        total = total.astype(BF)
        for p, out in enumerate(outs):
            if pieces == 1:
                out[...] = total
            else:

                @pl.when(pl.program_id(0) // each == p)
                def _():
                    out[...] = total

    def spec_of(p):
        if pieces == 1:
            return pl.BlockSpec((tile, width), lambda n, at: (n, 0))
        return pl.BlockSpec((tile, width), lambda n, at: (jnp.clip(n - p * each, 0, each - 1), 0))

    spec = pltpu.PrefetchScalarGridSpec(
        num_scalar_prefetch=1,
        grid=(steps * len(blocks),),
        in_specs=[pl.BlockSpec((tokens, tile), lambda n, at: (0, at[1 + n]))] * count
        + [pl.BlockSpec((tokens, width), lambda n, at: (0, at[0]))] * count
        + [pl.BlockSpec((tile, width), lambda n, at: (n, 0))] * len(adds),
        out_specs=[spec_of(p) for p in range(pieces)],
    )
    at = [jnp.int32(half)]
    for block in blocks:
        at += [jnp.int32(block) * steps + i for i in range(steps)]
    outs = pl.pallas_call(
        kernel,
        grid_spec=spec,
        out_shape=[jax.ShapeDtypeStruct((piece, width), BF)] * pieces,
        compiler_params=params(),
        cost_estimate=cost(
            2 * tokens * count * total_rows * width, 2 * (tokens * count + total_rows) * width
        ),
        name="weight_grad",
    )(jnp.stack(at), *left, *right, *adds)
    return outs[0] if pieces == 1 else list(outs)


def row_grads(left, right, blocks, half, added, y, cuts):
    tokens = left.shape[0]
    width = right.shape[1] // 2
    rows = left.shape[1] // LINE
    each = rows // cuts
    count = len(blocks)

    def kernel(at_ref, l_ref, r_ref, add_ref, *refs):
        outs, total_s = refs[:-1], refs[-1]
        total = lax.dot_general(
            l_ref[...], r_ref[...], (((0,), (0,)), ((), ())), preferred_element_type=F32
        )
        total_s[...] = (total + add_ref[...].astype(F32)).astype(BF)
        for j in range(count):

            @pl.when(pl.program_id(0) == j)
            def _():
                for k in range(cuts):
                    start = pl.multiple_of((at_ref[1] + cuts - k) % cuts * each, each)
                    outs[j * cuts + k][...] = total_s[pl.ds(start, each), :]

    spec = pltpu.PrefetchScalarGridSpec(
        num_scalar_prefetch=1,
        grid=(count,),
        in_specs=[
            pl.BlockSpec((tokens, rows), lambda n, at: (0, at[2 + n])),
            pl.BlockSpec((tokens, width), lambda n, at: (0, at[0])),
            pl.BlockSpec((rows, width), lambda n, at: (n, 0)),
        ],
        out_specs=[pl.BlockSpec((each, width), lambda n, at: (0, 0))] * (count * cuts),
        scratch_shapes=[pltpu.VMEM((rows, width), BF)],
    )
    at = jnp.stack([jnp.int32(half), jnp.int32(y)] + [jnp.int32(b) for b in blocks])
    outs = pl.pallas_call(
        kernel,
        grid_spec=spec,
        out_shape=[jax.ShapeDtypeStruct((each, width), BF)] * (count * cuts),
        compiler_params=params(),
        cost_estimate=cost(2 * tokens * count * rows * width, 6 * count * rows * width),
        name="row_grads",
    )(at, left, right, added)
    return [outs[j * cuts : (j + 1) * cuts] for j in range(count)]


def join(core, mine, other, widths):
    rows, half = mine.shape
    tile = min(rows, 256)

    def kernel(core_ref, mine_ref, other_ref, *refs):
        outs, full = refs[:-1], refs[-1]
        target = outs[0] if len(outs) == 1 else full
        at = pl.multiple_of(core_ref[0] * half, half)
        target[:, pl.ds(at, half)] = mine_ref[...].astype(F32)
        at = pl.multiple_of((1 - core_ref[0]) * half, half)
        target[:, pl.ds(at, half)] = other_ref[...].astype(F32)
        if len(outs) > 1:
            lane = 0
            for out in outs:
                out[...] = full[:, lane : lane + out.shape[1]]
                lane += out.shape[1]

    def block(width):
        return pl.BlockSpec((tile, width), lambda n: (n, 0))

    return pl.pallas_call(
        kernel,
        grid=(rows // tile,),
        out_shape=[jax.ShapeDtypeStruct((rows, width), F32) for width in widths],
        in_specs=[smem(), block(half), block(half)],
        out_specs=[block(width) for width in widths],
        scratch_shapes=[pltpu.VMEM((tile, 2 * half) if len(widths) > 1 else (8, 128), F32)],
        compiler_params=params(),
        cost_estimate=cost(0, rows * half * 12),
        name="join",
    )(core.reshape(1), mine, other)
def half_of(array, which, axis=1):
    size = array.shape[axis] // 2
    return lax.dynamic_slice_in_dim(array, which * size, size, axis)


def join_halves(core, top, bottom):
    rows, half = top[0].shape
    tile = min(rows, 256)
    steps = rows // tile

    def kernel(core_ref, a_ref, b_ref, c_ref, d_ref, out):
        mine = pl.multiple_of(core_ref[0] * half, half)
        other = pl.multiple_of((1 - core_ref[0]) * half, half)
        upper = pl.program_id(0) < steps

        @pl.when(upper)
        def _():
            out[:, pl.ds(mine, half)] = a_ref[...].astype(F32)
            out[:, pl.ds(other, half)] = b_ref[...].astype(F32)

        @pl.when(jnp.logical_not(upper))
        def _():
            out[:, pl.ds(mine, half)] = c_ref[...].astype(F32)
            out[:, pl.ds(other, half)] = d_ref[...].astype(F32)

    first = pl.BlockSpec((tile, half), lambda n: (jnp.minimum(n, steps - 1), 0))
    second = pl.BlockSpec((tile, half), lambda n: (jnp.maximum(n - steps, 0), 0))
    return pl.pallas_call(
        kernel,
        grid=(2 * steps,),
        out_shape=jax.ShapeDtypeStruct((2 * rows, 2 * half), F32),
        in_specs=[smem(), first, first, second, second],
        out_specs=pl.BlockSpec((tile, 2 * half), lambda n: (n, 0)),
        compiler_params=params(),
        cost_estimate=cost(0, rows * half * 24),
        name="join_halves",
    )(core.reshape(1), *top, *bottom)


class Order:
    def __init__(self):
        self.marks = ()

    def tie(self, *values):
        if self.marks:
            values = lax.optimization_barrier(tuple(values) + self.marks)[: len(values)]
        return values[0] if len(values) == 1 else list(values)

    def done(self, *values):
        self.marks = tuple(values)


def y_hops(value):
    return ring_gather(value, y_next, columns())[1:]


def add_low(left, right):
    return (left.astype(F32) + right.astype(F32)).astype(BF)


def rope_tables(positions, repeat):
    frequency = THETA ** (-(jnp.arange(HD // 2, dtype=F32) * 2.0) / HD)
    angles = positions.astype(F32)[:, None] * frequency[None, :]
    cos, sin = jnp.cos(angles), jnp.sin(angles)
    return (
        jnp.tile(jnp.concatenate([cos, cos], axis=1), (1, repeat)),
        jnp.tile(jnp.concatenate([-sin, sin], axis=1), (1, repeat)),
    )


def exchange(packs):
    return [packs[0]] + [seq_swap(packs[k], k) for k in range(1, len(packs))]


def shards(
    inputs,
    query_weight,
    key_weight,
    value_weight,
    output_weight,
    gate_weight,
    up_weight,
    down_weight,
    gain_attn,
    gain_ffn,
    cotangent,
):
    seq_count, local_len, width = inputs.shape
    assert seq_count == 1
    tokens = local_len
    parts = lax.axis_size("seq")
    kv_local = KVH // parts
    cols = columns()
    seq = lax.axis_index("seq")
    core, side = seq % 2, seq // 2
    fsdp = lax.axis_index("fsdp")
    z, y = fsdp // cols, fsdp % cols
    q_width, kv_width = query_weight.shape[1], key_weight.shape[1]
    heads_local = q_width // HD // parts
    flat_in = inputs.reshape(tokens, width)
    grad_out = cotangent.reshape(tokens, width)

    qkv_shard = jnp.concatenate([query_weight, key_weight, value_weight], axis=1)
    rows = qkv_shard.shape[0]
    part, half = rows // 2, qkv_shard.shape[1] // 2
    positions = seq * local_len + jnp.arange(local_len)
    cos_table, sin_table = rope_tables(positions, kv_width // HD)
    order = Order()

    def swapped(pieces):
        return [core_swap(p) for p in pieces]

    def place_halves(pieces, others, whole_first=None):
        each = pieces[-1].shape[1]
        placed, offsets = [], []
        for k, (piece, other) in enumerate(zip(pieces, others)):
            row = (y - k) % cols * rows
            if k == 0 and whole_first is not None:
                placed.append(whole_first)
                offsets.append((row, 0))
            else:
                placed += [piece, other]
                offsets += [(row, core * each), (row, (1 - core) * each)]
        return place((rows * cols, 2 * each), placed, offsets)

    def place_quarters(pieces, others, sides, count, size, first):
        each = pieces[0].shape[1]
        placed, offsets = [], []
        for i, (piece, other) in enumerate(zip(pieces, others)):
            k, at = i // 2, sides[i % 2]
            row = first(k) * size + at * (size // 2)
            placed += [piece, other]
            offsets += [(row, core * each), (row, (1 - core) * each)]
        return place((size * count, 2 * each), placed, offsets)

    def line_row(k):
        return (y - k) % cols

    own = (gate_weight, up_weight, down_weight)
    far_rows = gate_weight.shape[0]
    far_part = far_rows // 4
    far_y, far_x = {}, {}

    def far_start(i, h):
        at = side * 2 * far_part + h * far_part
        return lax.dynamic_slice(own[i], (at, core * out_width), (far_part, out_width))

    out_width = width // 2
    far_starts = {(i, h): far_start(i, h) for i in range(3) for h in range(2)}

    def far_along_y(i, h):
        start = order.tie(far_starts[i, h]) if order.marks else far_starts[i, h]
        far_y[i, h] = y_hops(start)
        return far_y[i, h]

    def far_along_x(i, h):
        pieces = order.tie(*far_y[i, h], far_y[i, h][0])[:-1]
        far_x[i, h] = [x_swap(p) for p in pieces]
        return far_x[i, h]

    gains = jnp.concatenate([gain_attn, gain_ffn]).reshape(1, 2 * rows)
    start = half_of(qkv_shard, core)
    start = jnp.concatenate([start, jnp.pad(gains, ((0, 15), (0, half - 2 * rows)))], axis=0)
    out_half = half_of(output_weight, core)

    def quarter_of(piece):
        return lax.dynamic_slice_in_dim(piece, side * part, part, 0)

    def line_group(i):
        here = order.tie(line[i])
        placed, offsets = [], []
        row = y * rows
        if i:
            placed += [here, core_swap(here)]
            offsets += [(row, core * half), (row, (1 - core) * half)]
        else:
            placed.append(qkv_shard)
            offsets.append((row, 0))
        for k in range(1, cols):
            row = (y - k) % cols * rows
            if i < LINE - 1:
                for piece, at in ((beside[i][k - 1], side), (crossed[i][k - 1], 1 - side)):
                    piece = order.tie(piece)
                    placed += [piece, core_swap(piece)]
                    offsets += [
                        (row + at * part, core * half),
                        (row + at * part, (1 - core) * half),
                    ]
            else:
                piece = order.tie(beside[i][k - 1])
                placed += [piece, core_swap(piece)]
                offsets += [(row, core * half), (row, (1 - core) * half)]
        return place((rows * cols, 2 * half), placed, offsets, rows)

    line, beside, crossed, groups = [start], [], [], []
    for j in range(LINE):
        here = order.tie(line[j]) if j else line[j]
        if j + 1 < LINE:
            line.append(z_next(here))
            beside.append(y_hops(quarter_of(here)))
            marks = [line[j + 1]] + beside[j] + far_along_y(j // 2, j % 2)
        else:
            beside.append(y_hops(here))
            line_o = [out_half, z_next(order.tie(out_half))]
            grad_parts = [grad_out, z_next(order.tie(grad_out))]
            gains_near = jnp.concatenate([p[rows:, : 2 * rows] for p in line[:j]], axis=0)
            gains_far = y_hops(order.tie(gains_near))
            marks = beside[j] + [line_o[1]]
        if j:
            pieces = order.tie(*beside[j - 1], here)[:-1]
            crossed.append([x_swap(p) for p in pieces])
            marks += crossed[j - 1]
        if j > 1:
            groups.append(line_group(j - 2))
            marks.append(groups[-1])
        if j == 1:
            marks += [cos_table, sin_table] + list(far_starts.values())
        order.done(*marks)

    line_o.append(z_next(order.tie(line_o[1])))
    beside_o = [y_hops(order.tie(line_o[0])), y_hops(order.tie(line_o[1]))]
    groups += [line_group(LINE - 2), line_group(LINE - 1)]
    marks = far_along_x(0, 0)
    gain_full = jnp.zeros((2, width), BF)
    for j in range(LINE):
        for k in range(cols):
            if j == LINE - 1:
                g = line[j][rows] if k == 0 else beside[j][k - 1][rows]
                pair = g[: 2 * rows].reshape(2, rows)
            else:
                g = gains_near if k == 0 else gains_far[k - 1]
                pair = g[16 * j].reshape(2, rows)
            at = (((z - j) % LINE) * cols + (y - k) % cols) * rows
            gain_full = lax.dynamic_update_slice(gain_full, pair, (0, at))
    gain_one = gain_full[:1].astype(F32)
    gain_two = gain_full[1:].astype(F32)
    acts_one, *sent = project_in(seq, z, flat_in, gain_one, groups, cos_table, sin_table, parts)
    order.done(*sent, line_o[2], *beside_o[0], *beside_o[1], grad_parts[1], *marks)

    def out_swaps(j, *others):
        hops = order.tie(line_o[j], *beside_o[j], *others)[: cols]
        if j == 0:
            return [None] + hops[1:], [None] + swapped(hops[1:])
        return hops, swapped(hops)

    def out_group(pair, j):
        hops, others = pair
        first = 0 if j else 1
        tied = order.tie(*hops[first:], *others[first:])
        count = cols - first
        return place_halves(
            [None] * first + tied[:count],
            [None] * first + tied[count:],
            None if j else output_weight,
        )

    packs = exchange(order.tie(*sent))
    line_o.append(z_next(order.tie(line_o[2])))
    beside_o.append(y_hops(order.tie(line_o[2])))
    pairs = [out_swaps(j, packs[2]) for j in range(2)]
    grad_top = [z_next(order.tie(grad_parts[1])[: tokens // 2])]
    swaps = [p for pair in pairs for p in pair[1][1:]]
    order.done(*packs, line_o[3], *beside_o[2], grad_top[0], *swaps)

    beside_o.append(y_hops(order.tie(line_o[3])))
    grad_low = [z_next(order.tie(grad_parts[1])[tokens // 2 :])]
    pairs.append(out_swaps(2))
    *mixed_sent, log_totals = attend_forward(seq, order.tie(*packs), heads_local, kv_local)
    order.done(*mixed_sent, *beside_o[3], grad_low[0])

    mixed = exchange(order.tie(*mixed_sent))
    pairs.append(out_swaps(3))
    out_groups = [out_group(pairs[j], j) for j in range(LINE - 1)]
    out_groups.append(place_halves(*pairs[3]))
    grad_top.append(z_next(order.tie(grad_top[0])))
    order.done(*mixed, *out_groups, grad_top[1])

    grad_low.append(z_next(order.tie(grad_low[0])))
    grad_parts += [jnp.concatenate(pair, axis=0) for pair in zip(grad_top, grad_low)]
    marks = far_along_y(1, 1) + far_along_x(0, 1) + [grad_low[1]]
    mixed_flat, residual, acts_two = project_out(
        seq, z, order.tie(*mixed), flat_in, gain_two, out_groups
    )
    order.done(acts_two, *marks)

    def far_place(i, *others):
        placed, offsets = [], []
        for k in range(cols - 1):
            for h in range(2):
                pieces = order.tie(far_y[i, h][k], far_x[i, h][k], *others)[:2]
                for piece, at in zip(pieces, (side, 1 - side)):
                    row = k * far_rows + at * 2 * far_part + h * far_part
                    placed += [piece, core_swap(piece)]
                    offsets += [(row, core * out_width), (row, (1 - core) * out_width)]
        return place((far_rows * (cols - 1), width), placed, offsets)

    acts_parts, far, near_done, far_done = [acts_two], [], [], [None] * LINE

    def run_near(j):
        near_done.append(feed_forward(order.tie(acts_parts[j]), grad_parts[j], *own))
        return near_done[j][3]

    def run_far(j):
        far_done[j] = feed_forward(order.tie(acts_parts[j]), grad_parts[j], *far, near_done[j][3:])
        return far_done[j][4]

    acts_parts.append(z_next(order.tie(acts_parts[0])))
    marks = far_along_y(2, 0) + far_along_y(2, 1) + far_along_x(1, 0) + far_along_x(1, 1)
    far.append(far_place(0))
    order.done(acts_parts[1], *marks, *far, run_near(0))
    acts_parts.append(z_next(order.tie(acts_parts[1])))
    marks = far_along_x(2, 0) + far_along_x(2, 1)
    far.append(far_place(1))
    order.done(acts_parts[2], *marks, *far, run_near(1))
    acts_parts.append(z_next(order.tie(acts_parts[2])))
    far.append(far_place(2))
    marks = [run_near(2), run_far(1)]
    order.done(acts_parts[3], *marks)

    passed = z_next(order.tie(far_done[1][4]))
    marks = [run_near(3), run_far(2)]
    order.done(passed, *marks)
    passed = z_next(order.tie(add_low(passed, far_done[2][4])))
    marks = [run_far(3), run_far(0)]
    order.done(passed, *marks)
    passed = z_next(order.tie(add_low(passed, far_done[3][4])))

    rights = (grad_parts, acts_parts, acts_parts)
    far_size = far_rows * (cols - 1)
    far_sent, far_total, own_sent = [None] * 3, {}, [None] * 3

    def of(done, which):
        return order.tie(*[d[which] for d in done])

    def send_far(i):
        far_sent[i] = weight_grad(of(far_done, i), rights[i], far_size, [0], 1 - core)
        return far_sent[i]

    def keep_far(i):
        return weight_grad(
            of(far_done, i), rights[i], far_size, [0], core, [far_sent[i]], 2 * (cols - 1)
        )

    def pass_far(i, kept, h):
        total = y_next(order.tie(kept[h]))
        for k in range(1, cols - 1):
            total = y_next(add_low(total, order.tie(kept[2 * k + h])))
        far_total[i, h] = total
        return total

    def send_own(i):
        own_sent[i] = weight_grad(of(near_done, i), rights[i], far_rows, [0], 1 - core)
        return own_sent[i]

    def keep_own(i):
        return weight_grad(of(near_done, i), rights[i], far_rows, [0], core, [own_sent[i]])

    first = send_far(0)
    far_sent[0] = core_swap(first)
    marks = [send_far(1), send_far(2)]
    kept = [keep_far(0)]
    order.done(passed, *kept[0], *marks)

    marks = [pass_far(0, kept[0], 0)]
    far_sent[1:] = [core_swap(order.tie(term)) for term in far_sent[1:]]
    ffn_parts = [d[3] for d in far_done]
    ffn_sum = z_next(order.tie(ffn_parts[1]))
    grad_res, grad_res_low, grad_gain_two, *grad_sent = middle_back(
        seq, z, order.tie(passed, far_done[0][4]), residual, grad_out, gain_two, out_groups, parts
    )
    order.done(*grad_sent, *far_sent[1:])

    grad_packs = exchange(order.tie(*grad_sent))
    kept.append(keep_far(1))
    first = send_own(0)
    order.done(*grad_packs, ffn_sum, *kept[1], first, *marks)

    marks = [pass_far(0, kept[0], 1)]
    later = [pass_far(1, kept[1], 0)]
    ffn_sum = z_next(order.tie(add_low(ffn_sum, ffn_parts[2])))
    back_sent = attend_backward(
        seq, log_totals, packs, order.tie(*grad_packs), heads_local, kv_local
    )
    order.done(*back_sent, *marks)

    line_order = list(range(1, LINE)) + [0]
    blocks = [(z - j) % LINE for j in line_order]
    line_rows = rows * cols
    back_packs = exchange(order.tie(*back_sent))
    own_sent[0] = core_swap(order.tie(own_sent[0]))
    out_left, out_right = order.tie(mixed_flat, grad_res_low)
    out_sent = weight_grad([out_left], [out_right], line_rows, blocks, 1 - core)
    kept.append(keep_far(2))
    own_low = [keep_own(0)]
    marks = [*later, *kept[2], own_low[0], out_sent]
    later = [pass_far(1, kept[1], 1)]
    order.done(*back_packs, *marks, ffn_sum)

    size = far_rows // 2
    sums = {}

    def along_x(i, h):
        low = add_low(order.tie(own_low[i])[h * size : (h + 1) * size], far_total[i, h])
        sums[i, h] = (low, x_swap(low))
        return sums[i, h][1]

    def finish(i, h):
        low, crossed = order.tie(*sums[i, h])
        total = add_low(low, crossed)
        sums[i, h] = (total, core_swap(total))
        return sums[i, h][1]

    def joined(i):
        pairs = order.tie(*sums[i, 0], *sums[i, 1])
        return join_halves(core, pairs[:2], pairs[2:])

    def along_y(terms):
        terms = order.tie(*terms, terms[0])[:-1]
        total = None
        for k in list(range(1, cols)) + [0]:
            total = terms[k] if total is None else add_low(y_next(total), terms[k])
        return total

    marks = [*later, along_x(0, 0)]
    later = [pass_far(2, kept[2], 0)]
    out_recv = core_swap(order.tie(out_sent))
    ffn_sum = z_next(order.tie(add_low(ffn_sum, ffn_parts[3])))
    grad_qkv = unpack(seq, order.tie(*back_packs), cos_table, sin_table)
    qkv_sent = weight_grad([acts_one], [grad_qkv], line_rows, blocks, 1 - core)
    out_terms = row_grads(out_left, out_right, blocks, core, out_recv, y, 1)
    out_terms = [t[0] for t in out_terms]
    marks.append(send_own(1))
    order.done(qkv_sent, ffn_sum, *out_terms, *marks)

    qkv_recv = core_swap(order.tie(qkv_sent))
    out_total = z_next(order.tie(out_terms[0]))
    own_sent[1] = core_swap(order.tie(own_sent[1]))
    marks = [*later, send_own(2), along_x(0, 1), finish(0, 0)]
    later = [pass_far(2, kept[2], 1)]
    own_low.append(keep_own(1))
    order.done(qkv_recv, out_total, own_low[1], *marks)

    out_total = z_next(order.tie(add_low(out_total, out_terms[1])))
    qkv_terms = row_grads(acts_one, grad_qkv, blocks, core, order.tie(qkv_recv), y, cols)
    own_sent[2] = core_swap(order.tie(own_sent[2]))
    marks = [*later, along_x(1, 0), own_sent[2], finish(0, 1)]
    order.done(*[t for terms in qkv_terms for t in terms], out_total, *marks)

    out_total = z_next(order.tie(add_low(out_total, out_terms[2])))
    hops = [along_y(qkv_terms[0]), along_y(qkv_terms[1])]
    own_low.append(keep_own(2))
    d_down = joined(0)
    marks = [along_x(1, 1), finish(1, 0)]
    order.done(hops[0], out_total, d_down, own_low[2], *marks)

    passed = z_next(order.tie(hops[0]))
    hops.append(along_y(qkv_terms[2]))
    grad_inputs, grad_gain_one = inner_back(z, order.tie(grad_qkv), groups, flat_in, gain_one, grad_res)
    out_total = order.tie(add_low(out_total, out_terms[3]))
    pieces = [
        lax.dynamic_slice_in_dim(out_total, (y - k) % cols * rows, rows, 0) for k in range(cols)
    ]
    out_low = along_y(pieces)
    marks = [out_low, along_x(2, 0), finish(1, 1), grad_inputs]
    order.done(passed, hops[1], *marks)

    passed = z_next(order.tie(add_low(passed, hops[1])))
    hops.append(along_y(qkv_terms[3]))
    gain_sums = jnp.concatenate([grad_gain_one, grad_gain_two], axis=0)
    steps = sum_steps()
    gain_sums = gain_sums + steps[0](order.tie(gain_sums))
    d_gate = joined(1)
    marks = [along_x(2, 1), finish(2, 0), d_gate, gain_sums]
    order.done(passed, hops[2], *marks)

    passed = z_next(order.tie(add_low(passed, hops[2])))
    out_cross = x_swap(order.tie(out_low))
    outputs = (residual + ffn_sum.astype(F32) + order.tie(ffn_parts[0]).astype(F32)).astype(BF)
    gain_sums = gain_sums + steps[1](order.tie(gain_sums))
    finish(2, 1)
    d_up = joined(2)
    order.done(passed, hops[3], out_cross, d_up, outputs, gain_sums)

    low = order.tie(add_low(passed, hops[3]))
    crossed = x_swap(low)
    out_low = add_low(out_low, order.tie(out_cross))
    d_out = join(core, out_low, core_swap(out_low), [width])
    gain_sums = order.tie(gain_sums)
    for step in steps[2:-1]:
        gain_sums = gain_sums + step(gain_sums)
    order.done(crossed, d_out[0], gain_sums)
    gain_sums = gain_sums + steps[-1](order.tie(gain_sums))
    total = order.tie(add_low(low, crossed))
    d_qkv = join(core, total, core_swap(total), [q_width, kv_width, kv_width])

    gain_sums = lax.dynamic_slice_in_dim(gain_sums, fsdp * rows, rows, 1)
    return (
        outputs.reshape(inputs.shape),
        grad_inputs.reshape(inputs.shape),
        d_qkv[0],
        d_qkv[1],
        d_qkv[2],
        d_out[0],
        d_gate,
        d_up,
        d_down,
        gain_sums[0],
        gain_sums[1],
    )


def solution(mesh):
    token_spec, row_spec, gain_spec = P("fsdp", "seq", None), P("fsdp", None), P("fsdp")
    return jax.shard_map(
        shards,
        mesh=mesh,
        in_specs=(token_spec,) + (row_spec,) * 7 + (gain_spec,) * 2 + (token_spec,),
        out_specs=(token_spec,) * 2 + (row_spec,) * 7 + (gain_spec,) * 2,
        check_vma=False,
    )
```

```python
import functools
import math

import jax
import jax.numpy as jnp
from jax import lax
from jax.experimental import pallas as pl
from jax.experimental.pallas import tpu as pltpu
from jax.sharding import PartitionSpec as P

KVH = 8
HD = 64
BLOCK = 256
LINE = 4

EPSILON = 1e-05
THETA = 500000.0
LOG2E = 1.4426950408889634

BF = jnp.bfloat16
F32 = jnp.float32


def after(value, *others):
    return lax.optimization_barrier((value,) + others)[0]


def columns():
    return lax.axis_size("fsdp") // LINE


def z_next(value):
    cols = columns()
    count = lax.axis_size("fsdp")
    return lax.ppermute(value, "fsdp", [(i, (i + cols) % count) for i in range(count)])


def y_next(value):
    cols = columns()
    count = lax.axis_size("fsdp")
    return lax.ppermute(
        value, "fsdp", [(i, i // cols * cols + (i + 1) % cols) for i in range(count)]
    )


def seq_swap(value, bit):
    return lax.ppermute(value, "seq", [(i, i ^ bit) for i in range(lax.axis_size("seq"))])


def core_swap(value):
    return seq_swap(value, 1)


def x_swap(value):
    return seq_swap(value, 2)


def ring_gather(value, step, count):
    pieces = [value]
    for _ in range(count - 1):
        pieces.append(step(pieces[-1]))
    return pieces


def ring_scatter(part_of, step, count):
    total = None
    for j in list(range(1, count)) + [0]:
        total = part_of(j) if total is None else part_of(j) + total.astype(F32)
        if j:
            total = step(total.astype(BF))
    return total


def sum_steps():
    steps = []
    bit = 1
    while bit < lax.axis_size("seq"):
        steps.append(functools.partial(seq_swap, bit=bit))
        bit *= 2
    count = lax.axis_size("fsdp")
    bit = 1
    while bit < count:
        pairs = [(i, i ^ bit) for i in range(count)]
        steps.append(functools.partial(lax.ppermute, axis_name="fsdp", perm=pairs))
        bit *= 2
    return steps


def dot_nt(a, b):
    return lax.dot_general(a, b, (((1,), (1,)), ((), ())), preferred_element_type=F32)

def dot_nn(a, b):
    return jnp.dot(a, b, preferred_element_type=F32)


def attend_forward_kernel(parts, heads, kv, seq_ref, *refs):
    packs, outs = refs[:parts], refs[parts : 2 * parts]
    lse_ref, q_s, k_s, vt_s, o_s = refs[2 * parts :]
    tokens = packs[0].shape[0]
    seq = seq_ref[0]
    group = heads // kv
    for k in range(parts):
        rows = pl.ds(pl.multiple_of((seq ^ k) * tokens, tokens), tokens)
        q_s[rows, :] = packs[k][:, : heads * HD]
        for g in range(kv):
            lane = (heads + g) * HD
            k_s[g, rows, :] = packs[k][:, lane : lane + HD]
            lane = (heads + kv + g) * HD
            vt_s[g, :, rows] = packs[k][:, lane : lane + HD].T
    full = parts * tokens
    for g in range(kv):
        for i in range(full // BLOCK):
            keys = (i + 1) * BLOCK
            rows = slice(i * BLOCK, keys)
            for pair in range(group // 2):
                halves = []
                for h in (g * group + 2 * pair, g * group + 2 * pair + 1):
                    scores = dot_nt(k_s[g, :keys, :], q_s[rows, h * HD : (h + 1) * HD])
                    scores = scores * (HD**-0.5 * LOG2E)
                    top = jnp.max(scores, axis=0, keepdims=True)
                    powers = jnp.exp2(scores - top)
                    total = jnp.sum(powers, axis=0, keepdims=True)
                    halves.append(dot_nn(vt_s[g, :, :keys], powers.astype(BF)) / total)
                    lse_ref[h : h + 1, rows] = top + jnp.log2(total)
                lane = (g * group + 2 * pair) * HD
                o_s[rows, lane : lane + 2 * HD] = jnp.concatenate(halves, axis=0).T.astype(BF)
    for k in range(parts):
        rows = pl.ds(pl.multiple_of((seq ^ k) * tokens, tokens), tokens)
        outs[k][...] = o_s[rows, :]


def attend_forward(seq, packs, heads, kv):
    parts = len(packs)
    tokens = packs[0].shape[0]
    full = parts * tokens
    vmem = pl.BlockSpec(memory_space=pltpu.VMEM)
    flops = 4 * heads * full * full * HD * 5 // 8
    return pl.pallas_call(
        functools.partial(attend_forward_kernel, parts, heads, kv),
        out_shape=[jax.ShapeDtypeStruct((tokens, heads * HD), BF)] * parts
        + [jax.ShapeDtypeStruct((heads, full), F32)],
        in_specs=[pl.BlockSpec(memory_space=pltpu.SMEM)] + [vmem] * parts,
        out_specs=[vmem] * (parts + 1),
        scratch_shapes=[
            pltpu.VMEM((full, heads * HD), BF),
            pltpu.VMEM((kv, full, HD), BF),
            pltpu.VMEM((kv, HD, full), BF),
            pltpu.VMEM((full, heads * HD), BF),
        ],
        compiler_params=pltpu.CompilerParams(vmem_limit_bytes=48 * 2**20),
        cost_estimate=cost(flops * 4, 4 * 2**20),
        name="attend_forward",
    )(seq.reshape(1), *packs)


def attend_backward_kernel(parts, heads, kv, seq_ref, lse_ref, *refs):
    packs, grads, outs = refs[:parts], refs[parts : 2 * parts], refs[2 * parts : 3 * parts]
    q_s, k_s, kt_s, v_s, g_s, dq_s, dk_s, dv_s = refs[3 * parts :]
    tokens = packs[0].shape[0]
    seq = seq_ref[0]
    group = heads // kv
    for k in range(parts):
        rows = pl.ds(pl.multiple_of((seq ^ k) * tokens, tokens), tokens)
        q_s[rows, :] = packs[k][:, : heads * HD]
        g_s[rows, :] = grads[k][...]
        for g in range(kv):
            lane = (heads + g) * HD
            k_s[g, rows, :] = packs[k][:, lane : lane + HD]
            kt_s[g, :, rows] = packs[k][:, lane : lane + HD].T
            lane = (heads + kv + g) * HD
            v_s[g, rows, :] = packs[k][:, lane : lane + HD]
    full = parts * tokens
    dk_s[...] = jnp.zeros_like(dk_s)
    dv_s[...] = jnp.zeros_like(dv_s)
    for g in range(kv):
        for i in range(full // BLOCK):
            keys = (i + 1) * BLOCK
            rows = slice(i * BLOCK, keys)
            for pair in range(group // 2):
                halves = []
                for h in (g * group + 2 * pair, g * group + 2 * pair + 1):
                    query = q_s[rows, h * HD : (h + 1) * HD]
                    grad = g_s[rows, h * HD : (h + 1) * HD]
                    scores = dot_nt(k_s[g, :keys, :], query) * (HD**-0.5 * LOG2E)
                    probs = jnp.exp2(scores - lse_ref[h : h + 1, rows])
                    grad_probs = dot_nt(v_s[g, :keys, :], grad)
                    inner = jnp.sum(probs * grad_probs, axis=0, keepdims=True)
                    grad_scores = (probs * (grad_probs - inner)).astype(BF)
                    dv_s[g, :keys, :] += dot_nn(probs.astype(BF), grad)
                    dk_s[g, :keys, :] += dot_nn(grad_scores, query)
                    halves.append(dot_nn(kt_s[g, :, :keys], grad_scores) * HD**-0.5)
                lane = (g * group + 2 * pair) * HD
                dq_s[rows, lane : lane + 2 * HD] = jnp.concatenate(halves, axis=0).T.astype(BF)
    for k in range(parts):
        rows = pl.ds(pl.multiple_of((seq ^ k) * tokens, tokens), tokens)
        outs[k][:, : heads * HD] = dq_s[rows, :]
        for g in range(kv):
            lane = (heads + g) * HD
            outs[k][:, lane : lane + HD] = (dk_s[g, rows, :] * HD**-0.5).astype(BF)
            lane = (heads + kv + g) * HD
            outs[k][:, lane : lane + HD] = dv_s[g, rows, :].astype(BF)


def attend_backward(seq, lse, packs, grads, heads, kv):
    parts = len(packs)
    tokens = packs[0].shape[0]
    full = parts * tokens
    vmem = pl.BlockSpec(memory_space=pltpu.VMEM)
    flops = 10 * heads * full * full * HD * 5 // 8
    return pl.pallas_call(
        functools.partial(attend_backward_kernel, parts, heads, kv),
        out_shape=[jax.ShapeDtypeStruct(packs[0].shape, BF)] * parts,
        in_specs=[pl.BlockSpec(memory_space=pltpu.SMEM)] + [vmem] * (2 * parts + 1),
        out_specs=[vmem] * parts,
        scratch_shapes=[
            pltpu.VMEM((full, heads * HD), BF),
            pltpu.VMEM((kv, full, HD), BF),
            pltpu.VMEM((kv, HD, full), BF),
            pltpu.VMEM((kv, full, HD), BF),
            pltpu.VMEM((full, heads * HD), BF),
            pltpu.VMEM((full, heads * HD), BF),
            pltpu.VMEM((kv, full, HD), F32),
            pltpu.VMEM((kv, full, HD), F32),
        ],
        compiler_params=pltpu.CompilerParams(vmem_limit_bytes=48 * 2**20),
        cost_estimate=cost(flops * 4, 8 * 2**20),
        name="attend_backward",
    )(seq.reshape(1), lse, *packs, *grads)


def smem():
    return pl.BlockSpec(memory_space=pltpu.SMEM)


def params(mib=56):
    return pltpu.CompilerParams(vmem_limit_bytes=mib * 2**20)


def cost(flops, moved):
    return pl.CostEstimate(flops=flops // 8, bytes_accessed=moved // 8, transcendentals=0)


def place(shape, pieces, offsets, most=None):
    count = len(pieces)

    def kernel(at_ref, *refs):
        sources, target, sems = refs[:-2], refs[-2], refs[-1]
        copies = []
        for i, source in enumerate(sources):
            rows, width = source.shape
            rows = min(rows, most or rows)
            row = pl.multiple_of(at_ref[2 * i], rows)
            column = pl.multiple_of(at_ref[2 * i + 1], width)
            spot = target.at[pl.ds(row, rows), pl.ds(column, width)]
            copies.append(pltpu.make_async_copy(source.at[pl.ds(0, rows), :], spot, sems.at[i]))
            copies[-1].start()
        for copy in copies:
            copy.wait()

    moved = 2 * sum(piece.size * 2 for piece in pieces)
    return pl.pallas_call(
        kernel,
        out_shape=jax.ShapeDtypeStruct(shape, pieces[0].dtype),
        in_specs=[smem()] + [pl.BlockSpec(memory_space=pl.ANY)] * count,
        out_specs=pl.BlockSpec(memory_space=pltpu.HBM),
        scratch_shapes=[pltpu.SemaphoreType.DMA((count,))],
        compiler_params=params(16),
        cost_estimate=cost(0, moved),
        name="place",
    )(jnp.stack([jnp.int32(v) for pair in offsets for v in pair]), *pieces)


def turn(values, cos_table, sin_table):
    width = values.shape[1]
    lane = lax.broadcasted_iota(jnp.int32, values.shape, 1)
    swapped = jnp.where(
        lane % HD < HD // 2,
        pltpu.roll(values, width - HD // 2, 1),
        pltpu.roll(values, HD // 2, 1),
    )
    return values * cos_table + swapped * sin_table


def whole(shape):
    return pl.BlockSpec(shape, lambda n: (0,) * len(shape))


def project_in(seq, z, inputs, gain, groups, cos_table, sin_table, parts):
    tokens, width = inputs.shape
    tile = cos_table.shape[1]
    each = tile // parts
    pack = tile + 2 * each
    count = len(groups)
    depth = width // count

    def kernel(at_ref, in_ref, gain_ref, *refs):
        w_refs, (cos_ref, sin_ref, acts_ref), packs = refs[:count], refs[count : count + 3], refs[count + 3 :]
        step = pl.program_id(0)

        @pl.when(step == 0)
        def _():
            values = in_ref[...].astype(F32)
            scale = lax.rsqrt(jnp.mean(values * values, axis=-1, keepdims=True) + EPSILON)
            acts_ref[...] = (values * scale * gain_ref[...]).astype(BF)

        rows = None
        for j in range(count):
            lanes = pl.ds(pl.multiple_of((at_ref[1] + count - j) % count * depth, depth), depth)
            term = dot_nn(acts_ref[:, lanes], w_refs[j][...])
            rows = term if rows is None else rows + term
        turned = jnp.where(
            step == parts + 1, rows, turn(rows, cos_ref[...], sin_ref[...])
        ).astype(BF)
        seq_now = at_ref[0]
        for k in range(parts):

            @pl.when((seq_now ^ k) == step)
            def _():
                packs[k][:, :tile] = turned

            for d in range(parts):
                for which in range(2):

                    @pl.when(((seq_now ^ k) == d) & (step == parts + which))
                    def _():
                        lane = tile + which * each
                        packs[k][:, lane : lane + each] = turned[:, d * each : (d + 1) * each]

    return pl.pallas_call(
        kernel,
        grid=(parts + 2,),
        out_shape=[jax.ShapeDtypeStruct((tokens, width), BF)]
        + [jax.ShapeDtypeStruct((tokens, pack), BF)] * parts,
        in_specs=[smem(), whole((tokens, width)), whole((1, width))]
        + [pl.BlockSpec((depth, tile), lambda n: (0, n))] * count
        + [whole((tokens, tile))] * 2,
        out_specs=[whole((tokens, width))] + [whole((tokens, pack))] * parts,
        compiler_params=params(),
        cost_estimate=cost(2 * tokens * width * tile * (parts + 2), 2 * width * tile * (parts + 2)),
        name="project_in",
    )(jnp.stack([seq, z]), inputs, gain, *groups, cos_table, sin_table)


def project_out(seq, z, mixed, inputs, gain, groups):
    parts = len(mixed)
    tokens, width = inputs.shape
    each = mixed[0].shape[1]
    tile = width // parts
    count = len(groups)
    depth = parts * each // count

    def kernel(at_ref, *refs):
        parts_in, (in_ref, gain_ref) = refs[:parts], refs[parts : parts + 2]
        w_refs, (flat_ref, res_ref, acts_ref) = refs[parts + 2 : -3], refs[-3:]
        step = pl.program_id(0)

        @pl.when(step == 0)
        def _():
            for k in range(parts):
                lane = pl.multiple_of((at_ref[0] ^ k) * each, each)
                flat_ref[:, pl.ds(lane, each)] = parts_in[k][...]

        lanes = pl.ds(pl.multiple_of(step * tile, tile), tile)
        total = in_ref[:, lanes].astype(F32)
        for j in range(count):
            rows = pl.ds(pl.multiple_of((at_ref[1] + count - j) % count * depth, depth), depth)
            total = total + dot_nn(flat_ref[:, rows], w_refs[j][...])
        res_ref[:, lanes] = total

        @pl.when(step == parts - 1)
        def _():
            values = res_ref[...]
            scale = lax.rsqrt(jnp.mean(values * values, axis=-1, keepdims=True) + EPSILON)
            acts_ref[...] = (values * scale * gain_ref[...]).astype(BF)

    return pl.pallas_call(
        kernel,
        grid=(parts,),
        out_shape=[
            jax.ShapeDtypeStruct((tokens, parts * each), BF),
            jax.ShapeDtypeStruct((tokens, width), F32),
            jax.ShapeDtypeStruct((tokens, width), BF),
        ],
        in_specs=[smem()]
        + [whole((tokens, each))] * parts
        + [whole((tokens, width)), whole((1, width))]
        + [pl.BlockSpec((depth, tile), lambda n: (0, n))] * count,
        out_specs=[whole((tokens, parts * each)), whole((tokens, width)), whole((tokens, width))],
        compiler_params=params(),
        cost_estimate=cost(2 * tokens * width * parts * each, 2 * width * parts * each),
        name="project_out",
    )(jnp.stack([seq, z]), *mixed, inputs, gain, *groups)


def feed_forward(acts, grads, gate, up, down, begun=None):
    tokens, width = acts.shape
    hidden = gate.shape[0]
    tile = 256
    steps = hidden // tile
    kind = F32 if begun is None else BF
    begun = [] if begun is None else list(begun)

    def kernel(a_ref, c_ref, g_ref, u_ref, d_ref, *refs):
        starts, (h_ref, gg_ref, gu_ref, o_ref, ga_ref, o_s, ga_s) = refs[:-7], refs[-7:]
        step = pl.program_id(0)

        @pl.when(step == 0)
        def _():
            if starts:
                o_s[...] = starts[0][...]
                ga_s[...] = starts[1][...]
            else:
                o_s[...] = jnp.zeros_like(o_s)
                ga_s[...] = jnp.zeros_like(ga_s)

        gate_act = dot_nt(a_ref[...], g_ref[...])
        up_act = dot_nt(a_ref[...], u_ref[...])
        grad_hidden = dot_nt(c_ref[...], d_ref[...])
        sigma = jax.nn.sigmoid(gate_act)
        silu = gate_act * sigma
        low = (silu * up_act).astype(BF)
        grad_gate = (grad_hidden * up_act * (sigma * (1.0 + gate_act * (1.0 - sigma)))).astype(BF)
        grad_up = (grad_hidden * silu).astype(BF)
        h_ref[...] = low
        gg_ref[...] = grad_gate
        gu_ref[...] = grad_up
        o_s[...] += dot_nn(low, d_ref[...])
        ga_s[...] += dot_nn(grad_gate, g_ref[...]) + dot_nn(grad_up, u_ref[...])

        @pl.when(step == steps - 1)
        def _():
            o_ref[...] = o_s[...].astype(kind)
            ga_ref[...] = ga_s[...].astype(kind)

    whole = pl.BlockSpec((tokens, width), lambda n: (0, 0))
    rows = pl.BlockSpec((tile, width), lambda n: (n, 0))
    lanes = pl.BlockSpec((tokens, tile), lambda n: (0, n))
    return pl.pallas_call(
        kernel,
        grid=(steps,),
        out_shape=[jax.ShapeDtypeStruct((tokens, hidden), BF)] * 3
        + [jax.ShapeDtypeStruct((tokens, width), kind)] * 2,
        in_specs=[whole, whole, rows, rows, rows] + [whole] * len(begun),
        out_specs=[lanes] * 3 + [whole] * 2,
        scratch_shapes=[pltpu.VMEM((tokens, width), F32)] * 2,
        compiler_params=params(),
        cost_estimate=cost(12 * tokens * width * hidden, 6 * width * hidden),
        name="feed_forward",
    )(acts, grads, gate, up, down, *begun)


def middle_back(seq, z, terms, residual, grad_out, gain, groups, parts):
    tokens, width = residual.shape
    tile = groups[0].shape[0]
    count = len(groups)
    assert count == parts

    def kernel(at_ref, t0_ref, t1_ref, res_ref, go_ref, gain_ref, *refs):
        w_refs, (gr_ref, low_ref, gg_ref), outs = refs[:count], refs[count : count + 3], refs[count + 3 :]
        grad = t0_ref[...].astype(F32) + t1_ref[...].astype(F32)
        values = res_ref[...]
        scale = lax.rsqrt(jnp.mean(values * values, axis=-1, keepdims=True) + EPSILON)
        weighted = grad * gain_ref[...]
        inner = jnp.mean(weighted * values, axis=-1, keepdims=True)
        result = go_ref[...].astype(F32) + scale * weighted - values * (scale**3 * inner)
        gr_ref[...] = result
        low_ref[...] = result.astype(BF)
        gg_ref[...] = jnp.sum(grad * values * scale, axis=0, keepdims=True)
        for j in range(count):
            part = dot_nt(low_ref[...], w_refs[j][...]).astype(BF)
            at = ((at_ref[1] + count - j) % count) ^ at_ref[0]
            for k in range(parts):

                @pl.when(at == k)
                def _():
                    outs[k][...] = part

    vmem = pl.BlockSpec(memory_space=pltpu.VMEM)
    return pl.pallas_call(
        kernel,
        out_shape=[
            jax.ShapeDtypeStruct((tokens, width), F32),
            jax.ShapeDtypeStruct((tokens, width), BF),
            jax.ShapeDtypeStruct((1, width), F32),
        ]
        + [jax.ShapeDtypeStruct((tokens, tile), BF)] * parts,
        in_specs=[smem()] + [vmem] * (5 + count),
        out_specs=[vmem] * (3 + parts),
        compiler_params=params(),
        cost_estimate=cost(2 * tokens * width * tile * parts, 2 * width * tile * parts + 8 * tokens * width),
        name="middle_back",
    )(jnp.stack([seq, z]), terms[0], terms[1], residual, grad_out, gain, *groups)


def unpack(seq, packs, cos_table, sin_table):
    parts = len(packs)
    tokens, tile = cos_table.shape
    each = tile // parts

    def kernel(seq_ref, *refs):
        ins, (cos_ref, sin_ref, out_ref) = refs[:parts], refs[parts:]
        for k in range(parts):
            at = seq_ref[0] ^ k
            queries = turn(ins[k][:, :tile].astype(F32), cos_ref[...], -sin_ref[...])
            out_ref[:, pl.ds(pl.multiple_of(at * tile, tile), tile)] = queries.astype(BF)
            keys = turn(
                ins[k][:, tile : tile + each].astype(F32), cos_ref[:, :each], -sin_ref[:, :each]
            )
            lane = pl.multiple_of(parts * tile + at * each, each)
            out_ref[:, pl.ds(lane, each)] = keys.astype(BF)
            lane = pl.multiple_of((parts + 1) * tile + at * each, each)
            out_ref[:, pl.ds(lane, each)] = ins[k][:, tile + each :]

    vmem = pl.BlockSpec(memory_space=pltpu.VMEM)
    return pl.pallas_call(
        kernel,
        out_shape=jax.ShapeDtypeStruct((tokens, (parts + 2) * tile), BF),
        in_specs=[smem()] + [vmem] * (parts + 2),
        out_specs=vmem,
        compiler_params=params(),
        cost_estimate=cost(0, 6 * 2**20),
        name="unpack",
    )(seq.reshape(1), *packs, cos_table, sin_table)


def inner_back(z, grad_qkv, groups, inputs, gain, grad_res):
    tokens, width = inputs.shape
    count = len(groups)
    depth = width // count

    def kernel(at_ref, gq_ref, *refs):
        w_refs, (in_ref, gain_ref, gr_ref, out_ref, gg_ref, grad_s) = refs[:count], refs[count:]
        for j in range(count):
            lanes = pl.ds(pl.multiple_of((at_ref[0] + count - j) % count * depth, depth), depth)
            grad_s[:, lanes] = dot_nt(gq_ref[...], w_refs[j][...])
        grad = grad_s[...]
        values = in_ref[...].astype(F32)
        scale = lax.rsqrt(jnp.mean(values * values, axis=-1, keepdims=True) + EPSILON)
        weighted = grad * gain_ref[...]
        inner = jnp.mean(weighted * values, axis=-1, keepdims=True)
        result = gr_ref[...] + scale * weighted - values * (scale**3 * inner)
        out_ref[...] = result.astype(BF)
        gg_ref[...] = jnp.sum(grad * values * scale, axis=0, keepdims=True)

    vmem = pl.BlockSpec(memory_space=pltpu.VMEM)
    return pl.pallas_call(
        kernel,
        out_shape=[jax.ShapeDtypeStruct((tokens, width), BF), jax.ShapeDtypeStruct((1, width), F32)],
        in_specs=[smem()] + [vmem] * (4 + count),
        out_specs=[vmem] * 2,
        scratch_shapes=[pltpu.VMEM((tokens, width), F32)],
        compiler_params=params(),
        cost_estimate=cost(2 * tokens * groups[0].size * count, 2 * groups[0].size * count),
        name="inner_back",
    )(z.reshape(1), grad_qkv, *groups, inputs, gain, grad_res)


def weight_grad(left, right, rows, blocks, half, adds=(), pieces=1):
    count = len(left)
    tokens = left[0].shape[0]
    width = right[0].shape[1] // 2
    total_rows = rows * len(blocks)
    piece = total_rows // pieces
    tile = math.gcd(math.gcd(rows, 512), piece)
    steps = rows // tile
    each = piece // tile

    def kernel(at_ref, *refs):
        lefts, rights = refs[:count], refs[count : 2 * count]
        extra, outs = refs[2 * count : -pieces], refs[-pieces:]
        total = None
        for l_ref, r_ref in zip(lefts, rights):
            term = lax.dot_general(
                l_ref[...], r_ref[...], (((0,), (0,)), ((), ())), preferred_element_type=F32
            )
            total = term if total is None else total + term
        for ref in extra:
            total = total + ref[...].astype(F32)
        total = total.astype(BF)
        for p, out in enumerate(outs):
            if pieces == 1:
                out[...] = total
            else:

                @pl.when(pl.program_id(0) // each == p)
                def _():
                    out[...] = total

    def spec_of(p):
        if pieces == 1:
            return pl.BlockSpec((tile, width), lambda n, at: (n, 0))
        return pl.BlockSpec((tile, width), lambda n, at: (jnp.clip(n - p * each, 0, each - 1), 0))

    spec = pltpu.PrefetchScalarGridSpec(
        num_scalar_prefetch=1,
        grid=(steps * len(blocks),),
        in_specs=[pl.BlockSpec((tokens, tile), lambda n, at: (0, at[1 + n]))] * count
        + [pl.BlockSpec((tokens, width), lambda n, at: (0, at[0]))] * count
        + [pl.BlockSpec((tile, width), lambda n, at: (n, 0))] * len(adds),
        out_specs=[spec_of(p) for p in range(pieces)],
    )
    at = [jnp.int32(half)]
    for block in blocks:
        at += [jnp.int32(block) * steps + i for i in range(steps)]
    outs = pl.pallas_call(
        kernel,
        grid_spec=spec,
        out_shape=[jax.ShapeDtypeStruct((piece, width), BF)] * pieces,
        compiler_params=params(),
        cost_estimate=cost(
            2 * tokens * count * total_rows * width, 2 * (tokens * count + total_rows) * width
        ),
        name="weight_grad",
    )(jnp.stack(at), *left, *right, *adds)
    return outs[0] if pieces == 1 else list(outs)


def row_grads(left, right, blocks, half, added, y, cuts):
    tokens = left.shape[0]
    width = right.shape[1] // 2
    rows = left.shape[1] // LINE
    each = rows // cuts
    count = len(blocks)

    def kernel(at_ref, l_ref, r_ref, add_ref, *refs):
        outs, total_s = refs[:-1], refs[-1]
        total = lax.dot_general(
            l_ref[...], r_ref[...], (((0,), (0,)), ((), ())), preferred_element_type=F32
        )
        total_s[...] = (total + add_ref[...].astype(F32)).astype(BF)
        for j in range(count):

            @pl.when(pl.program_id(0) == j)
            def _():
                for k in range(cuts):
                    start = pl.multiple_of((at_ref[1] + cuts - k) % cuts * each, each)
                    outs[j * cuts + k][...] = total_s[pl.ds(start, each), :]

    spec = pltpu.PrefetchScalarGridSpec(
        num_scalar_prefetch=1,
        grid=(count,),
        in_specs=[
            pl.BlockSpec((tokens, rows), lambda n, at: (0, at[2 + n])),
            pl.BlockSpec((tokens, width), lambda n, at: (0, at[0])),
            pl.BlockSpec((rows, width), lambda n, at: (n, 0)),
        ],
        out_specs=[pl.BlockSpec((each, width), lambda n, at: (0, 0))] * (count * cuts),
        scratch_shapes=[pltpu.VMEM((rows, width), BF)],
    )
    at = jnp.stack([jnp.int32(half), jnp.int32(y)] + [jnp.int32(b) for b in blocks])
    outs = pl.pallas_call(
        kernel,
        grid_spec=spec,
        out_shape=[jax.ShapeDtypeStruct((each, width), BF)] * (count * cuts),
        compiler_params=params(),
        cost_estimate=cost(2 * tokens * count * rows * width, 6 * count * rows * width),
        name="row_grads",
    )(at, left, right, added)
    return [outs[j * cuts : (j + 1) * cuts] for j in range(count)]


def join(core, mine, other, widths):
    rows, half = mine.shape
    tile = min(rows, 256)

    def kernel(core_ref, mine_ref, other_ref, *refs):
        outs, full = refs[:-1], refs[-1]
        target = outs[0] if len(outs) == 1 else full
        at = pl.multiple_of(core_ref[0] * half, half)
        target[:, pl.ds(at, half)] = mine_ref[...].astype(F32)
        at = pl.multiple_of((1 - core_ref[0]) * half, half)
        target[:, pl.ds(at, half)] = other_ref[...].astype(F32)
        if len(outs) > 1:
            lane = 0
            for out in outs:
                out[...] = full[:, lane : lane + out.shape[1]]
                lane += out.shape[1]

    def block(width):
        return pl.BlockSpec((tile, width), lambda n: (n, 0))

    return pl.pallas_call(
        kernel,
        grid=(rows // tile,),
        out_shape=[jax.ShapeDtypeStruct((rows, width), F32) for width in widths],
        in_specs=[smem(), block(half), block(half)],
        out_specs=[block(width) for width in widths],
        scratch_shapes=[pltpu.VMEM((tile, 2 * half) if len(widths) > 1 else (8, 128), F32)],
        compiler_params=params(),
        cost_estimate=cost(0, rows * half * 12),
        name="join",
    )(core.reshape(1), mine, other)
def half_of(array, which, axis=1):
    size = array.shape[axis] // 2
    return lax.dynamic_slice_in_dim(array, which * size, size, axis)


def join_halves(core, top, bottom):
    rows, half = top[0].shape
    tile = min(rows, 256)
    steps = rows // tile

    def kernel(core_ref, a_ref, b_ref, c_ref, d_ref, out):
        mine = pl.multiple_of(core_ref[0] * half, half)
        other = pl.multiple_of((1 - core_ref[0]) * half, half)
        upper = pl.program_id(0) < steps

        @pl.when(upper)
        def _():
            out[:, pl.ds(mine, half)] = a_ref[...].astype(F32)
            out[:, pl.ds(other, half)] = b_ref[...].astype(F32)

        @pl.when(jnp.logical_not(upper))
        def _():
            out[:, pl.ds(mine, half)] = c_ref[...].astype(F32)
            out[:, pl.ds(other, half)] = d_ref[...].astype(F32)

    first = pl.BlockSpec((tile, half), lambda n: (jnp.minimum(n, steps - 1), 0))
    second = pl.BlockSpec((tile, half), lambda n: (jnp.maximum(n - steps, 0), 0))
    return pl.pallas_call(
        kernel,
        grid=(2 * steps,),
        out_shape=jax.ShapeDtypeStruct((2 * rows, 2 * half), F32),
        in_specs=[smem(), first, first, second, second],
        out_specs=pl.BlockSpec((tile, 2 * half), lambda n: (n, 0)),
        compiler_params=params(),
        cost_estimate=cost(0, rows * half * 24),
        name="join_halves",
    )(core.reshape(1), *top, *bottom)


class Order:
    def __init__(self):
        self.marks = ()

    def tie(self, *values):
        if self.marks:
            values = lax.optimization_barrier(tuple(values) + self.marks)[: len(values)]
        return values[0] if len(values) == 1 else list(values)

    def done(self, *values):
        self.marks = tuple(values)


def y_hops(value):
    return ring_gather(value, y_next, columns())[1:]


def add_low(left, right):
    return (left.astype(F32) + right.astype(F32)).astype(BF)


def rope_tables(positions, repeat):
    frequency = THETA ** (-(jnp.arange(HD // 2, dtype=F32) * 2.0) / HD)
    angles = positions.astype(F32)[:, None] * frequency[None, :]
    cos, sin = jnp.cos(angles), jnp.sin(angles)
    return (
        jnp.tile(jnp.concatenate([cos, cos], axis=1), (1, repeat)),
        jnp.tile(jnp.concatenate([-sin, sin], axis=1), (1, repeat)),
    )


def exchange(packs):
    return [packs[0]] + [seq_swap(packs[k], k) for k in range(1, len(packs))]


def shards(
    inputs,
    query_weight,
    key_weight,
    value_weight,
    output_weight,
    gate_weight,
    up_weight,
    down_weight,
    gain_attn,
    gain_ffn,
    cotangent,
):
    seq_count, local_len, width = inputs.shape
    assert seq_count == 1
    tokens = local_len
    parts = lax.axis_size("seq")
    kv_local = KVH // parts
    cols = columns()
    seq = lax.axis_index("seq")
    core, side = seq % 2, seq // 2
    fsdp = lax.axis_index("fsdp")
    z, y = fsdp // cols, fsdp % cols
    q_width, kv_width = query_weight.shape[1], key_weight.shape[1]
    heads_local = q_width // HD // parts
    flat_in = inputs.reshape(tokens, width)
    grad_out = cotangent.reshape(tokens, width)

    qkv_shard = jnp.concatenate([query_weight, key_weight, value_weight], axis=1)
    rows = qkv_shard.shape[0]
    part, half = rows // 2, qkv_shard.shape[1] // 2
    positions = seq * local_len + jnp.arange(local_len)
    cos_table, sin_table = rope_tables(positions, kv_width // HD)
    order = Order()

    def swapped(pieces):
        return [core_swap(p) for p in pieces]

    def place_halves(pieces, others, whole_first=None):
        each = pieces[-1].shape[1]
        placed, offsets = [], []
        for k, (piece, other) in enumerate(zip(pieces, others)):
            row = (y - k) % cols * rows
            if k == 0 and whole_first is not None:
                placed.append(whole_first)
                offsets.append((row, 0))
            else:
                placed += [piece, other]
                offsets += [(row, core * each), (row, (1 - core) * each)]
        return place((rows * cols, 2 * each), placed, offsets)

    def place_quarters(pieces, others, sides, count, size, first):
        each = pieces[0].shape[1]
        placed, offsets = [], []
        for i, (piece, other) in enumerate(zip(pieces, others)):
            k, at = i // 2, sides[i % 2]
            row = first(k) * size + at * (size // 2)
            placed += [piece, other]
            offsets += [(row, core * each), (row, (1 - core) * each)]
        return place((size * count, 2 * each), placed, offsets)

    def line_row(k):
        return (y - k) % cols

    own = (gate_weight, up_weight, down_weight)
    far_rows = gate_weight.shape[0]
    far_part = far_rows // 4
    far_y, far_x = {}, {}

    def far_start(i, h):
        at = side * 2 * far_part + h * far_part
        return lax.dynamic_slice(own[i], (at, core * out_width), (far_part, out_width))

    out_width = width // 2
    far_starts = {(i, h): far_start(i, h) for i in range(3) for h in range(2)}

    def far_along_y(i, h):
        start = order.tie(far_starts[i, h]) if order.marks else far_starts[i, h]
        far_y[i, h] = y_hops(start)
        return far_y[i, h]

    def far_along_x(i, h):
        pieces = order.tie(*far_y[i, h], far_y[i, h][0])[:-1]
        far_x[i, h] = [x_swap(p) for p in pieces]
        return far_x[i, h]

    gains = jnp.concatenate([gain_attn, gain_ffn]).reshape(1, 2 * rows)
    start = half_of(qkv_shard, core)
    start = jnp.concatenate([start, jnp.pad(gains, ((0, 15), (0, half - 2 * rows)))], axis=0)
    out_half = half_of(output_weight, core)

    def quarter_of(piece):
        return lax.dynamic_slice_in_dim(piece, side * part, part, 0)

    def line_group(i):
        here = order.tie(line[i])
        placed, offsets = [], []
        row = y * rows
        if i:
            placed += [here, core_swap(here)]
            offsets += [(row, core * half), (row, (1 - core) * half)]
        else:
            placed.append(qkv_shard)
            offsets.append((row, 0))
        for k in range(1, cols):
            row = (y - k) % cols * rows
            if i < LINE - 1:
                for piece, at in ((beside[i][k - 1], side), (crossed[i][k - 1], 1 - side)):
                    piece = order.tie(piece)
                    placed += [piece, core_swap(piece)]
                    offsets += [
                        (row + at * part, core * half),
                        (row + at * part, (1 - core) * half),
                    ]
            else:
                piece = order.tie(beside[i][k - 1])
                placed += [piece, core_swap(piece)]
                offsets += [(row, core * half), (row, (1 - core) * half)]
        return place((rows * cols, 2 * half), placed, offsets, rows)

    line, beside, crossed, groups = [start], [], [], []
    for j in range(LINE):
        here = order.tie(line[j]) if j else line[j]
        if j + 1 < LINE:
            line.append(z_next(here))
            beside.append(y_hops(quarter_of(here)))
            marks = [line[j + 1]] + beside[j] + far_along_y(j // 2, j % 2)
        else:
            beside.append(y_hops(here))
            line_o = [out_half, z_next(order.tie(out_half))]
            grad_parts = [grad_out, z_next(order.tie(grad_out))]
            gains_near = jnp.concatenate([p[rows:, : 2 * rows] for p in line[:j]], axis=0)
            gains_far = y_hops(order.tie(gains_near))
            marks = beside[j] + [line_o[1]]
        if j:
            pieces = order.tie(*beside[j - 1], here)[:-1]
            crossed.append([x_swap(p) for p in pieces])
            marks += crossed[j - 1]
        if j > 1:
            groups.append(line_group(j - 2))
            marks.append(groups[-1])
        if j == 1:
            marks += [cos_table, sin_table] + list(far_starts.values())
        order.done(*marks)

    line_o.append(z_next(order.tie(line_o[1])))
    beside_o = [y_hops(order.tie(line_o[0])), y_hops(order.tie(line_o[1]))]
    groups += [line_group(LINE - 2), line_group(LINE - 1)]
    marks = far_along_x(0, 0)
    gain_full = jnp.zeros((2, width), BF)
    for j in range(LINE):
        for k in range(cols):
            if j == LINE - 1:
                g = line[j][rows] if k == 0 else beside[j][k - 1][rows]
                pair = g[: 2 * rows].reshape(2, rows)
            else:
                g = gains_near if k == 0 else gains_far[k - 1]
                pair = g[16 * j].reshape(2, rows)
            at = (((z - j) % LINE) * cols + (y - k) % cols) * rows
            gain_full = lax.dynamic_update_slice(gain_full, pair, (0, at))
    gain_one = gain_full[:1].astype(F32)
    gain_two = gain_full[1:].astype(F32)
    acts_one, *sent = project_in(seq, z, flat_in, gain_one, groups, cos_table, sin_table, parts)
    order.done(*sent, line_o[2], *beside_o[0], *beside_o[1], grad_parts[1], *marks)

    def out_swaps(j, *others):
        hops = order.tie(line_o[j], *beside_o[j], *others)[: cols]
        if j == 0:
            return [None] + hops[1:], [None] + swapped(hops[1:])
        return hops, swapped(hops)

    def out_group(pair, j):
        hops, others = pair
        first = 0 if j else 1
        tied = order.tie(*hops[first:], *others[first:])
        count = cols - first
        return place_halves(
            [None] * first + tied[:count],
            [None] * first + tied[count:],
            None if j else output_weight,
        )

    packs = exchange(order.tie(*sent))
    line_o.append(z_next(order.tie(line_o[2])))
    beside_o.append(y_hops(order.tie(line_o[2])))
    pairs = [out_swaps(j, packs[2]) for j in range(2)]
    grad_top = [z_next(order.tie(grad_parts[1], packs[2])[0][: tokens // 2])]
    swaps = [p for pair in pairs for p in pair[1][1:]]
    order.done(*packs, line_o[3], *beside_o[2], *swaps)

    beside_o.append(y_hops(order.tie(line_o[3])))
    grad_low = [z_next(order.tie(grad_parts[1])[tokens // 2 :])]
    pairs.append(out_swaps(2))
    *mixed_sent, log_totals = attend_forward(seq, order.tie(*packs), heads_local, kv_local)
    order.done(*mixed_sent, *beside_o[3], grad_top[0], grad_low[0])

    mixed = exchange(order.tie(*mixed_sent))
    pairs.append(out_swaps(3))
    out_groups = [out_group(pairs[j], j) for j in range(LINE - 1)]
    out_groups.append(place_halves(*pairs[3]))
    grad_top.append(z_next(order.tie(grad_top[0])))
    order.done(*mixed, *out_groups, grad_top[1])

    grad_low.append(z_next(order.tie(grad_low[0])))
    grad_parts += [jnp.concatenate(pair, axis=0) for pair in zip(grad_top, grad_low)]
    marks = far_along_y(1, 1) + far_along_x(0, 1) + [grad_low[1]]
    mixed_flat, residual, acts_two = project_out(
        seq, z, order.tie(*mixed), flat_in, gain_two, out_groups
    )
    order.done(acts_two, *marks)

    def far_place(i, *others):
        placed, offsets = [], []
        for k in range(cols - 1):
            for h in range(2):
                pieces = order.tie(far_y[i, h][k], far_x[i, h][k], *others)[:2]
                for piece, at in zip(pieces, (side, 1 - side)):
                    row = k * far_rows + at * 2 * far_part + h * far_part
                    placed += [piece, core_swap(piece)]
                    offsets += [(row, core * out_width), (row, (1 - core) * out_width)]
        return place((far_rows * (cols - 1), width), placed, offsets)

    acts_parts, far, near_done, far_done = [acts_two], [], [], [None] * LINE

    def run_near(j):
        near_done.append(feed_forward(order.tie(acts_parts[j]), grad_parts[j], *own))
        return near_done[j][3]

    def run_far(j):
        far_done[j] = feed_forward(order.tie(acts_parts[j]), grad_parts[j], *far, near_done[j][3:])
        return far_done[j][4]

    acts_parts.append(z_next(order.tie(acts_parts[0])))
    marks = far_along_y(2, 0) + far_along_y(2, 1) + far_along_x(1, 0) + far_along_x(1, 1)
    far.append(far_place(0))
    order.done(acts_parts[1], *marks, *far, run_near(0))
    acts_parts.append(z_next(order.tie(acts_parts[1])))
    marks = far_along_x(2, 0) + far_along_x(2, 1)
    far.append(far_place(1))
    order.done(acts_parts[2], *marks, *far, run_near(1))
    acts_parts.append(z_next(order.tie(acts_parts[2])))
    far.append(far_place(2))
    marks = [run_near(2), run_far(1)]
    order.done(acts_parts[3], *marks)

    passed = z_next(order.tie(far_done[1][4]))
    marks = [run_near(3), run_far(2)]
    order.done(passed, *marks)
    passed = z_next(order.tie(add_low(passed, far_done[2][4])))
    marks = [run_far(3), run_far(0)]
    order.done(passed, *marks)
    passed = z_next(order.tie(add_low(passed, far_done[3][4])))

    rights = (grad_parts, acts_parts, acts_parts)
    far_size = far_rows * (cols - 1)
    far_sent, far_total, own_sent = [None] * 3, {}, [None] * 3

    def of(done, which):
        return order.tie(*[d[which] for d in done])

    def send_far(i):
        far_sent[i] = weight_grad(of(far_done, i), rights[i], far_size, [0], 1 - core)
        return far_sent[i]

    def keep_far(i):
        return weight_grad(
            of(far_done, i), rights[i], far_size, [0], core, [far_sent[i]], 2 * (cols - 1)
        )

    def pass_far(i, kept, h):
        total = y_next(order.tie(kept[h]))
        for k in range(1, cols - 1):
            total = y_next(add_low(total, order.tie(kept[2 * k + h])))
        far_total[i, h] = total
        return total

    def send_own(i):
        own_sent[i] = weight_grad(of(near_done, i), rights[i], far_rows, [0], 1 - core)
        return own_sent[i]

    def keep_own(i):
        return weight_grad(of(near_done, i), rights[i], far_rows, [0], core, [own_sent[i]])

    first = send_far(0)
    far_sent[0] = core_swap(first)
    marks = [send_far(1), send_far(2)]
    kept = [keep_far(0)]
    order.done(passed, *kept[0], *marks)

    marks = [pass_far(0, kept[0], 0)]
    far_sent[1:] = [core_swap(order.tie(term)) for term in far_sent[1:]]
    ffn_parts = [d[3] for d in far_done]
    ffn_sum = z_next(order.tie(ffn_parts[1]))
    grad_res, grad_res_low, grad_gain_two, *grad_sent = middle_back(
        seq, z, order.tie(passed, far_done[0][4]), residual, grad_out, gain_two, out_groups, parts
    )
    order.done(*grad_sent, *far_sent[1:])

    grad_packs = exchange(order.tie(*grad_sent))
    kept.append(keep_far(1))
    first = send_own(0)
    order.done(*grad_packs, ffn_sum, *kept[1], first, *marks)

    marks = [pass_far(0, kept[0], 1)]
    later = [pass_far(1, kept[1], 0)]
    ffn_sum = z_next(order.tie(add_low(ffn_sum, ffn_parts[2])))
    back_sent = attend_backward(
        seq, log_totals, packs, order.tie(*grad_packs), heads_local, kv_local
    )
    order.done(*back_sent, *marks)

    line_order = list(range(1, LINE)) + [0]
    blocks = [(z - j) % LINE for j in line_order]
    line_rows = rows * cols
    back_packs = exchange(order.tie(*back_sent))
    own_sent[0] = core_swap(order.tie(own_sent[0]))
    out_left, out_right = order.tie(mixed_flat, grad_res_low)
    out_sent = weight_grad([out_left], [out_right], line_rows, blocks, 1 - core)
    kept.append(keep_far(2))
    own_low = [keep_own(0)]
    marks = [*later, *kept[2], own_low[0], out_sent]
    later = [pass_far(1, kept[1], 1)]
    order.done(*back_packs, *marks, ffn_sum)

    size = far_rows // 2
    sums = {}

    def along_x(i, h):
        low = add_low(order.tie(own_low[i])[h * size : (h + 1) * size], far_total[i, h])
        sums[i, h] = (low, x_swap(low))
        return sums[i, h][1]

    def finish(i, h):
        low, crossed = order.tie(*sums[i, h])
        total = add_low(low, crossed)
        sums[i, h] = (total, core_swap(total))
        return sums[i, h][1]

    def joined(i):
        pairs = order.tie(*sums[i, 0], *sums[i, 1])
        return join_halves(core, pairs[:2], pairs[2:])

    def along_y(terms):
        terms = order.tie(*terms, terms[0])[:-1]
        total = None
        for k in list(range(1, cols)) + [0]:
            total = terms[k] if total is None else add_low(y_next(total), terms[k])
        return total

    marks = [*later, along_x(0, 0)]
    later = [pass_far(2, kept[2], 0)]
    out_recv = core_swap(order.tie(out_sent))
    ffn_sum = z_next(order.tie(add_low(ffn_sum, ffn_parts[3])))
    grad_qkv = unpack(seq, order.tie(*back_packs), cos_table, sin_table)
    qkv_sent = weight_grad([acts_one], [grad_qkv], line_rows, blocks, 1 - core)
    out_terms = row_grads(out_left, out_right, blocks, core, out_recv, y, 1)
    out_terms = [t[0] for t in out_terms]
    marks.append(send_own(1))
    order.done(qkv_sent, ffn_sum, *out_terms, *marks)

    qkv_recv = core_swap(order.tie(qkv_sent))
    out_total = z_next(order.tie(out_terms[0]))
    own_sent[1] = core_swap(order.tie(own_sent[1]))
    marks = [*later, send_own(2), along_x(0, 1), finish(0, 0)]
    later = [pass_far(2, kept[2], 1)]
    own_low.append(keep_own(1))
    order.done(qkv_recv, out_total, own_low[1], *marks)

    out_total = z_next(order.tie(add_low(out_total, out_terms[1])))
    qkv_terms = row_grads(acts_one, grad_qkv, blocks, core, order.tie(qkv_recv), y, cols)
    own_sent[2] = core_swap(order.tie(own_sent[2]))
    marks = [*later, along_x(1, 0), own_sent[2], finish(0, 1)]
    order.done(*[t for terms in qkv_terms for t in terms], out_total, *marks)

    out_total = z_next(order.tie(add_low(out_total, out_terms[2])))
    hops = [along_y(qkv_terms[0]), along_y(qkv_terms[1])]
    own_low.append(keep_own(2))
    d_down = joined(0)
    marks = [along_x(1, 1), finish(1, 0)]
    order.done(hops[0], out_total, d_down, own_low[2], *marks)

    passed = z_next(order.tie(hops[0]))
    hops.append(along_y(qkv_terms[2]))
    grad_inputs, grad_gain_one = inner_back(z, order.tie(grad_qkv), groups, flat_in, gain_one, grad_res)
    out_total = order.tie(add_low(out_total, out_terms[3]))
    pieces = [
        lax.dynamic_slice_in_dim(out_total, (y - k) % cols * rows, rows, 0) for k in range(cols)
    ]
    out_low = along_y(pieces)
    marks = [out_low, along_x(2, 0), finish(1, 1), grad_inputs]
    order.done(passed, hops[1], *marks)

    passed = z_next(order.tie(add_low(passed, hops[1])))
    hops.append(along_y(qkv_terms[3]))
    gain_sums = jnp.concatenate([grad_gain_one, grad_gain_two], axis=0)
    steps = sum_steps()
    gain_sums = gain_sums + steps[0](order.tie(gain_sums))
    d_gate = joined(1)
    marks = [along_x(2, 1), finish(2, 0), d_gate, gain_sums]
    order.done(passed, hops[2], *marks)

    passed = z_next(order.tie(add_low(passed, hops[2])))
    out_cross = x_swap(order.tie(out_low))
    outputs = (residual + ffn_sum.astype(F32) + order.tie(ffn_parts[0]).astype(F32)).astype(BF)
    gain_sums = gain_sums + steps[1](order.tie(gain_sums))
    gain_sums = order.tie(gain_sums)
    gain_sums = gain_sums + steps[2](gain_sums)
    order.done(passed, hops[3], out_cross, finish(2, 1), outputs, gain_sums)

    low = order.tie(add_low(passed, hops[3]))
    crossed = x_swap(low)
    out_low = add_low(out_low, order.tie(out_cross))
    d_out = join(core, out_low, core_swap(out_low), [width])
    d_up = joined(2)
    gain_sums = order.tie(gain_sums)
    for step in steps[3:]:
        gain_sums = gain_sums + step(gain_sums)
    order.done(crossed, d_out[0], d_up, gain_sums)
    total = order.tie(add_low(low, crossed))
    d_qkv = join(core, total, core_swap(total), [q_width, kv_width, kv_width])

    gain_sums = lax.dynamic_slice_in_dim(gain_sums, fsdp * rows, rows, 1)
    return (
        outputs.reshape(inputs.shape),
        grad_inputs.reshape(inputs.shape),
        d_qkv[0],
        d_qkv[1],
        d_qkv[2],
        d_out[0],
        d_gate,
        d_up,
        d_down,
        gain_sums[0],
        gain_sums[1],
    )


def solution(mesh):
    token_spec, row_spec, gain_spec = P("fsdp", "seq", None), P("fsdp", None), P("fsdp")
    return jax.shard_map(
        shards,
        mesh=mesh,
        in_specs=(token_spec,) + (row_spec,) * 7 + (gain_spec,) * 2 + (token_spec,),
        out_specs=(token_spec,) * 2 + (row_spec,) * 7 + (gain_spec,) * 2,
        check_vma=False,
    )
```

```python
import functools
import math

import jax
import jax.numpy as jnp
from jax import lax
from jax.experimental import pallas as pl
from jax.experimental.pallas import tpu as pltpu
from jax.sharding import PartitionSpec as P

KVH = 8
HD = 64
BLOCK = 256
LINE = 4

EPSILON = 1e-05
THETA = 500000.0
LOG2E = 1.4426950408889634

BF = jnp.bfloat16
F32 = jnp.float32


def after(value, *others):
    return lax.optimization_barrier((value,) + others)[0]


def columns():
    return lax.axis_size("fsdp") // LINE


def z_next(value):
    cols = columns()
    count = lax.axis_size("fsdp")
    return lax.ppermute(value, "fsdp", [(i, (i + cols) % count) for i in range(count)])


def y_next(value):
    cols = columns()
    count = lax.axis_size("fsdp")
    return lax.ppermute(
        value, "fsdp", [(i, i // cols * cols + (i + 1) % cols) for i in range(count)]
    )


def seq_swap(value, bit):
    return lax.ppermute(value, "seq", [(i, i ^ bit) for i in range(lax.axis_size("seq"))])


def core_swap(value):
    return seq_swap(value, 1)


def x_swap(value):
    return seq_swap(value, 2)


def ring_gather(value, step, count):
    pieces = [value]
    for _ in range(count - 1):
        pieces.append(step(pieces[-1]))
    return pieces


def ring_scatter(part_of, step, count):
    total = None
    for j in list(range(1, count)) + [0]:
        total = part_of(j) if total is None else part_of(j) + total.astype(F32)
        if j:
            total = step(total.astype(BF))
    return total


def sum_steps():
    steps = []
    bit = 1
    while bit < lax.axis_size("seq"):
        steps.append(functools.partial(seq_swap, bit=bit))
        bit *= 2
    count = lax.axis_size("fsdp")
    bit = 1
    while bit < count:
        pairs = [(i, i ^ bit) for i in range(count)]
        steps.append(functools.partial(lax.ppermute, axis_name="fsdp", perm=pairs))
        bit *= 2
    return steps


def dot_nt(a, b):
    return lax.dot_general(a, b, (((1,), (1,)), ((), ())), preferred_element_type=F32)

def dot_nn(a, b):
    return jnp.dot(a, b, preferred_element_type=F32)


def attend_forward_kernel(parts, heads, kv, seq_ref, *refs):
    packs, outs = refs[:parts], refs[parts : 2 * parts]
    lse_ref, q_s, k_s, vt_s, o_s = refs[2 * parts :]
    tokens = packs[0].shape[0]
    seq = seq_ref[0]
    group = heads // kv
    for k in range(parts):
        rows = pl.ds(pl.multiple_of((seq ^ k) * tokens, tokens), tokens)
        q_s[rows, :] = packs[k][:, : heads * HD]
        for g in range(kv):
            lane = (heads + g) * HD
            k_s[g, rows, :] = packs[k][:, lane : lane + HD]
            lane = (heads + kv + g) * HD
            vt_s[g, :, rows] = packs[k][:, lane : lane + HD].T
    full = parts * tokens
    for g in range(kv):
        for i in range(full // BLOCK):
            keys = (i + 1) * BLOCK
            rows = slice(i * BLOCK, keys)
            for pair in range(group // 2):
                halves = []
                for h in (g * group + 2 * pair, g * group + 2 * pair + 1):
                    scores = dot_nt(k_s[g, :keys, :], q_s[rows, h * HD : (h + 1) * HD])
                    scores = scores * (HD**-0.5 * LOG2E)
                    top = jnp.max(scores, axis=0, keepdims=True)
                    powers = jnp.exp2(scores - top)
                    total = jnp.sum(powers, axis=0, keepdims=True)
                    halves.append(dot_nn(vt_s[g, :, :keys], powers.astype(BF)) / total)
                    lse_ref[h : h + 1, rows] = top + jnp.log2(total)
                lane = (g * group + 2 * pair) * HD
                o_s[rows, lane : lane + 2 * HD] = jnp.concatenate(halves, axis=0).T.astype(BF)
    for k in range(parts):
        rows = pl.ds(pl.multiple_of((seq ^ k) * tokens, tokens), tokens)
        outs[k][...] = o_s[rows, :]


def attend_forward(seq, packs, heads, kv):
    parts = len(packs)
    tokens = packs[0].shape[0]
    full = parts * tokens
    vmem = pl.BlockSpec(memory_space=pltpu.VMEM)
    flops = 4 * heads * full * full * HD * 5 // 8
    return pl.pallas_call(
        functools.partial(attend_forward_kernel, parts, heads, kv),
        out_shape=[jax.ShapeDtypeStruct((tokens, heads * HD), BF)] * parts
        + [jax.ShapeDtypeStruct((heads, full), F32)],
        in_specs=[pl.BlockSpec(memory_space=pltpu.SMEM)] + [vmem] * parts,
        out_specs=[vmem] * (parts + 1),
        scratch_shapes=[
            pltpu.VMEM((full, heads * HD), BF),
            pltpu.VMEM((kv, full, HD), BF),
            pltpu.VMEM((kv, HD, full), BF),
            pltpu.VMEM((full, heads * HD), BF),
        ],
        compiler_params=pltpu.CompilerParams(vmem_limit_bytes=48 * 2**20),
        cost_estimate=cost(flops * 4, 4 * 2**20),
        name="attend_forward",
    )(seq.reshape(1), *packs)


def attend_backward_kernel(parts, heads, kv, seq_ref, lse_ref, *refs):
    packs, grads, outs = refs[:parts], refs[parts : 2 * parts], refs[2 * parts : 3 * parts]
    q_s, k_s, kt_s, v_s, g_s, dq_s, dk_s, dv_s = refs[3 * parts :]
    tokens = packs[0].shape[0]
    seq = seq_ref[0]
    group = heads // kv
    for k in range(parts):
        rows = pl.ds(pl.multiple_of((seq ^ k) * tokens, tokens), tokens)
        q_s[rows, :] = packs[k][:, : heads * HD]
        g_s[rows, :] = grads[k][...]
        for g in range(kv):
            lane = (heads + g) * HD
            k_s[g, rows, :] = packs[k][:, lane : lane + HD]
            kt_s[g, :, rows] = packs[k][:, lane : lane + HD].T
            lane = (heads + kv + g) * HD
            v_s[g, rows, :] = packs[k][:, lane : lane + HD]
    full = parts * tokens
    dk_s[...] = jnp.zeros_like(dk_s)
    dv_s[...] = jnp.zeros_like(dv_s)
    for g in range(kv):
        for i in range(full // BLOCK):
            keys = (i + 1) * BLOCK
            rows = slice(i * BLOCK, keys)
            for pair in range(group // 2):
                halves = []
                for h in (g * group + 2 * pair, g * group + 2 * pair + 1):
                    query = q_s[rows, h * HD : (h + 1) * HD]
                    grad = g_s[rows, h * HD : (h + 1) * HD]
                    scores = dot_nt(k_s[g, :keys, :], query) * (HD**-0.5 * LOG2E)
                    probs = jnp.exp2(scores - lse_ref[h : h + 1, rows])
                    grad_probs = dot_nt(v_s[g, :keys, :], grad)
                    inner = jnp.sum(probs * grad_probs, axis=0, keepdims=True)
                    grad_scores = (probs * (grad_probs - inner)).astype(BF)
                    dv_s[g, :keys, :] += dot_nn(probs.astype(BF), grad)
                    dk_s[g, :keys, :] += dot_nn(grad_scores, query)
                    halves.append(dot_nn(kt_s[g, :, :keys], grad_scores) * HD**-0.5)
                lane = (g * group + 2 * pair) * HD
                dq_s[rows, lane : lane + 2 * HD] = jnp.concatenate(halves, axis=0).T.astype(BF)
    for k in range(parts):
        rows = pl.ds(pl.multiple_of((seq ^ k) * tokens, tokens), tokens)
        outs[k][:, : heads * HD] = dq_s[rows, :]
        for g in range(kv):
            lane = (heads + g) * HD
            outs[k][:, lane : lane + HD] = (dk_s[g, rows, :] * HD**-0.5).astype(BF)
            lane = (heads + kv + g) * HD
            outs[k][:, lane : lane + HD] = dv_s[g, rows, :].astype(BF)


def attend_backward(seq, lse, packs, grads, heads, kv):
    parts = len(packs)
    tokens = packs[0].shape[0]
    full = parts * tokens
    vmem = pl.BlockSpec(memory_space=pltpu.VMEM)
    flops = 10 * heads * full * full * HD * 5 // 8
    return pl.pallas_call(
        functools.partial(attend_backward_kernel, parts, heads, kv),
        out_shape=[jax.ShapeDtypeStruct(packs[0].shape, BF)] * parts,
        in_specs=[pl.BlockSpec(memory_space=pltpu.SMEM)] + [vmem] * (2 * parts + 1),
        out_specs=[vmem] * parts,
        scratch_shapes=[
            pltpu.VMEM((full, heads * HD), BF),
            pltpu.VMEM((kv, full, HD), BF),
            pltpu.VMEM((kv, HD, full), BF),
            pltpu.VMEM((kv, full, HD), BF),
            pltpu.VMEM((full, heads * HD), BF),
            pltpu.VMEM((full, heads * HD), BF),
            pltpu.VMEM((kv, full, HD), F32),
            pltpu.VMEM((kv, full, HD), F32),
        ],
        compiler_params=pltpu.CompilerParams(vmem_limit_bytes=48 * 2**20),
        cost_estimate=cost(flops * 4, 8 * 2**20),
        name="attend_backward",
    )(seq.reshape(1), lse, *packs, *grads)


def smem():
    return pl.BlockSpec(memory_space=pltpu.SMEM)


def params(mib=63):
    return pltpu.CompilerParams(vmem_limit_bytes=mib * 2**20)


def cost(flops, moved):
    return pl.CostEstimate(flops=flops // 8, bytes_accessed=moved // 8, transcendentals=0)


def place(shape, pieces, offsets, most=None):
    count = len(pieces)

    def kernel(at_ref, *refs):
        sources, target, sems = refs[:-2], refs[-2], refs[-1]
        copies = []
        for i, source in enumerate(sources):
            rows, width = source.shape
            rows = min(rows, most or rows)
            row = pl.multiple_of(at_ref[2 * i], rows)
            column = pl.multiple_of(at_ref[2 * i + 1], width)
            spot = target.at[pl.ds(row, rows), pl.ds(column, width)]
            copies.append(pltpu.make_async_copy(source.at[pl.ds(0, rows), :], spot, sems.at[i]))
            copies[-1].start()
        for copy in copies:
            copy.wait()

    moved = 2 * sum(piece.size * 2 for piece in pieces)
    return pl.pallas_call(
        kernel,
        out_shape=jax.ShapeDtypeStruct(shape, pieces[0].dtype),
        in_specs=[smem()] + [pl.BlockSpec(memory_space=pl.ANY)] * count,
        out_specs=pl.BlockSpec(memory_space=pltpu.HBM),
        scratch_shapes=[pltpu.SemaphoreType.DMA((count,))],
        compiler_params=params(16),
        cost_estimate=cost(0, moved),
        name="place",
    )(jnp.stack([jnp.int32(v) for pair in offsets for v in pair]), *pieces)


def turn(values, cos_table, sin_table):
    width = values.shape[1]
    lane = lax.broadcasted_iota(jnp.int32, values.shape, 1)
    swapped = jnp.where(
        lane % HD < HD // 2,
        pltpu.roll(values, width - HD // 2, 1),
        pltpu.roll(values, HD // 2, 1),
    )
    return values * cos_table + swapped * sin_table


def whole(shape):
    return pl.BlockSpec(shape, lambda n: (0,) * len(shape))


def project_in(seq, z, inputs, gain, groups, cos_table, sin_table, parts):
    tokens, width = inputs.shape
    tile = cos_table.shape[1]
    each = tile // parts
    pack = tile + 2 * each
    count = len(groups)
    depth = width // count

    def kernel(at_ref, in_ref, gain_ref, *refs):
        w_refs, (cos_ref, sin_ref, acts_ref), packs = refs[:count], refs[count : count + 3], refs[count + 3 :]
        step = pl.program_id(0)

        @pl.when(step == 0)
        def _():
            values = in_ref[...].astype(F32)
            scale = lax.rsqrt(jnp.mean(values * values, axis=-1, keepdims=True) + EPSILON)
            acts_ref[...] = (values * scale * gain_ref[...]).astype(BF)

        rows = None
        for j in range(count):
            lanes = pl.ds(pl.multiple_of((at_ref[1] + count - j) % count * depth, depth), depth)
            term = dot_nn(acts_ref[:, lanes], w_refs[j][...])
            rows = term if rows is None else rows + term
        turned = jnp.where(
            step == parts + 1, rows, turn(rows, cos_ref[...], sin_ref[...])
        ).astype(BF)
        seq_now = at_ref[0]
        for k in range(parts):

            @pl.when((seq_now ^ k) == step)
            def _():
                packs[k][:, :tile] = turned

            for d in range(parts):
                for which in range(2):

                    @pl.when(((seq_now ^ k) == d) & (step == parts + which))
                    def _():
                        lane = tile + which * each
                        packs[k][:, lane : lane + each] = turned[:, d * each : (d + 1) * each]

    return pl.pallas_call(
        kernel,
        grid=(parts + 2,),
        out_shape=[jax.ShapeDtypeStruct((tokens, width), BF)]
        + [jax.ShapeDtypeStruct((tokens, pack), BF)] * parts,
        in_specs=[smem(), whole((tokens, width)), whole((1, width))]
        + [pl.BlockSpec((depth, tile), lambda n: (0, n))] * count
        + [whole((tokens, tile))] * 2,
        out_specs=[whole((tokens, width))] + [whole((tokens, pack))] * parts,
        compiler_params=params(),
        cost_estimate=cost(2 * tokens * width * tile * (parts + 2), 2 * width * tile * (parts + 2)),
        name="project_in",
    )(jnp.stack([seq, z]), inputs, gain, *groups, cos_table, sin_table)


def project_out(seq, z, mixed, inputs, gain, groups):
    parts = len(mixed)
    tokens, width = inputs.shape
    each = mixed[0].shape[1]
    tile = width // parts
    count = len(groups)
    depth = parts * each // count

    def kernel(at_ref, *refs):
        parts_in, (in_ref, gain_ref) = refs[:parts], refs[parts : parts + 2]
        w_refs, (flat_ref, res_ref, acts_ref) = refs[parts + 2 : -3], refs[-3:]
        step = pl.program_id(0)

        @pl.when(step == 0)
        def _():
            for k in range(parts):
                lane = pl.multiple_of((at_ref[0] ^ k) * each, each)
                flat_ref[:, pl.ds(lane, each)] = parts_in[k][...]

        lanes = pl.ds(pl.multiple_of(step * tile, tile), tile)
        total = in_ref[:, lanes].astype(F32)
        for j in range(count):
            rows = pl.ds(pl.multiple_of((at_ref[1] + count - j) % count * depth, depth), depth)
            total = total + dot_nn(flat_ref[:, rows], w_refs[j][...])
        res_ref[:, lanes] = total

        @pl.when(step == parts - 1)
        def _():
            values = res_ref[...]
            scale = lax.rsqrt(jnp.mean(values * values, axis=-1, keepdims=True) + EPSILON)
            acts_ref[...] = (values * scale * gain_ref[...]).astype(BF)

    return pl.pallas_call(
        kernel,
        grid=(parts,),
        out_shape=[
            jax.ShapeDtypeStruct((tokens, parts * each), BF),
            jax.ShapeDtypeStruct((tokens, width), F32),
            jax.ShapeDtypeStruct((tokens, width), BF),
        ],
        in_specs=[smem()]
        + [whole((tokens, each))] * parts
        + [whole((tokens, width)), whole((1, width))]
        + [pl.BlockSpec((depth, tile), lambda n: (0, n))] * count,
        out_specs=[whole((tokens, parts * each)), whole((tokens, width)), whole((tokens, width))],
        compiler_params=params(),
        cost_estimate=cost(2 * tokens * width * parts * each, 2 * width * parts * each),
        name="project_out",
    )(jnp.stack([seq, z]), *mixed, inputs, gain, *groups)


def feed_forward(acts, grads, gate, up, down, begun=None):
    tokens, width = acts.shape
    hidden = gate.shape[0]
    tile = 256
    steps = hidden // tile
    kind = F32 if begun is None else BF
    begun = [] if begun is None else list(begun)

    def kernel(a_ref, c_ref, g_ref, u_ref, d_ref, *refs):
        starts, (h_ref, gg_ref, gu_ref, o_ref, ga_ref, o_s, ga_s) = refs[:-7], refs[-7:]
        step = pl.program_id(0)

        @pl.when(step == 0)
        def _():
            if starts:
                o_s[...] = starts[0][...]
                ga_s[...] = starts[1][...]
            else:
                o_s[...] = jnp.zeros_like(o_s)
                ga_s[...] = jnp.zeros_like(ga_s)

        gate_act = dot_nt(a_ref[...], g_ref[...])
        up_act = dot_nt(a_ref[...], u_ref[...])
        grad_hidden = dot_nt(c_ref[...], d_ref[...])
        sigma = jax.nn.sigmoid(gate_act)
        silu = gate_act * sigma
        low = (silu * up_act).astype(BF)
        grad_gate = (grad_hidden * up_act * (sigma * (1.0 + gate_act * (1.0 - sigma)))).astype(BF)
        grad_up = (grad_hidden * silu).astype(BF)
        h_ref[...] = low
        gg_ref[...] = grad_gate
        gu_ref[...] = grad_up
        o_s[...] += dot_nn(low, d_ref[...])
        ga_s[...] += dot_nn(grad_gate, g_ref[...]) + dot_nn(grad_up, u_ref[...])

        @pl.when(step == steps - 1)
        def _():
            o_ref[...] = o_s[...].astype(kind)
            ga_ref[...] = ga_s[...].astype(kind)

    whole = pl.BlockSpec((tokens, width), lambda n: (0, 0))
    rows = pl.BlockSpec((tile, width), lambda n: (n, 0))
    lanes = pl.BlockSpec((tokens, tile), lambda n: (0, n))
    return pl.pallas_call(
        kernel,
        grid=(steps,),
        out_shape=[jax.ShapeDtypeStruct((tokens, hidden), BF)] * 3
        + [jax.ShapeDtypeStruct((tokens, width), kind)] * 2,
        in_specs=[whole, whole, rows, rows, rows] + [whole] * len(begun),
        out_specs=[lanes] * 3 + [whole] * 2,
        scratch_shapes=[pltpu.VMEM((tokens, width), F32)] * 2,
        compiler_params=params(),
        cost_estimate=cost(12 * tokens * width * hidden, 6 * width * hidden),
        name="feed_forward",
    )(acts, grads, gate, up, down, *begun)


def middle_back(seq, z, terms, residual, grad_out, gain, groups, parts):
    tokens, width = residual.shape
    tile = groups[0].shape[0]
    count = len(groups)
    assert count == parts

    def kernel(at_ref, t0_ref, t1_ref, res_ref, go_ref, gain_ref, *refs):
        w_refs, (gr_ref, low_ref, gg_ref), outs = refs[:count], refs[count : count + 3], refs[count + 3 :]
        grad = t0_ref[...].astype(F32) + t1_ref[...].astype(F32)
        values = res_ref[...]
        scale = lax.rsqrt(jnp.mean(values * values, axis=-1, keepdims=True) + EPSILON)
        weighted = grad * gain_ref[...]
        inner = jnp.mean(weighted * values, axis=-1, keepdims=True)
        result = go_ref[...].astype(F32) + scale * weighted - values * (scale**3 * inner)
        gr_ref[...] = result
        low_ref[...] = result.astype(BF)
        gg_ref[...] = jnp.sum(grad * values * scale, axis=0, keepdims=True)
        for j in range(count):
            part = dot_nt(low_ref[...], w_refs[j][...]).astype(BF)
            at = ((at_ref[1] + count - j) % count) ^ at_ref[0]
            for k in range(parts):

                @pl.when(at == k)
                def _():
                    outs[k][...] = part

    vmem = pl.BlockSpec(memory_space=pltpu.VMEM)
    return pl.pallas_call(
        kernel,
        out_shape=[
            jax.ShapeDtypeStruct((tokens, width), F32),
            jax.ShapeDtypeStruct((tokens, width), BF),
            jax.ShapeDtypeStruct((1, width), F32),
        ]
        + [jax.ShapeDtypeStruct((tokens, tile), BF)] * parts,
        in_specs=[smem()] + [vmem] * (5 + count),
        out_specs=[vmem] * (3 + parts),
        compiler_params=params(),
        cost_estimate=cost(2 * tokens * width * tile * parts, 2 * width * tile * parts + 8 * tokens * width),
        name="middle_back",
    )(jnp.stack([seq, z]), terms[0], terms[1], residual, grad_out, gain, *groups)


def unpack(seq, packs, cos_table, sin_table):
    parts = len(packs)
    tokens, tile = cos_table.shape
    each = tile // parts

    def kernel(seq_ref, *refs):
        ins, (cos_ref, sin_ref, out_ref) = refs[:parts], refs[parts:]
        for k in range(parts):
            at = seq_ref[0] ^ k
            queries = turn(ins[k][:, :tile].astype(F32), cos_ref[...], -sin_ref[...])
            out_ref[:, pl.ds(pl.multiple_of(at * tile, tile), tile)] = queries.astype(BF)
            keys = turn(
                ins[k][:, tile : tile + each].astype(F32), cos_ref[:, :each], -sin_ref[:, :each]
            )
            lane = pl.multiple_of(parts * tile + at * each, each)
            out_ref[:, pl.ds(lane, each)] = keys.astype(BF)
            lane = pl.multiple_of((parts + 1) * tile + at * each, each)
            out_ref[:, pl.ds(lane, each)] = ins[k][:, tile + each :]

    vmem = pl.BlockSpec(memory_space=pltpu.VMEM)
    return pl.pallas_call(
        kernel,
        out_shape=jax.ShapeDtypeStruct((tokens, (parts + 2) * tile), BF),
        in_specs=[smem()] + [vmem] * (parts + 2),
        out_specs=vmem,
        compiler_params=params(),
        cost_estimate=cost(0, 6 * 2**20),
        name="unpack",
    )(seq.reshape(1), *packs, cos_table, sin_table)


def inner_back(z, grad_qkv, groups, inputs, gain, grad_res):
    tokens, width = inputs.shape
    count = len(groups)
    depth = width // count

    def kernel(at_ref, gq_ref, *refs):
        w_refs, (in_ref, gain_ref, gr_ref, out_ref, gg_ref, grad_s) = refs[:count], refs[count:]
        for j in range(count):
            lanes = pl.ds(pl.multiple_of((at_ref[0] + count - j) % count * depth, depth), depth)
            grad_s[:, lanes] = dot_nt(gq_ref[...], w_refs[j][...])
        grad = grad_s[...]
        values = in_ref[...].astype(F32)
        scale = lax.rsqrt(jnp.mean(values * values, axis=-1, keepdims=True) + EPSILON)
        weighted = grad * gain_ref[...]
        inner = jnp.mean(weighted * values, axis=-1, keepdims=True)
        result = gr_ref[...] + scale * weighted - values * (scale**3 * inner)
        out_ref[...] = result.astype(BF)
        gg_ref[...] = jnp.sum(grad * values * scale, axis=0, keepdims=True)

    vmem = pl.BlockSpec(memory_space=pltpu.VMEM)
    return pl.pallas_call(
        kernel,
        out_shape=[jax.ShapeDtypeStruct((tokens, width), BF), jax.ShapeDtypeStruct((1, width), F32)],
        in_specs=[smem()] + [vmem] * (4 + count),
        out_specs=[vmem] * 2,
        scratch_shapes=[pltpu.VMEM((tokens, width), F32)],
        compiler_params=params(),
        cost_estimate=cost(2 * tokens * groups[0].size * count, 2 * groups[0].size * count),
        name="inner_back",
    )(z.reshape(1), grad_qkv, *groups, inputs, gain, grad_res)


def weight_grad(left, right, rows, blocks, half, adds=(), pieces=1):
    count = len(left)
    tokens = left[0].shape[0]
    width = right[0].shape[1] // 2
    total_rows = rows * len(blocks)
    piece = total_rows // pieces
    tile = math.gcd(math.gcd(rows, 512), piece)
    steps = rows // tile
    each = piece // tile

    def kernel(at_ref, *refs):
        lefts, rights = refs[:count], refs[count : 2 * count]
        extra, outs = refs[2 * count : -pieces], refs[-pieces:]
        total = None
        for l_ref, r_ref in zip(lefts, rights):
            term = lax.dot_general(
                l_ref[...], r_ref[...], (((0,), (0,)), ((), ())), preferred_element_type=F32
            )
            total = term if total is None else total + term
        for ref in extra:
            total = total + ref[...].astype(F32)
        total = total.astype(BF)
        for p, out in enumerate(outs):
            if pieces == 1:
                out[...] = total
            else:

                @pl.when(pl.program_id(0) // each == p)
                def _():
                    out[...] = total

    def spec_of(p):
        if pieces == 1:
            return pl.BlockSpec((tile, width), lambda n, at: (n, 0))
        return pl.BlockSpec((tile, width), lambda n, at: (jnp.clip(n - p * each, 0, each - 1), 0))

    spec = pltpu.PrefetchScalarGridSpec(
        num_scalar_prefetch=1,
        grid=(steps * len(blocks),),
        in_specs=[pl.BlockSpec((tokens, tile), lambda n, at: (0, at[1 + n]))] * count
        + [pl.BlockSpec((tokens, width), lambda n, at: (0, at[0]))] * count
        + [pl.BlockSpec((tile, width), lambda n, at: (n, 0))] * len(adds),
        out_specs=[spec_of(p) for p in range(pieces)],
    )
    at = [jnp.int32(half)]
    for block in blocks:
        at += [jnp.int32(block) * steps + i for i in range(steps)]
    outs = pl.pallas_call(
        kernel,
        grid_spec=spec,
        out_shape=[jax.ShapeDtypeStruct((piece, width), BF)] * pieces,
        compiler_params=params(),
        cost_estimate=cost(
            2 * tokens * count * total_rows * width, 2 * (tokens * count + total_rows) * width
        ),
        name="weight_grad",
    )(jnp.stack(at), *left, *right, *adds)
    return outs[0] if pieces == 1 else list(outs)


def row_grads(left, right, blocks, half, added, y, cuts):
    tokens = left.shape[0]
    width = right.shape[1] // 2
    rows = left.shape[1] // LINE
    each = rows // cuts
    count = len(blocks)

    def kernel(at_ref, l_ref, r_ref, add_ref, *refs):
        outs, total_s = refs[:-1], refs[-1]
        total = lax.dot_general(
            l_ref[...], r_ref[...], (((0,), (0,)), ((), ())), preferred_element_type=F32
        )
        total_s[...] = (total + add_ref[...].astype(F32)).astype(BF)
        for j in range(count):

            @pl.when(pl.program_id(0) == j)
            def _():
                for k in range(cuts):
                    start = pl.multiple_of((at_ref[1] + cuts - k) % cuts * each, each)
                    outs[j * cuts + k][...] = total_s[pl.ds(start, each), :]

    spec = pltpu.PrefetchScalarGridSpec(
        num_scalar_prefetch=1,
        grid=(count,),
        in_specs=[
            pl.BlockSpec((tokens, rows), lambda n, at: (0, at[2 + n])),
            pl.BlockSpec((tokens, width), lambda n, at: (0, at[0])),
            pl.BlockSpec((rows, width), lambda n, at: (n, 0)),
        ],
        out_specs=[pl.BlockSpec((each, width), lambda n, at: (0, 0))] * (count * cuts),
        scratch_shapes=[pltpu.VMEM((rows, width), BF)],
    )
    at = jnp.stack([jnp.int32(half), jnp.int32(y)] + [jnp.int32(b) for b in blocks])
    outs = pl.pallas_call(
        kernel,
        grid_spec=spec,
        out_shape=[jax.ShapeDtypeStruct((each, width), BF)] * (count * cuts),
        compiler_params=params(),
        cost_estimate=cost(2 * tokens * count * rows * width, 6 * count * rows * width),
        name="row_grads",
    )(at, left, right, added)
    return [outs[j * cuts : (j + 1) * cuts] for j in range(count)]


def join(core, mine, other, widths):
    rows, half = mine.shape
    tile = min(rows, 256)

    def kernel(core_ref, mine_ref, other_ref, *refs):
        outs, full = refs[:-1], refs[-1]
        target = outs[0] if len(outs) == 1 else full
        at = pl.multiple_of(core_ref[0] * half, half)
        target[:, pl.ds(at, half)] = mine_ref[...].astype(F32)
        at = pl.multiple_of((1 - core_ref[0]) * half, half)
        target[:, pl.ds(at, half)] = other_ref[...].astype(F32)
        if len(outs) > 1:
            lane = 0
            for out in outs:
                out[...] = full[:, lane : lane + out.shape[1]]
                lane += out.shape[1]

    def block(width):
        return pl.BlockSpec((tile, width), lambda n: (n, 0))

    return pl.pallas_call(
        kernel,
        grid=(rows // tile,),
        out_shape=[jax.ShapeDtypeStruct((rows, width), F32) for width in widths],
        in_specs=[smem(), block(half), block(half)],
        out_specs=[block(width) for width in widths],
        scratch_shapes=[pltpu.VMEM((tile, 2 * half) if len(widths) > 1 else (8, 128), F32)],
        compiler_params=params(),
        cost_estimate=cost(0, rows * half * 12),
        name="join",
    )(core.reshape(1), mine, other)
def half_of(array, which, axis=1):
    size = array.shape[axis] // 2
    return lax.dynamic_slice_in_dim(array, which * size, size, axis)


def join_halves(core, top, bottom):
    rows, half = top[0].shape
    tile = min(rows, 256)
    steps = rows // tile

    def kernel(core_ref, a_ref, b_ref, c_ref, d_ref, out):
        mine = pl.multiple_of(core_ref[0] * half, half)
        other = pl.multiple_of((1 - core_ref[0]) * half, half)
        upper = pl.program_id(0) < steps

        @pl.when(upper)
        def _():
            out[:, pl.ds(mine, half)] = a_ref[...].astype(F32)
            out[:, pl.ds(other, half)] = b_ref[...].astype(F32)

        @pl.when(jnp.logical_not(upper))
        def _():
            out[:, pl.ds(mine, half)] = c_ref[...].astype(F32)
            out[:, pl.ds(other, half)] = d_ref[...].astype(F32)

    first = pl.BlockSpec((tile, half), lambda n: (jnp.minimum(n, steps - 1), 0))
    second = pl.BlockSpec((tile, half), lambda n: (jnp.maximum(n - steps, 0), 0))
    return pl.pallas_call(
        kernel,
        grid=(2 * steps,),
        out_shape=jax.ShapeDtypeStruct((2 * rows, 2 * half), F32),
        in_specs=[smem(), first, first, second, second],
        out_specs=pl.BlockSpec((tile, 2 * half), lambda n: (n, 0)),
        compiler_params=params(),
        cost_estimate=cost(0, rows * half * 24),
        name="join_halves",
    )(core.reshape(1), *top, *bottom)


class Order:
    def __init__(self):
        self.marks = ()

    def tie(self, *values):
        if self.marks:
            values = lax.optimization_barrier(tuple(values) + self.marks)[: len(values)]
        return values[0] if len(values) == 1 else list(values)

    def done(self, *values):
        self.marks = tuple(values)


def y_hops(value):
    return ring_gather(value, y_next, columns())[1:]


def add_low(left, right):
    return (left.astype(F32) + right.astype(F32)).astype(BF)


def rope_tables(positions, repeat):
    frequency = THETA ** (-(jnp.arange(HD // 2, dtype=F32) * 2.0) / HD)
    angles = positions.astype(F32)[:, None] * frequency[None, :]
    cos, sin = jnp.cos(angles), jnp.sin(angles)
    return (
        jnp.tile(jnp.concatenate([cos, cos], axis=1), (1, repeat)),
        jnp.tile(jnp.concatenate([-sin, sin], axis=1), (1, repeat)),
    )


def exchange(packs):
    return [packs[0]] + [seq_swap(packs[k], k) for k in range(1, len(packs))]


def shards(
    inputs,
    query_weight,
    key_weight,
    value_weight,
    output_weight,
    gate_weight,
    up_weight,
    down_weight,
    gain_attn,
    gain_ffn,
    cotangent,
):
    seq_count, local_len, width = inputs.shape
    assert seq_count == 1
    tokens = local_len
    parts = lax.axis_size("seq")
    kv_local = KVH // parts
    cols = columns()
    seq = lax.axis_index("seq")
    core, side = seq % 2, seq // 2
    fsdp = lax.axis_index("fsdp")
    z, y = fsdp // cols, fsdp % cols
    q_width, kv_width = query_weight.shape[1], key_weight.shape[1]
    heads_local = q_width // HD // parts
    flat_in = inputs.reshape(tokens, width)
    grad_out = cotangent.reshape(tokens, width)

    qkv_shard = jnp.concatenate([query_weight, key_weight, value_weight], axis=1)
    rows = qkv_shard.shape[0]
    part, half = rows // 2, qkv_shard.shape[1] // 2
    positions = seq * local_len + jnp.arange(local_len)
    cos_table, sin_table = rope_tables(positions, kv_width // HD)
    order = Order()

    def swapped(pieces):
        return [core_swap(p) for p in pieces]

    def place_halves(pieces, others, whole_first=None):
        each = pieces[-1].shape[1]
        placed, offsets = [], []
        for k, (piece, other) in enumerate(zip(pieces, others)):
            row = (y - k) % cols * rows
            if k == 0 and whole_first is not None:
                placed.append(whole_first)
                offsets.append((row, 0))
            else:
                placed += [piece, other]
                offsets += [(row, core * each), (row, (1 - core) * each)]
        return place((rows * cols, 2 * each), placed, offsets)

    def place_quarters(pieces, others, sides, count, size, first):
        each = pieces[0].shape[1]
        placed, offsets = [], []
        for i, (piece, other) in enumerate(zip(pieces, others)):
            k, at = i // 2, sides[i % 2]
            row = first(k) * size + at * (size // 2)
            placed += [piece, other]
            offsets += [(row, core * each), (row, (1 - core) * each)]
        return place((size * count, 2 * each), placed, offsets)

    def line_row(k):
        return (y - k) % cols

    own = (gate_weight, up_weight, down_weight)
    far_rows = gate_weight.shape[0]
    far_part = far_rows // 4
    far_y, far_x = {}, {}

    def far_start(i, h):
        at = side * 2 * far_part + h * far_part
        return lax.dynamic_slice(own[i], (at, core * out_width), (far_part, out_width))

    out_width = width // 2
    far_starts = {(i, h): far_start(i, h) for i in range(3) for h in range(2)}

    def far_along_y(i, h):
        start = order.tie(far_starts[i, h]) if order.marks else far_starts[i, h]
        far_y[i, h] = y_hops(start)
        return far_y[i, h]

    def far_along_x(i, h):
        pieces = order.tie(*far_y[i, h], far_y[i, h][0])[:-1]
        far_x[i, h] = [x_swap(p) for p in pieces]
        return far_x[i, h]

    gains = jnp.concatenate([gain_attn, gain_ffn]).reshape(1, 2 * rows)
    start = half_of(qkv_shard, core)
    start = jnp.concatenate([start, jnp.pad(gains, ((0, 15), (0, half - 2 * rows)))], axis=0)
    out_half = half_of(output_weight, core)

    def quarter_of(piece):
        return lax.dynamic_slice_in_dim(piece, side * part, part, 0)

    def line_group(i):
        here = order.tie(line[i])
        placed, offsets = [], []
        row = y * rows
        if i:
            placed += [here, core_swap(here)]
            offsets += [(row, core * half), (row, (1 - core) * half)]
        else:
            placed.append(qkv_shard)
            offsets.append((row, 0))
        for k in range(1, cols):
            row = (y - k) % cols * rows
            if i < LINE - 1:
                for piece, at in ((beside[i][k - 1], side), (crossed[i][k - 1], 1 - side)):
                    piece = order.tie(piece)
                    placed += [piece, core_swap(piece)]
                    offsets += [
                        (row + at * part, core * half),
                        (row + at * part, (1 - core) * half),
                    ]
            else:
                piece = order.tie(beside[i][k - 1])
                placed += [piece, core_swap(piece)]
                offsets += [(row, core * half), (row, (1 - core) * half)]
        return place((rows * cols, 2 * half), placed, offsets, rows)

    line, beside, crossed, groups = [start], [], [], []
    for j in range(LINE):
        here = order.tie(line[j]) if j else line[j]
        if j + 1 < LINE:
            line.append(z_next(here))
            beside.append(y_hops(quarter_of(here)))
            marks = [line[j + 1]] + beside[j] + far_along_y(j // 2, j % 2)
        else:
            beside.append(y_hops(here))
            line_o = [out_half, z_next(order.tie(out_half))]
            grad_parts = [grad_out, z_next(order.tie(grad_out))]
            gains_near = jnp.concatenate([p[rows:, : 2 * rows] for p in line[:j]], axis=0)
            gains_far = y_hops(order.tie(gains_near))
            marks = beside[j] + [line_o[1]]
        if j:
            pieces = order.tie(*beside[j - 1], here)[:-1]
            crossed.append([x_swap(p) for p in pieces])
            marks += crossed[j - 1]
        if j > 1:
            groups.append(line_group(j - 2))
            marks.append(groups[-1])
        if j == 1:
            marks += [cos_table, sin_table] + list(far_starts.values())
        order.done(*marks)

    line_o.append(z_next(order.tie(line_o[1])))
    beside_o = [y_hops(order.tie(line_o[0])), y_hops(order.tie(line_o[1]))]
    groups += [line_group(LINE - 2), line_group(LINE - 1)]
    marks = far_along_x(0, 0)
    gain_full = jnp.zeros((2, width), BF)
    for j in range(LINE):
        for k in range(cols):
            if j == LINE - 1:
                g = line[j][rows] if k == 0 else beside[j][k - 1][rows]
                pair = g[: 2 * rows].reshape(2, rows)
            else:
                g = gains_near if k == 0 else gains_far[k - 1]
                pair = g[16 * j].reshape(2, rows)
            at = (((z - j) % LINE) * cols + (y - k) % cols) * rows
            gain_full = lax.dynamic_update_slice(gain_full, pair, (0, at))
    gain_one = gain_full[:1].astype(F32)
    gain_two = gain_full[1:].astype(F32)
    acts_one, *sent = project_in(seq, z, flat_in, gain_one, groups, cos_table, sin_table, parts)
    order.done(*sent, line_o[2], *beside_o[0], *beside_o[1], grad_parts[1], *marks)

    def out_swaps(j, *others):
        hops = order.tie(line_o[j], *beside_o[j], *others)[: cols]
        if j == 0:
            return [None] + hops[1:], [None] + swapped(hops[1:])
        return hops, swapped(hops)

    def out_group(pair, j):
        hops, others = pair
        first = 0 if j else 1
        tied = order.tie(*hops[first:], *others[first:])
        count = cols - first
        return place_halves(
            [None] * first + tied[:count],
            [None] * first + tied[count:],
            None if j else output_weight,
        )

    packs = exchange(order.tie(*sent))
    line_o.append(z_next(order.tie(line_o[2])))
    beside_o.append(y_hops(order.tie(line_o[2])))
    pairs = [out_swaps(j, packs[2]) for j in range(2)]
    grad_top = [z_next(order.tie(grad_parts[1], packs[2])[0][: tokens // 2])]
    swaps = [p for pair in pairs for p in pair[1][1:]]
    order.done(*packs, line_o[3], *beside_o[2], *swaps)

    beside_o.append(y_hops(order.tie(line_o[3])))
    grad_low = [z_next(order.tie(grad_parts[1])[tokens // 2 :])]
    pairs.append(out_swaps(2))
    *mixed_sent, log_totals = attend_forward(seq, order.tie(*packs), heads_local, kv_local)
    order.done(*mixed_sent, *beside_o[3], grad_top[0], grad_low[0])

    mixed = exchange(order.tie(*mixed_sent))
    pairs.append(out_swaps(3))
    out_groups = [out_group(pairs[j], j) for j in range(LINE - 1)]
    out_groups.append(place_halves(*pairs[3]))
    grad_top.append(z_next(order.tie(grad_top[0])))
    order.done(*mixed, *out_groups, grad_top[1])

    grad_low.append(z_next(order.tie(grad_low[0])))
    grad_parts += [jnp.concatenate(pair, axis=0) for pair in zip(grad_top, grad_low)]
    marks = far_along_y(1, 1) + far_along_x(0, 1) + [grad_low[1]]
    mixed_flat, residual, acts_two = project_out(
        seq, z, order.tie(*mixed), flat_in, gain_two, out_groups
    )
    order.done(acts_two, *marks)

    def far_place(i, *others):
        placed, offsets = [], []
        for k in range(cols - 1):
            for h in range(2):
                pieces = order.tie(far_y[i, h][k], far_x[i, h][k], *others)[:2]
                for piece, at in zip(pieces, (side, 1 - side)):
                    row = k * far_rows + at * 2 * far_part + h * far_part
                    placed += [piece, core_swap(piece)]
                    offsets += [(row, core * out_width), (row, (1 - core) * out_width)]
        return place((far_rows * (cols - 1), width), placed, offsets)

    acts_parts, far, near_done, far_done = [acts_two], [], [], [None] * LINE

    def run_near(j):
        near_done.append(feed_forward(order.tie(acts_parts[j]), grad_parts[j], *own))
        return near_done[j][3]

    def run_far(j):
        far_done[j] = feed_forward(order.tie(acts_parts[j]), grad_parts[j], *far, near_done[j][3:])
        return far_done[j][4]

    acts_parts.append(z_next(order.tie(acts_parts[0])))
    marks = far_along_y(2, 0) + far_along_y(2, 1) + far_along_x(1, 0) + far_along_x(1, 1)
    far.append(far_place(0))
    order.done(acts_parts[1], *marks, *far, run_near(0))
    acts_parts.append(z_next(order.tie(acts_parts[1])))
    marks = far_along_x(2, 0) + far_along_x(2, 1)
    far.append(far_place(1))
    order.done(acts_parts[2], *marks, *far, *grad_parts[2:], run_near(1))
    acts_parts.append(z_next(order.tie(acts_parts[2])))
    far.append(far_place(2))
    marks = [run_near(2), run_far(1)]
    order.done(acts_parts[3], *marks)

    passed = z_next(order.tie(far_done[1][4]))
    marks = [run_near(3), run_far(2)]
    order.done(passed, *marks)
    passed = z_next(order.tie(add_low(passed, far_done[2][4])))
    marks = [run_far(3), run_far(0)]

    rights = (grad_parts, acts_parts, acts_parts)
    far_size = far_rows * (cols - 1)
    far_sent, far_total, own_sent = [None] * 3, {}, [None] * 3

    def of(done, which):
        return order.tie(*[d[which] for d in done])

    def send_far(i):
        far_sent[i] = weight_grad(of(far_done, i), rights[i], far_size, [0], 1 - core)
        return far_sent[i]

    def keep_far(i):
        return weight_grad(
            of(far_done, i), rights[i], far_size, [0], core, [far_sent[i]], 2 * (cols - 1)
        )

    def pass_far(i, kept, h):
        total = y_next(order.tie(kept[h]))
        for k in range(1, cols - 1):
            total = y_next(add_low(total, order.tie(kept[2 * k + h])))
        far_total[i, h] = total
        return total

    def send_own(i):
        own_sent[i] = weight_grad(of(near_done, i), rights[i], far_rows, [0], 1 - core)
        return own_sent[i]

    def keep_own(i):
        return weight_grad(of(near_done, i), rights[i], far_rows, [0], core, [own_sent[i]])

    order.done(passed, *marks, send_far(0))
    passed = z_next(order.tie(add_low(passed, far_done[3][4])))
    far_sent[0] = core_swap(order.tie(far_sent[0]))
    marks = [send_far(1), send_far(2)]
    kept = [keep_far(0)]
    order.done(passed, *kept[0], *marks)

    marks = [pass_far(0, kept[0], 0)]
    far_sent[1:] = [core_swap(order.tie(term)) for term in far_sent[1:]]
    ffn_parts = [d[3] for d in far_done]
    ffn_sum = z_next(order.tie(ffn_parts[1]))
    grad_res, grad_res_low, grad_gain_two, *grad_sent = middle_back(
        seq, z, order.tie(passed, far_done[0][4]), residual, grad_out, gain_two, out_groups, parts
    )
    order.done(*grad_sent, *far_sent[1:])

    grad_packs = exchange(order.tie(*grad_sent))
    kept.append(keep_far(1))
    first = send_own(0)
    order.done(*grad_packs, ffn_sum, *kept[1], first, *marks)

    marks = [pass_far(0, kept[0], 1)]
    later = [pass_far(1, kept[1], 0)]
    ffn_sum = z_next(order.tie(add_low(ffn_sum, ffn_parts[2])))
    back_sent = attend_backward(
        seq, log_totals, packs, order.tie(*grad_packs), heads_local, kv_local
    )
    order.done(*back_sent, *marks)

    line_order = list(range(1, LINE)) + [0]
    blocks = [(z - j) % LINE for j in line_order]
    line_rows = rows * cols
    back_packs = exchange(order.tie(*back_sent))
    own_sent[0] = core_swap(order.tie(own_sent[0]))
    out_left, out_right = order.tie(mixed_flat, grad_res_low)
    out_sent = weight_grad([out_left], [out_right], line_rows, blocks, 1 - core)
    kept.append(keep_far(2))
    own_low = [keep_own(0)]
    marks = [*later, *kept[2], own_low[0], out_sent]
    later = [pass_far(1, kept[1], 1)]
    order.done(*back_packs, *marks, ffn_sum)

    size = far_rows // 2
    sums = {}

    def along_x(i, h):
        low = add_low(order.tie(own_low[i])[h * size : (h + 1) * size], far_total[i, h])
        sums[i, h] = (low, x_swap(low))
        return sums[i, h][1]

    def finish(i, h):
        low, crossed = order.tie(*sums[i, h])
        total = add_low(low, crossed)
        sums[i, h] = (total, core_swap(total))
        return sums[i, h][1]

    def joined(i):
        pairs = order.tie(*sums[i, 0], *sums[i, 1])
        return join_halves(core, pairs[:2], pairs[2:])

    def along_y(terms):
        terms = order.tie(*terms, terms[0])[:-1]
        total = None
        for k in list(range(1, cols)) + [0]:
            total = terms[k] if total is None else add_low(y_next(total), terms[k])
        return total

    marks = [*later, along_x(0, 0)]
    later = [pass_far(2, kept[2], 0)]
    out_recv = core_swap(order.tie(out_sent))
    ffn_sum = z_next(order.tie(add_low(ffn_sum, ffn_parts[3])))
    grad_qkv = unpack(seq, order.tie(*back_packs), cos_table, sin_table)
    qkv_sent = weight_grad([acts_one], [grad_qkv], line_rows, blocks, 1 - core)
    out_terms = row_grads(out_left, out_right, blocks, core, out_recv, y, 1)
    out_terms = [t[0] for t in out_terms]
    marks.append(send_own(1))
    order.done(qkv_sent, ffn_sum, *out_terms, *marks)

    qkv_recv = core_swap(order.tie(qkv_sent))
    out_total = z_next(order.tie(out_terms[0]))
    own_sent[1] = core_swap(order.tie(own_sent[1]))
    marks = [*later, send_own(2), along_x(0, 1), finish(0, 0)]
    later = [pass_far(2, kept[2], 1)]
    own_low.append(keep_own(1))
    order.done(qkv_recv, out_total, own_low[1], *marks)

    out_total = z_next(order.tie(add_low(out_total, out_terms[1])))
    qkv_terms = row_grads(acts_one, grad_qkv, blocks, core, order.tie(qkv_recv), y, cols)
    own_sent[2] = core_swap(order.tie(own_sent[2]))
    marks = [*later, along_x(1, 0), own_sent[2], finish(0, 1)]
    order.done(*[t for terms in qkv_terms for t in terms], out_total, *marks)

    out_total = z_next(order.tie(add_low(out_total, out_terms[2])))
    hops = [along_y(qkv_terms[0]), along_y(qkv_terms[1])]
    own_low.append(keep_own(2))
    d_down = joined(0)
    marks = [along_x(1, 1), finish(1, 0)]
    order.done(hops[0], out_total, d_down, own_low[2], *marks)

    passed = z_next(order.tie(hops[0]))
    hops.append(along_y(qkv_terms[2]))
    grad_inputs, grad_gain_one = inner_back(z, order.tie(grad_qkv), groups, flat_in, gain_one, grad_res)
    out_total = order.tie(add_low(out_total, out_terms[3]))
    pieces = [
        lax.dynamic_slice_in_dim(out_total, (y - k) % cols * rows, rows, 0) for k in range(cols)
    ]
    out_low = along_y(pieces)
    marks = [out_low, along_x(2, 0), finish(1, 1), grad_inputs]
    order.done(passed, hops[1], *marks)

    passed = z_next(order.tie(add_low(passed, hops[1])))
    hops.append(along_y(qkv_terms[3]))
    gain_sums = jnp.concatenate([grad_gain_one, grad_gain_two], axis=0)
    steps = sum_steps()
    gain_sums = gain_sums + steps[0](order.tie(gain_sums))
    d_gate = joined(1)
    marks = [along_x(2, 1), finish(2, 0), d_gate, gain_sums]
    order.done(passed, hops[2], *marks)

    passed = z_next(order.tie(add_low(passed, hops[2])))
    out_cross = x_swap(order.tie(out_low))
    outputs = (residual + ffn_sum.astype(F32) + order.tie(ffn_parts[0]).astype(F32)).astype(BF)
    gain_sums = gain_sums + steps[1](order.tie(gain_sums))
    gain_sums = order.tie(gain_sums)
    gain_sums = gain_sums + steps[2](gain_sums)
    order.done(passed, hops[3], out_cross, finish(2, 1), outputs, gain_sums)

    low = order.tie(add_low(passed, hops[3]))
    crossed = x_swap(low)
    out_low = add_low(out_low, order.tie(out_cross))
    d_out = join(core, out_low, core_swap(out_low), [width])
    d_up = joined(2)
    gain_sums = order.tie(gain_sums)
    for step in steps[3:]:
        gain_sums = gain_sums + step(gain_sums)
    order.done(crossed, d_out[0], d_up, gain_sums)
    total = order.tie(add_low(low, crossed))
    d_qkv = join(core, total, core_swap(total), [q_width, kv_width, kv_width])

    gain_sums = lax.dynamic_slice_in_dim(gain_sums, fsdp * rows, rows, 1)
    return (
        outputs.reshape(inputs.shape),
        grad_inputs.reshape(inputs.shape),
        d_qkv[0],
        d_qkv[1],
        d_qkv[2],
        d_out[0],
        d_gate,
        d_up,
        d_down,
        gain_sums[0],
        gain_sums[1],
    )


def solution(mesh):
    token_spec, row_spec, gain_spec = P("fsdp", "seq", None), P("fsdp", None), P("fsdp")
    return jax.shard_map(
        shards,
        mesh=mesh,
        in_specs=(token_spec,) + (row_spec,) * 7 + (gain_spec,) * 2 + (token_spec,),
        out_specs=(token_spec,) * 2 + (row_spec,) * 7 + (gain_spec,) * 2,
        check_vma=False,
    )
```

```python
import functools
import math

import jax
import jax.numpy as jnp
from jax import lax
from jax.experimental import pallas as pl
from jax.experimental.pallas import tpu as pltpu
from jax.sharding import PartitionSpec as P

KVH = 8
HD = 64
BLOCK = 256
LINE = 4

EPSILON = 1e-05
THETA = 500000.0
LOG2E = 1.4426950408889634

BF = jnp.bfloat16
F32 = jnp.float32


def after(value, *others):
    return lax.optimization_barrier((value,) + others)[0]


def columns():
    return lax.axis_size("fsdp") // LINE


def z_next(value):
    cols = columns()
    count = lax.axis_size("fsdp")
    return lax.ppermute(value, "fsdp", [(i, (i + cols) % count) for i in range(count)])


def y_next(value):
    cols = columns()
    count = lax.axis_size("fsdp")
    return lax.ppermute(
        value, "fsdp", [(i, i // cols * cols + (i + 1) % cols) for i in range(count)]
    )


def seq_swap(value, bit):
    return lax.ppermute(value, "seq", [(i, i ^ bit) for i in range(lax.axis_size("seq"))])


def core_swap(value):
    return seq_swap(value, 1)


def x_swap(value):
    return seq_swap(value, 2)


def ring_gather(value, step, count):
    pieces = [value]
    for _ in range(count - 1):
        pieces.append(step(pieces[-1]))
    return pieces


def ring_scatter(part_of, step, count):
    total = None
    for j in list(range(1, count)) + [0]:
        total = part_of(j) if total is None else part_of(j) + total.astype(F32)
        if j:
            total = step(total.astype(BF))
    return total


def sum_steps():
    steps = []
    bit = 1
    while bit < lax.axis_size("seq"):
        steps.append(functools.partial(seq_swap, bit=bit))
        bit *= 2
    count = lax.axis_size("fsdp")
    bit = 1
    while bit < count:
        pairs = [(i, i ^ bit) for i in range(count)]
        steps.append(functools.partial(lax.ppermute, axis_name="fsdp", perm=pairs))
        bit *= 2
    return steps


def dot_nt(a, b):
    return lax.dot_general(a, b, (((1,), (1,)), ((), ())), preferred_element_type=F32)

def dot_nn(a, b):
    return jnp.dot(a, b, preferred_element_type=F32)


def attend_forward_kernel(parts, heads, kv, seq_ref, *refs):
    packs, outs = refs[:parts], refs[parts : 2 * parts]
    lse_ref, q_s, k_s, vt_s, o_s = refs[2 * parts :]
    tokens = packs[0].shape[0]
    seq = seq_ref[0]
    group = heads // kv
    for k in range(parts):
        rows = pl.ds(pl.multiple_of((seq ^ k) * tokens, tokens), tokens)
        q_s[rows, :] = packs[k][:, : heads * HD]
        for g in range(kv):
            lane = (heads + g) * HD
            k_s[g, rows, :] = packs[k][:, lane : lane + HD]
            lane = (heads + kv + g) * HD
            vt_s[g, :, rows] = packs[k][:, lane : lane + HD].T
    full = parts * tokens
    for g in range(kv):
        for i in range(full // BLOCK):
            keys = (i + 1) * BLOCK
            rows = slice(i * BLOCK, keys)
            for pair in range(group // 2):
                halves = []
                for h in (g * group + 2 * pair, g * group + 2 * pair + 1):
                    scores = dot_nt(k_s[g, :keys, :], q_s[rows, h * HD : (h + 1) * HD])
                    scores = scores * (HD**-0.5 * LOG2E)
                    top = jnp.max(scores, axis=0, keepdims=True)
                    powers = jnp.exp2(scores - top)
                    total = jnp.sum(powers, axis=0, keepdims=True)
                    halves.append(dot_nn(vt_s[g, :, :keys], powers.astype(BF)) / total)
                    lse_ref[h : h + 1, rows] = top + jnp.log2(total)
                lane = (g * group + 2 * pair) * HD
                o_s[rows, lane : lane + 2 * HD] = jnp.concatenate(halves, axis=0).T.astype(BF)
    for k in range(parts):
        rows = pl.ds(pl.multiple_of((seq ^ k) * tokens, tokens), tokens)
        outs[k][...] = o_s[rows, :]


def attend_forward(seq, packs, heads, kv):
    parts = len(packs)
    tokens = packs[0].shape[0]
    full = parts * tokens
    vmem = pl.BlockSpec(memory_space=pltpu.VMEM)
    flops = 4 * heads * full * full * HD * 5 // 8
    return pl.pallas_call(
        functools.partial(attend_forward_kernel, parts, heads, kv),
        out_shape=[jax.ShapeDtypeStruct((tokens, heads * HD), BF)] * parts
        + [jax.ShapeDtypeStruct((heads, full), F32)],
        in_specs=[pl.BlockSpec(memory_space=pltpu.SMEM)] + [vmem] * parts,
        out_specs=[vmem] * (parts + 1),
        scratch_shapes=[
            pltpu.VMEM((full, heads * HD), BF),
            pltpu.VMEM((kv, full, HD), BF),
            pltpu.VMEM((kv, HD, full), BF),
            pltpu.VMEM((full, heads * HD), BF),
        ],
        compiler_params=pltpu.CompilerParams(vmem_limit_bytes=48 * 2**20),
        cost_estimate=cost(flops * 4, 4 * 2**20),
        name="attend_forward",
    )(seq.reshape(1), *packs)


def attend_backward_kernel(parts, heads, kv, seq_ref, lse_ref, *refs):
    packs, grads, outs = refs[:parts], refs[parts : 2 * parts], refs[2 * parts : 3 * parts]
    q_s, k_s, kt_s, v_s, g_s, dq_s, dk_s, dv_s = refs[3 * parts :]
    tokens = packs[0].shape[0]
    seq = seq_ref[0]
    group = heads // kv
    for k in range(parts):
        rows = pl.ds(pl.multiple_of((seq ^ k) * tokens, tokens), tokens)
        q_s[rows, :] = packs[k][:, : heads * HD]
        g_s[rows, :] = grads[k][...]
        for g in range(kv):
            lane = (heads + g) * HD
            k_s[g, rows, :] = packs[k][:, lane : lane + HD]
            kt_s[g, :, rows] = packs[k][:, lane : lane + HD].T
            lane = (heads + kv + g) * HD
            v_s[g, rows, :] = packs[k][:, lane : lane + HD]
    full = parts * tokens
    dk_s[...] = jnp.zeros_like(dk_s)
    dv_s[...] = jnp.zeros_like(dv_s)
    for g in range(kv):
        for i in range(full // BLOCK):
            keys = (i + 1) * BLOCK
            rows = slice(i * BLOCK, keys)
            for pair in range(group // 2):
                halves = []
                for h in (g * group + 2 * pair, g * group + 2 * pair + 1):
                    query = q_s[rows, h * HD : (h + 1) * HD]
                    grad = g_s[rows, h * HD : (h + 1) * HD]
                    scores = dot_nt(k_s[g, :keys, :], query) * (HD**-0.5 * LOG2E)
                    probs = jnp.exp2(scores - lse_ref[h : h + 1, rows])
                    grad_probs = dot_nt(v_s[g, :keys, :], grad)
                    inner = jnp.sum(probs * grad_probs, axis=0, keepdims=True)
                    grad_scores = (probs * (grad_probs - inner)).astype(BF)
                    dv_s[g, :keys, :] += dot_nn(probs.astype(BF), grad)
                    dk_s[g, :keys, :] += dot_nn(grad_scores, query)
                    halves.append(dot_nn(kt_s[g, :, :keys], grad_scores) * HD**-0.5)
                lane = (g * group + 2 * pair) * HD
                dq_s[rows, lane : lane + 2 * HD] = jnp.concatenate(halves, axis=0).T.astype(BF)
    for k in range(parts):
        rows = pl.ds(pl.multiple_of((seq ^ k) * tokens, tokens), tokens)
        outs[k][:, : heads * HD] = dq_s[rows, :]
        for g in range(kv):
            lane = (heads + g) * HD
            outs[k][:, lane : lane + HD] = (dk_s[g, rows, :] * HD**-0.5).astype(BF)
            lane = (heads + kv + g) * HD
            outs[k][:, lane : lane + HD] = dv_s[g, rows, :].astype(BF)


def attend_backward(seq, lse, packs, grads, heads, kv):
    parts = len(packs)
    tokens = packs[0].shape[0]
    full = parts * tokens
    vmem = pl.BlockSpec(memory_space=pltpu.VMEM)
    flops = 10 * heads * full * full * HD * 5 // 8
    return pl.pallas_call(
        functools.partial(attend_backward_kernel, parts, heads, kv),
        out_shape=[jax.ShapeDtypeStruct(packs[0].shape, BF)] * parts,
        in_specs=[pl.BlockSpec(memory_space=pltpu.SMEM)] + [vmem] * (2 * parts + 1),
        out_specs=[vmem] * parts,
        scratch_shapes=[
            pltpu.VMEM((full, heads * HD), BF),
            pltpu.VMEM((kv, full, HD), BF),
            pltpu.VMEM((kv, HD, full), BF),
            pltpu.VMEM((kv, full, HD), BF),
            pltpu.VMEM((full, heads * HD), BF),
            pltpu.VMEM((full, heads * HD), BF),
            pltpu.VMEM((kv, full, HD), F32),
            pltpu.VMEM((kv, full, HD), F32),
        ],
        compiler_params=pltpu.CompilerParams(vmem_limit_bytes=48 * 2**20),
        cost_estimate=cost(flops * 4, 8 * 2**20),
        name="attend_backward",
    )(seq.reshape(1), lse, *packs, *grads)


def smem():
    return pl.BlockSpec(memory_space=pltpu.SMEM)


def params(mib=56):
    return pltpu.CompilerParams(vmem_limit_bytes=mib * 2**20)


def cost(flops, moved):
    return pl.CostEstimate(flops=flops // 8, bytes_accessed=moved // 8, transcendentals=0)


def place(shape, pieces, offsets, most=None):
    count = len(pieces)

    def kernel(at_ref, *refs):
        sources, target, sems = refs[:-2], refs[-2], refs[-1]
        copies = []
        for i, source in enumerate(sources):
            rows, width = source.shape
            rows = min(rows, most or rows)
            row = pl.multiple_of(at_ref[2 * i], rows)
            column = pl.multiple_of(at_ref[2 * i + 1], width)
            spot = target.at[pl.ds(row, rows), pl.ds(column, width)]
            copies.append(pltpu.make_async_copy(source.at[pl.ds(0, rows), :], spot, sems.at[i]))
            copies[-1].start()
        for copy in copies:
            copy.wait()

    moved = 2 * sum(piece.size * 2 for piece in pieces)
    return pl.pallas_call(
        kernel,
        out_shape=jax.ShapeDtypeStruct(shape, pieces[0].dtype),
        in_specs=[smem()] + [pl.BlockSpec(memory_space=pl.ANY)] * count,
        out_specs=pl.BlockSpec(memory_space=pltpu.HBM),
        scratch_shapes=[pltpu.SemaphoreType.DMA((count,))],
        compiler_params=params(16),
        cost_estimate=cost(0, moved),
        name="place",
    )(jnp.stack([jnp.int32(v) for pair in offsets for v in pair]), *pieces)


def turn(values, cos_table, sin_table):
    width = values.shape[1]
    lane = lax.broadcasted_iota(jnp.int32, values.shape, 1)
    swapped = jnp.where(
        lane % HD < HD // 2,
        pltpu.roll(values, width - HD // 2, 1),
        pltpu.roll(values, HD // 2, 1),
    )
    return values * cos_table + swapped * sin_table


def whole(shape):
    return pl.BlockSpec(shape, lambda n: (0,) * len(shape))


def project_in(seq, z, inputs, gain, groups, cos_table, sin_table, parts):
    tokens, width = inputs.shape
    tile = cos_table.shape[1]
    each = tile // parts
    pack = tile + 2 * each
    count = len(groups)
    depth = width // count

    def kernel(at_ref, in_ref, gain_ref, *refs):
        w_refs, (cos_ref, sin_ref, acts_ref), packs = refs[:count], refs[count : count + 3], refs[count + 3 :]
        step = pl.program_id(0)

        @pl.when(step == 0)
        def _():
            values = in_ref[...].astype(F32)
            scale = lax.rsqrt(jnp.mean(values * values, axis=-1, keepdims=True) + EPSILON)
            acts_ref[...] = (values * scale * gain_ref[...]).astype(BF)

        rows = None
        for j in range(count):
            lanes = pl.ds(pl.multiple_of((at_ref[1] + count - j) % count * depth, depth), depth)
            term = dot_nn(acts_ref[:, lanes], w_refs[j][...])
            rows = term if rows is None else rows + term
        turned = jnp.where(
            step == parts + 1, rows, turn(rows, cos_ref[...], sin_ref[...])
        ).astype(BF)
        seq_now = at_ref[0]
        for k in range(parts):

            @pl.when((seq_now ^ k) == step)
            def _():
                packs[k][:, :tile] = turned

            for d in range(parts):
                for which in range(2):

                    @pl.when(((seq_now ^ k) == d) & (step == parts + which))
                    def _():
                        lane = tile + which * each
                        packs[k][:, lane : lane + each] = turned[:, d * each : (d + 1) * each]

    return pl.pallas_call(
        kernel,
        grid=(parts + 2,),
        out_shape=[jax.ShapeDtypeStruct((tokens, width), BF)]
        + [jax.ShapeDtypeStruct((tokens, pack), BF)] * parts,
        in_specs=[smem(), whole((tokens, width)), whole((1, width))]
        + [pl.BlockSpec((depth, tile), lambda n: (0, n))] * count
        + [whole((tokens, tile))] * 2,
        out_specs=[whole((tokens, width))] + [whole((tokens, pack))] * parts,
        compiler_params=params(),
        cost_estimate=cost(2 * tokens * width * tile * (parts + 2), 2 * width * tile * (parts + 2)),
        name="project_in",
    )(jnp.stack([seq, z]), inputs, gain, *groups, cos_table, sin_table)


def project_out(seq, z, mixed, inputs, gain, groups):
    parts = len(mixed)
    tokens, width = inputs.shape
    each = mixed[0].shape[1]
    tile = width // parts
    count = len(groups)
    depth = parts * each // count

    def kernel(at_ref, *refs):
        parts_in, (in_ref, gain_ref) = refs[:parts], refs[parts : parts + 2]
        w_refs, (flat_ref, res_ref, acts_ref) = refs[parts + 2 : -3], refs[-3:]
        step = pl.program_id(0)

        @pl.when(step == 0)
        def _():
            for k in range(parts):
                lane = pl.multiple_of((at_ref[0] ^ k) * each, each)
                flat_ref[:, pl.ds(lane, each)] = parts_in[k][...]

        lanes = pl.ds(pl.multiple_of(step * tile, tile), tile)
        total = in_ref[:, lanes].astype(F32)
        for j in range(count):
            rows = pl.ds(pl.multiple_of((at_ref[1] + count - j) % count * depth, depth), depth)
            total = total + dot_nn(flat_ref[:, rows], w_refs[j][...])
        res_ref[:, lanes] = total

        @pl.when(step == parts - 1)
        def _():
            values = res_ref[...]
            scale = lax.rsqrt(jnp.mean(values * values, axis=-1, keepdims=True) + EPSILON)
            acts_ref[...] = (values * scale * gain_ref[...]).astype(BF)

    return pl.pallas_call(
        kernel,
        grid=(parts,),
        out_shape=[
            jax.ShapeDtypeStruct((tokens, parts * each), BF),
            jax.ShapeDtypeStruct((tokens, width), F32),
            jax.ShapeDtypeStruct((tokens, width), BF),
        ],
        in_specs=[smem()]
        + [whole((tokens, each))] * parts
        + [whole((tokens, width)), whole((1, width))]
        + [pl.BlockSpec((depth, tile), lambda n: (0, n))] * count,
        out_specs=[whole((tokens, parts * each)), whole((tokens, width)), whole((tokens, width))],
        compiler_params=params(),
        cost_estimate=cost(2 * tokens * width * parts * each, 2 * width * parts * each),
        name="project_out",
    )(jnp.stack([seq, z]), *mixed, inputs, gain, *groups)


def feed_forward(acts, grads, gate, up, down, begun=None):
    tokens, width = acts.shape
    hidden = gate.shape[0]
    tile = 256
    steps = hidden // tile
    kind = BF
    begun = [] if begun is None else list(begun)

    def kernel(a_ref, c_ref, g_ref, u_ref, d_ref, *refs):
        starts, (h_ref, gg_ref, gu_ref, o_ref, ga_ref, o_s, ga_s) = refs[:-7], refs[-7:]
        step = pl.program_id(0)

        @pl.when(step == 0)
        def _():
            if starts:
                o_s[...] = starts[0][...].astype(F32)
                ga_s[...] = starts[1][...].astype(F32)
            else:
                o_s[...] = jnp.zeros_like(o_s)
                ga_s[...] = jnp.zeros_like(ga_s)

        gate_act = dot_nt(a_ref[...], g_ref[...])
        up_act = dot_nt(a_ref[...], u_ref[...])
        grad_hidden = dot_nt(c_ref[...], d_ref[...])
        sigma = jax.nn.sigmoid(gate_act)
        silu = gate_act * sigma
        low = (silu * up_act).astype(BF)
        grad_gate = (grad_hidden * up_act * (sigma * (1.0 + gate_act * (1.0 - sigma)))).astype(BF)
        grad_up = (grad_hidden * silu).astype(BF)
        h_ref[...] = low
        gg_ref[...] = grad_gate
        gu_ref[...] = grad_up
        o_s[...] += dot_nn(low, d_ref[...])
        ga_s[...] += dot_nn(grad_gate, g_ref[...]) + dot_nn(grad_up, u_ref[...])

        @pl.when(step == steps - 1)
        def _():
            o_ref[...] = o_s[...].astype(kind)
            ga_ref[...] = ga_s[...].astype(kind)

    whole = pl.BlockSpec((tokens, width), lambda n: (0, 0))
    rows = pl.BlockSpec((tile, width), lambda n: (n, 0))
    lanes = pl.BlockSpec((tokens, tile), lambda n: (0, n))
    return pl.pallas_call(
        kernel,
        grid=(steps,),
        out_shape=[jax.ShapeDtypeStruct((tokens, hidden), BF)] * 3
        + [jax.ShapeDtypeStruct((tokens, width), kind)] * 2,
        in_specs=[whole, whole, rows, rows, rows] + [whole] * len(begun),
        out_specs=[lanes] * 3 + [whole] * 2,
        scratch_shapes=[pltpu.VMEM((tokens, width), F32)] * 2,
        compiler_params=params(),
        cost_estimate=cost(12 * tokens * width * hidden, 6 * width * hidden),
        name="feed_forward",
    )(acts, grads, gate, up, down, *begun)


def middle_back(seq, z, terms, residual, grad_out, gain, groups, parts):
    tokens, width = residual.shape
    tile = groups[0].shape[0]
    count = len(groups)
    assert count == parts

    def kernel(at_ref, t0_ref, t1_ref, res_ref, go_ref, gain_ref, *refs):
        w_refs, (gr_ref, low_ref, gg_ref), outs = refs[:count], refs[count : count + 3], refs[count + 3 :]
        grad = t0_ref[...].astype(F32) + t1_ref[...].astype(F32)
        values = res_ref[...]
        scale = lax.rsqrt(jnp.mean(values * values, axis=-1, keepdims=True) + EPSILON)
        weighted = grad * gain_ref[...]
        inner = jnp.mean(weighted * values, axis=-1, keepdims=True)
        result = go_ref[...].astype(F32) + scale * weighted - values * (scale**3 * inner)
        gr_ref[...] = result
        low_ref[...] = result.astype(BF)
        gg_ref[...] = jnp.sum(grad * values * scale, axis=0, keepdims=True)
        for j in range(count):
            part = dot_nt(low_ref[...], w_refs[j][...]).astype(BF)
            at = ((at_ref[1] + count - j) % count) ^ at_ref[0]
            for k in range(parts):

                @pl.when(at == k)
                def _():
                    outs[k][...] = part

    vmem = pl.BlockSpec(memory_space=pltpu.VMEM)
    return pl.pallas_call(
        kernel,
        out_shape=[
            jax.ShapeDtypeStruct((tokens, width), F32),
            jax.ShapeDtypeStruct((tokens, width), BF),
            jax.ShapeDtypeStruct((1, width), F32),
        ]
        + [jax.ShapeDtypeStruct((tokens, tile), BF)] * parts,
        in_specs=[smem()] + [vmem] * (5 + count),
        out_specs=[vmem] * (3 + parts),
        compiler_params=params(),
        cost_estimate=cost(2 * tokens * width * tile * parts, 2 * width * tile * parts + 8 * tokens * width),
        name="middle_back",
    )(jnp.stack([seq, z]), terms[0], terms[1], residual, grad_out, gain, *groups)


def unpack(seq, packs, cos_table, sin_table):
    parts = len(packs)
    tokens, tile = cos_table.shape
    each = tile // parts

    def kernel(seq_ref, *refs):
        ins, (cos_ref, sin_ref, out_ref) = refs[:parts], refs[parts:]
        for k in range(parts):
            at = seq_ref[0] ^ k
            queries = turn(ins[k][:, :tile].astype(F32), cos_ref[...], -sin_ref[...])
            out_ref[:, pl.ds(pl.multiple_of(at * tile, tile), tile)] = queries.astype(BF)
            keys = turn(
                ins[k][:, tile : tile + each].astype(F32), cos_ref[:, :each], -sin_ref[:, :each]
            )
            lane = pl.multiple_of(parts * tile + at * each, each)
            out_ref[:, pl.ds(lane, each)] = keys.astype(BF)
            lane = pl.multiple_of((parts + 1) * tile + at * each, each)
            out_ref[:, pl.ds(lane, each)] = ins[k][:, tile + each :]

    vmem = pl.BlockSpec(memory_space=pltpu.VMEM)
    return pl.pallas_call(
        kernel,
        out_shape=jax.ShapeDtypeStruct((tokens, (parts + 2) * tile), BF),
        in_specs=[smem()] + [vmem] * (parts + 2),
        out_specs=vmem,
        compiler_params=params(),
        cost_estimate=cost(0, 6 * 2**20),
        name="unpack",
    )(seq.reshape(1), *packs, cos_table, sin_table)


def inner_back(z, grad_qkv, groups, inputs, gain, grad_res):
    tokens, width = inputs.shape
    count = len(groups)
    depth = width // count

    def kernel(at_ref, gq_ref, *refs):
        w_refs, (in_ref, gain_ref, gr_ref, out_ref, gg_ref, grad_s) = refs[:count], refs[count:]
        for j in range(count):
            lanes = pl.ds(pl.multiple_of((at_ref[0] + count - j) % count * depth, depth), depth)
            grad_s[:, lanes] = dot_nt(gq_ref[...], w_refs[j][...])
        grad = grad_s[...]
        values = in_ref[...].astype(F32)
        scale = lax.rsqrt(jnp.mean(values * values, axis=-1, keepdims=True) + EPSILON)
        weighted = grad * gain_ref[...]
        inner = jnp.mean(weighted * values, axis=-1, keepdims=True)
        result = gr_ref[...] + scale * weighted - values * (scale**3 * inner)
        out_ref[...] = result.astype(BF)
        gg_ref[...] = jnp.sum(grad * values * scale, axis=0, keepdims=True)

    vmem = pl.BlockSpec(memory_space=pltpu.VMEM)
    return pl.pallas_call(
        kernel,
        out_shape=[jax.ShapeDtypeStruct((tokens, width), BF), jax.ShapeDtypeStruct((1, width), F32)],
        in_specs=[smem()] + [vmem] * (4 + count),
        out_specs=[vmem] * 2,
        scratch_shapes=[pltpu.VMEM((tokens, width), F32)],
        compiler_params=params(),
        cost_estimate=cost(2 * tokens * groups[0].size * count, 2 * groups[0].size * count),
        name="inner_back",
    )(z.reshape(1), grad_qkv, *groups, inputs, gain, grad_res)


def weight_grad(left, right, rows, blocks, half, adds=(), pieces=1):
    count = len(left)
    tokens = left[0].shape[0]
    width = right[0].shape[1] // 2
    total_rows = rows * len(blocks)
    piece = total_rows // pieces
    tile = math.gcd(math.gcd(rows, 512), piece)
    steps = rows // tile
    each = piece // tile

    def kernel(at_ref, *refs):
        lefts, rights = refs[:count], refs[count : 2 * count]
        extra, outs = refs[2 * count : -pieces], refs[-pieces:]
        total = None
        for l_ref, r_ref in zip(lefts, rights):
            term = lax.dot_general(
                l_ref[...], r_ref[...], (((0,), (0,)), ((), ())), preferred_element_type=F32
            )
            total = term if total is None else total + term
        for ref in extra:
            total = total + ref[...].astype(F32)
        total = total.astype(BF)
        for p, out in enumerate(outs):
            if pieces == 1:
                out[...] = total
            else:

                @pl.when(pl.program_id(0) // each == p)
                def _():
                    out[...] = total

    def spec_of(p):
        if pieces == 1:
            return pl.BlockSpec((tile, width), lambda n, at: (n, 0))
        return pl.BlockSpec((tile, width), lambda n, at: (jnp.clip(n - p * each, 0, each - 1), 0))

    spec = pltpu.PrefetchScalarGridSpec(
        num_scalar_prefetch=1,
        grid=(steps * len(blocks),),
        in_specs=[pl.BlockSpec((tokens, tile), lambda n, at: (0, at[1 + n]))] * count
        + [pl.BlockSpec((tokens, width), lambda n, at: (0, at[0]))] * count
        + [pl.BlockSpec((tile, width), lambda n, at: (n, 0))] * len(adds),
        out_specs=[spec_of(p) for p in range(pieces)],
    )
    at = [jnp.int32(half)]
    for block in blocks:
        at += [jnp.int32(block) * steps + i for i in range(steps)]
    outs = pl.pallas_call(
        kernel,
        grid_spec=spec,
        out_shape=[jax.ShapeDtypeStruct((piece, width), BF)] * pieces,
        compiler_params=params(),
        cost_estimate=cost(
            2 * tokens * count * total_rows * width, 2 * (tokens * count + total_rows) * width
        ),
        name="weight_grad",
    )(jnp.stack(at), *left, *right, *adds)
    return outs[0] if pieces == 1 else list(outs)


def row_grads(left, right, blocks, half, added, y, cuts):
    tokens = left.shape[0]
    width = right.shape[1] // 2
    rows = left.shape[1] // LINE
    each = rows // cuts
    count = len(blocks)

    def kernel(at_ref, l_ref, r_ref, add_ref, *refs):
        outs, total_s = refs[:-1], refs[-1]
        total = lax.dot_general(
            l_ref[...], r_ref[...], (((0,), (0,)), ((), ())), preferred_element_type=F32
        )
        total_s[...] = (total + add_ref[...].astype(F32)).astype(BF)
        for j in range(count):

            @pl.when(pl.program_id(0) == j)
            def _():
                for k in range(cuts):
                    start = pl.multiple_of((at_ref[1] + cuts - k) % cuts * each, each)
                    outs[j * cuts + k][...] = total_s[pl.ds(start, each), :]

    spec = pltpu.PrefetchScalarGridSpec(
        num_scalar_prefetch=1,
        grid=(count,),
        in_specs=[
            pl.BlockSpec((tokens, rows), lambda n, at: (0, at[2 + n])),
            pl.BlockSpec((tokens, width), lambda n, at: (0, at[0])),
            pl.BlockSpec((rows, width), lambda n, at: (n, 0)),
        ],
        out_specs=[pl.BlockSpec((each, width), lambda n, at: (0, 0))] * (count * cuts),
        scratch_shapes=[pltpu.VMEM((rows, width), BF)],
    )
    at = jnp.stack([jnp.int32(half), jnp.int32(y)] + [jnp.int32(b) for b in blocks])
    outs = pl.pallas_call(
        kernel,
        grid_spec=spec,
        out_shape=[jax.ShapeDtypeStruct((each, width), BF)] * (count * cuts),
        compiler_params=params(),
        cost_estimate=cost(2 * tokens * count * rows * width, 6 * count * rows * width),
        name="row_grads",
    )(at, left, right, added)
    return [outs[j * cuts : (j + 1) * cuts] for j in range(count)]


def join(core, mine, other, widths):
    rows, half = mine.shape
    tile = min(rows, 256)

    def kernel(core_ref, mine_ref, other_ref, *refs):
        outs, full = refs[:-1], refs[-1]
        target = outs[0] if len(outs) == 1 else full
        at = pl.multiple_of(core_ref[0] * half, half)
        target[:, pl.ds(at, half)] = mine_ref[...].astype(F32)
        at = pl.multiple_of((1 - core_ref[0]) * half, half)
        target[:, pl.ds(at, half)] = other_ref[...].astype(F32)
        if len(outs) > 1:
            lane = 0
            for out in outs:
                out[...] = full[:, lane : lane + out.shape[1]]
                lane += out.shape[1]

    def block(width):
        return pl.BlockSpec((tile, width), lambda n: (n, 0))

    return pl.pallas_call(
        kernel,
        grid=(rows // tile,),
        out_shape=[jax.ShapeDtypeStruct((rows, width), F32) for width in widths],
        in_specs=[smem(), block(half), block(half)],
        out_specs=[block(width) for width in widths],
        scratch_shapes=[pltpu.VMEM((tile, 2 * half) if len(widths) > 1 else (8, 128), F32)],
        compiler_params=params(),
        cost_estimate=cost(0, rows * half * 12),
        name="join",
    )(core.reshape(1), mine, other)
def half_of(array, which, axis=1):
    size = array.shape[axis] // 2
    return lax.dynamic_slice_in_dim(array, which * size, size, axis)


def join_halves(core, top, bottom):
    rows, half = top[0].shape
    tile = min(rows, 256)
    steps = rows // tile

    def kernel(core_ref, a_ref, b_ref, c_ref, d_ref, out):
        mine = pl.multiple_of(core_ref[0] * half, half)
        other = pl.multiple_of((1 - core_ref[0]) * half, half)
        upper = pl.program_id(0) < steps

        @pl.when(upper)
        def _():
            out[:, pl.ds(mine, half)] = a_ref[...].astype(F32)
            out[:, pl.ds(other, half)] = b_ref[...].astype(F32)

        @pl.when(jnp.logical_not(upper))
        def _():
            out[:, pl.ds(mine, half)] = c_ref[...].astype(F32)
            out[:, pl.ds(other, half)] = d_ref[...].astype(F32)

    first = pl.BlockSpec((tile, half), lambda n: (jnp.minimum(n, steps - 1), 0))
    second = pl.BlockSpec((tile, half), lambda n: (jnp.maximum(n - steps, 0), 0))
    return pl.pallas_call(
        kernel,
        grid=(2 * steps,),
        out_shape=jax.ShapeDtypeStruct((2 * rows, 2 * half), F32),
        in_specs=[smem(), first, first, second, second],
        out_specs=pl.BlockSpec((tile, 2 * half), lambda n: (n, 0)),
        compiler_params=params(),
        cost_estimate=cost(0, rows * half * 24),
        name="join_halves",
    )(core.reshape(1), *top, *bottom)


class Order:
    def __init__(self):
        self.marks = ()

    def tie(self, *values):
        if self.marks:
            values = lax.optimization_barrier(tuple(values) + self.marks)[: len(values)]
        return values[0] if len(values) == 1 else list(values)

    def done(self, *values):
        self.marks = tuple(values)


def y_hops(value):
    return ring_gather(value, y_next, columns())[1:]


def add_low(left, right):
    return (left.astype(F32) + right.astype(F32)).astype(BF)


def rope_tables(positions, repeat):
    frequency = THETA ** (-(jnp.arange(HD // 2, dtype=F32) * 2.0) / HD)
    angles = positions.astype(F32)[:, None] * frequency[None, :]
    cos, sin = jnp.cos(angles), jnp.sin(angles)
    return (
        jnp.tile(jnp.concatenate([cos, cos], axis=1), (1, repeat)),
        jnp.tile(jnp.concatenate([-sin, sin], axis=1), (1, repeat)),
    )


def exchange(packs):
    return [packs[0]] + [seq_swap(packs[k], k) for k in range(1, len(packs))]


def shards(
    inputs,
    query_weight,
    key_weight,
    value_weight,
    output_weight,
    gate_weight,
    up_weight,
    down_weight,
    gain_attn,
    gain_ffn,
    cotangent,
):
    seq_count, local_len, width = inputs.shape
    assert seq_count == 1
    tokens = local_len
    parts = lax.axis_size("seq")
    kv_local = KVH // parts
    cols = columns()
    seq = lax.axis_index("seq")
    core, side = seq % 2, seq // 2
    fsdp = lax.axis_index("fsdp")
    z, y = fsdp // cols, fsdp % cols
    q_width, kv_width = query_weight.shape[1], key_weight.shape[1]
    heads_local = q_width // HD // parts
    flat_in = inputs.reshape(tokens, width)
    grad_out = cotangent.reshape(tokens, width)

    qkv_shard = jnp.concatenate([query_weight, key_weight, value_weight], axis=1)
    rows = qkv_shard.shape[0]
    part, half = rows // 2, qkv_shard.shape[1] // 2
    positions = seq * local_len + jnp.arange(local_len)
    cos_table, sin_table = rope_tables(positions, kv_width // HD)
    order = Order()

    def swapped(pieces):
        return [core_swap(p) for p in pieces]

    def place_halves(pieces, others, whole_first=None):
        each = pieces[-1].shape[1]
        placed, offsets = [], []
        for k, (piece, other) in enumerate(zip(pieces, others)):
            row = (y - k) % cols * rows
            if k == 0 and whole_first is not None:
                placed.append(whole_first)
                offsets.append((row, 0))
            else:
                placed += [piece, other]
                offsets += [(row, core * each), (row, (1 - core) * each)]
        return place((rows * cols, 2 * each), placed, offsets)

    def place_quarters(pieces, others, sides, count, size, first):
        each = pieces[0].shape[1]
        placed, offsets = [], []
        for i, (piece, other) in enumerate(zip(pieces, others)):
            k, at = i // 2, sides[i % 2]
            row = first(k) * size + at * (size // 2)
            placed += [piece, other]
            offsets += [(row, core * each), (row, (1 - core) * each)]
        return place((size * count, 2 * each), placed, offsets)

    def line_row(k):
        return (y - k) % cols

    own = (gate_weight, up_weight, down_weight)
    far_rows = gate_weight.shape[0]
    far_part = far_rows // 4
    far_y, far_x = {}, {}

    def far_start(i, h):
        at = side * 2 * far_part + h * far_part
        return lax.dynamic_slice(own[i], (at, core * out_width), (far_part, out_width))

    out_width = width // 2
    far_starts = {(i, h): far_start(i, h) for i in range(3) for h in range(2)}

    def far_along_y(i, h):
        start = order.tie(far_starts[i, h]) if order.marks else far_starts[i, h]
        far_y[i, h] = y_hops(start)
        return far_y[i, h]

    def far_along_x(i, h):
        pieces = order.tie(*far_y[i, h], far_y[i, h][0])[:-1]
        far_x[i, h] = [x_swap(p) for p in pieces]
        return far_x[i, h]

    gains = jnp.concatenate([gain_attn, gain_ffn]).reshape(1, 2 * rows)
    start = half_of(qkv_shard, core)
    start = jnp.concatenate([start, jnp.pad(gains, ((0, 15), (0, half - 2 * rows)))], axis=0)
    out_half = half_of(output_weight, core)

    def quarter_of(piece):
        return lax.dynamic_slice_in_dim(piece, side * part, part, 0)

    def line_group(i):
        here = order.tie(line[i])
        placed, offsets = [], []
        row = y * rows
        if i:
            placed += [here, core_swap(here)]
            offsets += [(row, core * half), (row, (1 - core) * half)]
        else:
            placed.append(qkv_shard)
            offsets.append((row, 0))
        for k in range(1, cols):
            row = (y - k) % cols * rows
            if i < LINE - 1:
                for piece, at in ((beside[i][k - 1], side), (crossed[i][k - 1], 1 - side)):
                    piece = order.tie(piece)
                    placed += [piece, core_swap(piece)]
                    offsets += [
                        (row + at * part, core * half),
                        (row + at * part, (1 - core) * half),
                    ]
            else:
                piece = order.tie(beside[i][k - 1])
                placed += [piece, core_swap(piece)]
                offsets += [(row, core * half), (row, (1 - core) * half)]
        return place((rows * cols, 2 * half), placed, offsets, rows)

    line, beside, crossed, groups = [start], [], [], []
    for j in range(LINE):
        here = order.tie(line[j]) if j else line[j]
        if j + 1 < LINE:
            line.append(z_next(here))
            beside.append(y_hops(quarter_of(here)))
            marks = [line[j + 1]] + beside[j] + far_along_y(j // 2, j % 2)
        else:
            beside.append(y_hops(here))
            line_o = [out_half, z_next(order.tie(out_half))]
            grad_parts = [grad_out, z_next(order.tie(grad_out))]
            gains_near = jnp.concatenate([p[rows:, : 2 * rows] for p in line[:j]], axis=0)
            gains_far = y_hops(order.tie(gains_near))
            marks = beside[j] + [line_o[1]]
        if j:
            pieces = order.tie(*beside[j - 1], here)[:-1]
            crossed.append([x_swap(p) for p in pieces])
            marks += crossed[j - 1]
        if j > 1:
            groups.append(line_group(j - 2))
            marks.append(groups[-1])
        if j == 1:
            marks += [cos_table, sin_table] + list(far_starts.values())
        order.done(*marks)

    line_o.append(z_next(order.tie(line_o[1])))
    beside_o = [y_hops(order.tie(line_o[0])), y_hops(order.tie(line_o[1]))]
    groups += [line_group(LINE - 2), line_group(LINE - 1)]
    marks = far_along_x(0, 0)
    gain_full = jnp.zeros((2, width), BF)
    for j in range(LINE):
        for k in range(cols):
            if j == LINE - 1:
                g = line[j][rows] if k == 0 else beside[j][k - 1][rows]
                pair = g[: 2 * rows].reshape(2, rows)
            else:
                g = gains_near if k == 0 else gains_far[k - 1]
                pair = g[16 * j].reshape(2, rows)
            at = (((z - j) % LINE) * cols + (y - k) % cols) * rows
            gain_full = lax.dynamic_update_slice(gain_full, pair, (0, at))
    gain_one = gain_full[:1].astype(F32)
    gain_two = gain_full[1:].astype(F32)
    acts_one, *sent = project_in(seq, z, flat_in, gain_one, groups, cos_table, sin_table, parts)
    order.done(*sent, line_o[2], *beside_o[0], *beside_o[1], grad_parts[1], *marks)

    def out_swaps(j, *others):
        hops = order.tie(line_o[j], *beside_o[j], *others)[: cols]
        if j == 0:
            return [None] + hops[1:], [None] + swapped(hops[1:])
        return hops, swapped(hops)

    def out_group(pair, j):
        hops, others = pair
        first = 0 if j else 1
        tied = order.tie(*hops[first:], *others[first:])
        count = cols - first
        return place_halves(
            [None] * first + tied[:count],
            [None] * first + tied[count:],
            None if j else output_weight,
        )

    packs = exchange(order.tie(*sent))
    line_o.append(z_next(order.tie(line_o[2])))
    beside_o.append(y_hops(order.tie(line_o[2])))
    pairs = [out_swaps(j, packs[2]) for j in range(2)]
    grad_top = [z_next(order.tie(grad_parts[1], packs[2])[0][: tokens // 2])]
    swaps = [p for pair in pairs for p in pair[1][1:]]
    order.done(*packs, line_o[3], *beside_o[2], *swaps)

    beside_o.append(y_hops(order.tie(line_o[3])))
    grad_low = [z_next(order.tie(grad_parts[1])[tokens // 2 :])]
    pairs.append(out_swaps(2))
    *mixed_sent, log_totals = attend_forward(seq, order.tie(*packs), heads_local, kv_local)
    order.done(*mixed_sent, *beside_o[3], grad_top[0], grad_low[0])

    mixed = exchange(order.tie(*mixed_sent))
    pairs.append(out_swaps(3))
    out_groups = [out_group(pairs[j], j) for j in range(LINE - 1)]
    out_groups.append(place_halves(*pairs[3]))
    grad_top.append(z_next(order.tie(grad_top[0])))
    order.done(*mixed, *out_groups, grad_top[1])

    grad_low.append(z_next(order.tie(grad_low[0])))
    grad_parts += [jnp.concatenate(pair, axis=0) for pair in zip(grad_top, grad_low)]
    marks = far_along_y(1, 1) + far_along_x(0, 1) + [grad_low[1]]
    mixed_flat, residual, acts_two = project_out(
        seq, z, order.tie(*mixed), flat_in, gain_two, out_groups
    )
    order.done(acts_two, *marks)

    def far_place(i, *others):
        placed, offsets = [], []
        for k in range(cols - 1):
            for h in range(2):
                pieces = order.tie(far_y[i, h][k], far_x[i, h][k], *others)[:2]
                for piece, at in zip(pieces, (side, 1 - side)):
                    row = k * far_rows + at * 2 * far_part + h * far_part
                    placed += [piece, core_swap(piece)]
                    offsets += [(row, core * out_width), (row, (1 - core) * out_width)]
        return place((far_rows * (cols - 1), width), placed, offsets)

    acts_parts, far, near_done, far_done = [acts_two], [], [], [None] * LINE

    def run_near(j):
        near_done.append(feed_forward(order.tie(acts_parts[j]), grad_parts[j], *own))
        return near_done[j][3]

    def run_far(j):
        far_done[j] = feed_forward(order.tie(acts_parts[j]), grad_parts[j], *far, near_done[j][3:])
        return far_done[j][4]

    acts_parts.append(z_next(order.tie(acts_parts[0])))
    marks = far_along_y(2, 0) + far_along_y(2, 1) + far_along_x(1, 0) + far_along_x(1, 1)
    far.append(far_place(0))
    order.done(acts_parts[1], *marks, *far, run_near(0))
    acts_parts.append(z_next(order.tie(acts_parts[1])))
    marks = far_along_x(2, 0) + far_along_x(2, 1)
    far.append(far_place(1))
    order.done(acts_parts[2], *marks, *far, run_near(1))
    acts_parts.append(z_next(order.tie(acts_parts[2])))
    far.append(far_place(2))
    marks = [run_near(2), run_far(1)]
    order.done(acts_parts[3], *marks)

    passed = z_next(order.tie(far_done[1][4]))
    marks = [run_near(3), run_far(2)]
    order.done(passed, *marks)
    passed = z_next(order.tie(add_low(passed, far_done[2][4])))
    marks = [run_far(3), run_far(0)]
    order.done(passed, *marks)
    passed = z_next(order.tie(add_low(passed, far_done[3][4])))

    rights = (grad_parts, acts_parts, acts_parts)
    far_size = far_rows * (cols - 1)
    far_sent, far_total, own_sent = [None] * 3, {}, [None] * 3

    def of(done, which):
        return order.tie(*[d[which] for d in done])

    def send_far(i):
        far_sent[i] = weight_grad(of(far_done, i), rights[i], far_size, [0], 1 - core)
        return far_sent[i]

    def keep_far(i):
        return weight_grad(
            of(far_done, i), rights[i], far_size, [0], core, [far_sent[i]], 2 * (cols - 1)
        )

    def pass_far(i, kept, h):
        total = y_next(order.tie(kept[h]))
        for k in range(1, cols - 1):
            total = y_next(add_low(total, order.tie(kept[2 * k + h])))
        far_total[i, h] = total
        return total

    def send_own(i):
        own_sent[i] = weight_grad(of(near_done, i), rights[i], far_rows, [0], 1 - core)
        return own_sent[i]

    def keep_own(i):
        return weight_grad(of(near_done, i), rights[i], far_rows, [0], core, [own_sent[i]])

    first = send_far(0)
    far_sent[0] = core_swap(first)
    marks = [send_far(1), send_far(2)]
    kept = [keep_far(0)]
    order.done(passed, *kept[0], *marks)

    marks = [pass_far(0, kept[0], 0)]
    far_sent[1:] = [core_swap(order.tie(term)) for term in far_sent[1:]]
    ffn_parts = [d[3] for d in far_done]
    ffn_sum = z_next(order.tie(ffn_parts[1]))
    grad_res, grad_res_low, grad_gain_two, *grad_sent = middle_back(
        seq, z, order.tie(passed, far_done[0][4]), residual, grad_out, gain_two, out_groups, parts
    )
    order.done(*grad_sent, *far_sent[1:])

    grad_packs = exchange(order.tie(*grad_sent))
    kept.append(keep_far(1))
    first = send_own(0)
    order.done(*grad_packs, ffn_sum, *kept[1], first, *marks)

    marks = [pass_far(0, kept[0], 1)]
    later = [pass_far(1, kept[1], 0)]
    ffn_sum = z_next(order.tie(add_low(ffn_sum, ffn_parts[2])))
    back_sent = attend_backward(
        seq, log_totals, packs, order.tie(*grad_packs), heads_local, kv_local
    )
    order.done(*back_sent, *marks)

    line_order = list(range(1, LINE)) + [0]
    blocks = [(z - j) % LINE for j in line_order]
    line_rows = rows * cols
    back_packs = exchange(order.tie(*back_sent))
    own_sent[0] = core_swap(order.tie(own_sent[0]))
    out_left, out_right = order.tie(mixed_flat, grad_res_low)
    out_sent = weight_grad([out_left], [out_right], line_rows, blocks, 1 - core)
    kept.append(keep_far(2))
    own_low = [keep_own(0)]
    marks = [*later, *kept[2], own_low[0], out_sent]
    later = [pass_far(1, kept[1], 1)]
    order.done(*back_packs, *marks, ffn_sum)

    size = far_rows // 2
    sums = {}

    def along_x(i, h):
        low = add_low(order.tie(own_low[i])[h * size : (h + 1) * size], far_total[i, h])
        sums[i, h] = (low, x_swap(low))
        return sums[i, h][1]

    def finish(i, h):
        low, crossed = order.tie(*sums[i, h])
        total = add_low(low, crossed)
        sums[i, h] = (total, core_swap(total))
        return sums[i, h][1]

    def joined(i):
        pairs = order.tie(*sums[i, 0], *sums[i, 1])
        return join_halves(core, pairs[:2], pairs[2:])

    def along_y(terms):
        terms = order.tie(*terms, terms[0])[:-1]
        total = None
        for k in list(range(1, cols)) + [0]:
            total = terms[k] if total is None else add_low(y_next(total), terms[k])
        return total

    marks = [*later, along_x(0, 0)]
    later = [pass_far(2, kept[2], 0)]
    out_recv = core_swap(order.tie(out_sent))
    ffn_sum = z_next(order.tie(add_low(ffn_sum, ffn_parts[3])))
    grad_qkv = unpack(seq, order.tie(*back_packs), cos_table, sin_table)
    qkv_sent = weight_grad([acts_one], [grad_qkv], line_rows, blocks, 1 - core)
    out_terms = row_grads(out_left, out_right, blocks, core, out_recv, y, 1)
    out_terms = [t[0] for t in out_terms]
    marks.append(send_own(1))
    order.done(qkv_sent, ffn_sum, *out_terms, *marks)

    qkv_recv = core_swap(order.tie(qkv_sent))
    out_total = z_next(order.tie(out_terms[0]))
    own_sent[1] = core_swap(order.tie(own_sent[1]))
    marks = [*later, send_own(2), along_x(0, 1), finish(0, 0)]
    later = [pass_far(2, kept[2], 1)]
    own_low.append(keep_own(1))
    order.done(qkv_recv, out_total, own_low[1], *marks)

    out_total = z_next(order.tie(add_low(out_total, out_terms[1])))
    qkv_terms = row_grads(acts_one, grad_qkv, blocks, core, order.tie(qkv_recv), y, cols)
    own_sent[2] = core_swap(order.tie(own_sent[2]))
    marks = [*later, along_x(1, 0), own_sent[2], finish(0, 1)]
    order.done(*[t for terms in qkv_terms for t in terms], out_total, *marks)

    out_total = z_next(order.tie(add_low(out_total, out_terms[2])))
    hops = [along_y(qkv_terms[0]), along_y(qkv_terms[1])]
    own_low.append(keep_own(2))
    d_down = joined(0)
    marks = [along_x(1, 1), finish(1, 0)]
    order.done(hops[0], out_total, d_down, own_low[2], *marks)

    passed = z_next(order.tie(hops[0]))
    hops.append(along_y(qkv_terms[2]))
    grad_inputs, grad_gain_one = inner_back(z, order.tie(grad_qkv), groups, flat_in, gain_one, grad_res)
    out_total = order.tie(add_low(out_total, out_terms[3]))
    pieces = [
        lax.dynamic_slice_in_dim(out_total, (y - k) % cols * rows, rows, 0) for k in range(cols)
    ]
    out_low = along_y(pieces)
    marks = [out_low, along_x(2, 0), finish(1, 1), grad_inputs]
    order.done(passed, hops[1], *marks)

    passed = z_next(order.tie(add_low(passed, hops[1])))
    hops.append(along_y(qkv_terms[3]))
    gain_sums = jnp.concatenate([grad_gain_one, grad_gain_two], axis=0)
    steps = sum_steps()
    gain_sums = gain_sums + steps[0](order.tie(gain_sums))
    d_gate = joined(1)
    marks = [along_x(2, 1), finish(2, 0), d_gate, gain_sums]
    order.done(passed, hops[2], *marks)

    passed = z_next(order.tie(add_low(passed, hops[2])))
    out_cross = x_swap(order.tie(out_low))
    outputs = (residual + ffn_sum.astype(F32) + order.tie(ffn_parts[0]).astype(F32)).astype(BF)
    gain_sums = gain_sums + steps[1](order.tie(gain_sums))
    gain_sums = order.tie(gain_sums)
    gain_sums = gain_sums + steps[2](gain_sums)
    order.done(passed, hops[3], out_cross, finish(2, 1), outputs, gain_sums)

    low = order.tie(add_low(passed, hops[3]))
    crossed = x_swap(low)
    out_low = add_low(out_low, order.tie(out_cross))
    d_out = join(core, out_low, core_swap(out_low), [width])
    d_up = joined(2)
    gain_sums = order.tie(gain_sums)
    for step in steps[3:]:
        gain_sums = gain_sums + step(gain_sums)
    order.done(crossed, d_out[0], d_up, gain_sums)
    total = order.tie(add_low(low, crossed))
    d_qkv = join(core, total, core_swap(total), [q_width, kv_width, kv_width])

    gain_sums = lax.dynamic_slice_in_dim(gain_sums, fsdp * rows, rows, 1)
    return (
        outputs.reshape(inputs.shape),
        grad_inputs.reshape(inputs.shape),
        d_qkv[0],
        d_qkv[1],
        d_qkv[2],
        d_out[0],
        d_gate,
        d_up,
        d_down,
        gain_sums[0],
        gain_sums[1],
    )


def solution(mesh):
    token_spec, row_spec, gain_spec = P("fsdp", "seq", None), P("fsdp", None), P("fsdp")
    return jax.shard_map(
        shards,
        mesh=mesh,
        in_specs=(token_spec,) + (row_spec,) * 7 + (gain_spec,) * 2 + (token_spec,),
        out_specs=(token_spec,) * 2 + (row_spec,) * 7 + (gain_spec,) * 2,
        check_vma=False,
    )
```

```python
import functools
import math

import jax
import jax.numpy as jnp
from jax import lax
from jax.experimental import pallas as pl
from jax.experimental.pallas import tpu as pltpu
from jax.sharding import PartitionSpec as P

KVH = 8
HD = 64
BLOCK = 256
LINE = 4

EPSILON = 1e-05
THETA = 500000.0
LOG2E = 1.4426950408889634

BF = jnp.bfloat16
F32 = jnp.float32


def after(value, *others):
    return lax.optimization_barrier((value,) + others)[0]


def columns():
    return lax.axis_size("fsdp") // LINE


def z_next(value):
    cols = columns()
    count = lax.axis_size("fsdp")
    return lax.ppermute(value, "fsdp", [(i, (i + cols) % count) for i in range(count)])


def y_next(value):
    cols = columns()
    count = lax.axis_size("fsdp")
    return lax.ppermute(
        value, "fsdp", [(i, i // cols * cols + (i + 1) % cols) for i in range(count)]
    )


def seq_swap(value, bit):
    return lax.ppermute(value, "seq", [(i, i ^ bit) for i in range(lax.axis_size("seq"))])


def core_swap(value):
    return seq_swap(value, 1)


def x_swap(value):
    return seq_swap(value, 2)


def ring_gather(value, step, count):
    pieces = [value]
    for _ in range(count - 1):
        pieces.append(step(pieces[-1]))
    return pieces


def ring_scatter(part_of, step, count):
    total = None
    for j in list(range(1, count)) + [0]:
        total = part_of(j) if total is None else part_of(j) + total.astype(F32)
        if j:
            total = step(total.astype(BF))
    return total


def sum_steps():
    steps = []
    bit = 1
    while bit < lax.axis_size("seq"):
        steps.append(functools.partial(seq_swap, bit=bit))
        bit *= 2
    count = lax.axis_size("fsdp")
    bit = 1
    while bit < count:
        pairs = [(i, i ^ bit) for i in range(count)]
        steps.append(functools.partial(lax.ppermute, axis_name="fsdp", perm=pairs))
        bit *= 2
    return steps


def dot_nt(a, b):
    return lax.dot_general(a, b, (((1,), (1,)), ((), ())), preferred_element_type=F32)

def dot_nn(a, b):
    return jnp.dot(a, b, preferred_element_type=F32)


def attend_forward_kernel(parts, heads, kv, seq_ref, *refs):
    packs, outs = refs[:parts], refs[parts : 2 * parts]
    lse_ref, q_s, k_s, vt_s, o_s = refs[2 * parts :]
    tokens = packs[0].shape[0]
    seq = seq_ref[0]
    group = heads // kv
    for k in range(parts):
        rows = pl.ds(pl.multiple_of((seq ^ k) * tokens, tokens), tokens)
        q_s[rows, :] = packs[k][:, : heads * HD]
        for g in range(kv):
            lane = (heads + g) * HD
            k_s[g, rows, :] = packs[k][:, lane : lane + HD]
            lane = (heads + kv + g) * HD
            vt_s[g, :, rows] = packs[k][:, lane : lane + HD].T
    full = parts * tokens
    for g in range(kv):
        for i in range(full // BLOCK):
            keys = (i + 1) * BLOCK
            rows = slice(i * BLOCK, keys)
            for pair in range(group // 2):
                halves = []
                for h in (g * group + 2 * pair, g * group + 2 * pair + 1):
                    scores = dot_nt(k_s[g, :keys, :], q_s[rows, h * HD : (h + 1) * HD])
                    scores = scores * (HD**-0.5 * LOG2E)
                    top = jnp.max(scores, axis=0, keepdims=True)
                    powers = jnp.exp2(scores - top)
                    total = jnp.sum(powers, axis=0, keepdims=True)
                    halves.append(dot_nn(vt_s[g, :, :keys], powers.astype(BF)) / total)
                    lse_ref[h : h + 1, rows] = top + jnp.log2(total)
                lane = (g * group + 2 * pair) * HD
                o_s[rows, lane : lane + 2 * HD] = jnp.concatenate(halves, axis=0).T.astype(BF)
    for k in range(parts):
        rows = pl.ds(pl.multiple_of((seq ^ k) * tokens, tokens), tokens)
        outs[k][...] = o_s[rows, :]


def attend_forward(seq, packs, heads, kv):
    parts = len(packs)
    tokens = packs[0].shape[0]
    full = parts * tokens
    vmem = pl.BlockSpec(memory_space=pltpu.VMEM)
    flops = 4 * heads * full * full * HD * 5 // 8
    return pl.pallas_call(
        functools.partial(attend_forward_kernel, parts, heads, kv),
        out_shape=[jax.ShapeDtypeStruct((tokens, heads * HD), BF)] * parts
        + [jax.ShapeDtypeStruct((heads, full), F32)],
        in_specs=[pl.BlockSpec(memory_space=pltpu.SMEM)] + [vmem] * parts,
        out_specs=[vmem] * (parts + 1),
        scratch_shapes=[
            pltpu.VMEM((full, heads * HD), BF),
            pltpu.VMEM((kv, full, HD), BF),
            pltpu.VMEM((kv, HD, full), BF),
            pltpu.VMEM((full, heads * HD), BF),
        ],
        compiler_params=pltpu.CompilerParams(vmem_limit_bytes=48 * 2**20),
        cost_estimate=cost(flops * 4, 4 * 2**20),
        name="attend_forward",
    )(seq.reshape(1), *packs)


def attend_backward_kernel(parts, heads, kv, seq_ref, lse_ref, *refs):
    packs, grads, outs = refs[:parts], refs[parts : 2 * parts], refs[2 * parts : 3 * parts]
    q_s, k_s, kt_s, v_s, g_s, dq_s, dk_s, dv_s = refs[3 * parts :]
    tokens = packs[0].shape[0]
    seq = seq_ref[0]
    group = heads // kv
    for k in range(parts):
        rows = pl.ds(pl.multiple_of((seq ^ k) * tokens, tokens), tokens)
        q_s[rows, :] = packs[k][:, : heads * HD]
        g_s[rows, :] = grads[k][...]
        for g in range(kv):
            lane = (heads + g) * HD
            k_s[g, rows, :] = packs[k][:, lane : lane + HD]
            kt_s[g, :, rows] = packs[k][:, lane : lane + HD].T
            lane = (heads + kv + g) * HD
            v_s[g, rows, :] = packs[k][:, lane : lane + HD]
    full = parts * tokens
    dk_s[...] = jnp.zeros_like(dk_s)
    dv_s[...] = jnp.zeros_like(dv_s)
    for g in range(kv):
        for i in range(full // BLOCK):
            keys = (i + 1) * BLOCK
            rows = slice(i * BLOCK, keys)
            for pair in range(group // 2):
                halves = []
                for h in (g * group + 2 * pair, g * group + 2 * pair + 1):
                    query = q_s[rows, h * HD : (h + 1) * HD]
                    grad = g_s[rows, h * HD : (h + 1) * HD]
                    scores = dot_nt(k_s[g, :keys, :], query) * (HD**-0.5 * LOG2E)
                    probs = jnp.exp2(scores - lse_ref[h : h + 1, rows])
                    grad_probs = dot_nt(v_s[g, :keys, :], grad)
                    inner = jnp.sum(probs * grad_probs, axis=0, keepdims=True)
                    grad_scores = (probs * (grad_probs - inner)).astype(BF)
                    dv_s[g, :keys, :] += dot_nn(probs.astype(BF), grad)
                    dk_s[g, :keys, :] += dot_nn(grad_scores, query)
                    halves.append(dot_nn(kt_s[g, :, :keys], grad_scores) * HD**-0.5)
                lane = (g * group + 2 * pair) * HD
                dq_s[rows, lane : lane + 2 * HD] = jnp.concatenate(halves, axis=0).T.astype(BF)
    for k in range(parts):
        rows = pl.ds(pl.multiple_of((seq ^ k) * tokens, tokens), tokens)
        outs[k][:, : heads * HD] = dq_s[rows, :]
        for g in range(kv):
            lane = (heads + g) * HD
            outs[k][:, lane : lane + HD] = (dk_s[g, rows, :] * HD**-0.5).astype(BF)
            lane = (heads + kv + g) * HD
            outs[k][:, lane : lane + HD] = dv_s[g, rows, :].astype(BF)


def attend_backward(seq, lse, packs, grads, heads, kv):
    parts = len(packs)
    tokens = packs[0].shape[0]
    full = parts * tokens
    vmem = pl.BlockSpec(memory_space=pltpu.VMEM)
    flops = 10 * heads * full * full * HD * 5 // 8
    return pl.pallas_call(
        functools.partial(attend_backward_kernel, parts, heads, kv),
        out_shape=[jax.ShapeDtypeStruct(packs[0].shape, BF)] * parts,
        in_specs=[pl.BlockSpec(memory_space=pltpu.SMEM)] + [vmem] * (2 * parts + 1),
        out_specs=[vmem] * parts,
        scratch_shapes=[
            pltpu.VMEM((full, heads * HD), BF),
            pltpu.VMEM((kv, full, HD), BF),
            pltpu.VMEM((kv, HD, full), BF),
            pltpu.VMEM((kv, full, HD), BF),
            pltpu.VMEM((full, heads * HD), BF),
            pltpu.VMEM((full, heads * HD), BF),
            pltpu.VMEM((kv, full, HD), F32),
            pltpu.VMEM((kv, full, HD), F32),
        ],
        compiler_params=pltpu.CompilerParams(vmem_limit_bytes=48 * 2**20),
        cost_estimate=cost(flops * 4, 8 * 2**20),
        name="attend_backward",
    )(seq.reshape(1), lse, *packs, *grads)


def smem():
    return pl.BlockSpec(memory_space=pltpu.SMEM)


def params(mib=56):
    return pltpu.CompilerParams(vmem_limit_bytes=mib * 2**20)


def cost(flops, moved):
    return pl.CostEstimate(flops=flops // 8, bytes_accessed=moved // 8, transcendentals=0)


def place(shape, pieces, offsets, most=None):
    count = len(pieces)

    def kernel(at_ref, *refs):
        sources, target, sems = refs[:-2], refs[-2], refs[-1]
        copies = []
        for i, source in enumerate(sources):
            rows, width = source.shape
            rows = min(rows, most or rows)
            row = pl.multiple_of(at_ref[2 * i], rows)
            column = pl.multiple_of(at_ref[2 * i + 1], width)
            spot = target.at[pl.ds(row, rows), pl.ds(column, width)]
            copies.append(pltpu.make_async_copy(source.at[pl.ds(0, rows), :], spot, sems.at[i]))
            copies[-1].start()
        for copy in copies:
            copy.wait()

    moved = 2 * sum(piece.size * 2 for piece in pieces)
    return pl.pallas_call(
        kernel,
        out_shape=jax.ShapeDtypeStruct(shape, pieces[0].dtype),
        in_specs=[smem()] + [pl.BlockSpec(memory_space=pl.ANY)] * count,
        out_specs=pl.BlockSpec(memory_space=pl.ANY),
        scratch_shapes=[pltpu.SemaphoreType.DMA((count,))],
        compiler_params=params(60),
        cost_estimate=cost(0, moved),
        name="place",
    )(jnp.stack([jnp.int32(v) for pair in offsets for v in pair]), *pieces)


def turn(values, cos_table, sin_table):
    width = values.shape[1]
    lane = lax.broadcasted_iota(jnp.int32, values.shape, 1)
    swapped = jnp.where(
        lane % HD < HD // 2,
        pltpu.roll(values, width - HD // 2, 1),
        pltpu.roll(values, HD // 2, 1),
    )
    return values * cos_table + swapped * sin_table


def whole(shape):
    return pl.BlockSpec(shape, lambda n: (0,) * len(shape))


def project_in(seq, z, inputs, gain, groups, cos_table, sin_table, parts):
    tokens, width = inputs.shape
    tile = cos_table.shape[1]
    each = tile // parts
    pack = tile + 2 * each
    count = len(groups)
    depth = width // count

    def kernel(at_ref, in_ref, gain_ref, *refs):
        w_refs, (cos_ref, sin_ref, acts_ref), packs = refs[:count], refs[count : count + 3], refs[count + 3 :]
        step = pl.program_id(0)

        @pl.when(step == 0)
        def _():
            values = in_ref[...].astype(F32)
            scale = lax.rsqrt(jnp.mean(values * values, axis=-1, keepdims=True) + EPSILON)
            acts_ref[...] = (values * scale * gain_ref[...]).astype(BF)

        rows = None
        for j in range(count):
            lanes = pl.ds(pl.multiple_of((at_ref[1] + count - j) % count * depth, depth), depth)
            term = dot_nn(acts_ref[:, lanes], w_refs[j][...])
            rows = term if rows is None else rows + term
        turned = jnp.where(
            step == parts + 1, rows, turn(rows, cos_ref[...], sin_ref[...])
        ).astype(BF)
        seq_now = at_ref[0]
        for k in range(parts):

            @pl.when((seq_now ^ k) == step)
            def _():
                packs[k][:, :tile] = turned

            for d in range(parts):
                for which in range(2):

                    @pl.when(((seq_now ^ k) == d) & (step == parts + which))
                    def _():
                        lane = tile + which * each
                        packs[k][:, lane : lane + each] = turned[:, d * each : (d + 1) * each]

    return pl.pallas_call(
        kernel,
        grid=(parts + 2,),
        out_shape=[jax.ShapeDtypeStruct((tokens, width), BF)]
        + [jax.ShapeDtypeStruct((tokens, pack), BF)] * parts,
        in_specs=[smem(), whole((tokens, width)), whole((1, width))]
        + [pl.BlockSpec((depth, tile), lambda n: (0, n))] * count
        + [whole((tokens, tile))] * 2,
        out_specs=[whole((tokens, width))] + [whole((tokens, pack))] * parts,
        compiler_params=params(),
        cost_estimate=cost(2 * tokens * width * tile * (parts + 2), 2 * width * tile * (parts + 2)),
        name="project_in",
    )(jnp.stack([seq, z]), inputs, gain, *groups, cos_table, sin_table)


def project_out(seq, z, mixed, inputs, gain, groups):
    parts = len(mixed)
    tokens, width = inputs.shape
    each = mixed[0].shape[1]
    tile = width // parts
    count = len(groups)
    depth = parts * each // count

    def kernel(at_ref, *refs):
        parts_in, (in_ref, gain_ref) = refs[:parts], refs[parts : parts + 2]
        w_refs, (flat_ref, res_ref, acts_ref) = refs[parts + 2 : -3], refs[-3:]
        step = pl.program_id(0)

        @pl.when(step == 0)
        def _():
            for k in range(parts):
                lane = pl.multiple_of((at_ref[0] ^ k) * each, each)
                flat_ref[:, pl.ds(lane, each)] = parts_in[k][...]

        lanes = pl.ds(pl.multiple_of(step * tile, tile), tile)
        total = in_ref[:, lanes].astype(F32)
        for j in range(count):
            rows = pl.ds(pl.multiple_of((at_ref[1] + count - j) % count * depth, depth), depth)
            total = total + dot_nn(flat_ref[:, rows], w_refs[j][...])
        res_ref[:, lanes] = total

        @pl.when(step == parts - 1)
        def _():
            values = res_ref[...]
            scale = lax.rsqrt(jnp.mean(values * values, axis=-1, keepdims=True) + EPSILON)
            acts_ref[...] = (values * scale * gain_ref[...]).astype(BF)

    return pl.pallas_call(
        kernel,
        grid=(parts,),
        out_shape=[
            jax.ShapeDtypeStruct((tokens, parts * each), BF),
            jax.ShapeDtypeStruct((tokens, width), F32),
            jax.ShapeDtypeStruct((tokens, width), BF),
        ],
        in_specs=[smem()]
        + [whole((tokens, each))] * parts
        + [whole((tokens, width)), whole((1, width))]
        + [pl.BlockSpec((depth, tile), lambda n: (0, n))] * count,
        out_specs=[whole((tokens, parts * each)), whole((tokens, width)), whole((tokens, width))],
        compiler_params=params(),
        cost_estimate=cost(2 * tokens * width * parts * each, 2 * width * parts * each),
        name="project_out",
    )(jnp.stack([seq, z]), *mixed, inputs, gain, *groups)


def feed_forward(acts, grads, gate, up, down, begun=None):
    tokens, width = acts.shape
    hidden = gate.shape[0]
    tile = 256
    steps = hidden // tile
    kind = BF
    begun = [] if begun is None else list(begun)

    def kernel(a_ref, c_ref, g_ref, u_ref, d_ref, *refs):
        starts, (h_ref, gg_ref, gu_ref, o_ref, ga_ref, o_s, ga_s) = refs[:-7], refs[-7:]
        step = pl.program_id(0)

        @pl.when(step == 0)
        def _():
            if starts:
                o_s[...] = starts[0][...].astype(F32)
                ga_s[...] = starts[1][...].astype(F32)
            else:
                o_s[...] = jnp.zeros_like(o_s)
                ga_s[...] = jnp.zeros_like(ga_s)

        gate_act = dot_nt(a_ref[...], g_ref[...])
        up_act = dot_nt(a_ref[...], u_ref[...])
        grad_hidden = dot_nt(c_ref[...], d_ref[...])
        sigma = jax.nn.sigmoid(gate_act)
        silu = gate_act * sigma
        low = (silu * up_act).astype(BF)
        grad_gate = (grad_hidden * up_act * (sigma * (1.0 + gate_act * (1.0 - sigma)))).astype(BF)
        grad_up = (grad_hidden * silu).astype(BF)
        h_ref[...] = low
        gg_ref[...] = grad_gate
        gu_ref[...] = grad_up
        o_s[...] += dot_nn(low, d_ref[...])
        ga_s[...] += dot_nn(grad_gate, g_ref[...]) + dot_nn(grad_up, u_ref[...])

        @pl.when(step == steps - 1)
        def _():
            o_ref[...] = o_s[...].astype(kind)
            ga_ref[...] = ga_s[...].astype(kind)

    whole = pl.BlockSpec((tokens, width), lambda n: (0, 0))
    rows = pl.BlockSpec((tile, width), lambda n: (n, 0))
    lanes = pl.BlockSpec((tokens, tile), lambda n: (0, n))
    return pl.pallas_call(
        kernel,
        grid=(steps,),
        out_shape=[jax.ShapeDtypeStruct((tokens, hidden), BF)] * 3
        + [jax.ShapeDtypeStruct((tokens, width), kind)] * 2,
        in_specs=[whole, whole, rows, rows, rows] + [whole] * len(begun),
        out_specs=[lanes] * 3 + [whole] * 2,
        scratch_shapes=[pltpu.VMEM((tokens, width), F32)] * 2,
        compiler_params=params(),
        cost_estimate=cost(12 * tokens * width * hidden, 6 * width * hidden),
        name="feed_forward",
    )(acts, grads, gate, up, down, *begun)


def middle_back(seq, z, terms, residual, grad_out, gain, groups, parts):
    tokens, width = residual.shape
    tile = groups[0].shape[0]
    count = len(groups)
    assert count == parts

    def kernel(at_ref, t0_ref, t1_ref, res_ref, go_ref, gain_ref, *refs):
        w_refs, (gr_ref, low_ref, gg_ref), outs = refs[:count], refs[count : count + 3], refs[count + 3 :]
        grad = t0_ref[...].astype(F32) + t1_ref[...].astype(F32)
        values = res_ref[...]
        scale = lax.rsqrt(jnp.mean(values * values, axis=-1, keepdims=True) + EPSILON)
        weighted = grad * gain_ref[...]
        inner = jnp.mean(weighted * values, axis=-1, keepdims=True)
        result = go_ref[...].astype(F32) + scale * weighted - values * (scale**3 * inner)
        gr_ref[...] = result
        low_ref[...] = result.astype(BF)
        gg_ref[...] = jnp.sum(grad * values * scale, axis=0, keepdims=True)
        for j in range(count):
            part = dot_nt(low_ref[...], w_refs[j][...]).astype(BF)
            at = ((at_ref[1] + count - j) % count) ^ at_ref[0]
            for k in range(parts):

                @pl.when(at == k)
                def _():
                    outs[k][...] = part

    vmem = pl.BlockSpec(memory_space=pltpu.VMEM)
    return pl.pallas_call(
        kernel,
        out_shape=[
            jax.ShapeDtypeStruct((tokens, width), F32),
            jax.ShapeDtypeStruct((tokens, width), BF),
            jax.ShapeDtypeStruct((1, width), F32),
        ]
        + [jax.ShapeDtypeStruct((tokens, tile), BF)] * parts,
        in_specs=[smem()] + [vmem] * (5 + count),
        out_specs=[vmem] * (3 + parts),
        compiler_params=params(),
        cost_estimate=cost(2 * tokens * width * tile * parts, 2 * width * tile * parts + 8 * tokens * width),
        name="middle_back",
    )(jnp.stack([seq, z]), terms[0], terms[1], residual, grad_out, gain, *groups)


def unpack(seq, packs, cos_table, sin_table):
    parts = len(packs)
    tokens, tile = cos_table.shape
    each = tile // parts

    def kernel(seq_ref, *refs):
        ins, (cos_ref, sin_ref, out_ref) = refs[:parts], refs[parts:]
        for k in range(parts):
            at = seq_ref[0] ^ k
            queries = turn(ins[k][:, :tile].astype(F32), cos_ref[...], -sin_ref[...])
            out_ref[:, pl.ds(pl.multiple_of(at * tile, tile), tile)] = queries.astype(BF)
            keys = turn(
                ins[k][:, tile : tile + each].astype(F32), cos_ref[:, :each], -sin_ref[:, :each]
            )
            lane = pl.multiple_of(parts * tile + at * each, each)
            out_ref[:, pl.ds(lane, each)] = keys.astype(BF)
            lane = pl.multiple_of((parts + 1) * tile + at * each, each)
            out_ref[:, pl.ds(lane, each)] = ins[k][:, tile + each :]

    vmem = pl.BlockSpec(memory_space=pltpu.VMEM)
    return pl.pallas_call(
        kernel,
        out_shape=jax.ShapeDtypeStruct((tokens, (parts + 2) * tile), BF),
        in_specs=[smem()] + [vmem] * (parts + 2),
        out_specs=vmem,
        compiler_params=params(),
        cost_estimate=cost(0, 6 * 2**20),
        name="unpack",
    )(seq.reshape(1), *packs, cos_table, sin_table)


def inner_back(z, grad_qkv, groups, inputs, gain, grad_res):
    tokens, width = inputs.shape
    count = len(groups)
    depth = width // count

    def kernel(at_ref, gq_ref, *refs):
        w_refs, (in_ref, gain_ref, gr_ref, out_ref, gg_ref, grad_s) = refs[:count], refs[count:]
        for j in range(count):
            lanes = pl.ds(pl.multiple_of((at_ref[0] + count - j) % count * depth, depth), depth)
            grad_s[:, lanes] = dot_nt(gq_ref[...], w_refs[j][...])
        grad = grad_s[...]
        values = in_ref[...].astype(F32)
        scale = lax.rsqrt(jnp.mean(values * values, axis=-1, keepdims=True) + EPSILON)
        weighted = grad * gain_ref[...]
        inner = jnp.mean(weighted * values, axis=-1, keepdims=True)
        result = gr_ref[...] + scale * weighted - values * (scale**3 * inner)
        out_ref[...] = result.astype(BF)
        gg_ref[...] = jnp.sum(grad * values * scale, axis=0, keepdims=True)

    vmem = pl.BlockSpec(memory_space=pltpu.VMEM)
    return pl.pallas_call(
        kernel,
        out_shape=[jax.ShapeDtypeStruct((tokens, width), BF), jax.ShapeDtypeStruct((1, width), F32)],
        in_specs=[smem()] + [vmem] * (4 + count),
        out_specs=[vmem] * 2,
        scratch_shapes=[pltpu.VMEM((tokens, width), F32)],
        compiler_params=params(),
        cost_estimate=cost(2 * tokens * groups[0].size * count, 2 * groups[0].size * count),
        name="inner_back",
    )(z.reshape(1), grad_qkv, *groups, inputs, gain, grad_res)


def weight_grad(left, right, rows, blocks, half, adds=(), pieces=1):
    count = len(left)
    tokens = left[0].shape[0]
    width = right[0].shape[1] // 2
    total_rows = rows * len(blocks)
    piece = total_rows // pieces
    tile = math.gcd(math.gcd(rows, 512), piece)
    steps = rows // tile
    each = piece // tile

    def kernel(at_ref, *refs):
        lefts, rights = refs[:count], refs[count : 2 * count]
        extra, outs = refs[2 * count : -pieces], refs[-pieces:]
        total = None
        for l_ref, r_ref in zip(lefts, rights):
            term = lax.dot_general(
                l_ref[...], r_ref[...], (((0,), (0,)), ((), ())), preferred_element_type=F32
            )
            total = term if total is None else total + term
        for ref in extra:
            total = total + ref[...].astype(F32)
        total = total.astype(BF)
        for p, out in enumerate(outs):
            if pieces == 1:
                out[...] = total
            else:

                @pl.when(pl.program_id(0) // each == p)
                def _():
                    out[...] = total

    def spec_of(p):
        if pieces == 1:
            return pl.BlockSpec((tile, width), lambda n, at: (n, 0))
        return pl.BlockSpec((tile, width), lambda n, at: (jnp.clip(n - p * each, 0, each - 1), 0))

    spec = pltpu.PrefetchScalarGridSpec(
        num_scalar_prefetch=1,
        grid=(steps * len(blocks),),
        in_specs=[pl.BlockSpec((tokens, tile), lambda n, at: (0, at[1 + n]))] * count
        + [pl.BlockSpec((tokens, width), lambda n, at: (0, at[0]))] * count
        + [pl.BlockSpec((tile, width), lambda n, at: (n, 0))] * len(adds),
        out_specs=[spec_of(p) for p in range(pieces)],
    )
    at = [jnp.int32(half)]
    for block in blocks:
        at += [jnp.int32(block) * steps + i for i in range(steps)]
    outs = pl.pallas_call(
        kernel,
        grid_spec=spec,
        out_shape=[jax.ShapeDtypeStruct((piece, width), BF)] * pieces,
        compiler_params=params(),
        cost_estimate=cost(
            2 * tokens * count * total_rows * width, 2 * (tokens * count + total_rows) * width
        ),
        name="weight_grad",
    )(jnp.stack(at), *left, *right, *adds)
    return outs[0] if pieces == 1 else list(outs)


def row_grads(left, right, blocks, half, added, y, cuts):
    tokens = left.shape[0]
    width = right.shape[1] // 2
    rows = left.shape[1] // LINE
    each = rows // cuts
    count = len(blocks)

    def kernel(at_ref, l_ref, r_ref, add_ref, *refs):
        outs, total_s = refs[:-1], refs[-1]
        total = lax.dot_general(
            l_ref[...], r_ref[...], (((0,), (0,)), ((), ())), preferred_element_type=F32
        )
        total_s[...] = (total + add_ref[...].astype(F32)).astype(BF)
        for j in range(count):

            @pl.when(pl.program_id(0) == j)
            def _():
                for k in range(cuts):
                    start = pl.multiple_of((at_ref[1] + cuts - k) % cuts * each, each)
                    outs[j * cuts + k][...] = total_s[pl.ds(start, each), :]

    spec = pltpu.PrefetchScalarGridSpec(
        num_scalar_prefetch=1,
        grid=(count,),
        in_specs=[
            pl.BlockSpec((tokens, rows), lambda n, at: (0, at[2 + n])),
            pl.BlockSpec((tokens, width), lambda n, at: (0, at[0])),
            pl.BlockSpec((rows, width), lambda n, at: (n, 0)),
        ],
        out_specs=[pl.BlockSpec((each, width), lambda n, at: (0, 0))] * (count * cuts),
        scratch_shapes=[pltpu.VMEM((rows, width), BF)],
    )
    at = jnp.stack([jnp.int32(half), jnp.int32(y)] + [jnp.int32(b) for b in blocks])
    outs = pl.pallas_call(
        kernel,
        grid_spec=spec,
        out_shape=[jax.ShapeDtypeStruct((each, width), BF)] * (count * cuts),
        compiler_params=params(),
        cost_estimate=cost(2 * tokens * count * rows * width, 6 * count * rows * width),
        name="row_grads",
    )(at, left, right, added)
    return [outs[j * cuts : (j + 1) * cuts] for j in range(count)]


def join(core, mine, other, widths):
    rows, half = mine.shape
    tile = min(rows, 256)

    def kernel(core_ref, mine_ref, other_ref, *refs):
        outs, full = refs[:-1], refs[-1]
        target = outs[0] if len(outs) == 1 else full
        at = pl.multiple_of(core_ref[0] * half, half)
        target[:, pl.ds(at, half)] = mine_ref[...].astype(F32)
        at = pl.multiple_of((1 - core_ref[0]) * half, half)
        target[:, pl.ds(at, half)] = other_ref[...].astype(F32)
        if len(outs) > 1:
            lane = 0
            for out in outs:
                out[...] = full[:, lane : lane + out.shape[1]]
                lane += out.shape[1]

    def block(width):
        return pl.BlockSpec((tile, width), lambda n: (n, 0))

    return pl.pallas_call(
        kernel,
        grid=(rows // tile,),
        out_shape=[jax.ShapeDtypeStruct((rows, width), F32) for width in widths],
        in_specs=[smem(), block(half), block(half)],
        out_specs=[block(width) for width in widths],
        scratch_shapes=[pltpu.VMEM((tile, 2 * half) if len(widths) > 1 else (8, 128), F32)],
        compiler_params=params(),
        cost_estimate=cost(0, rows * half * 12),
        name="join",
    )(core.reshape(1), mine, other)
def half_of(array, which, axis=1):
    size = array.shape[axis] // 2
    return lax.dynamic_slice_in_dim(array, which * size, size, axis)


def join_halves(core, top, bottom):
    rows, half = top[0].shape
    tile = min(rows, 256)
    steps = rows // tile

    def kernel(core_ref, a_ref, b_ref, c_ref, d_ref, out):
        mine = pl.multiple_of(core_ref[0] * half, half)
        other = pl.multiple_of((1 - core_ref[0]) * half, half)
        upper = pl.program_id(0) < steps

        @pl.when(upper)
        def _():
            out[:, pl.ds(mine, half)] = a_ref[...].astype(F32)
            out[:, pl.ds(other, half)] = b_ref[...].astype(F32)

        @pl.when(jnp.logical_not(upper))
        def _():
            out[:, pl.ds(mine, half)] = c_ref[...].astype(F32)
            out[:, pl.ds(other, half)] = d_ref[...].astype(F32)

    first = pl.BlockSpec((tile, half), lambda n: (jnp.minimum(n, steps - 1), 0))
    second = pl.BlockSpec((tile, half), lambda n: (jnp.maximum(n - steps, 0), 0))
    return pl.pallas_call(
        kernel,
        grid=(2 * steps,),
        out_shape=jax.ShapeDtypeStruct((2 * rows, 2 * half), F32),
        in_specs=[smem(), first, first, second, second],
        out_specs=pl.BlockSpec((tile, 2 * half), lambda n: (n, 0)),
        compiler_params=params(),
        cost_estimate=cost(0, rows * half * 24),
        name="join_halves",
    )(core.reshape(1), *top, *bottom)


class Order:
    def __init__(self):
        self.marks = ()

    def tie(self, *values):
        if self.marks:
            values = lax.optimization_barrier(tuple(values) + self.marks)[: len(values)]
        return values[0] if len(values) == 1 else list(values)

    def done(self, *values):
        self.marks = tuple(values)


def y_hops(value):
    return ring_gather(value, y_next, columns())[1:]


def add_low(left, right):
    return (left.astype(F32) + right.astype(F32)).astype(BF)


def rope_tables(positions, repeat):
    frequency = THETA ** (-(jnp.arange(HD // 2, dtype=F32) * 2.0) / HD)
    angles = positions.astype(F32)[:, None] * frequency[None, :]
    cos, sin = jnp.cos(angles), jnp.sin(angles)
    return (
        jnp.tile(jnp.concatenate([cos, cos], axis=1), (1, repeat)),
        jnp.tile(jnp.concatenate([-sin, sin], axis=1), (1, repeat)),
    )


def exchange(packs):
    return [packs[0]] + [seq_swap(packs[k], k) for k in range(1, len(packs))]


def shards(
    inputs,
    query_weight,
    key_weight,
    value_weight,
    output_weight,
    gate_weight,
    up_weight,
    down_weight,
    gain_attn,
    gain_ffn,
    cotangent,
):
    seq_count, local_len, width = inputs.shape
    assert seq_count == 1
    tokens = local_len
    parts = lax.axis_size("seq")
    kv_local = KVH // parts
    cols = columns()
    seq = lax.axis_index("seq")
    core, side = seq % 2, seq // 2
    fsdp = lax.axis_index("fsdp")
    z, y = fsdp // cols, fsdp % cols
    q_width, kv_width = query_weight.shape[1], key_weight.shape[1]
    heads_local = q_width // HD // parts
    flat_in = inputs.reshape(tokens, width)
    grad_out = cotangent.reshape(tokens, width)

    qkv_shard = jnp.concatenate([query_weight, key_weight, value_weight], axis=1)
    rows = qkv_shard.shape[0]
    part, half = rows // 2, qkv_shard.shape[1] // 2
    positions = seq * local_len + jnp.arange(local_len)
    cos_table, sin_table = rope_tables(positions, kv_width // HD)
    order = Order()

    def swapped(pieces):
        return [core_swap(p) for p in pieces]

    def place_halves(pieces, others, whole_first=None):
        each = pieces[-1].shape[1]
        placed, offsets = [], []
        for k, (piece, other) in enumerate(zip(pieces, others)):
            row = (y - k) % cols * rows
            if k == 0 and whole_first is not None:
                placed.append(whole_first)
                offsets.append((row, 0))
            else:
                placed += [piece, other]
                offsets += [(row, core * each), (row, (1 - core) * each)]
        return place((rows * cols, 2 * each), placed, offsets)

    def place_quarters(pieces, others, sides, count, size, first):
        each = pieces[0].shape[1]
        placed, offsets = [], []
        for i, (piece, other) in enumerate(zip(pieces, others)):
            k, at = i // 2, sides[i % 2]
            row = first(k) * size + at * (size // 2)
            placed += [piece, other]
            offsets += [(row, core * each), (row, (1 - core) * each)]
        return place((size * count, 2 * each), placed, offsets)

    def line_row(k):
        return (y - k) % cols

    own = (gate_weight, up_weight, down_weight)
    far_rows = gate_weight.shape[0]
    far_part = far_rows // 4
    far_y, far_x = {}, {}

    def far_start(i, h):
        at = side * 2 * far_part + h * far_part
        return lax.dynamic_slice(own[i], (at, core * out_width), (far_part, out_width))

    out_width = width // 2
    far_starts = {(i, h): far_start(i, h) for i in range(3) for h in range(2)}

    def far_along_y(i, h):
        start = order.tie(far_starts[i, h]) if order.marks else far_starts[i, h]
        far_y[i, h] = y_hops(start)
        return far_y[i, h]

    def far_along_x(i, h):
        pieces = order.tie(*far_y[i, h], far_y[i, h][0])[:-1]
        far_x[i, h] = [x_swap(p) for p in pieces]
        return far_x[i, h]

    gains = jnp.concatenate([gain_attn, gain_ffn]).reshape(1, 2 * rows)
    start = half_of(qkv_shard, core)
    start = jnp.concatenate([start, jnp.pad(gains, ((0, 15), (0, half - 2 * rows)))], axis=0)
    out_half = half_of(output_weight, core)

    def quarter_of(piece):
        return lax.dynamic_slice_in_dim(piece, side * part, part, 0)

    def line_group(i):
        here = order.tie(line[i])
        placed, offsets = [], []
        row = y * rows
        if i:
            placed += [here, core_swap(here)]
            offsets += [(row, core * half), (row, (1 - core) * half)]
        else:
            placed.append(qkv_shard)
            offsets.append((row, 0))
        for k in range(1, cols):
            row = (y - k) % cols * rows
            if i < LINE - 1:
                for piece, at in ((beside[i][k - 1], side), (crossed[i][k - 1], 1 - side)):
                    piece = order.tie(piece)
                    placed += [piece, core_swap(piece)]
                    offsets += [
                        (row + at * part, core * half),
                        (row + at * part, (1 - core) * half),
                    ]
            else:
                piece = order.tie(beside[i][k - 1])
                placed += [piece, core_swap(piece)]
                offsets += [(row, core * half), (row, (1 - core) * half)]
        return place((rows * cols, 2 * half), placed, offsets, rows)

    line, beside, crossed, groups = [start], [], [], []
    for j in range(LINE):
        here = order.tie(line[j]) if j else line[j]
        if j + 1 < LINE:
            line.append(z_next(here))
            beside.append(y_hops(quarter_of(here)))
            marks = [line[j + 1]] + beside[j] + far_along_y(j // 2, j % 2)
        else:
            beside.append(y_hops(here))
            line_o = [out_half, z_next(order.tie(out_half))]
            grad_parts = [grad_out, z_next(order.tie(grad_out))]
            gains_near = jnp.concatenate([p[rows:, : 2 * rows] for p in line[:j]], axis=0)
            gains_far = y_hops(order.tie(gains_near))
            marks = beside[j] + [line_o[1]]
        if j:
            pieces = order.tie(*beside[j - 1], here)[:-1]
            crossed.append([x_swap(p) for p in pieces])
            marks += crossed[j - 1]
        if j > 1:
            groups.append(line_group(j - 2))
            marks.append(groups[-1])
        if j == 1:
            marks += [cos_table, sin_table] + list(far_starts.values())
        order.done(*marks)

    line_o.append(z_next(order.tie(line_o[1])))
    beside_o = [y_hops(order.tie(line_o[0])), y_hops(order.tie(line_o[1]))]
    groups += [line_group(LINE - 2), line_group(LINE - 1)]
    marks = far_along_x(0, 0)
    gain_full = jnp.zeros((2, width), BF)
    for j in range(LINE):
        for k in range(cols):
            if j == LINE - 1:
                g = line[j][rows] if k == 0 else beside[j][k - 1][rows]
                pair = g[: 2 * rows].reshape(2, rows)
            else:
                g = gains_near if k == 0 else gains_far[k - 1]
                pair = g[16 * j].reshape(2, rows)
            at = (((z - j) % LINE) * cols + (y - k) % cols) * rows
            gain_full = lax.dynamic_update_slice(gain_full, pair, (0, at))
    gain_one = gain_full[:1].astype(F32)
    gain_two = gain_full[1:].astype(F32)
    acts_one, *sent = project_in(seq, z, flat_in, gain_one, groups, cos_table, sin_table, parts)
    order.done(*sent, line_o[2], *beside_o[0], *beside_o[1], grad_parts[1], *marks)

    def out_swaps(j, *others):
        hops = order.tie(line_o[j], *beside_o[j], *others)[: cols]
        if j == 0:
            return [None] + hops[1:], [None] + swapped(hops[1:])
        return hops, swapped(hops)

    def out_group(pair, j):
        hops, others = pair
        first = 0 if j else 1
        tied = order.tie(*hops[first:], *others[first:])
        count = cols - first
        return place_halves(
            [None] * first + tied[:count],
            [None] * first + tied[count:],
            None if j else output_weight,
        )

    packs = exchange(order.tie(*sent))
    line_o.append(z_next(order.tie(line_o[2])))
    beside_o.append(y_hops(order.tie(line_o[2])))
    pairs = [out_swaps(j, packs[2]) for j in range(2)]
    grad_top = [z_next(order.tie(grad_parts[1], packs[2])[0][: tokens // 2])]
    swaps = [p for pair in pairs for p in pair[1][1:]]
    order.done(*packs, line_o[3], *beside_o[2], *swaps)

    beside_o.append(y_hops(order.tie(line_o[3])))
    grad_low = [z_next(order.tie(grad_parts[1])[tokens // 2 :])]
    pairs.append(out_swaps(2))
    *mixed_sent, log_totals = attend_forward(seq, order.tie(*packs), heads_local, kv_local)
    order.done(*mixed_sent, *beside_o[3], grad_top[0], grad_low[0])

    mixed = exchange(order.tie(*mixed_sent))
    pairs.append(out_swaps(3))
    out_groups = [out_group(pairs[j], j) for j in range(LINE - 1)]
    out_groups.append(place_halves(*pairs[3]))
    grad_top.append(z_next(order.tie(grad_top[0])))
    order.done(*mixed, *out_groups, grad_top[1])

    grad_low.append(z_next(order.tie(grad_low[0])))
    grad_parts += [jnp.concatenate(pair, axis=0) for pair in zip(grad_top, grad_low)]
    marks = far_along_y(1, 1) + far_along_x(0, 1) + [grad_low[1]]
    mixed_flat, residual, acts_two = project_out(
        seq, z, order.tie(*mixed), flat_in, gain_two, out_groups
    )
    order.done(acts_two, *marks)

    def far_place(i, *others):
        placed, offsets = [], []
        for k in range(cols - 1):
            for h in range(2):
                pieces = order.tie(far_y[i, h][k], far_x[i, h][k], *others)[:2]
                for piece, at in zip(pieces, (side, 1 - side)):
                    row = k * far_rows + at * 2 * far_part + h * far_part
                    placed += [piece, core_swap(piece)]
                    offsets += [(row, core * out_width), (row, (1 - core) * out_width)]
        return place((far_rows * (cols - 1), width), placed, offsets)

    acts_parts, far, near_done, far_done = [acts_two], [], [], [None] * LINE

    def run_near(j):
        near_done.append(feed_forward(order.tie(acts_parts[j]), grad_parts[j], *own))
        return near_done[j][3]

    def run_far(j):
        far_done[j] = feed_forward(order.tie(acts_parts[j]), grad_parts[j], *far, near_done[j][3:])
        return far_done[j][4]

    acts_parts.append(z_next(order.tie(acts_parts[0])))
    marks = far_along_y(2, 0) + far_along_y(2, 1) + far_along_x(1, 0) + far_along_x(1, 1)
    far.append(far_place(0))
    order.done(acts_parts[1], *marks, *far, run_near(0))
    acts_parts.append(z_next(order.tie(acts_parts[1])))
    marks = far_along_x(2, 0) + far_along_x(2, 1)
    far.append(far_place(1))
    order.done(acts_parts[2], *marks, *far, run_near(1))
    acts_parts.append(z_next(order.tie(acts_parts[2])))
    far.append(far_place(2))
    marks = [run_near(2), run_far(1)]
    order.done(acts_parts[3], *marks)

    passed = z_next(order.tie(far_done[1][4]))
    marks = [run_near(3), run_far(2)]
    order.done(passed, *marks)
    passed = z_next(order.tie(add_low(passed, far_done[2][4])))
    marks = [run_far(3), run_far(0)]
    order.done(passed, *marks)
    passed = z_next(order.tie(add_low(passed, far_done[3][4])))

    rights = (grad_parts, acts_parts, acts_parts)
    far_size = far_rows * (cols - 1)
    far_sent, far_total, own_sent = [None] * 3, {}, [None] * 3

    def of(done, which):
        return order.tie(*[d[which] for d in done])

    def send_far(i):
        far_sent[i] = weight_grad(of(far_done, i), rights[i], far_size, [0], 1 - core)
        return far_sent[i]

    def keep_far(i):
        return weight_grad(
            of(far_done, i), rights[i], far_size, [0], core, [far_sent[i]], 2 * (cols - 1)
        )

    def pass_far(i, kept, h):
        total = y_next(order.tie(kept[h]))
        for k in range(1, cols - 1):
            total = y_next(add_low(total, order.tie(kept[2 * k + h])))
        far_total[i, h] = total
        return total

    def send_own(i):
        own_sent[i] = weight_grad(of(near_done, i), rights[i], far_rows, [0], 1 - core)
        return own_sent[i]

    def keep_own(i):
        return weight_grad(of(near_done, i), rights[i], far_rows, [0], core, [own_sent[i]])

    first = send_far(0)
    far_sent[0] = core_swap(first)
    marks = [send_far(1), send_far(2)]
    kept = [keep_far(0)]
    order.done(passed, *kept[0], *marks)

    marks = [pass_far(0, kept[0], 0)]
    far_sent[1:] = [core_swap(order.tie(term)) for term in far_sent[1:]]
    ffn_parts = [d[3] for d in far_done]
    ffn_sum = z_next(order.tie(ffn_parts[1]))
    grad_res, grad_res_low, grad_gain_two, *grad_sent = middle_back(
        seq, z, order.tie(passed, far_done[0][4]), residual, grad_out, gain_two, out_groups, parts
    )
    order.done(*grad_sent, *far_sent[1:])

    grad_packs = exchange(order.tie(*grad_sent))
    kept.append(keep_far(1))
    first = send_own(0)
    order.done(*grad_packs, ffn_sum, *kept[1], first, *marks)

    marks = [pass_far(0, kept[0], 1)]
    later = [pass_far(1, kept[1], 0)]
    ffn_sum = z_next(order.tie(add_low(ffn_sum, ffn_parts[2])))
    back_sent = attend_backward(
        seq, log_totals, packs, order.tie(*grad_packs), heads_local, kv_local
    )
    order.done(*back_sent, *marks)

    line_order = list(range(1, LINE)) + [0]
    blocks = [(z - j) % LINE for j in line_order]
    line_rows = rows * cols
    back_packs = exchange(order.tie(*back_sent))
    own_sent[0] = core_swap(order.tie(own_sent[0]))
    out_left, out_right = order.tie(mixed_flat, grad_res_low)
    out_sent = weight_grad([out_left], [out_right], line_rows, blocks, 1 - core)
    kept.append(keep_far(2))
    own_low = [keep_own(0)]
    marks = [*later, *kept[2], own_low[0], out_sent]
    later = [pass_far(1, kept[1], 1)]
    order.done(*back_packs, *marks, ffn_sum)

    size = far_rows // 2
    sums = {}

    def along_x(i, h):
        low = add_low(order.tie(own_low[i])[h * size : (h + 1) * size], far_total[i, h])
        sums[i, h] = (low, x_swap(low))
        return sums[i, h][1]

    def finish(i, h):
        low, crossed = order.tie(*sums[i, h])
        total = add_low(low, crossed)
        sums[i, h] = (total, core_swap(total))
        return sums[i, h][1]

    def joined(i):
        pairs = order.tie(*sums[i, 0], *sums[i, 1])
        return join_halves(core, pairs[:2], pairs[2:])

    def along_y(terms):
        terms = order.tie(*terms, terms[0])[:-1]
        total = None
        for k in list(range(1, cols)) + [0]:
            total = terms[k] if total is None else add_low(y_next(total), terms[k])
        return total

    marks = [*later, along_x(0, 0)]
    later = [pass_far(2, kept[2], 0)]
    out_recv = core_swap(order.tie(out_sent))
    ffn_sum = z_next(order.tie(add_low(ffn_sum, ffn_parts[3])))
    grad_qkv = unpack(seq, order.tie(*back_packs), cos_table, sin_table)
    qkv_sent = weight_grad([acts_one], [grad_qkv], line_rows, blocks, 1 - core)
    out_terms = row_grads(out_left, out_right, blocks, core, out_recv, y, 1)
    out_terms = [t[0] for t in out_terms]
    marks.append(send_own(1))
    order.done(qkv_sent, ffn_sum, *out_terms, *marks)

    qkv_recv = core_swap(order.tie(qkv_sent))
    out_total = z_next(order.tie(out_terms[0]))
    own_sent[1] = core_swap(order.tie(own_sent[1]))
    marks = [*later, send_own(2), along_x(0, 1), finish(0, 0)]
    later = [pass_far(2, kept[2], 1)]
    own_low.append(keep_own(1))
    order.done(qkv_recv, out_total, own_low[1], *marks)

    out_total = z_next(order.tie(add_low(out_total, out_terms[1])))
    qkv_terms = row_grads(acts_one, grad_qkv, blocks, core, order.tie(qkv_recv), y, cols)
    own_sent[2] = core_swap(order.tie(own_sent[2]))
    marks = [*later, along_x(1, 0), own_sent[2], finish(0, 1)]
    order.done(*[t for terms in qkv_terms for t in terms], out_total, *marks)

    out_total = z_next(order.tie(add_low(out_total, out_terms[2])))
    hops = [along_y(qkv_terms[0]), along_y(qkv_terms[1])]
    own_low.append(keep_own(2))
    d_down = joined(0)
    marks = [along_x(1, 1), finish(1, 0)]
    order.done(hops[0], out_total, d_down, own_low[2], *marks)

    passed = z_next(order.tie(hops[0]))
    hops.append(along_y(qkv_terms[2]))
    grad_inputs, grad_gain_one = inner_back(z, order.tie(grad_qkv), groups, flat_in, gain_one, grad_res)
    out_total = order.tie(add_low(out_total, out_terms[3]))
    pieces = [
        lax.dynamic_slice_in_dim(out_total, (y - k) % cols * rows, rows, 0) for k in range(cols)
    ]
    out_low = along_y(pieces)
    marks = [out_low, along_x(2, 0), finish(1, 1), grad_inputs]
    order.done(passed, hops[1], *marks)

    passed = z_next(order.tie(add_low(passed, hops[1])))
    hops.append(along_y(qkv_terms[3]))
    gain_sums = jnp.concatenate([grad_gain_one, grad_gain_two], axis=0)
    steps = sum_steps()
    gain_sums = gain_sums + steps[0](order.tie(gain_sums))
    d_gate = joined(1)
    marks = [along_x(2, 1), finish(2, 0), d_gate, gain_sums]
    order.done(passed, hops[2], *marks)

    passed = z_next(order.tie(add_low(passed, hops[2])))
    out_cross = x_swap(order.tie(out_low))
    outputs = (residual + ffn_sum.astype(F32) + order.tie(ffn_parts[0]).astype(F32)).astype(BF)
    gain_sums = gain_sums + steps[1](order.tie(gain_sums))
    gain_sums = order.tie(gain_sums)
    gain_sums = gain_sums + steps[2](gain_sums)
    order.done(passed, hops[3], out_cross, finish(2, 1), outputs, gain_sums)

    low = order.tie(add_low(passed, hops[3]))
    crossed = x_swap(low)
    out_low = add_low(out_low, order.tie(out_cross))
    d_out = join(core, out_low, core_swap(out_low), [width])
    d_up = joined(2)
    gain_sums = order.tie(gain_sums)
    for step in steps[3:]:
        gain_sums = gain_sums + step(gain_sums)
    order.done(crossed, d_out[0], d_up, gain_sums)
    total = order.tie(add_low(low, crossed))
    d_qkv = join(core, total, core_swap(total), [q_width, kv_width, kv_width])

    gain_sums = lax.dynamic_slice_in_dim(gain_sums, fsdp * rows, rows, 1)
    return (
        outputs.reshape(inputs.shape),
        grad_inputs.reshape(inputs.shape),
        d_qkv[0],
        d_qkv[1],
        d_qkv[2],
        d_out[0],
        d_gate,
        d_up,
        d_down,
        gain_sums[0],
        gain_sums[1],
    )


def solution(mesh):
    token_spec, row_spec, gain_spec = P("fsdp", "seq", None), P("fsdp", None), P("fsdp")
    return jax.shard_map(
        shards,
        mesh=mesh,
        in_specs=(token_spec,) + (row_spec,) * 7 + (gain_spec,) * 2 + (token_spec,),
        out_specs=(token_spec,) * 2 + (row_spec,) * 7 + (gain_spec,) * 2,
        check_vma=False,
    )
```
